32 devices in a mesh: dp: 4 (over z), seq: 8 (over y, x, core).
Axes of the slice: x: 2, y: 2, z: 4, core: 2. Of those that a mesh axis runs over, the one named last changes fastest.
Arguments:
- tokens: bfloat16 [4, 1024, 896], P('dp', 'seq'), may hold values from -6 to 6
- retrieved: bfloat16 [4, 16, 2, 128, 896], P('dp', 'seq'), may hold values from -6 to 6
- span_doc: int32 [4, 16], P('dp', 'seq'), may hold values from 0 to 3
- neigh_doc: int32 [4, 16, 2], P('dp', 'seq'), may hold values from 0 to 3
- cotangent: bfloat16 [4, 1024, 896], P('dp', 'seq'), may hold values from -6 to 6
- dec_gain: bfloat16 [2, 2, 896], P(None, None, ('dp', 'seq')), may hold values from 0.5 to 1.5
- dec_qkv: bfloat16 [2, 896, 2688], P(None, ('dp', 'seq')), may hold values from -0.1875 to 0.1875
- dec_out: bfloat16 [2, 896, 896], P(None, ('dp', 'seq')), may hold values from -1.5 to 1.5
- dec_in: bfloat16 [2, 896, 3584], P(None, ('dp', 'seq')), may hold values from -0.1875 to 0.1875
- dec_down: bfloat16 [2, 3584, 896], P(None, ('dp', 'seq')), may hold values from -0.09375 to 0.09375
- cca_gain: bfloat16 [896], P(('dp', 'seq')), may hold values from 0.5 to 1.5
- cca_q: bfloat16 [896, 896], P(('dp', 'seq')), may hold values from -0.1875 to 0.1875
- cca_kv: bfloat16 [896, 1792], P(('dp', 'seq')), may hold values from -0.1875 to 0.1875
- cca_out: bfloat16 [896, 896], P(('dp', 'seq')), may hold values from -1.5 to 1.5
- enc_gain: bfloat16 [2, 896], P(None, ('dp', 'seq')), may hold values from 0.5 to 1.5
- enc_in: bfloat16 [2, 896, 3584], P(None, ('dp', 'seq')), may hold values from -0.1875 to 0.1875
- enc_down: bfloat16 [2, 3584, 896], P(None, ('dp', 'seq')), may hold values from -0.09375 to 0.09375
- enc_final: bfloat16 [896], P(('dp', 'seq')), may hold values from 0.5 to 1.5
Outputs:
- result: bfloat16 [4, 1024, 896], P('dp', 'seq')
- tokens_grad: float32 [4, 1024, 896], P('dp', 'seq')
- dec_gain_grad: float32 [2, 2, 896], P(None, None, ('dp', 'seq'))
- dec_qkv_grad: float32 [2, 896, 2688], P(None, ('dp', 'seq'))
- dec_out_grad: float32 [2, 896, 896], P(None, ('dp', 'seq'))
- dec_in_grad: float32 [2, 896, 3584], P(None, ('dp', 'seq'))
- dec_down_grad: float32 [2, 3584, 896], P(None, None, ('dp', 'seq'))
- cca_gain_grad: float32 [896], P(('dp', 'seq'))
- cca_q_grad: float32 [896, 896], P(('dp', 'seq'))
- cca_kv_grad: float32 [896, 1792], P(('dp', 'seq'))
- cca_out_grad: float32 [896, 896], P(('dp', 'seq'))
- enc_gain_grad: float32 [2, 896], P(None, ('dp', 'seq'))
- enc_in_grad: float32 [2, 896, 3584], P(None, ('dp', 'seq'))
- enc_down_grad: float32 [2, 3584, 896], P(None, None, ('dp', 'seq'))
- enc_final_grad: float32 [896], P(('dp', 'seq'))
The draws below stay inside these ranges and needn't reach their ends.
All inputs are finite; a program needn't handle non-finite values.
Results may differ from the reference program's by a relative error of at most 0.023.
Values may be sent and summed in bfloat16 or wider, within the bound.
A program may use at most 768 MiB of HBM per device.

```python
import jax
import jax.numpy as jnp
from jax import lax

D = 896
HEADS = 14
HEAD = 64
FF = 3584
SPAN = 64
NEIGH = 2
RET = 128
ENC_LAYERS = 2
DEC_LAYERS = 2
BATCH = 4
SEQLEN = 1024
SPANS = 16


def place_ends(result, stream_key, smallest, largest):
    longest = result.shape.index(max(result.shape))
    spots = []
    for shift in (0, 1):
        where = [jax.random.randint(jax.random.fold_in(stream_key, axis), (), 0, length) for axis, length in enumerate(result.shape)]
        where[longest] = (where[longest] + shift) % result.shape[longest]
        spots.append(tuple(where))
    return result.at[spots[0]].set(smallest).at[spots[1]].set(largest)


def block_scale(own_key, extent, split, least, largest):
    def one(position, shards_of):
        draws = jax.random.uniform(jax.random.fold_in(jax.random.fold_in(own_key, 6), position), (shards_of,), jnp.float32, least / len(split), largest / len(split))
        return jnp.repeat(jnp.exp(draws), extent[position] // shards_of).reshape((-1,) + (1,) * (len(extent) - position - 1))

    level = one(*split[0])
    for cut in split[1:]:
        level = level * one(*cut)
    return level


def bell_draw(key, dims, deviation, most, split=(), kind=jnp.bfloat16):
    result = deviation * jax.random.normal(key, dims, jnp.float32)
    if split:
        result = result * block_scale(key, dims, split, -0.22, 0.18)
    return jnp.clip(result, -most, most).astype(kind)


def setup_inputs(seed: int = 0) -> dict:
    keys = jax.random.split(jax.random.key(seed), 19)
    return {
        "tokens": bell_draw(keys[0], (BATCH, SEQLEN, D), 1.0, 6.0, ((0, 4), (1, 8))),
        "retrieved": bell_draw(keys[1], (BATCH, SPANS, NEIGH, RET, D), 1.0, 6.0, ((0, 4), (1, 8))),
        "span_doc": place_ends(jax.random.randint(keys[2], (BATCH, SPANS), 0, 4), jax.random.fold_in(keys[2], 1), 0, 3).astype(jnp.int32),
        "neigh_doc": place_ends(jax.random.randint(keys[3], (BATCH, SPANS, NEIGH), 0, 4), jax.random.fold_in(keys[3], 1), 0, 3).astype(jnp.int32),
        "cotangent": bell_draw(keys[4], (BATCH, SEQLEN, D), 1.0, 6.0, ((0, 4), (1, 8))),
        "dec_gain": jnp.clip(1.0 + 0.1 * jax.random.normal(keys[5], (DEC_LAYERS, 2, D), jnp.float32), 0.5, 1.5).astype(jnp.bfloat16),
        "dec_qkv": bell_draw(keys[6], (DEC_LAYERS, D, 3 * D), D ** -0.5, 0.1875, ((1, 32),)),
        "dec_out": bell_draw(keys[7], (DEC_LAYERS, D, D), (D // 64) ** -0.5, 1.5, ((1, 32),)),
        "dec_in": bell_draw(keys[8], (DEC_LAYERS, D, FF), D ** -0.5, 0.1875, ((1, 32),)),
        "dec_down": bell_draw(keys[9], (DEC_LAYERS, FF, D), FF ** -0.5, 0.09375, ((1, 32),)),
        "cca_gain": jnp.clip(1.0 + 0.1 * jax.random.normal(keys[10], (D,), jnp.float32), 0.5, 1.5).astype(jnp.bfloat16),
        "cca_q": bell_draw(keys[11], (D, D), D ** -0.5, 0.1875, ((0, 32),)),
        "cca_kv": bell_draw(keys[12], (D, 2 * D), D ** -0.5, 0.1875, ((0, 32),)),
        "cca_out": bell_draw(keys[13], (D, D), (D // 64) ** -0.5, 1.5, ((0, 32),)),
        "enc_gain": jnp.clip(1.0 + 0.1 * jax.random.normal(keys[14], (ENC_LAYERS, D), jnp.float32), 0.5, 1.5).astype(jnp.bfloat16),
        "enc_in": bell_draw(keys[15], (ENC_LAYERS, D, FF), D ** -0.5, 0.1875, ((1, 32),)),
        "enc_down": bell_draw(keys[16], (ENC_LAYERS, FF, D), FF ** -0.5, 0.09375, ((1, 32),)),
        "enc_final": jnp.clip(1.0 + 0.1 * jax.random.normal(keys[17], (D,), jnp.float32), 0.5, 1.5).astype(jnp.bfloat16),
    }


@jax.custom_vjp
def low(v):
    return lax.optimization_barrier(v.astype(jnp.bfloat16)).astype(jnp.float32)

@jax.custom_vjp
def low_back(v):
    return v

def low_keep(v):
    return (low(v), None)

def low_pass(kept, grad):
    return (grad,)

def back_keep(v):
    return (v, None)

def back_low(kept, grad):
    return (low(grad),)
low.defvjp(low_keep, low_pass)
low_back.defvjp(back_keep, back_low)
EPSILON = 1e-06
SCORE_SCALE = 0.125
MASKED_SCORE = -1000000000.0
EXACT = lax.Precision.HIGHEST

def normed(values, norm_gain):
    return values * lax.rsqrt(lax.optimization_barrier(jnp.mean(values * values, -1, keepdims=True)) + EPSILON) * norm_gain

def project(values, weight):
    return jnp.einsum('...i,ij->...j', values, weight, precision=EXACT)

def softmax_rows(scores):
    row_peak = lax.optimization_barrier(jnp.max(scores, -1, keepdims=True))
    powers = jnp.exp(scores - row_peak)
    return powers / lax.optimization_barrier(jnp.sum(powers, -1, keepdims=True))

def feed_forward(stream, norm_gain, weight_in, weight_down):
    inputs = low(normed(stream, norm_gain))
    hidden_pre = low_back(project(inputs, weight_in))
    hidden = low(jax.nn.gelu(hidden_pre, approximate=False))
    return stream + low_back(project(hidden, weight_down))

def self_attention(stream, norm_gain, weight_qkv, weight_out):
    length = stream.shape[0]
    inputs = low(normed(stream, norm_gain))
    joined = low_back(low(project(inputs, weight_qkv)))
    queries = joined[:, :D].reshape(length, HEADS, HEAD)
    keys_all = joined[:, D:2 * D].reshape(length, HEADS, HEAD)
    vals_all = joined[:, 2 * D:].reshape(length, HEADS, HEAD)
    raw_scores = jnp.einsum('qhd,khd->hqk', queries, keys_all, precision=EXACT) * SCORE_SCALE
    places = jnp.arange(length)
    scores = low_back(jnp.where(places[None, :] <= places[:, None], raw_scores, MASKED_SCORE))
    attn_probs = low(softmax_rows(scores))
    attn_mixed = low_back(low(jnp.einsum('hqk,khd->qhd', attn_probs, vals_all, precision=EXACT).reshape(length, D)))
    return stream + low_back(project(attn_mixed, weight_out))

def cross_attention(stream, encoded, keep_flag, norm_gain, weight_q, weight_kv, weight_out):
    length = stream.shape[0]
    span_count = length // SPAN
    inputs = low(normed(stream, norm_gain))
    queries = low_back(low(project(inputs, weight_q))).reshape(span_count, SPAN, HEADS, HEAD)
    prior_enc = jnp.concatenate([jnp.zeros_like(encoded[:1]), encoded[:-1]], 0)
    prior_flag = jnp.concatenate([jnp.zeros_like(keep_flag[:1]), keep_flag[:-1]], 0)
    keys_vals = low_back(low(project(prior_enc, weight_kv))).reshape(span_count, NEIGH * RET, 2 * D)
    keys_part = keys_vals[..., :D].reshape(span_count, NEIGH * RET, HEADS, HEAD)
    vals_part = keys_vals[..., D:].reshape(span_count, NEIGH * RET, HEADS, HEAD)
    raw_scores = jnp.einsum('cqhd,ckhd->chqk', queries, keys_part, precision=EXACT) * SCORE_SCALE
    allowed = jnp.repeat(prior_flag, RET, axis=1) > 0.5
    scores = low_back(jnp.where(allowed[:, None, None, :], raw_scores, MASKED_SCORE))
    attn_probs = low(softmax_rows(scores))
    attn_mixed = low_back(low(jnp.einsum('chqk,ckhd->cqhd', attn_probs, vals_part, precision=EXACT).reshape(length, D)))
    present = jnp.repeat(lax.optimization_barrier(jnp.max(prior_flag, -1)), SPAN)[:, None]
    return stream + present * low_back(project(attn_mixed, weight_out))

def one_sequence(tokens_row, retrieved_row, flag_row, weights):
    dec_gain, dec_qkv, dec_out, dec_in, dec_down, cca_gain, cca_q, cca_kv, cca_out, enc_gain, enc_in, enc_down, enc_final = weights
    hidden_enc = retrieved_row
    for layer_idx in range(ENC_LAYERS):
        hidden_enc = feed_forward(hidden_enc, enc_gain[layer_idx], enc_in[layer_idx], enc_down[layer_idx])
    encoded = low(normed(hidden_enc, enc_final))
    stream = self_attention(tokens_row, dec_gain[0, 0], dec_qkv[0], dec_out[0])
    stream = cross_attention(stream, encoded, flag_row, cca_gain, cca_q, cca_kv, cca_out)
    stream = feed_forward(stream, dec_gain[0, 1], dec_in[0], dec_down[0])
    for layer_idx in range(1, DEC_LAYERS):
        stream = self_attention(stream, dec_gain[layer_idx, 0], dec_qkv[layer_idx], dec_out[layer_idx])
        stream = feed_forward(stream, dec_gain[layer_idx, 1], dec_in[layer_idx], dec_down[layer_idx])
    return stream

def reference(tokens, retrieved, span_doc, neigh_doc, cotangent, dec_gain, dec_qkv, dec_out, dec_in, dec_down, cca_gain, cca_q, cca_kv, cca_out, enc_gain, enc_in, enc_down, enc_final):
    keep_flag = (neigh_doc != span_doc[..., None]).astype(jnp.float32)
    weights = tuple((item.astype(jnp.float32) for item in (dec_gain, dec_qkv, dec_out, dec_in, dec_down, cca_gain, cca_q, cca_kv, cca_out, enc_gain, enc_in, enc_down, enc_final)))
    tokens_f32 = tokens.astype(jnp.float32)
    retrieved_f32 = retrieved.astype(jnp.float32)
    seq_step = jax.checkpoint(lambda item, params: one_sequence(item[0], item[1], item[2], params))

    def whole(inputs, params):
        return lax.map(lambda item: seq_step(item, params), (inputs, retrieved_f32, keep_flag))
    final_stream, pullback = jax.vjp(whole, tokens_f32, weights)
    tokens_grad, weight_grads = pullback(cotangent.astype(jnp.float32))
    return (final_stream.astype(jnp.bfloat16), tokens_grad, weight_grads[0], weight_grads[1], weight_grads[2], weight_grads[3], weight_grads[4], weight_grads[5], weight_grads[6], weight_grads[7], weight_grads[8], weight_grads[9], weight_grads[10], weight_grads[11], weight_grads[12])
```

```python
import functools
import jax
import jax.numpy as jnp
from jax import lax
from jax.experimental import pallas as pl
from jax.experimental.pallas import tpu as pltpu
from jax.sharding import PartitionSpec as P

D = 896
FF = 3584
BF = jnp.bfloat16
MESH_ID = pl.DeviceIdType.MESH
ANY = pl.BlockSpec(memory_space=pl.ANY)


def grid_sizes():
    return (lax.axis_size("dp"), lax.axis_size("seq") // 4, 2, 2)


def grid_place():
    seq = lax.axis_index("seq")
    return (lax.axis_index("dp"), seq // 4, (seq // 2) % 2, seq % 2)


def device_at(place):
    z, y, x, core = place
    return (z, (y * 2 + x) * 2 + core)


def moved(place, sizes, axis, by):
    size = sizes[axis]
    there = lax.rem(place[axis] + (by % size), size)
    return place[:axis] + (there,) + place[axis + 1 :]


def greet(place, sizes):
    barrier = pltpu.get_barrier_semaphore()
    for axis in range(4):
        size, here = sizes[axis], place[axis]
        for by in (1, -1):
            there = here + by

            @pl.when(inside(there, size))
            def _():
                other = place[:axis] + (jnp.clip(there, 0, size - 1),) + place[axis + 1 :]
                pl.semaphore_signal(barrier, inc=1, device_id=device_at(other), device_id_type=MESH_ID)

    count = 0
    for axis in range(4):
        for by in (1, -1):
            count = count + inside(place[axis] + by, sizes[axis]).astype(jnp.int32)
    pl.semaphore_wait(barrier, count)


class Hop:
    def __init__(self, copy, sends, receives):
        self.copy, self.sends, self.receives = copy, sends, receives

    def start(self):
        pl.when(self.sends)(self.copy[0].start)

    def wait(self):
        pl.when(self.sends)(self.copy[0].wait_send)
        pl.when(self.receives)(self.copy[1].wait_recv)


def inside(place, size):
    return jnp.logical_and(place >= 0, place < size)


ROUTES = ((2, 0, 1), (1, 0, 2), (0, 2, 1), (1, 0, 2), (2, 0, 1), (0, 1, 2))
LAGS = (0, 1, 2, 3, 5, 8, 9)
PIECE = 896


def narrow_groups():
    qkv = 3 * D
    wide = FF // 2
    whole = lambda arg, layer: [[(arg, layer, 0, wide)], [(arg, layer, wide, wide)]]
    return [
        whole(0, 0),
        whole(0, 1),
        [
            [(7, None, 0, D), (6, None, 0, D), (2, 0, 0, qkv), (3, 0, 0, D), (9, None, 0, 128)],
            [(7, None, D, D), (8, None, 0, D), (2, 1, 0, qkv), (3, 1, 0, D), (9, None, 0, 128)],
        ],
        whole(4, 0),
        whole(4, 1),
    ]


def half_width(group):
    return sum(part[3] for part in group[0])


def gather_plan():
    groups = narrow_groups()
    starts, cursor = [], 0
    for group in groups:
        starts.append(cursor)
        cursor += half_width(group)
    pieces = []
    for kind, number in (("n", 0), ("r", 0), ("n", 1), ("r", 1), ("n", 2), ("n", 3), ("r", 2), ("n", 4), ("r", 3)):
        if kind == "n":
            width = half_width(groups[number])
            count = width // PIECE
            for k in range(count):
                size = PIECE if k < count - 1 else width - k * PIECE
                pieces.append((kind, number, k * PIECE, size))
        else:
            pieces.append((kind, number, 0, D))
            pieces.append((kind, number, 1, D))
    return groups, starts, cursor, pieces


def gather_kernel(sizes, *refs):
    groups, starts, _, pieces = gather_plan()
    ins, outs = refs[:10], refs[10:19]
    halves, other, joined, send_sem, recv_sem, load_sem, swap_sem = refs[19:]
    place = grid_place()
    z, y, x, core = place
    sibling = device_at(moved(place, sizes, 3, 1))
    loads = []
    for number, group in enumerate(groups):
        for half in range(2):
            cursor = starts[number]
            for arg, layer, first, size in group[half]:
                source = ins[arg] if layer is None else ins[arg].at[layer]
                loads.append((source.at[:, pl.ds(first, size)], halves.at[half, :, pl.ds(cursor, size)]))
                cursor += size
    for number, (arg, layer) in enumerate(((1, 0), (1, 1), (5, 0), (5, 1))):
        for part in range(2):
            loads.append((ins[arg].at[layer, part], outs[5 + number].at[z, y, x, core, part]))
    started = []
    for k, (source, target) in enumerate(loads):
        copy = pltpu.make_async_copy(source, target, load_sem.at[k])
        copy.start()
        started.append(copy)
    greet(place, sizes)
    for copy in started:
        copy.wait()
    swaps = []
    for number, group in enumerate(groups):
        columns = pl.ds(starts[number], half_width(group))
        copy = pltpu.make_async_remote_copy(
            src_ref=halves.at[1 - core, :, columns],
            dst_ref=other.at[:, columns],
            send_sem=swap_sem.at[0, number],
            recv_sem=swap_sem.at[1, number],
            device_id=sibling,
            device_id_type=MESH_ID,
        )
        copy.start()
        swaps.append(copy)

    def view(piece, where):
        kind, number, first, size = piece
        iz, iy, ix = where[:3]
        if kind == "n":
            start = pl.multiple_of(core * half_width(groups[number]) + first, 128)
            return outs[number].at[iz, iy, ix, :, pl.ds(start, size)]
        return outs[5 + number].at[iz, iy, ix, core, first]

    prepared = {}

    def prepare(piece):
        kind, number, first, size = piece
        if kind == "n" and number not in prepared:
            swaps[number].wait()
            group = groups[number]
            for begin in range(starts[number], starts[number] + half_width(group), 128):
                columns = pl.ds(begin, 128)
                mine = halves[core, :, columns].astype(jnp.float32)
                theirs = other[:, columns].astype(jnp.float32)
                both = [jnp.where(core == 0, mine, theirs), jnp.where(core == 0, theirs, mine)]
                joined[:, columns] = jnp.concatenate(both, 0).astype(BF)
            width = half_width(group)
            copy = pltpu.make_async_copy(
                joined.at[:, pl.ds(starts[number], width)],
                outs[number].at[z, y, x, :, pl.ds(pl.multiple_of(core * width, 128), width)],
                load_sem.at[len(loads) + number],
            )
            copy.start()
            copy.wait()
            prepared[number] = True

    semaphores = [0]

    def transfers(number):
        piece = pieces[number]
        steps, done = [], []
        for axis in ROUTES[number % len(ROUTES)] + (3,):
            size, here = sizes[axis], place[axis]

            def block(at):
                where = list(place)
                for old in done:
                    where[old] = slice(None)
                where[axis] = jnp.clip(at, 0, size - 1)
                return view(piece, where)

            for hop in range(1, size):
                hops = []
                for way in (1, -1):
                    ahead, behind = here + way, here - way
                    sent, got = here - way * (hop - 1), here - way * hop
                    if size == 2 and way == -1:
                        continue
                    if size == 2:
                        ahead, behind, got = 1 - here, 1 - here, 1 - here
                    pair = []
                    for at, other_end in ((sent, ahead), (got, behind)):
                        ref = block(at)
                        target = place[:axis] + (jnp.clip(other_end, 0, size - 1),) + place[axis + 1 :]
                        pair.append(
                            pltpu.make_async_remote_copy(
                                src_ref=ref,
                                dst_ref=ref,
                                send_sem=send_sem.at[semaphores[0]],
                                recv_sem=recv_sem.at[semaphores[0]],
                                device_id=device_at(target),
                                device_id_type=MESH_ID,
                            )
                        )
                    semaphores[0] += 1
                    sends = jnp.logical_and(inside(sent, size), inside(ahead, size))
                    hops.append(Hop(pair, sends, inside(got, size)))
                steps.append(hops)
            done.append(axis)
        return steps

    running = {}
    depth = sum(size - 1 for size in sizes)
    lags = LAGS if depth + 1 == len(LAGS) else list(range(depth + 1))
    for tick in range(len(pieces) + lags[-1]):
        for step in reversed(range(depth + 1)):
            number = tick - lags[step]
            if number < 0 or number >= len(pieces):
                continue
            if step == 0:
                prepare(pieces[number])
                running[number] = transfers(number)
            else:
                for copy in running[number][step - 1]:
                    copy.wait()
            if step < depth:
                for copy in running[number][step]:
                    copy.start()
    for number in range(len(groups)):
        if number not in prepared:
            swaps[number].wait()


def gather_plainly(enc_in, enc_down, dec_qkv, dec_out, dec_in, dec_down, cca_q, cca_kv, cca_out, gains):
    get = lambda w: lax.all_gather(w, ("dp", "seq"), axis=w.ndim - 2, tiled=True)
    kv = get(cca_kv)
    return dict(
        enc_in=get(enc_in), enc_down=get(enc_down), dec_in=get(dec_in), dec_down=get(dec_down), dec_qkv=get(dec_qkv),
        dec_out=get(dec_out), cca_kv=[kv[:, :D], kv[:, D:]], cca_q=get(cca_q), cca_out=get(cca_out), gains=get(gains)[:, :8],
    )


def gather_weights(enc_in, enc_down, dec_qkv, dec_out, dec_in, dec_down, cca_q, cca_kv, cca_out, gains):
    sizes = grid_sizes()
    rows = cca_q.shape[0]
    groups, starts, total, pieces = gather_plan()
    part = enc_down.shape[1] // 2
    if rows % 4 or part % 8 or sizes[1:] != (2, 2, 2):
        return gather_plainly(enc_in, enc_down, dec_qkv, dec_out, dec_in, dec_down, cca_q, cca_kv, cca_out, gains)
    lead = sizes[:3]
    shapes = [lead + (2 * rows, 2 * half_width(group)) for group in groups] + [lead + (2, 2, part, D)] * 4
    per_piece = sum((size - 1) * (1 if size == 2 else 2) for size in sizes)
    n_loads = sum(len(half) for group in groups for half in group) + 8 + len(groups)
    split = lambda w: w.reshape(w.shape[0], 2, part, D)
    outs = pl.pallas_call(
        functools.partial(gather_kernel, sizes),
        out_shape=[jax.ShapeDtypeStruct(shape, BF) for shape in shapes],
        in_specs=[ANY] * 10,
        out_specs=[ANY] * 9,
        scratch_shapes=[
            pltpu.VMEM((2, rows, total), BF),
            pltpu.VMEM((rows, total), BF),
            pltpu.VMEM((2 * rows, total), BF),
            pltpu.SemaphoreType.DMA((per_piece * len(pieces),)),
            pltpu.SemaphoreType.DMA((per_piece * len(pieces),)),
            pltpu.SemaphoreType.DMA((n_loads,)),
            pltpu.SemaphoreType.DMA((2, len(groups))),
        ],
        compiler_params=pltpu.CompilerParams(collective_id=0, has_side_effects=True),
        name="gather_weights",
    )(enc_in, split(enc_down), dec_qkv, dec_out, dec_in, split(dec_down), cca_q, cca_kv, cca_out, gains)
    narrow = [out.reshape(D, out.shape[-1]) for out in outs[:5]]
    tall = [out.reshape(FF, D) for out in outs[5:]]
    mixed = narrow[2]
    half = mixed.shape[1] // 2
    sides = [mixed[:, :half], mixed[:, half:]]
    qkv = [side[:, 2 * D : 5 * D] for side in sides]
    out = [side[:, 5 * D : 6 * D] for side in sides]
    return dict(
        enc_in=narrow[:2], enc_down=tall[:2], dec_in=narrow[3:], dec_down=tall[2:], dec_qkv=qkv, dec_out=out,
        cca_kv=[side[:, :D] for side in sides], cca_q=sides[0][:, D : 2 * D], cca_out=sides[1][:, D : 2 * D],
        gains=sides[0][:, 6 * D : 6 * D + 8],
    )


HEADS = 14
HEAD = 64
SPAN = 64
NEIGH = 2
RET = 128
ENC_LAYERS = 2
DEC_LAYERS = 2


EPSILON = 1e-06
SCORE_SCALE = 0.125
MASKED_SCORE = -1000000000.0


def shifted(x, axis, by):
    count = lax.axis_size(axis)
    pairs = [(i, i + by) for i in range(count) if 0 <= i + by < count]
    return lax.ppermute(x, axis, pairs)


def normed(values, norm_gain):
    return values * lax.rsqrt(jnp.mean(values * values, -1, keepdims=True) + EPSILON) * norm_gain


def gelu_exact(values):
    return jax.nn.gelu(values, approximate=False)


def project(values, weight):
    return jnp.dot(values, weight, preferred_element_type=jnp.float32)


def back_project(upstream, weight):
    return lax.dot_general(
        upstream,
        weight,
        (((upstream.ndim - 1,), (1,)), ((), ())),
        preferred_element_type=jnp.float32,
    )


def slab_term(left, right):
    flat_left = left.reshape(-1, left.shape[-1])
    flat_right = right.reshape(-1, right.shape[-1])
    return lax.dot_general(
        flat_left, flat_right, (((0,), (0,)), ((), ())), preferred_element_type=jnp.float32
    )


def norm_back(stream, norm_gain, upstream):
    _, pullback = jax.vjp(normed, stream, norm_gain)
    return pullback(upstream)


def split_heads(values):
    return values.reshape(values.shape[:-1] + (HEADS, HEAD))


def softmax_parts(scores):
    row_peak = jnp.max(scores, -1, keepdims=True)
    powers = jnp.exp(scores - row_peak)
    row_total = jnp.sum(powers, -1, keepdims=True)
    return (powers / row_total, (row_peak + jnp.log(row_total))[..., 0])


def feed_forward(stream, norm_gain, weight_in, weight_down):
    inputs = normed(stream, norm_gain).astype(jnp.bfloat16)
    hidden_pre = project(inputs, weight_in)
    hidden = gelu_exact(hidden_pre).astype(jnp.bfloat16)
    return (stream + project(hidden, weight_down), (stream, inputs, hidden_pre, hidden))


def feed_back(stored, norm_gain, weight_in, weight_down, upstream):
    stream, inputs, hidden_pre, hidden = stored
    grad_low = upstream.astype(jnp.bfloat16)
    grad_hidden = back_project(grad_low, weight_down)
    _, gelu_pull = jax.vjp(gelu_exact, hidden_pre)
    grad_pre = gelu_pull(grad_hidden)[0].astype(jnp.bfloat16)
    stream_grad, gain_grad = norm_back(stream, norm_gain, back_project(grad_pre, weight_in))
    return (upstream + stream_grad, gain_grad, ((inputs, grad_pre), (grad_low, hidden)))


def score_table(queries, keys_all, offset):
    raw_scores = (
        jnp.einsum("bqhd,bkhd->bhqk", queries, keys_all, preferred_element_type=jnp.float32)
        * SCORE_SCALE
    )
    key_place = jnp.arange(keys_all.shape[1])
    query_place = offset + jnp.arange(queries.shape[1])
    return jnp.where(key_place[None, :] <= query_place[:, None], raw_scores, MASKED_SCORE)


def self_forward(stream, norm_gain, weight_qkv, weight_out, offset):
    inputs = normed(stream, norm_gain).astype(jnp.bfloat16)
    joined = project(inputs, weight_qkv).astype(jnp.bfloat16)
    keys_vals = lax.all_gather(joined[..., D:], "seq", axis=1, tiled=True)
    queries = split_heads(joined[..., :D])
    scores = score_table(queries, split_heads(keys_vals[..., :D]), offset)
    attn_probs, log_total = softmax_parts(scores)
    attn_mixed = jnp.einsum(
        "bhqk,bkhd->bqhd",
        attn_probs.astype(jnp.bfloat16),
        split_heads(keys_vals[..., D:]),
        preferred_element_type=jnp.float32,
    )
    attn_mixed = attn_mixed.astype(jnp.bfloat16).reshape(stream.shape)
    return (
        stream + project(attn_mixed, weight_out),
        (stream, inputs, joined, keys_vals, log_total, attn_mixed),
    )


def self_back(stored, norm_gain, weight_qkv, weight_out, offset, upstream):
    stream, inputs, joined, keys_vals, log_total, attn_mixed = stored
    grad_low = upstream.astype(jnp.bfloat16)
    grad_mixed = split_heads(back_project(grad_low, weight_out).astype(jnp.bfloat16))
    queries = split_heads(joined[..., :D])
    keys_all = split_heads(keys_vals[..., :D])
    vals_all = split_heads(keys_vals[..., D:])
    scores = score_table(queries, keys_all, offset)
    attn_probs = jnp.exp(scores - log_total[..., None])
    grad_probs = jnp.einsum(
        "bqhd,bkhd->bhqk", grad_mixed, vals_all, preferred_element_type=jnp.float32
    )
    row_delta = jnp.sum(attn_probs * grad_probs, -1)
    grad_scores = (attn_probs * (grad_probs - row_delta[..., None])).astype(jnp.bfloat16)
    grad_queries = (
        jnp.einsum("bhqk,bkhd->bqhd", grad_scores, keys_all, preferred_element_type=jnp.float32)
        * SCORE_SCALE
    )
    seqs_here = queries.shape[0]
    grad_vals = jnp.einsum(
        "bhqk,bqhd->bkhd",
        attn_probs.astype(jnp.bfloat16),
        grad_mixed,
        preferred_element_type=jnp.float32,
    )
    grad_keys = (
        jnp.einsum("bhqk,bqhd->bkhd", grad_scores, queries, preferred_element_type=jnp.float32)
        * SCORE_SCALE
    )
    length = grad_keys.shape[1]
    grad_pairs = jnp.concatenate(
        [grad_keys.reshape(seqs_here, length, D), grad_vals.reshape(seqs_here, length, D)], -1
    )
    own_pairs = lax.psum_scatter(
        grad_pairs.astype(jnp.bfloat16), "seq", scatter_dimension=1, tiled=True
    ).astype(jnp.float32)
    grad_joined = jnp.concatenate([grad_queries.reshape(stream.shape), own_pairs], -1).astype(
        jnp.bfloat16
    )
    stream_grad, gain_grad = norm_back(stream, norm_gain, back_project(grad_joined, weight_qkv))
    return (upstream + stream_grad, gain_grad, ((inputs, grad_joined), (attn_mixed, grad_low)))


def cross_scores(queries, keys_vals, prior_flag):
    raw_scores = (
        jnp.einsum(
            "bcqhd,bckhd->bchqk",
            queries,
            split_heads(keys_vals[..., :D]),
            preferred_element_type=jnp.float32,
        )
        * SCORE_SCALE
    )
    allowed = jnp.repeat(prior_flag, RET, axis=2) > 0.5
    return jnp.where(allowed[:, :, None, None, :], raw_scores, MASKED_SCORE)


def row_gate(prior_flag):
    return jnp.repeat(jnp.max(prior_flag, -1).astype(jnp.float32), SPAN, axis=1)[..., None]


def cross_forward(stream, encoded, keep_flag, norm_gain, weight_q, weight_kv, weight_out):
    seqs_here = stream.shape[0]
    spans_here = encoded.shape[1]
    last_enc, last_flag = shifted((encoded[:, -1], keep_flag[:, -1]), "seq", 1)
    prior_enc = jnp.concatenate([last_enc[:, None], encoded[:, :-1]], 1)
    prior_flag = jnp.concatenate([last_flag[:, None], keep_flag[:, :-1]], 1)
    inputs = normed(stream, norm_gain).astype(jnp.bfloat16)
    queries = (
        project(inputs, weight_q)
        .astype(jnp.bfloat16)
        .reshape(seqs_here, spans_here, SPAN, HEADS, HEAD)
    )
    keys_vals = (
        project(prior_enc, weight_kv)
        .astype(jnp.bfloat16)
        .reshape(seqs_here, spans_here, NEIGH * RET, 2 * D)
    )
    scores = cross_scores(queries, keys_vals, prior_flag)
    attn_probs, log_total = softmax_parts(scores)
    attn_mixed = jnp.einsum(
        "bchqk,bckhd->bcqhd",
        attn_probs.astype(jnp.bfloat16),
        split_heads(keys_vals[..., D:]),
        preferred_element_type=jnp.float32,
    )
    attn_mixed = attn_mixed.astype(jnp.bfloat16).reshape(stream.shape)
    branch = row_gate(prior_flag) * project(attn_mixed, weight_out)
    return (
        stream + branch,
        (stream, inputs, prior_enc, prior_flag, queries, keys_vals, log_total, attn_mixed),
    )


def cross_back(stored, norm_gain, weight_q, weight_kv, weight_out, upstream):
    stream, inputs, prior_enc, prior_flag, queries, keys_vals, log_total, attn_mixed = stored
    grad_low = (upstream * row_gate(prior_flag)).astype(jnp.bfloat16)
    grad_mixed = back_project(grad_low, weight_out).astype(jnp.bfloat16).reshape(queries.shape)
    scores = cross_scores(queries, keys_vals, prior_flag)
    attn_probs = jnp.exp(scores - log_total[..., None])
    keys_part = split_heads(keys_vals[..., :D])
    vals_part = split_heads(keys_vals[..., D:])
    grad_vals = jnp.einsum(
        "bchqk,bcqhd->bckhd",
        attn_probs.astype(jnp.bfloat16),
        grad_mixed,
        preferred_element_type=jnp.float32,
    )
    grad_probs = jnp.einsum(
        "bcqhd,bckhd->bchqk", grad_mixed, vals_part, preferred_element_type=jnp.float32
    )
    grad_scores = attn_probs * (grad_probs - jnp.sum(attn_probs * grad_probs, -1, keepdims=True))
    grad_scores = grad_scores.astype(jnp.bfloat16)
    grad_queries = (
        jnp.einsum("bchqk,bckhd->bcqhd", grad_scores, keys_part, preferred_element_type=jnp.float32)
        * SCORE_SCALE
    )
    grad_keys = (
        jnp.einsum("bchqk,bcqhd->bckhd", grad_scores, queries, preferred_element_type=jnp.float32)
        * SCORE_SCALE
    )
    pair_shape = keys_vals.shape[:-1] + (D,)
    grad_pairs = jnp.concatenate([grad_keys.reshape(pair_shape), grad_vals.reshape(pair_shape)], -1)
    grad_pairs = grad_pairs.astype(jnp.bfloat16)
    grad_prior = back_project(grad_pairs, weight_kv).reshape(prior_enc.shape)
    query_low = grad_queries.reshape(stream.shape).astype(jnp.bfloat16)
    stream_grad, gain_grad = norm_back(stream, norm_gain, back_project(query_low, weight_q))
    from_next = shifted(grad_prior[:, 0].astype(jnp.bfloat16), "seq", -1).astype(jnp.float32)
    encoded_grad = jnp.concatenate([grad_prior[:, 1:], from_next[:, None]], 1)
    pairs = ((inputs, query_low), (prior_enc, grad_pairs), (attn_mixed, grad_low))
    return (upstream + stream_grad, gain_grad, pairs, encoded_grad)


def encode(retrieved, enc_gain, enc_in, enc_down, enc_final):
    stream = retrieved.astype(jnp.float32)
    stored = []
    for layer_idx in range(ENC_LAYERS):
        stream, layer_store = feed_forward(
            stream, enc_gain[layer_idx], enc_in[layer_idx], enc_down[layer_idx]
        )
        stored.append(layer_store)
    return (normed(stream, enc_final).astype(jnp.bfloat16), (stream, stored))


def encode_back(retrieved, enc_weights, encoded_grad):
    enc_gain, enc_in, enc_down, enc_final = enc_weights
    _, (stream, stored) = encode(retrieved, enc_gain, enc_in, enc_down, enc_final)
    upstream, final_grad = norm_back(stream, enc_final, encoded_grad)
    gain_list = [None] * ENC_LAYERS
    pair_list = [None] * ENC_LAYERS
    for layer_idx in reversed(range(ENC_LAYERS)):
        upstream, gain_list[layer_idx], pair_list[layer_idx] = feed_back(
            stored[layer_idx], enc_gain[layer_idx], enc_in[layer_idx], enc_down[layer_idx], upstream
        )
    return (gain_list, pair_list, final_grad)


def on_device(
    tokens,
    retrieved,
    span_doc,
    neigh_doc,
    cotangent,
    dec_gain,
    dec_qkv,
    dec_out,
    dec_in,
    dec_down,
    cca_gain,
    cca_q,
    cca_kv,
    cca_out,
    enc_gain,
    enc_in,
    enc_down,
    enc_final,
):
    offset = lax.axis_index("seq") * tokens.shape[1]
    rows = cca_q.shape[0]
    own_gains = jnp.concatenate([dec_gain.reshape(4, rows), cca_gain[None], enc_gain, enc_final[None]], 0).T
    own_gains = jnp.pad(own_gains, ((0, 0), (0, 120)))
    full = gather_weights(enc_in, enc_down, dec_qkv, dec_out, dec_in, dec_down, cca_q, cca_kv, cca_out, own_gains)
    gains = full["gains"].T
    enc_weights = (gains[5:7], full["enc_in"], full["enc_down"], gains[7])
    encoded, _ = encode(retrieved, enc_weights[0], enc_weights[1], enc_weights[2], enc_weights[3])
    keep_flag = (neigh_doc != span_doc[..., None]).astype(jnp.bfloat16)
    dec_weights = (
        gains[:4].reshape(2, 2, D), full["dec_qkv"], full["dec_out"], full["dec_in"], full["dec_down"],
        gains[4], full["cca_q"], jnp.concatenate(full["cca_kv"], 1), full["cca_out"],
    )
    norm_gains, qkv_all, out_all, in_all, down_all, cross_gain, cross_q, cross_kv, cross_out = (
        dec_weights
    )
    stream = tokens.astype(jnp.float32)
    attn_stores, ffn_stores = ([], [])
    stream, attn_store = self_forward(stream, norm_gains[0, 0], qkv_all[0], out_all[0], offset)
    attn_stores.append(attn_store)
    stream, cross_store = cross_forward(
        stream, encoded, keep_flag, cross_gain, cross_q, cross_kv, cross_out
    )
    stream, ffn_store = feed_forward(stream, norm_gains[0, 1], in_all[0], down_all[0])
    ffn_stores.append(ffn_store)
    layer_idx = 1
    stream, attn_store = self_forward(
        stream, norm_gains[layer_idx, 0], qkv_all[layer_idx], out_all[layer_idx], offset
    )
    attn_stores.append(attn_store)
    stream, ffn_store = feed_forward(
        stream, norm_gains[layer_idx, 1], in_all[layer_idx], down_all[layer_idx]
    )
    ffn_stores.append(ffn_store)
    result = stream.astype(jnp.bfloat16)
    upstream = cotangent.astype(jnp.float32)
    attn_gain_g = [None] * DEC_LAYERS
    ffn_gain_g = [None] * DEC_LAYERS
    attn_pairs = [None] * DEC_LAYERS
    ffn_pairs = [None] * DEC_LAYERS
    for layer_idx in reversed(range(1, DEC_LAYERS)):
        upstream, ffn_gain_g[layer_idx], ffn_pairs[layer_idx] = feed_back(
            ffn_stores[layer_idx],
            norm_gains[layer_idx, 1],
            in_all[layer_idx],
            down_all[layer_idx],
            upstream,
        )
        upstream, attn_gain_g[layer_idx], attn_pairs[layer_idx] = self_back(
            attn_stores[layer_idx],
            norm_gains[layer_idx, 0],
            qkv_all[layer_idx],
            out_all[layer_idx],
            offset,
            upstream,
        )
    upstream, ffn_gain_g[0], ffn_pairs[0] = feed_back(
        ffn_stores[0], norm_gains[0, 1], in_all[0], down_all[0], upstream
    )
    upstream, cross_gain_g, cross_pairs, encoded_grad = cross_back(
        cross_store, cross_gain, cross_q, cross_kv, cross_out, upstream
    )
    upstream, attn_gain_g[0], attn_pairs[0] = self_back(
        attn_stores[0], norm_gains[0, 0], qkv_all[0], out_all[0], offset, upstream
    )
    enc_gain_g, enc_pairs, final_gain_g = encode_back(retrieved, enc_weights, encoded_grad)
    pair_list = []
    for layer_idx in range(DEC_LAYERS):
        pair_list = pair_list + list(attn_pairs[layer_idx]) + list(ffn_pairs[layer_idx])
    pair_list = pair_list + list(cross_pairs)
    for layer_idx in range(ENC_LAYERS):
        pair_list = pair_list + list(enc_pairs[layer_idx])
    gain_list = []
    for layer_idx in range(DEC_LAYERS):
        gain_list = gain_list + [attn_gain_g[layer_idx], ffn_gain_g[layer_idx]]
    gain_list = gain_list + [cross_gain_g] + list(enc_gain_g) + [final_gain_g]

    def term():
        blocks = [slab_term(left, right) for left, right in pair_list]
        blocks = blocks + [vector[:, None] for vector in gain_list]
        return jnp.concatenate(blocks, 1).astype(jnp.bfloat16)

    owned = lax.psum_scatter(term(), ("dp", "seq"), scatter_dimension=0, tiled=True).astype(jnp.float32)
    pieces = []
    cursor = 0
    for left, right in pair_list:
        width = right.shape[-1]
        pieces.append(owned[:, cursor : cursor + width])
        cursor = cursor + width
    gain_cols = owned[:, cursor:]
    dec_qkv_g = jnp.stack([pieces[4 * idx] for idx in range(DEC_LAYERS)])
    dec_out_g = jnp.stack([pieces[4 * idx + 1] for idx in range(DEC_LAYERS)])
    dec_in_g = jnp.stack([pieces[4 * idx + 2] for idx in range(DEC_LAYERS)])
    dec_down_g = jnp.stack([pieces[4 * idx + 3].T for idx in range(DEC_LAYERS)])
    base = 4 * DEC_LAYERS
    cross_q_g = pieces[base]
    cross_kv_g = pieces[base + 1]
    cross_out_g = pieces[base + 2]
    base = base + 3
    enc_in_g = jnp.stack([pieces[base + 2 * idx] for idx in range(ENC_LAYERS)])
    enc_down_g = jnp.stack([pieces[base + 2 * idx + 1].T for idx in range(ENC_LAYERS)])
    dec_gain_g = jnp.stack(
        [jnp.stack([gain_cols[:, 2 * idx], gain_cols[:, 2 * idx + 1]]) for idx in range(DEC_LAYERS)]
    )
    cross_gain_out = gain_cols[:, 2 * DEC_LAYERS]
    enc_gain_out = jnp.stack([gain_cols[:, 2 * DEC_LAYERS + 1 + idx] for idx in range(ENC_LAYERS)])
    final_out = gain_cols[:, 2 * DEC_LAYERS + 1 + ENC_LAYERS]
    return (
        result,
        upstream,
        dec_gain_g,
        dec_qkv_g,
        dec_out_g,
        dec_in_g,
        dec_down_g,
        cross_gain_out,
        cross_q_g,
        cross_kv_g,
        cross_out_g,
        enc_gain_out,
        enc_in_g,
        enc_down_g,
        final_out,
    )


def solution(mesh):
    return jax.shard_map(
        on_device,
        mesh=mesh,
        in_specs=(
            P("dp", "seq", None),
            P("dp", "seq", None, None, None),
            P("dp", "seq"),
            P("dp", "seq", None),
            P("dp", "seq", None),
            P(None, None, ("dp", "seq")),
            P(None, ("dp", "seq"), None),
            P(None, ("dp", "seq"), None),
            P(None, ("dp", "seq"), None),
            P(None, ("dp", "seq"), None),
            P(("dp", "seq")),
            P(("dp", "seq"), None),
            P(("dp", "seq"), None),
            P(("dp", "seq"), None),
            P(None, ("dp", "seq")),
            P(None, ("dp", "seq"), None),
            P(None, ("dp", "seq"), None),
            P(("dp", "seq")),
        ),
        out_specs=(
            P("dp", "seq", None),
            P("dp", "seq", None),
            P(None, None, ("dp", "seq")),
            P(None, ("dp", "seq"), None),
            P(None, ("dp", "seq"), None),
            P(None, ("dp", "seq"), None),
            P(None, None, ("dp", "seq")),
            P(("dp", "seq")),
            P(("dp", "seq"), None),
            P(("dp", "seq"), None),
            P(("dp", "seq"), None),
            P(None, ("dp", "seq")),
            P(None, ("dp", "seq"), None),
            P(None, None, ("dp", "seq")),
            P(("dp", "seq")),
        ),
        check_vma=False,
    )
```

```python
import functools
import jax
import jax.numpy as jnp
from jax import lax
from jax.experimental import pallas as pl
from jax.experimental.pallas import tpu as pltpu
from jax.sharding import PartitionSpec as P

D = 896
FF = 3584
BF = jnp.bfloat16
MESH_ID = pl.DeviceIdType.MESH
ANY = pl.BlockSpec(memory_space=pl.ANY)


def grid_sizes():
    return (lax.axis_size("dp"), lax.axis_size("seq") // 4, 2, 2)


def grid_place():
    seq = lax.axis_index("seq")
    return (lax.axis_index("dp"), seq // 4, (seq // 2) % 2, seq % 2)


def device_at(place):
    z, y, x, core = place
    return (z, (y * 2 + x) * 2 + core)


def moved(place, sizes, axis, by):
    size = sizes[axis]
    there = lax.rem(place[axis] + (by % size), size)
    return place[:axis] + (there,) + place[axis + 1 :]


def greet(place, sizes):
    barrier = pltpu.get_barrier_semaphore()
    for axis in range(4):
        size, here = sizes[axis], place[axis]
        for by in (1, -1):
            there = here + by

            @pl.when(inside(there, size))
            def _():
                other = place[:axis] + (jnp.clip(there, 0, size - 1),) + place[axis + 1 :]
                pl.semaphore_signal(barrier, inc=1, device_id=device_at(other), device_id_type=MESH_ID)

    count = 0
    for axis in range(4):
        for by in (1, -1):
            count = count + inside(place[axis] + by, sizes[axis]).astype(jnp.int32)
    pl.semaphore_wait(barrier, count)


class Hop:
    def __init__(self, copy, sends, receives):
        self.copy, self.sends, self.receives = copy, sends, receives

    def start(self):
        pl.when(self.sends)(self.copy[0].start)

    def wait(self):
        pl.when(self.sends)(self.copy[0].wait_send)
        pl.when(self.receives)(self.copy[1].wait_recv)


def inside(place, size):
    return jnp.logical_and(place >= 0, place < size)


ROUTES = ((2, 0, 1), (1, 0, 2), (0, 2, 1), (1, 0, 2), (2, 0, 1), (0, 1, 2))
LAGS = (0, 1, 2, 3, 5, 8, 9)
PIECE = 896


def narrow_groups():
    qkv = 3 * D
    wide = FF // 2
    whole = lambda arg, layer: [[(arg, layer, 0, wide)], [(arg, layer, wide, wide)]]
    return [
        whole(0, 0),
        whole(0, 1),
        [
            [(7, None, 0, D), (6, None, 0, D), (2, 0, 0, qkv), (3, 0, 0, D), (9, None, 0, 128)],
            [(7, None, D, D), (8, None, 0, D), (2, 1, 0, qkv), (3, 1, 0, D), (9, None, 0, 128)],
        ],
        whole(4, 0),
        whole(4, 1),
    ]


def half_width(group):
    return sum(part[3] for part in group[0])


def gather_plan():
    groups = narrow_groups()
    starts, cursor = [], 0
    for group in groups:
        starts.append(cursor)
        cursor += half_width(group)
    pieces = []
    for kind, number in (("n", 0), ("r", 0), ("n", 1), ("r", 1), ("n", 2), ("n", 3), ("r", 2), ("n", 4), ("r", 3)):
        if kind == "n":
            width = half_width(groups[number])
            count = width // PIECE
            for k in range(count):
                size = PIECE if k < count - 1 else width - k * PIECE
                pieces.append((kind, number, k * PIECE, size))
        else:
            pieces.append((kind, number, 0, D))
            pieces.append((kind, number, 1, D))
    return groups, starts, cursor, pieces


def gather_kernel(sizes, *refs):
    groups, starts, _, pieces = gather_plan()
    ins, outs = refs[:10], refs[10:19]
    halves, other, joined, send_sem, recv_sem, load_sem, swap_sem = refs[19:]
    place = grid_place()
    z, y, x, core = place
    sibling = device_at(moved(place, sizes, 3, 1))
    loads = []
    for number, group in enumerate(groups):
        for half in range(2):
            cursor = starts[number]
            for arg, layer, first, size in group[half]:
                source = ins[arg] if layer is None else ins[arg].at[layer]
                loads.append((source.at[:, pl.ds(first, size)], halves.at[half, :, pl.ds(cursor, size)]))
                cursor += size
    for number, (arg, layer) in enumerate(((1, 0), (1, 1), (5, 0), (5, 1))):
        for part in range(2):
            loads.append((ins[arg].at[layer, part], outs[5 + number].at[z, y, x, core, part]))
    started = []
    for k, (source, target) in enumerate(loads):
        copy = pltpu.make_async_copy(source, target, load_sem.at[k])
        copy.start()
        started.append(copy)
    greet(place, sizes)
    for copy in started:
        copy.wait()
    swaps = []
    for number, group in enumerate(groups):
        columns = pl.ds(starts[number], half_width(group))
        copy = pltpu.make_async_remote_copy(
            src_ref=halves.at[1 - core, :, columns],
            dst_ref=other.at[:, columns],
            send_sem=swap_sem.at[0, number],
            recv_sem=swap_sem.at[1, number],
            device_id=sibling,
            device_id_type=MESH_ID,
        )
        copy.start()
        swaps.append(copy)

    def view(piece, where):
        kind, number, first, size = piece
        iz, iy, ix = where[:3]
        if kind == "n":
            start = pl.multiple_of(core * half_width(groups[number]) + first, 128)
            return outs[number].at[iz, iy, ix, :, pl.ds(start, size)]
        return outs[5 + number].at[iz, iy, ix, core, first]

    prepared = {}

    def prepare(piece):
        kind, number, first, size = piece
        if kind == "n" and number not in prepared:
            swaps[number].wait()
            group = groups[number]
            for begin in range(starts[number], starts[number] + half_width(group), 128):
                columns = pl.ds(begin, 128)
                mine = halves[core, :, columns].astype(jnp.float32)
                theirs = other[:, columns].astype(jnp.float32)
                both = [jnp.where(core == 0, mine, theirs), jnp.where(core == 0, theirs, mine)]
                joined[:, columns] = jnp.concatenate(both, 0).astype(BF)
            width = half_width(group)
            copy = pltpu.make_async_copy(
                joined.at[:, pl.ds(starts[number], width)],
                outs[number].at[z, y, x, :, pl.ds(pl.multiple_of(core * width, 128), width)],
                load_sem.at[len(loads) + number],
            )
            copy.start()
            copy.wait()
            prepared[number] = True

    semaphores = [0]

    def transfers(number):
        piece = pieces[number]
        steps, done = [], []
        for axis in ROUTES[number % len(ROUTES)] + (3,):
            size, here = sizes[axis], place[axis]

            def block(at):
                where = list(place)
                for old in done:
                    where[old] = slice(None)
                where[axis] = jnp.clip(at, 0, size - 1)
                return view(piece, where)

            for hop in range(1, size):
                hops = []
                for way in (1, -1):
                    ahead, behind = here + way, here - way
                    sent, got = here - way * (hop - 1), here - way * hop
                    if size == 2 and way == -1:
                        continue
                    if size == 2:
                        ahead, behind, got = 1 - here, 1 - here, 1 - here
                    pair = []
                    for at, other_end in ((sent, ahead), (got, behind)):
                        ref = block(at)
                        target = place[:axis] + (jnp.clip(other_end, 0, size - 1),) + place[axis + 1 :]
                        pair.append(
                            pltpu.make_async_remote_copy(
                                src_ref=ref,
                                dst_ref=ref,
                                send_sem=send_sem.at[semaphores[0]],
                                recv_sem=recv_sem.at[semaphores[0]],
                                device_id=device_at(target),
                                device_id_type=MESH_ID,
                            )
                        )
                    semaphores[0] += 1
                    sends = jnp.logical_and(inside(sent, size), inside(ahead, size))
                    hops.append(Hop(pair, sends, inside(got, size)))
                steps.append(hops)
            done.append(axis)
        return steps

    running = {}
    depth = sum(size - 1 for size in sizes)
    lags = LAGS if depth + 1 == len(LAGS) else list(range(depth + 1))
    for tick in range(len(pieces) + lags[-1]):
        for step in reversed(range(depth + 1)):
            number = tick - lags[step]
            if number < 0 or number >= len(pieces):
                continue
            if step == 0:
                prepare(pieces[number])
                running[number] = transfers(number)
            else:
                for copy in running[number][step - 1]:
                    copy.wait()
            if step < depth:
                for copy in running[number][step]:
                    copy.start()
    for number in range(len(groups)):
        if number not in prepared:
            swaps[number].wait()


def gather_plainly(enc_in, enc_down, dec_qkv, dec_out, dec_in, dec_down, cca_q, cca_kv, cca_out, gains):
    get = lambda w: lax.all_gather(w, ("dp", "seq"), axis=w.ndim - 2, tiled=True)
    kv = get(cca_kv)
    return dict(
        enc_in=get(enc_in), enc_down=get(enc_down), dec_in=get(dec_in), dec_down=get(dec_down), dec_qkv=get(dec_qkv),
        dec_out=get(dec_out), cca_kv=[kv[:, :D], kv[:, D:]], cca_q=get(cca_q), cca_out=get(cca_out), gains=get(gains)[:, :8],
    )


def gather_weights(enc_in, enc_down, dec_qkv, dec_out, dec_in, dec_down, cca_q, cca_kv, cca_out, gains):
    sizes = grid_sizes()
    rows = cca_q.shape[0]
    groups, starts, total, pieces = gather_plan()
    part = enc_down.shape[1] // 2
    if rows % 4 or part % 8 or sizes[1:] != (2, 2, 2):
        return gather_plainly(enc_in, enc_down, dec_qkv, dec_out, dec_in, dec_down, cca_q, cca_kv, cca_out, gains)
    lead = sizes[:3]
    shapes = [lead + (2 * rows, 2 * half_width(group)) for group in groups] + [lead + (2, 2, part, D)] * 4
    per_piece = sum((size - 1) * (1 if size == 2 else 2) for size in sizes)
    n_loads = sum(len(half) for group in groups for half in group) + 8 + len(groups)
    split = lambda w: w.reshape(w.shape[0], 2, part, D)
    outs = pl.pallas_call(
        functools.partial(gather_kernel, sizes),
        out_shape=[jax.ShapeDtypeStruct(shape, BF) for shape in shapes],
        in_specs=[ANY] * 10,
        out_specs=[ANY] * 9,
        scratch_shapes=[
            pltpu.VMEM((2, rows, total), BF),
            pltpu.VMEM((rows, total), BF),
            pltpu.VMEM((2 * rows, total), BF),
            pltpu.SemaphoreType.DMA((per_piece * len(pieces),)),
            pltpu.SemaphoreType.DMA((per_piece * len(pieces),)),
            pltpu.SemaphoreType.DMA((n_loads,)),
            pltpu.SemaphoreType.DMA((2, len(groups))),
        ],
        compiler_params=pltpu.CompilerParams(collective_id=0, has_side_effects=True),
        name="gather_weights",
    )(enc_in, split(enc_down), dec_qkv, dec_out, dec_in, split(dec_down), cca_q, cca_kv, cca_out, gains)
    narrow = [out.reshape(D, out.shape[-1]) for out in outs[:5]]
    tall = [out.reshape(FF, D) for out in outs[5:]]
    mixed = narrow[2]
    half = mixed.shape[1] // 2
    sides = [mixed[:, :half], mixed[:, half:]]
    qkv = [side[:, 2 * D : 5 * D] for side in sides]
    out = [side[:, 5 * D : 6 * D] for side in sides]
    return dict(
        enc_in=narrow[:2], enc_down=tall[:2], dec_in=narrow[3:], dec_down=tall[2:], dec_qkv=qkv, dec_out=out,
        cca_kv=[side[:, :D] for side in sides], cca_q=sides[0][:, D : 2 * D], cca_out=sides[1][:, D : 2 * D],
        gains=sides[0][:, 6 * D : 6 * D + 8],
    )


ORDERS = ((1, False), (2, False), (1, True), (2, False), (1, False), (2, True))
CORE, HEAVY, ZED, PAIR, CORE_AGAIN, PER_PIECE = 0, 1, 2, 8, 9, 10
START = (0, 1, 4, 6, 7, 8, 9, 10, 11)
SLOTS = dict(part=2, whole=5, half=8, sibling=3, heavy=8, middle=8, last=8, zed=6, final=4)


def gradient_pieces():
    pieces = []
    both = lambda left, right, out, layer, k: tuple(
        (left, right, 2 * D * half + D * k, out, layer, 2 * D * half + D * k) for half in range(2)
    )
    for layer in reversed(range(2)):
        base = 8 * layer
        for k in range(2):
            pieces.append(both(base + 6, base + 7, 5, layer, k))
        for k in range(2):
            pieces.append(both(base + 4, base + 5, 4, layer, k))
    pieces.append(tuple((8 * layer + 2, 8 * layer + 3, 0, 3, layer, 0) for layer in range(2)))
    for k in range(3):
        pieces.append(tuple((8 * layer, 8 * layer + 1, D * k, 2, layer, D * k) for layer in range(2)))
    pieces.append(((16, 17, 0, 6, None, 0), (20, 21, 0, 8, None, 0)))
    pieces.append(tuple((18, 19, D * half, 7, None, D * half) for half in range(2)))
    for layer in reversed(range(2)):
        base = 22 + 4 * layer
        for k in range(2):
            pieces.append(both(base + 2, base + 3, 1, layer, k))
        for k in range(2):
            pieces.append(both(base, base + 1, 0, layer, k))
    return pieces


N_OPERANDS = 30


class Sums:
    def __init__(self, place, sizes, sems, buffers, slots, width):
        self.place, self.sizes, self.width = place, sizes, width
        self.send_sem, self.recv_sem = sems
        self.part, self.whole, self.half, self.sibling, self.heavy, self.middle, self.last, self.zed, self.final = buffers
        self.slots = slots

    def slot(self, name, number):
        return lax.rem(number, self.slots[name])

    def copy(self, number, which, source, target, device):
        index = number * PER_PIECE + which
        return pltpu.make_async_remote_copy(
            src_ref=source,
            dst_ref=target,
            send_sem=self.send_sem.at[index],
            recv_sem=self.recv_sem.at[index],
            device_id=device_at(device),
            device_id_type=MESH_ID,
        )

    def core_copy(self, number):
        return self.copy(
            number,
            CORE,
            self.part.at[self.slot("part", number)],
            self.sibling.at[self.slot("sibling", number)],
            self.swapped(3),
        )

    def swapped(self, axis):
        return self.place[:axis] + (1 - self.place[axis],) + self.place[axis + 1 :]

    def heavy_copy(self, number, axis):
        whole = self.whole.at[self.slot("whole", number)]
        there = 1 - self.place[axis]
        source = whole.at[:, there] if axis == 1 else whole.at[:, :, there]
        return self.copy(number, HEAVY, source, self.heavy.at[self.slot("heavy", number)], self.swapped(axis))

    def pair_copy(self, number, axis, early):
        half = self.half.at[self.slot("half", number)]
        there = 1 - self.place[axis]
        if early:
            source, target = half.at[:, there], self.middle.at[self.slot("middle", number)]
        else:
            source, target = half.at[self.place[0], there], self.last.at[self.slot("last", number)]
        return self.copy(number, PAIR, source, target, self.swapped(axis))

    def zed_block(self, number, axis, early, at):
        half = self.half.at[self.slot("half", number)]
        at = jnp.clip(at, 0, self.sizes[0] - 1)
        return half.at[at, pl.ds(self.place[axis], 1)] if early else half.at[at]

    def zed_room(self, number, early, hop, way):
        room = self.zed.at[self.slot("zed", number), hop - 1, way]
        return room.at[pl.ds(0, 1)] if early else room

    def zed_hops(self, number, axis, early, hop):
        z, size = self.place[0], self.sizes[0]
        found = []
        for way, by in enumerate((-1, 1)):
            sent, ahead = z + by * hop, z + by
            behind, got = z - by, z - by + by * hop
            room = self.zed_room(number, early, hop, way)
            device = (jnp.clip(ahead, 0, size - 1),) + self.place[1:]
            copy = self.copy(number, ZED + 2 * (hop - 1) + way, self.zed_block(number, axis, early, sent), room, device)
            sends = jnp.logical_and(inside(sent, size), inside(ahead, size))
            receives = jnp.logical_and(inside(got, size), inside(behind, size))
            found.append((copy, sends, receives, self.zed_block(number, axis, early, got), room))
        return found

    def start_zed(self, number, axis, early, hop):
        for copy, sends, _, _, _ in self.zed_hops(number, axis, early, hop):
            pl.when(sends)(copy.start)

    def finish_zed(self, number, axis, early, hop):
        for copy, sends, receives, block, room in self.zed_hops(number, axis, early, hop):
            pl.when(sends)(copy.wait_send)

            @pl.when(receives)
            def _():
                copy.wait_recv()
                for k in range(1 if early else 2):
                    block[k] = block[k] + room[k]

    def add_core(self, number):
        self.core_copy(number).wait()
        whole, sibling = self.slot("whole", number), self.slot("sibling", number)

        def one(k, _):
            at = (k // 4, (k // 2) % 2, k % 2)
            self.whole[(whole, *at)] = self.whole[(whole, *at)] + self.sibling[(sibling, *at)]
            return 0

        lax.fori_loop(0, 4 * self.sizes[0], one, 0)

    def add_heavy(self, number, axis):
        self.heavy_copy(number, axis).wait()
        whole, half, heavy = (self.slot(name, number) for name in ("whole", "half", "heavy"))

        def one(k, _):
            z, o = k // 2, k % 2
            at = (z, self.place[1], o) if axis == 1 else (z, o, self.place[2])
            self.half[half, z, o] = self.whole[(whole, *at)] + self.heavy[heavy, z, o]
            return 0

        lax.fori_loop(0, 2 * self.sizes[0], one, 0)

    def add_pair(self, number, axis, early):
        self.pair_copy(number, axis, early).wait()
        half, here = self.slot("half", number), self.place[axis]
        if early:
            for z in range(self.sizes[0]):
                self.half[half, z, here] = self.half[half, z, here] + self.middle[self.slot("middle", number), z]
        else:
            z = self.place[0]
            self.half[half, z, here] = self.half[half, z, here] + self.last[self.slot("last", number)]

    def split_rows(self, number, axis):
        half, final = self.slot("half", number), self.slot("final", number)
        rows = self.half[half, self.place[0], self.place[axis]].astype(jnp.float32)
        count = rows.shape[0] // 2
        first, second = rows[:count], rows[count:]
        self.final[final, 0] = jnp.where(self.place[3] == 0, first, second)
        self.final[final, 2] = jnp.where(self.place[3] == 0, second, first)

    def final_copy(self, number):
        final = self.slot("final", number)
        return self.copy(number, CORE_AGAIN, self.final.at[final, 2], self.final.at[final, 1], self.swapped(3))

    def step(self, step, number, first, early):
        other = 3 - first
        sequence = [("pair", 0), ("zed", 3), ("zed", 2), ("zed", 1)] if early else [("zed", 3), ("zed", 2), ("zed", 1), ("pair", 0)]
        if step == 1:
            self.heavy_copy(number, first).start()
            return
        if step == 2:
            self.add_heavy(number, first)
        else:
            kind, hop = sequence[step - 3]
            if kind == "pair":
                self.add_pair(number, other, early)
            else:
                self.finish_zed(number, other, early, hop)
        if step < 6:
            kind, hop = sequence[step - 2]
            if kind == "pair":
                self.pair_copy(number, other, early).start()
            else:
                self.start_zed(number, other, early, hop)
        else:
            self.split_rows(number, other)
            self.final_copy(number).start()


def reduce_kernel(sizes, tall, *refs):
    pieces = gradient_pieces()
    operands, gains = refs[:N_OPERANDS], refs[N_OPERANDS]
    outs = refs[N_OPERANDS + 1 : N_OPERANDS + 11]
    scratch = refs[N_OPERANDS + 11 :]
    left, right, product = scratch[:3]
    buffers, small = scratch[3:12], scratch[12:21]
    send_sem, recv_sem, small_send, small_recv, load_sem, out_sem = scratch[21:]
    place = grid_place()
    core = place[3]
    count = len(pieces)
    sums = Sums(place, sizes, (send_sem, recv_sem), buffers, SLOTS, D)
    once = Sums(place, sizes, (small_send, small_recv), small, {name: 1 for name in SLOTS}, 128)
    is_tall = [tall[piece[0][0]] for piece in pieces]
    first_tall = is_tall.index(True)
    long_rows, short_rows = left.shape[2], None

    def rows_of(k):
        return operands[pieces[k][0][0]].shape[0]

    def loads(k, slot):
        rows = rows_of(k)
        found = []
        for half in range(2):
            l, r, column, _, _, _ = pieces[k][half]
            mine = jnp.where(core == half, 1, 0)
            found.append((operands[l], left.at[slot, mine, pl.ds(0, rows)], load_sem.at[slot, half]))
            found.append((operands[r].at[:, pl.ds(column, D)], right.at[slot, mine, pl.ds(0, rows)], load_sem.at[slot, 2 + half]))
        return [pltpu.make_async_copy(*args) for args in found]

    def start_loads(number):
        for k in range(count):

            @pl.when(number == k)
            def _():
                for copy in loads(k, k % 2):
                    copy.start()

    def multiply(number, which, rows):
        slot = lax.rem(number, 2)

        def block(k, _):
            columns = pl.ds(pl.multiple_of(k * 128, 128), 128)
            product[pl.ds(pl.multiple_of(k * 128, 128), 128), :] = lax.dot_general(
                left[slot, which, pl.ds(0, rows), columns],
                right[slot, which, pl.ds(0, rows), :],
                (((0,), (0,)), ((), ())),
                preferred_element_type=jnp.float32,
            )
            return 0

        lax.fori_loop(0, D // 128, block, 0)
        chunk = sums.whole.shape[4]

        def store(k, _):
            values = product[pl.ds(pl.multiple_of(k * chunk, 8), chunk), :].astype(BF)
            at = (k // 4, (k // 2) % 2, k % 2)
            if which == 0:
                sums.part[(sums.slot("part", number), *at)] = values
            else:
                sums.whole[(sums.slot("whole", number), *at)] = values
            return 0

        lax.fori_loop(0, D // chunk, store, 0)

    def compute(number):
        for flag in sorted(set(is_tall)):
            wanted = jnp.logical_and(number >= first_tall, flag) if flag else number < first_tall
            k = first_tall if flag else 0

            @pl.when(wanted)
            def _():
                for copy in loads(k, lax.rem(number, 2)):
                    copy.wait()
                multiply(number, 0, rows_of(k))
                sums.core_copy(number).start()
                multiply(number, 1, rows_of(k))

    def out_copies(k):
        slot = k % SLOTS["final"]
        found = []
        for half in range(2):
            _, _, _, out, layer, column = pieces[k][half]
            target = outs[out] if layer is None else outs[out].at[layer]
            source = sums.final.at[slot, jnp.where(core == half, 0, 1)]
            found.append(pltpu.make_async_copy(source, target.at[:, pl.ds(column, D)], out_sem.at[slot, half]))
        return found

    greet(place, sizes)
    small_loads = []
    for k, target in enumerate((once.part.at[0], once.whole.at[0])):
        copy = pltpu.make_async_copy(gains, target, out_sem.at[SLOTS["final"], k])
        copy.start()
        small_loads.append(copy)
    start_loads(0)

    def tick(time, _):
        for step in reversed(range(8)):

            @pl.when(time == START[step])
            def _():
                if step == 0:
                    for copy in small_loads:
                        copy.wait()
                    once.core_copy(0).start()
                elif step == 7:
                    once.final_copy(0).wait()
                    copy = pltpu.make_async_copy(once.final.at[0, 0], outs[9], out_sem.at[SLOTS["final"], 0])
                    copy.start()
                    copy.wait()
                else:
                    if step == 1:
                        once.add_core(0)
                    once.step(step, 0, *ORDERS[-1])

        for step in reversed(range(9)):
            number = time - START[step]

            @pl.when(jnp.logical_and(number >= 0, number < count))
            def _():
                if step == 0:
                    start_loads(number + 1)
                    compute(number)
                elif step == 8:
                    for copy in out_copies_at(number):
                        copy.wait()
                elif step == 7:
                    sums.final_copy(number).wait()
                    for k in range(count):

                        @pl.when(number == k)
                        def _():
                            for copy in out_copies(k):
                                copy.start()

                else:
                    if step == 1:
                        sums.add_core(number)
                    turn = lax.rem(number, len(ORDERS))
                    for order in sorted(set(ORDERS)):
                        here = functools.reduce(jnp.logical_or, [turn == k for k, one in enumerate(ORDERS) if one == order])

                        @pl.when(here)
                        def _():
                            sums.step(step, number, *order)

        return 0

    def out_copies_at(number):
        slot = lax.rem(number, SLOTS["final"])
        return [
            pltpu.make_async_copy(sums.final.at[slot, 0], outs[3].at[0, :, pl.ds(0, D)], out_sem.at[slot, half])
            for half in range(2)
        ]

    lax.fori_loop(0, count + START[8], tick, 0)


def reduce_gradients(operands, gains, layers_rows):
    sizes = grid_sizes()
    rows = layers_rows
    chunk = 2 * rows
    lead = sizes[:3] + (chunk,)
    longest = max(x.shape[0] for x in operands)
    shortest = min(x.shape[0] for x in operands)
    tall = tuple(x.shape[0] == longest for x in operands)
    f32 = jnp.float32
    shapes = [(2, rows, FF), (2, rows, FF), (2, rows, 3 * D), (2, rows, D), (2, rows, FF), (2, rows, FF)]
    shapes += [(rows, D), (rows, 2 * D), (rows, D), (rows, 128)]

    def rooms(slots, width):
        z = sizes[0]
        return [
            pltpu.VMEM((slots["part"],) + lead + (width,), BF),
            pltpu.VMEM((slots["whole"],) + lead + (width,), BF),
            pltpu.VMEM((slots["half"], z, 2, chunk, width), BF),
            pltpu.VMEM((slots["sibling"],) + lead + (width,), BF),
            pltpu.VMEM((slots["heavy"], z, 2, chunk, width), BF),
            pltpu.VMEM((slots["middle"], z, chunk, width), BF),
            pltpu.VMEM((slots["last"], chunk, width), BF),
            pltpu.VMEM((slots["zed"], z - 1, 2, 2, chunk, width), BF),
            pltpu.VMEM((slots["final"], 3, rows, width), f32),
        ]

    count = len(gradient_pieces())
    return pl.pallas_call(
        functools.partial(reduce_kernel, sizes, tall),
        out_shape=[jax.ShapeDtypeStruct(shape, f32) for shape in shapes],
        in_specs=[ANY] * (N_OPERANDS + 1),
        out_specs=[ANY] * 10,
        scratch_shapes=[
            pltpu.VMEM((2, 2, longest, D), BF),
            pltpu.VMEM((2, 2, longest, D), BF),
            pltpu.VMEM((D, D), f32),
            *rooms(SLOTS, D),
            *rooms({name: 1 for name in SLOTS}, 128),
            pltpu.SemaphoreType.DMA((PER_PIECE * count,)),
            pltpu.SemaphoreType.DMA((PER_PIECE * count,)),
            pltpu.SemaphoreType.DMA((PER_PIECE,)),
            pltpu.SemaphoreType.DMA((PER_PIECE,)),
            pltpu.SemaphoreType.DMA((2, 4)),
            pltpu.SemaphoreType.DMA((SLOTS["final"] + 1, 2)),
        ],
        compiler_params=pltpu.CompilerParams(collective_id=1, has_side_effects=True, vmem_limit_bytes=62 << 20),
        name="reduce_gradients",
    )(*operands, gains.reshape(lead + (128,)))


HEADS = 14
HEAD = 64
SPAN = 64
NEIGH = 2
RET = 128
ENC_LAYERS = 2
DEC_LAYERS = 2


EPSILON = 1e-06
SCORE_SCALE = 0.125
MASKED_SCORE = -1000000000.0


def shifted(x, axis, by):
    count = lax.axis_size(axis)
    pairs = [(i, i + by) for i in range(count) if 0 <= i + by < count]
    return lax.ppermute(x, axis, pairs)


def normed(values, norm_gain):
    return values * lax.rsqrt(jnp.mean(values * values, -1, keepdims=True) + EPSILON) * norm_gain


def gelu_exact(values):
    return jax.nn.gelu(values, approximate=False)


def project(values, weight):
    return jnp.dot(values, weight, preferred_element_type=jnp.float32)


def back_project(upstream, weight):
    return lax.dot_general(
        upstream,
        weight,
        (((upstream.ndim - 1,), (1,)), ((), ())),
        preferred_element_type=jnp.float32,
    )


def slab_term(left, right):
    flat_left = left.reshape(-1, left.shape[-1])
    flat_right = right.reshape(-1, right.shape[-1])
    return lax.dot_general(
        flat_left, flat_right, (((0,), (0,)), ((), ())), preferred_element_type=jnp.float32
    )


def norm_back(stream, norm_gain, upstream):
    _, pullback = jax.vjp(normed, stream, norm_gain)
    return pullback(upstream)


def split_heads(values):
    return values.reshape(values.shape[:-1] + (HEADS, HEAD))


def softmax_parts(scores):
    row_peak = jnp.max(scores, -1, keepdims=True)
    powers = jnp.exp(scores - row_peak)
    row_total = jnp.sum(powers, -1, keepdims=True)
    return (powers / row_total, (row_peak + jnp.log(row_total))[..., 0])


def feed_forward(stream, norm_gain, weight_in, weight_down):
    inputs = normed(stream, norm_gain).astype(jnp.bfloat16)
    hidden_pre = project(inputs, weight_in)
    hidden = gelu_exact(hidden_pre).astype(jnp.bfloat16)
    return (stream + project(hidden, weight_down), (stream, inputs, hidden_pre, hidden))


def feed_back(stored, norm_gain, weight_in, weight_down, upstream):
    stream, inputs, hidden_pre, hidden = stored
    grad_low = upstream.astype(jnp.bfloat16)
    grad_hidden = back_project(grad_low, weight_down)
    _, gelu_pull = jax.vjp(gelu_exact, hidden_pre)
    grad_pre = gelu_pull(grad_hidden)[0].astype(jnp.bfloat16)
    stream_grad, gain_grad = norm_back(stream, norm_gain, back_project(grad_pre, weight_in))
    return (upstream + stream_grad, gain_grad, ((inputs, grad_pre), (grad_low, hidden)))


def score_table(queries, keys_all, offset):
    raw_scores = (
        jnp.einsum("bqhd,bkhd->bhqk", queries, keys_all, preferred_element_type=jnp.float32)
        * SCORE_SCALE
    )
    key_place = jnp.arange(keys_all.shape[1])
    query_place = offset + jnp.arange(queries.shape[1])
    return jnp.where(key_place[None, :] <= query_place[:, None], raw_scores, MASKED_SCORE)


def self_forward(stream, norm_gain, weight_qkv, weight_out, offset):
    inputs = normed(stream, norm_gain).astype(jnp.bfloat16)
    joined = project(inputs, weight_qkv).astype(jnp.bfloat16)
    keys_vals = lax.all_gather(joined[..., D:], "seq", axis=1, tiled=True)
    queries = split_heads(joined[..., :D])
    scores = score_table(queries, split_heads(keys_vals[..., :D]), offset)
    attn_probs, log_total = softmax_parts(scores)
    attn_mixed = jnp.einsum(
        "bhqk,bkhd->bqhd",
        attn_probs.astype(jnp.bfloat16),
        split_heads(keys_vals[..., D:]),
        preferred_element_type=jnp.float32,
    )
    attn_mixed = attn_mixed.astype(jnp.bfloat16).reshape(stream.shape)
    return (
        stream + project(attn_mixed, weight_out),
        (stream, inputs, joined, keys_vals, log_total, attn_mixed),
    )


def self_back(stored, norm_gain, weight_qkv, weight_out, offset, upstream):
    stream, inputs, joined, keys_vals, log_total, attn_mixed = stored
    grad_low = upstream.astype(jnp.bfloat16)
    grad_mixed = split_heads(back_project(grad_low, weight_out).astype(jnp.bfloat16))
    queries = split_heads(joined[..., :D])
    keys_all = split_heads(keys_vals[..., :D])
    vals_all = split_heads(keys_vals[..., D:])
    scores = score_table(queries, keys_all, offset)
    attn_probs = jnp.exp(scores - log_total[..., None])
    grad_probs = jnp.einsum(
        "bqhd,bkhd->bhqk", grad_mixed, vals_all, preferred_element_type=jnp.float32
    )
    row_delta = jnp.sum(attn_probs * grad_probs, -1)
    grad_scores = (attn_probs * (grad_probs - row_delta[..., None])).astype(jnp.bfloat16)
    grad_queries = (
        jnp.einsum("bhqk,bkhd->bqhd", grad_scores, keys_all, preferred_element_type=jnp.float32)
        * SCORE_SCALE
    )
    seqs_here = queries.shape[0]
    grad_vals = jnp.einsum(
        "bhqk,bqhd->bkhd",
        attn_probs.astype(jnp.bfloat16),
        grad_mixed,
        preferred_element_type=jnp.float32,
    )
    grad_keys = (
        jnp.einsum("bhqk,bqhd->bkhd", grad_scores, queries, preferred_element_type=jnp.float32)
        * SCORE_SCALE
    )
    length = grad_keys.shape[1]
    grad_pairs = jnp.concatenate(
        [grad_keys.reshape(seqs_here, length, D), grad_vals.reshape(seqs_here, length, D)], -1
    )
    own_pairs = lax.psum_scatter(
        grad_pairs.astype(jnp.bfloat16), "seq", scatter_dimension=1, tiled=True
    ).astype(jnp.float32)
    grad_joined = jnp.concatenate([grad_queries.reshape(stream.shape), own_pairs], -1).astype(
        jnp.bfloat16
    )
    stream_grad, gain_grad = norm_back(stream, norm_gain, back_project(grad_joined, weight_qkv))
    return (upstream + stream_grad, gain_grad, ((inputs, grad_joined), (attn_mixed, grad_low)))


def cross_scores(queries, keys_vals, prior_flag):
    raw_scores = (
        jnp.einsum(
            "bcqhd,bckhd->bchqk",
            queries,
            split_heads(keys_vals[..., :D]),
            preferred_element_type=jnp.float32,
        )
        * SCORE_SCALE
    )
    allowed = jnp.repeat(prior_flag, RET, axis=2) > 0.5
    return jnp.where(allowed[:, :, None, None, :], raw_scores, MASKED_SCORE)


def row_gate(prior_flag):
    return jnp.repeat(jnp.max(prior_flag, -1).astype(jnp.float32), SPAN, axis=1)[..., None]


def cross_forward(stream, encoded, keep_flag, norm_gain, weight_q, weight_kv, weight_out):
    seqs_here = stream.shape[0]
    spans_here = encoded.shape[1]
    last_enc, last_flag = shifted((encoded[:, -1], keep_flag[:, -1]), "seq", 1)
    prior_enc = jnp.concatenate([last_enc[:, None], encoded[:, :-1]], 1)
    prior_flag = jnp.concatenate([last_flag[:, None], keep_flag[:, :-1]], 1)
    inputs = normed(stream, norm_gain).astype(jnp.bfloat16)
    queries = (
        project(inputs, weight_q)
        .astype(jnp.bfloat16)
        .reshape(seqs_here, spans_here, SPAN, HEADS, HEAD)
    )
    keys_vals = (
        project(prior_enc, weight_kv)
        .astype(jnp.bfloat16)
        .reshape(seqs_here, spans_here, NEIGH * RET, 2 * D)
    )
    scores = cross_scores(queries, keys_vals, prior_flag)
    attn_probs, log_total = softmax_parts(scores)
    attn_mixed = jnp.einsum(
        "bchqk,bckhd->bcqhd",
        attn_probs.astype(jnp.bfloat16),
        split_heads(keys_vals[..., D:]),
        preferred_element_type=jnp.float32,
    )
    attn_mixed = attn_mixed.astype(jnp.bfloat16).reshape(stream.shape)
    branch = row_gate(prior_flag) * project(attn_mixed, weight_out)
    return (
        stream + branch,
        (stream, inputs, prior_enc, prior_flag, queries, keys_vals, log_total, attn_mixed),
    )


def cross_back(stored, norm_gain, weight_q, weight_kv, weight_out, upstream):
    stream, inputs, prior_enc, prior_flag, queries, keys_vals, log_total, attn_mixed = stored
    grad_low = (upstream * row_gate(prior_flag)).astype(jnp.bfloat16)
    grad_mixed = back_project(grad_low, weight_out).astype(jnp.bfloat16).reshape(queries.shape)
    scores = cross_scores(queries, keys_vals, prior_flag)
    attn_probs = jnp.exp(scores - log_total[..., None])
    keys_part = split_heads(keys_vals[..., :D])
    vals_part = split_heads(keys_vals[..., D:])
    grad_vals = jnp.einsum(
        "bchqk,bcqhd->bckhd",
        attn_probs.astype(jnp.bfloat16),
        grad_mixed,
        preferred_element_type=jnp.float32,
    )
    grad_probs = jnp.einsum(
        "bcqhd,bckhd->bchqk", grad_mixed, vals_part, preferred_element_type=jnp.float32
    )
    grad_scores = attn_probs * (grad_probs - jnp.sum(attn_probs * grad_probs, -1, keepdims=True))
    grad_scores = grad_scores.astype(jnp.bfloat16)
    grad_queries = (
        jnp.einsum("bchqk,bckhd->bcqhd", grad_scores, keys_part, preferred_element_type=jnp.float32)
        * SCORE_SCALE
    )
    grad_keys = (
        jnp.einsum("bchqk,bcqhd->bckhd", grad_scores, queries, preferred_element_type=jnp.float32)
        * SCORE_SCALE
    )
    pair_shape = keys_vals.shape[:-1] + (D,)
    grad_pairs = jnp.concatenate([grad_keys.reshape(pair_shape), grad_vals.reshape(pair_shape)], -1)
    grad_pairs = grad_pairs.astype(jnp.bfloat16)
    grad_prior = back_project(grad_pairs, weight_kv).reshape(prior_enc.shape)
    query_low = grad_queries.reshape(stream.shape).astype(jnp.bfloat16)
    stream_grad, gain_grad = norm_back(stream, norm_gain, back_project(query_low, weight_q))
    from_next = shifted(grad_prior[:, 0].astype(jnp.bfloat16), "seq", -1).astype(jnp.float32)
    encoded_grad = jnp.concatenate([grad_prior[:, 1:], from_next[:, None]], 1)
    pairs = ((inputs, query_low), (prior_enc, grad_pairs), (attn_mixed, grad_low))
    return (upstream + stream_grad, gain_grad, pairs, encoded_grad)


def encode(retrieved, enc_gain, enc_in, enc_down, enc_final):
    stream = retrieved.astype(jnp.float32)
    stored = []
    for layer_idx in range(ENC_LAYERS):
        stream, layer_store = feed_forward(
            stream, enc_gain[layer_idx], enc_in[layer_idx], enc_down[layer_idx]
        )
        stored.append(layer_store)
    return (normed(stream, enc_final).astype(jnp.bfloat16), (stream, stored))


def encode_back(retrieved, enc_weights, encoded_grad):
    enc_gain, enc_in, enc_down, enc_final = enc_weights
    _, (stream, stored) = encode(retrieved, enc_gain, enc_in, enc_down, enc_final)
    upstream, final_grad = norm_back(stream, enc_final, encoded_grad)
    gain_list = [None] * ENC_LAYERS
    pair_list = [None] * ENC_LAYERS
    for layer_idx in reversed(range(ENC_LAYERS)):
        upstream, gain_list[layer_idx], pair_list[layer_idx] = feed_back(
            stored[layer_idx], enc_gain[layer_idx], enc_in[layer_idx], enc_down[layer_idx], upstream
        )
    return (gain_list, pair_list, final_grad)


def on_device(
    tokens,
    retrieved,
    span_doc,
    neigh_doc,
    cotangent,
    dec_gain,
    dec_qkv,
    dec_out,
    dec_in,
    dec_down,
    cca_gain,
    cca_q,
    cca_kv,
    cca_out,
    enc_gain,
    enc_in,
    enc_down,
    enc_final,
):
    offset = lax.axis_index("seq") * tokens.shape[1]
    rows = cca_q.shape[0]
    own_gains = jnp.concatenate([dec_gain.reshape(4, rows), cca_gain[None], enc_gain, enc_final[None]], 0).T
    own_gains = jnp.pad(own_gains, ((0, 0), (0, 120)))
    full = gather_weights(enc_in, enc_down, dec_qkv, dec_out, dec_in, dec_down, cca_q, cca_kv, cca_out, own_gains)
    gains = full["gains"].T
    enc_weights = (gains[5:7], full["enc_in"], full["enc_down"], gains[7])
    encoded, _ = encode(retrieved, enc_weights[0], enc_weights[1], enc_weights[2], enc_weights[3])
    keep_flag = (neigh_doc != span_doc[..., None]).astype(jnp.bfloat16)
    dec_weights = (
        gains[:4].reshape(2, 2, D), full["dec_qkv"], full["dec_out"], full["dec_in"], full["dec_down"],
        gains[4], full["cca_q"], jnp.concatenate(full["cca_kv"], 1), full["cca_out"],
    )
    norm_gains, qkv_all, out_all, in_all, down_all, cross_gain, cross_q, cross_kv, cross_out = (
        dec_weights
    )
    stream = tokens.astype(jnp.float32)
    attn_stores, ffn_stores = ([], [])
    stream, attn_store = self_forward(stream, norm_gains[0, 0], qkv_all[0], out_all[0], offset)
    attn_stores.append(attn_store)
    stream, cross_store = cross_forward(
        stream, encoded, keep_flag, cross_gain, cross_q, cross_kv, cross_out
    )
    stream, ffn_store = feed_forward(stream, norm_gains[0, 1], in_all[0], down_all[0])
    ffn_stores.append(ffn_store)
    layer_idx = 1
    stream, attn_store = self_forward(
        stream, norm_gains[layer_idx, 0], qkv_all[layer_idx], out_all[layer_idx], offset
    )
    attn_stores.append(attn_store)
    stream, ffn_store = feed_forward(
        stream, norm_gains[layer_idx, 1], in_all[layer_idx], down_all[layer_idx]
    )
    ffn_stores.append(ffn_store)
    result = stream.astype(jnp.bfloat16)
    upstream = cotangent.astype(jnp.float32)
    attn_gain_g = [None] * DEC_LAYERS
    ffn_gain_g = [None] * DEC_LAYERS
    attn_pairs = [None] * DEC_LAYERS
    ffn_pairs = [None] * DEC_LAYERS
    for layer_idx in reversed(range(1, DEC_LAYERS)):
        upstream, ffn_gain_g[layer_idx], ffn_pairs[layer_idx] = feed_back(
            ffn_stores[layer_idx],
            norm_gains[layer_idx, 1],
            in_all[layer_idx],
            down_all[layer_idx],
            upstream,
        )
        upstream, attn_gain_g[layer_idx], attn_pairs[layer_idx] = self_back(
            attn_stores[layer_idx],
            norm_gains[layer_idx, 0],
            qkv_all[layer_idx],
            out_all[layer_idx],
            offset,
            upstream,
        )
    upstream, ffn_gain_g[0], ffn_pairs[0] = feed_back(
        ffn_stores[0], norm_gains[0, 1], in_all[0], down_all[0], upstream
    )
    upstream, cross_gain_g, cross_pairs, encoded_grad = cross_back(
        cross_store, cross_gain, cross_q, cross_kv, cross_out, upstream
    )
    upstream, attn_gain_g[0], attn_pairs[0] = self_back(
        attn_stores[0], norm_gains[0, 0], qkv_all[0], out_all[0], offset, upstream
    )
    enc_gain_g, enc_pairs, final_gain_g = encode_back(retrieved, enc_weights, encoded_grad)
    pair_list = []
    for layer_idx in range(DEC_LAYERS):
        pair_list = pair_list + list(attn_pairs[layer_idx]) + list(ffn_pairs[layer_idx])
    pair_list = pair_list + list(cross_pairs)
    for layer_idx in range(ENC_LAYERS):
        pair_list = pair_list + list(enc_pairs[layer_idx])
    gain_list = []
    for layer_idx in range(DEC_LAYERS):
        gain_list = gain_list + [attn_gain_g[layer_idx], ffn_gain_g[layer_idx]]
    gain_list = gain_list + [cross_gain_g] + list(enc_gain_g) + [final_gain_g]

    grads = sum_gradients(pair_list, gain_list, rows)
    (enc_in_g, enc_down_g, dec_qkv_g, dec_out_g, dec_in_g, dec_down_g, cross_q_g, cross_kv_g, cross_out_g, gain_cols) = grads
    gain_rows = gain_cols[:, :8].T
    return (
        result,
        upstream,
        gain_rows[:4].reshape(2, 2, rows),
        dec_qkv_g,
        dec_out_g,
        dec_in_g,
        jnp.swapaxes(dec_down_g, 1, 2),
        gain_rows[4],
        cross_q_g,
        cross_kv_g,
        cross_out_g,
        gain_rows[5:7],
        enc_in_g,
        jnp.swapaxes(enc_down_g, 1, 2),
        gain_rows[7],
    )


def sum_plainly(pair_list, gain_list):
    blocks = [slab_term(left, right) for left, right in pair_list] + [vector[:, None] for vector in gain_list]
    owned = lax.psum_scatter(
        jnp.concatenate(blocks, 1).astype(BF), ("dp", "seq"), scatter_dimension=0, tiled=True
    ).astype(jnp.float32)
    pieces, cursor = [], 0
    for _, right in pair_list:
        pieces.append(owned[:, cursor : cursor + right.shape[-1]])
        cursor += right.shape[-1]
    two = lambda first, second: jnp.stack([pieces[first], pieces[second]])
    return [
        two(11, 13), two(12, 14), two(0, 4), two(1, 5), two(2, 6), two(3, 7), pieces[8], pieces[9], pieces[10], owned[:, cursor:]
    ]


def sum_gradients(pair_list, gain_list, rows):
    sizes = grid_sizes()
    if rows % 4 or sizes != (4, 2, 2, 2):
        return sum_plainly(pair_list, gain_list)
    operands = [x.reshape(-1, x.shape[-1]) for pair in pair_list for x in pair]
    gains = jnp.pad(jnp.stack(gain_list).astype(BF).T, ((0, 0), (0, 128 - len(gain_list))))
    return reduce_gradients(operands, gains, rows)


def solution(mesh):
    return jax.shard_map(
        on_device,
        mesh=mesh,
        in_specs=(
            P("dp", "seq", None),
            P("dp", "seq", None, None, None),
            P("dp", "seq"),
            P("dp", "seq", None),
            P("dp", "seq", None),
            P(None, None, ("dp", "seq")),
            P(None, ("dp", "seq"), None),
            P(None, ("dp", "seq"), None),
            P(None, ("dp", "seq"), None),
            P(None, ("dp", "seq"), None),
            P(("dp", "seq")),
            P(("dp", "seq"), None),
            P(("dp", "seq"), None),
            P(("dp", "seq"), None),
            P(None, ("dp", "seq")),
            P(None, ("dp", "seq"), None),
            P(None, ("dp", "seq"), None),
            P(("dp", "seq")),
        ),
        out_specs=(
            P("dp", "seq", None),
            P("dp", "seq", None),
            P(None, None, ("dp", "seq")),
            P(None, ("dp", "seq"), None),
            P(None, ("dp", "seq"), None),
            P(None, ("dp", "seq"), None),
            P(None, None, ("dp", "seq")),
            P(("dp", "seq")),
            P(("dp", "seq"), None),
            P(("dp", "seq"), None),
            P(("dp", "seq"), None),
            P(None, ("dp", "seq")),
            P(None, ("dp", "seq"), None),
            P(None, None, ("dp", "seq")),
            P(("dp", "seq")),
        ),
        check_vma=False,
    )
```

```python
import functools
import jax
import jax.numpy as jnp
from jax import lax
from jax.experimental import pallas as pl
from jax.experimental.pallas import tpu as pltpu
from jax.sharding import PartitionSpec as P

D = 896
FF = 3584
HEADS = 14
HEAD = 64
SPAN = 64
NEIGH = 2
RET = 128
ENC_LAYERS = 2
DEC_LAYERS = 2
EPSILON = 1e-06
SCORE_SCALE = 0.125
MASKED_SCORE = -1000000000.0
BF = jnp.bfloat16
MESH_ID = pl.DeviceIdType.MESH
ANY = pl.BlockSpec(memory_space=pl.ANY)


def grid_sizes():
    return (lax.axis_size("dp"), lax.axis_size("seq") // 4, 2, 2)


def grid_place():
    seq = lax.axis_index("seq")
    return (lax.axis_index("dp"), seq // 4, (seq // 2) % 2, seq % 2)


def device_at(place):
    z, y, x, core = place
    return (z, (y * 2 + x) * 2 + core)


def moved(place, sizes, axis, by):
    size = sizes[axis]
    there = lax.rem(place[axis] + (by % size), size)
    return place[:axis] + (there,) + place[axis + 1 :]


def greet(place, sizes):
    barrier = pltpu.get_barrier_semaphore()
    for axis in range(4):
        size, here = sizes[axis], place[axis]
        for by in (1, -1):
            there = here + by

            @pl.when(inside(there, size))
            def _():
                other = place[:axis] + (jnp.clip(there, 0, size - 1),) + place[axis + 1 :]
                pl.semaphore_signal(barrier, inc=1, device_id=device_at(other), device_id_type=MESH_ID)

    count = 0
    for axis in range(4):
        for by in (1, -1):
            count = count + inside(place[axis] + by, sizes[axis]).astype(jnp.int32)
    pl.semaphore_wait(barrier, count)


class Hop:
    def __init__(self, copy, sends, receives):
        self.copy, self.sends, self.receives = copy, sends, receives

    def start(self):
        pl.when(self.sends)(self.copy[0].start)

    def wait(self):
        pl.when(self.sends)(self.copy[0].wait_send)
        pl.when(self.receives)(self.copy[1].wait_recv)


def inside(place, size):
    return jnp.logical_and(place >= 0, place < size)


ROUTES = ((2, 0, 1), (1, 0, 2), (0, 2, 1), (1, 0, 2), (2, 0, 1), (0, 1, 2))
LAGS = (0, 1, 2, 3, 5, 8, 9)
PIECE = 896


def narrow_groups():
    qkv = 3 * D
    wide = FF // 2
    whole = lambda arg, layer: [[(arg, layer, 0, wide)], [(arg, layer, wide, wide)]]
    return [
        whole(0, 0),
        whole(0, 1),
        [
            [(7, None, 0, D), (6, None, 0, D), (2, 0, 0, qkv), (3, 0, 0, D), (9, None, 0, 128)],
            [(7, None, D, D), (8, None, 0, D), (2, 1, 0, qkv), (3, 1, 0, D), (9, None, 0, 128)],
        ],
        whole(4, 0),
        whole(4, 1),
    ]


def half_width(group):
    return sum(part[3] for part in group[0])


def gather_plan():
    groups = narrow_groups()
    starts, cursor = [], 0
    for group in groups:
        starts.append(cursor)
        cursor += half_width(group)
    pieces = []
    for kind, number in (("n", 0), ("r", 0), ("n", 1), ("r", 1), ("n", 2), ("n", 3), ("r", 2), ("n", 4), ("r", 3)):
        if kind == "n":
            width = half_width(groups[number])
            count = width // PIECE
            for k in range(count):
                size = PIECE if k < count - 1 else width - k * PIECE
                pieces.append((kind, number, k * PIECE, size))
        else:
            pieces.append((kind, number, 0, D))
            pieces.append((kind, number, 1, D))
    return groups, starts, cursor, pieces


def gather_kernel(sizes, *refs):
    groups, starts, _, pieces = gather_plan()
    ins, outs = refs[:10], refs[10:19]
    halves, other, joined, send_sem, recv_sem, load_sem, swap_sem = refs[19:]
    place = grid_place()
    z, y, x, core = place
    sibling = device_at(moved(place, sizes, 3, 1))
    loads = []
    for number, group in enumerate(groups):
        for half in range(2):
            cursor = starts[number]
            for arg, layer, first, size in group[half]:
                source = ins[arg] if layer is None else ins[arg].at[layer]
                loads.append((source.at[:, pl.ds(first, size)], halves.at[half, :, pl.ds(cursor, size)]))
                cursor += size
    for number, (arg, layer) in enumerate(((1, 0), (1, 1), (5, 0), (5, 1))):
        for part in range(2):
            loads.append((ins[arg].at[layer, part], outs[5 + number].at[z, y, x, core, part]))
    started = []
    for k, (source, target) in enumerate(loads):
        copy = pltpu.make_async_copy(source, target, load_sem.at[k])
        copy.start()
        started.append(copy)
    greet(place, sizes)
    for copy in started:
        copy.wait()
    swaps = []
    for number, group in enumerate(groups):
        columns = pl.ds(starts[number], half_width(group))
        copy = pltpu.make_async_remote_copy(
            src_ref=halves.at[1 - core, :, columns],
            dst_ref=other.at[:, columns],
            send_sem=swap_sem.at[0, number],
            recv_sem=swap_sem.at[1, number],
            device_id=sibling,
            device_id_type=MESH_ID,
        )
        copy.start()
        swaps.append(copy)

    def view(piece, where):
        kind, number, first, size = piece
        iz, iy, ix = where[:3]
        if kind == "n":
            start = pl.multiple_of(core * half_width(groups[number]) + first, 128)
            return outs[number].at[iz, iy, ix, :, pl.ds(start, size)]
        return outs[5 + number].at[iz, iy, ix, core, first]

    prepared = {}

    def prepare(piece):
        kind, number, first, size = piece
        if kind == "n" and number not in prepared:
            swaps[number].wait()
            group = groups[number]
            for begin in range(starts[number], starts[number] + half_width(group), 128):
                columns = pl.ds(begin, 128)
                mine = halves[core, :, columns].astype(jnp.float32)
                theirs = other[:, columns].astype(jnp.float32)
                both = [jnp.where(core == 0, mine, theirs), jnp.where(core == 0, theirs, mine)]
                joined[:, columns] = jnp.concatenate(both, 0).astype(BF)
            width = half_width(group)
            copy = pltpu.make_async_copy(
                joined.at[:, pl.ds(starts[number], width)],
                outs[number].at[z, y, x, :, pl.ds(pl.multiple_of(core * width, 128), width)],
                load_sem.at[len(loads) + number],
            )
            copy.start()
            copy.wait()
            prepared[number] = True

    semaphores = [0]

    def transfers(number):
        piece = pieces[number]
        steps, done = [], []
        for axis in ROUTES[number % len(ROUTES)] + (3,):
            size, here = sizes[axis], place[axis]

            def block(at):
                where = list(place)
                for old in done:
                    where[old] = slice(None)
                where[axis] = jnp.clip(at, 0, size - 1)
                return view(piece, where)

            for hop in range(1, size):
                hops = []
                for way in (1, -1):
                    ahead, behind = here + way, here - way
                    sent, got = here - way * (hop - 1), here - way * hop
                    if size == 2 and way == -1:
                        continue
                    if size == 2:
                        ahead, behind, got = 1 - here, 1 - here, 1 - here
                    pair = []
                    for at, other_end in ((sent, ahead), (got, behind)):
                        ref = block(at)
                        target = place[:axis] + (jnp.clip(other_end, 0, size - 1),) + place[axis + 1 :]
                        pair.append(
                            pltpu.make_async_remote_copy(
                                src_ref=ref,
                                dst_ref=ref,
                                send_sem=send_sem.at[semaphores[0]],
                                recv_sem=recv_sem.at[semaphores[0]],
                                device_id=device_at(target),
                                device_id_type=MESH_ID,
                            )
                        )
                    semaphores[0] += 1
                    sends = jnp.logical_and(inside(sent, size), inside(ahead, size))
                    hops.append(Hop(pair, sends, inside(got, size)))
                steps.append(hops)
            done.append(axis)
        return steps

    running = {}
    depth = sum(size - 1 for size in sizes)
    lags = LAGS if depth + 1 == len(LAGS) else list(range(depth + 1))
    for tick in range(len(pieces) + lags[-1]):
        for step in reversed(range(depth + 1)):
            number = tick - lags[step]
            if number < 0 or number >= len(pieces):
                continue
            if step == 0:
                prepare(pieces[number])
                running[number] = transfers(number)
            else:
                for copy in running[number][step - 1]:
                    copy.wait()
            if step < depth:
                for copy in running[number][step]:
                    copy.start()
    for number in range(len(groups)):
        if number not in prepared:
            swaps[number].wait()


def gather_plainly(enc_in, enc_down, dec_qkv, dec_out, dec_in, dec_down, cca_q, cca_kv, cca_out, gains):
    get = lambda w: lax.all_gather(w, ("dp", "seq"), axis=w.ndim - 2, tiled=True)
    kv = get(cca_kv)
    return dict(
        enc_in=get(enc_in), enc_down=get(enc_down), dec_in=get(dec_in), dec_down=get(dec_down), dec_qkv=get(dec_qkv),
        dec_out=get(dec_out), cca_kv=[kv[:, :D], kv[:, D:]], cca_q=get(cca_q), cca_out=get(cca_out), gains=get(gains)[:, :8],
    )


def gather_weights(enc_in, enc_down, dec_qkv, dec_out, dec_in, dec_down, cca_q, cca_kv, cca_out, gains):
    sizes = grid_sizes()
    rows = cca_q.shape[0]
    groups, starts, total, pieces = gather_plan()
    part = enc_down.shape[1] // 2
    if rows % 4 or part % 8 or sizes[1:] != (2, 2, 2):
        return gather_plainly(enc_in, enc_down, dec_qkv, dec_out, dec_in, dec_down, cca_q, cca_kv, cca_out, gains)
    lead = sizes[:3]
    shapes = [lead + (2 * rows, 2 * half_width(group)) for group in groups] + [lead + (2, 2, part, D)] * 4
    per_piece = sum((size - 1) * (1 if size == 2 else 2) for size in sizes)
    n_loads = sum(len(half) for group in groups for half in group) + 8 + len(groups)
    split = lambda w: w.reshape(w.shape[0], 2, part, D)
    outs = pl.pallas_call(
        functools.partial(gather_kernel, sizes),
        out_shape=[jax.ShapeDtypeStruct(shape, BF) for shape in shapes],
        in_specs=[ANY] * 10,
        out_specs=[ANY] * 9,
        scratch_shapes=[
            pltpu.VMEM((2, rows, total), BF),
            pltpu.VMEM((rows, total), BF),
            pltpu.VMEM((2 * rows, total), BF),
            pltpu.SemaphoreType.DMA((per_piece * len(pieces),)),
            pltpu.SemaphoreType.DMA((per_piece * len(pieces),)),
            pltpu.SemaphoreType.DMA((n_loads,)),
            pltpu.SemaphoreType.DMA((2, len(groups))),
        ],
        compiler_params=pltpu.CompilerParams(collective_id=0, has_side_effects=True),
        name="gather_weights",
    )(enc_in, split(enc_down), dec_qkv, dec_out, dec_in, split(dec_down), cca_q, cca_kv, cca_out, gains)
    narrow = [out.reshape(D, out.shape[-1]) for out in outs[:5]]
    tall = [out.reshape(FF, D) for out in outs[5:]]
    mixed = narrow[2]
    half = mixed.shape[1] // 2
    sides = [mixed[:, :half], mixed[:, half:]]
    qkv = [side[:, 2 * D : 5 * D] for side in sides]
    out = [side[:, 5 * D : 6 * D] for side in sides]
    return dict(
        enc_in=narrow[:2], enc_down=tall[:2], dec_in=narrow[3:], dec_down=tall[2:], dec_qkv=qkv, dec_out=out,
        cca_kv=[side[:, :D] for side in sides], cca_q=sides[0][:, D : 2 * D], cca_out=sides[1][:, D : 2 * D],
        gains=sides[0][:, 6 * D : 6 * D + 8],
    )


ORDERS = ((1, False), (2, False), (1, True), (2, False), (1, False), (2, True))
CORE, HEAVY, ZED, PAIR, CORE_AGAIN, PER_PIECE = 0, 1, 2, 8, 9, 10
START = (0, 1, 4, 6, 7, 8, 9, 10, 11)
SLOTS = dict(part=2, whole=5, half=8, sibling=3, heavy=8, middle=8, last=8, zed=6, final=4)


def gradient_pieces():
    pieces = []
    both = lambda left, right, out, layer, k: tuple(
        (left, right, 2 * D * half + D * k, out, layer, 2 * D * half + D * k) for half in range(2)
    )
    for layer in reversed(range(2)):
        base = 8 * layer
        for k in range(2):
            pieces.append(both(base + 6, base + 7, 5, layer, k))
        for k in range(2):
            pieces.append(both(base + 4, base + 5, 4, layer, k))
    pieces.append(tuple((8 * layer + 2, 8 * layer + 3, 0, 3, layer, 0) for layer in range(2)))
    for k in range(3):
        pieces.append(tuple((8 * layer, 8 * layer + 1, D * k, 2, layer, D * k) for layer in range(2)))
    pieces.append(((16, 17, 0, 6, None, 0), (20, 21, 0, 8, None, 0)))
    pieces.append(tuple((18, 19, D * half, 7, None, D * half) for half in range(2)))
    for layer in reversed(range(2)):
        base = 22 + 4 * layer
        for k in range(2):
            pieces.append(both(base + 2, base + 3, 1, layer, k))
        for k in range(2):
            pieces.append(both(base, base + 1, 0, layer, k))
    return pieces


N_OPERANDS = 30


class Sums:
    def __init__(self, place, sizes, sems, buffers, slots, width):
        self.place, self.sizes, self.width = place, sizes, width
        self.send_sem, self.recv_sem = sems
        self.part, self.whole, self.half, self.sibling, self.heavy, self.middle, self.last, self.zed, self.final = buffers
        self.slots = slots

    def slot(self, name, number):
        return lax.rem(number, self.slots[name])

    def copy(self, number, which, source, target, device):
        index = number * PER_PIECE + which
        return pltpu.make_async_remote_copy(
            src_ref=source,
            dst_ref=target,
            send_sem=self.send_sem.at[index],
            recv_sem=self.recv_sem.at[index],
            device_id=device_at(device),
            device_id_type=MESH_ID,
        )

    def core_copy(self, number):
        return self.copy(
            number,
            CORE,
            self.part.at[self.slot("part", number)],
            self.sibling.at[self.slot("sibling", number)],
            self.swapped(3),
        )

    def swapped(self, axis):
        return self.place[:axis] + (1 - self.place[axis],) + self.place[axis + 1 :]

    def heavy_copy(self, number, axis):
        whole = self.whole.at[self.slot("whole", number)]
        there = 1 - self.place[axis]
        source = whole.at[:, there] if axis == 1 else whole.at[:, :, there]
        return self.copy(number, HEAVY, source, self.heavy.at[self.slot("heavy", number)], self.swapped(axis))

    def pair_copy(self, number, axis, early):
        half = self.half.at[self.slot("half", number)]
        there = 1 - self.place[axis]
        if early:
            source, target = half.at[:, there], self.middle.at[self.slot("middle", number)]
        else:
            source, target = half.at[self.place[0], there], self.last.at[self.slot("last", number)]
        return self.copy(number, PAIR, source, target, self.swapped(axis))

    def zed_block(self, number, axis, early, at):
        half = self.half.at[self.slot("half", number)]
        at = jnp.clip(at, 0, self.sizes[0] - 1)
        return half.at[at, pl.ds(self.place[axis], 1)] if early else half.at[at]

    def zed_room(self, number, early, hop, way):
        room = self.zed.at[self.slot("zed", number), hop - 1, way]
        return room.at[pl.ds(0, 1)] if early else room

    def zed_hops(self, number, axis, early, hop):
        z, size = self.place[0], self.sizes[0]
        found = []
        for way, by in enumerate((-1, 1)):
            sent, ahead = z + by * hop, z + by
            behind, got = z - by, z - by + by * hop
            room = self.zed_room(number, early, hop, way)
            device = (jnp.clip(ahead, 0, size - 1),) + self.place[1:]
            copy = self.copy(number, ZED + 2 * (hop - 1) + way, self.zed_block(number, axis, early, sent), room, device)
            sends = jnp.logical_and(inside(sent, size), inside(ahead, size))
            receives = jnp.logical_and(inside(got, size), inside(behind, size))
            found.append((copy, sends, receives, self.zed_block(number, axis, early, got), room))
        return found

    def start_zed(self, number, axis, early, hop):
        for copy, sends, _, _, _ in self.zed_hops(number, axis, early, hop):
            pl.when(sends)(copy.start)

    def finish_zed(self, number, axis, early, hop):
        for copy, sends, receives, block, room in self.zed_hops(number, axis, early, hop):
            pl.when(sends)(copy.wait_send)

            @pl.when(receives)
            def _():
                copy.wait_recv()
                for k in range(1 if early else 2):
                    block[k] = block[k] + room[k]

    def add_core(self, number):
        self.core_copy(number).wait()
        whole, sibling = self.slot("whole", number), self.slot("sibling", number)

        def one(k, _):
            at = (k // 4, (k // 2) % 2, k % 2)
            self.whole[(whole, *at)] = self.whole[(whole, *at)] + self.sibling[(sibling, *at)]
            return 0

        lax.fori_loop(0, 4 * self.sizes[0], one, 0)

    def add_heavy(self, number, axis):
        self.heavy_copy(number, axis).wait()
        whole, half, heavy = (self.slot(name, number) for name in ("whole", "half", "heavy"))

        def one(k, _):
            z, o = k // 2, k % 2
            at = (z, self.place[1], o) if axis == 1 else (z, o, self.place[2])
            self.half[half, z, o] = self.whole[(whole, *at)] + self.heavy[heavy, z, o]
            return 0

        lax.fori_loop(0, 2 * self.sizes[0], one, 0)

    def add_pair(self, number, axis, early):
        self.pair_copy(number, axis, early).wait()
        half, here = self.slot("half", number), self.place[axis]
        if early:
            for z in range(self.sizes[0]):
                self.half[half, z, here] = self.half[half, z, here] + self.middle[self.slot("middle", number), z]
        else:
            z = self.place[0]
            self.half[half, z, here] = self.half[half, z, here] + self.last[self.slot("last", number)]

    def split_rows(self, number, axis):
        half, final = self.slot("half", number), self.slot("final", number)
        rows = self.half[half, self.place[0], self.place[axis]].astype(jnp.float32)
        count = rows.shape[0] // 2
        first, second = rows[:count], rows[count:]
        self.final[final, 0] = jnp.where(self.place[3] == 0, first, second)
        self.final[final, 2] = jnp.where(self.place[3] == 0, second, first)

    def final_copy(self, number):
        final = self.slot("final", number)
        return self.copy(number, CORE_AGAIN, self.final.at[final, 2], self.final.at[final, 1], self.swapped(3))

    def step(self, step, number, first, early):
        other = 3 - first
        sequence = [("pair", 0), ("zed", 3), ("zed", 2), ("zed", 1)] if early else [("zed", 3), ("zed", 2), ("zed", 1), ("pair", 0)]
        if step == 1:
            self.heavy_copy(number, first).start()
            return
        if step == 2:
            self.add_heavy(number, first)
        else:
            kind, hop = sequence[step - 3]
            if kind == "pair":
                self.add_pair(number, other, early)
            else:
                self.finish_zed(number, other, early, hop)
        if step < 6:
            kind, hop = sequence[step - 2]
            if kind == "pair":
                self.pair_copy(number, other, early).start()
            else:
                self.start_zed(number, other, early, hop)
        else:
            self.split_rows(number, other)
            self.final_copy(number).start()


def reduce_kernel(sizes, tall, *refs):
    pieces = gradient_pieces()
    operands, gains = refs[:N_OPERANDS], refs[N_OPERANDS]
    outs = refs[N_OPERANDS + 1 : N_OPERANDS + 11]
    scratch = refs[N_OPERANDS + 11 :]
    left, right, product = scratch[:3]
    buffers, small = scratch[3:12], scratch[12:21]
    send_sem, recv_sem, small_send, small_recv, load_sem, out_sem = scratch[21:]
    place = grid_place()
    core = place[3]
    count = len(pieces)
    sums = Sums(place, sizes, (send_sem, recv_sem), buffers, SLOTS, D)
    once = Sums(place, sizes, (small_send, small_recv), small, {name: 1 for name in SLOTS}, 128)
    is_tall = [tall[piece[0][0]] for piece in pieces]
    first_tall = is_tall.index(True)
    long_rows, short_rows = left.shape[2], None

    def rows_of(k):
        return operands[pieces[k][0][0]].shape[0]

    def loads(k, slot):
        rows = rows_of(k)
        found = []
        for half in range(2):
            l, r, column, _, _, _ = pieces[k][half]
            mine = jnp.where(core == half, 1, 0)
            found.append((operands[l], left.at[slot, mine, pl.ds(0, rows)], load_sem.at[slot, half]))
            found.append((operands[r].at[:, pl.ds(column, D)], right.at[slot, mine, pl.ds(0, rows)], load_sem.at[slot, 2 + half]))
        return [pltpu.make_async_copy(*args) for args in found]

    def start_loads(number):
        for k in range(count):

            @pl.when(number == k)
            def _():
                for copy in loads(k, k % 2):
                    copy.start()

    def multiply(number, which, rows):
        slot = lax.rem(number, 2)

        def block(k, _):
            columns = pl.ds(pl.multiple_of(k * 128, 128), 128)
            product[pl.ds(pl.multiple_of(k * 128, 128), 128), :] = lax.dot_general(
                left[slot, which, pl.ds(0, rows), columns],
                right[slot, which, pl.ds(0, rows), :],
                (((0,), (0,)), ((), ())),
                preferred_element_type=jnp.float32,
            )
            return 0

        lax.fori_loop(0, D // 128, block, 0)
        chunk = sums.whole.shape[4]

        def store(k, _):
            values = product[pl.ds(pl.multiple_of(k * chunk, 8), chunk), :].astype(BF)
            at = (k // 4, (k // 2) % 2, k % 2)
            if which == 0:
                sums.part[(sums.slot("part", number), *at)] = values
            else:
                sums.whole[(sums.slot("whole", number), *at)] = values
            return 0

        lax.fori_loop(0, D // chunk, store, 0)

    def compute(number):
        for flag in sorted(set(is_tall)):
            wanted = jnp.logical_and(number >= first_tall, flag) if flag else number < first_tall
            k = first_tall if flag else 0

            @pl.when(wanted)
            def _():
                for copy in loads(k, lax.rem(number, 2)):
                    copy.wait()
                multiply(number, 0, rows_of(k))
                sums.core_copy(number).start()
                multiply(number, 1, rows_of(k))

    def out_copies(k):
        slot = k % SLOTS["final"]
        found = []
        for half in range(2):
            _, _, _, out, layer, column = pieces[k][half]
            target = outs[out] if layer is None else outs[out].at[layer]
            source = sums.final.at[slot, jnp.where(core == half, 0, 1)]
            found.append(pltpu.make_async_copy(source, target.at[:, pl.ds(column, D)], out_sem.at[slot, half]))
        return found

    greet(place, sizes)
    small_loads = []
    for k, target in enumerate((once.part.at[0], once.whole.at[0])):
        copy = pltpu.make_async_copy(gains, target, out_sem.at[SLOTS["final"], k])
        copy.start()
        small_loads.append(copy)
    start_loads(0)

    def tick(time, _):
        for step in reversed(range(8)):

            @pl.when(time == START[step])
            def _():
                if step == 0:
                    for copy in small_loads:
                        copy.wait()
                    once.core_copy(0).start()
                elif step == 7:
                    once.final_copy(0).wait()
                    copy = pltpu.make_async_copy(once.final.at[0, 0], outs[9], out_sem.at[SLOTS["final"], 0])
                    copy.start()
                    copy.wait()
                else:
                    if step == 1:
                        once.add_core(0)
                    once.step(step, 0, *ORDERS[-1])

        for step in reversed(range(9)):
            number = time - START[step]

            @pl.when(jnp.logical_and(number >= 0, number < count))
            def _():
                if step == 0:
                    start_loads(number + 1)
                    compute(number)
                elif step == 8:
                    for copy in out_copies_at(number):
                        copy.wait()
                elif step == 7:
                    sums.final_copy(number).wait()
                    for k in range(count):

                        @pl.when(number == k)
                        def _():
                            for copy in out_copies(k):
                                copy.start()

                else:
                    if step == 1:
                        sums.add_core(number)
                    turn = lax.rem(number, len(ORDERS))
                    for order in sorted(set(ORDERS)):
                        here = functools.reduce(jnp.logical_or, [turn == k for k, one in enumerate(ORDERS) if one == order])

                        @pl.when(here)
                        def _():
                            sums.step(step, number, *order)

        return 0

    def out_copies_at(number):
        slot = lax.rem(number, SLOTS["final"])
        return [
            pltpu.make_async_copy(sums.final.at[slot, 0], outs[3].at[0, :, pl.ds(0, D)], out_sem.at[slot, half])
            for half in range(2)
        ]

    lax.fori_loop(0, count + START[8], tick, 0)


def reduce_gradients(operands, gains, layers_rows):
    sizes = grid_sizes()
    rows = layers_rows
    chunk = 2 * rows
    lead = sizes[:3] + (chunk,)
    longest = max(x.shape[0] for x in operands)
    shortest = min(x.shape[0] for x in operands)
    tall = tuple(x.shape[0] == longest for x in operands)
    f32 = jnp.float32
    shapes = [(2, rows, FF), (2, rows, FF), (2, rows, 3 * D), (2, rows, D), (2, rows, FF), (2, rows, FF)]
    shapes += [(rows, D), (rows, 2 * D), (rows, D), (rows, 128)]

    def rooms(slots, width):
        z = sizes[0]
        return [
            pltpu.VMEM((slots["part"],) + lead + (width,), BF),
            pltpu.VMEM((slots["whole"],) + lead + (width,), BF),
            pltpu.VMEM((slots["half"], z, 2, chunk, width), BF),
            pltpu.VMEM((slots["sibling"],) + lead + (width,), BF),
            pltpu.VMEM((slots["heavy"], z, 2, chunk, width), BF),
            pltpu.VMEM((slots["middle"], z, chunk, width), BF),
            pltpu.VMEM((slots["last"], chunk, width), BF),
            pltpu.VMEM((slots["zed"], z - 1, 2, 2, chunk, width), BF),
            pltpu.VMEM((slots["final"], 3, rows, width), f32),
        ]

    count = len(gradient_pieces())
    return pl.pallas_call(
        functools.partial(reduce_kernel, sizes, tall),
        out_shape=[jax.ShapeDtypeStruct(shape, f32) for shape in shapes],
        in_specs=[ANY] * (N_OPERANDS + 1),
        out_specs=[ANY] * 10,
        scratch_shapes=[
            pltpu.VMEM((2, 2, longest, D), BF),
            pltpu.VMEM((2, 2, longest, D), BF),
            pltpu.VMEM((D, D), f32),
            *rooms(SLOTS, D),
            *rooms({name: 1 for name in SLOTS}, 128),
            pltpu.SemaphoreType.DMA((PER_PIECE * count,)),
            pltpu.SemaphoreType.DMA((PER_PIECE * count,)),
            pltpu.SemaphoreType.DMA((PER_PIECE,)),
            pltpu.SemaphoreType.DMA((PER_PIECE,)),
            pltpu.SemaphoreType.DMA((2, 4)),
            pltpu.SemaphoreType.DMA((SLOTS["final"] + 1, 2)),
        ],
        compiler_params=pltpu.CompilerParams(collective_id=1, has_side_effects=True, vmem_limit_bytes=62 << 20),
        name="reduce_gradients",
    )(*operands, gains.reshape(lead + (128,)))


NN = (((1,), (0,)), ((), ()))
NT = (((1,), (1,)), ((), ()))
TN = (((0,), (0,)), ((), ()))


def dot(left, right, dims):
    return lax.dot_general(left, right, dims, preferred_element_type=jnp.float32)


def head_sides(values):
    lane = lax.broadcasted_iota(jnp.int32, values.shape, 1)
    zero = jnp.zeros_like(values)
    return [jnp.where(lane < HEAD, values, zero), jnp.where(lane >= HEAD, values, zero)]


def attend_kernel(q_ref, k_ref, v_ref, bias_ref, out_ref, total_ref):
    keys, vals = k_ref[...], v_ref[...]
    outs = []
    for side, queries in enumerate(head_sides(q_ref[...])):
        scores = dot(keys, queries, NT) * SCORE_SCALE + bias_ref[...]
        peak = jnp.max(scores, 0, keepdims=True)
        powers = jnp.exp(scores - peak)
        total = jnp.sum(powers, 0, keepdims=True)
        total_ref[0, side : side + 1, :] = peak + jnp.log(total)
        probs = (powers * (1.0 / total)).astype(BF)
        outs.append(dot(probs, vals, TN))
    lane = lax.broadcasted_iota(jnp.int32, outs[0].shape, 1)
    out_ref[...] = jnp.where(lane < HEAD, outs[0], outs[1]).astype(BF)


def attend(joined, keys_vals, bias):
    queries, keys = joined.shape[0], keys_vals.shape[0]
    pairs = D // 128
    return pl.pallas_call(
        attend_kernel,
        grid=(pairs,),
        out_shape=[jax.ShapeDtypeStruct((queries, D), BF), jax.ShapeDtypeStruct((pairs, 2, queries), jnp.float32)],
        in_specs=[
            pl.BlockSpec((queries, 128), lambda p: (0, p)),
            pl.BlockSpec((keys, 128), lambda p: (0, p)),
            pl.BlockSpec((keys, 128), lambda p: (0, pairs + p)),
            pl.BlockSpec((keys, queries), lambda p: (0, 0)),
        ],
        out_specs=[pl.BlockSpec((queries, 128), lambda p: (0, p)), pl.BlockSpec((1, 2, queries), lambda p: (p, 0, 0))],
        cost_estimate=pl.CostEstimate(
            flops=4 * queries * keys * D * 2, bytes_accessed=2 * keys * 2 * D, transcendentals=14 * queries * keys
        ),
        name="attend",
    )(joined, keys_vals, keys_vals, bias)


def attend_back_kernel(q_ref, k_ref, v_ref, bias_ref, total_ref, grad_ref, gq_ref, gkv_ref):
    pair = pl.program_id(0)
    keys, vals = k_ref[...], v_ref[...]
    q_sides, g_sides = head_sides(q_ref[...]), head_sides(grad_ref[...])
    grad_q, grad_k, grad_v = [], 0.0, 0.0
    for side in range(2):
        scores = dot(keys, q_sides[side], NT) * SCORE_SCALE + bias_ref[...]
        probs = jnp.exp(scores - total_ref[0, side : side + 1, :])
        grad_probs = dot(vals, g_sides[side], NT)
        delta = jnp.sum(probs * grad_probs, 0, keepdims=True)
        grad_scores = (probs * (grad_probs - delta)).astype(BF)
        grad_v = grad_v + dot(probs.astype(BF), g_sides[side], NN)
        grad_k = grad_k + dot(grad_scores, q_sides[side], NN)
        grad_q.append(dot(grad_scores, keys, TN))
    lane = lax.broadcasted_iota(jnp.int32, grad_q[0].shape, 1)
    gq_ref[...] = (jnp.where(lane < HEAD, grad_q[0], grad_q[1]) * SCORE_SCALE).astype(BF)
    gkv_ref[:, pl.ds(pl.multiple_of(pair * 128, 128), 128)] = (grad_k * SCORE_SCALE).astype(BF)
    gkv_ref[:, pl.ds(pl.multiple_of(D + pair * 128, 128), 128)] = grad_v.astype(BF)


def attend_back(joined, keys_vals, bias, log_total, grad_mixed):
    queries, keys = joined.shape[0], keys_vals.shape[0]
    pairs = D // 128
    return pl.pallas_call(
        attend_back_kernel,
        grid=(pairs,),
        out_shape=[jax.ShapeDtypeStruct((queries, D), BF), jax.ShapeDtypeStruct((keys, 2 * D), BF)],
        in_specs=[
            pl.BlockSpec((queries, 128), lambda p: (0, p)),
            pl.BlockSpec((keys, 128), lambda p: (0, p)),
            pl.BlockSpec((keys, 128), lambda p: (0, pairs + p)),
            pl.BlockSpec((keys, queries), lambda p: (0, 0)),
            pl.BlockSpec((1, 2, queries), lambda p: (p, 0, 0)),
            pl.BlockSpec((queries, 128), lambda p: (0, p)),
        ],
        out_specs=[pl.BlockSpec((queries, 128), lambda p: (0, p)), pl.BlockSpec((keys, 2 * D), lambda p: (0, 0))],
        cost_estimate=pl.CostEstimate(
            flops=10 * queries * keys * D * 2, bytes_accessed=4 * keys * 2 * D, transcendentals=14 * queries * keys
        ),
        name="attend_back",
    )(joined, keys_vals, keys_vals, bias, log_total, grad_mixed)


def gelu_parts(values):
    size = jnp.abs(values)
    bell = jnp.exp(-0.5 * size * size)
    t = 1.0 / (1.0 + (0.3275911 * 0.7071067811865476) * size)
    tail = t * (0.127414796 + t * (-0.142248368 + t * (0.7107068705 + t * (-0.7265760135 + t * 0.5307027145)))) * bell
    share = jnp.where(values >= 0, 1.0 - tail, tail)
    return values * share, share + values * (0.3989422804014327 * bell)


def norm_parts(values):
    scale = lax.rsqrt(jnp.mean(values * values, -1, keepdims=True) + EPSILON)
    return values * scale, scale


def norm_gradient(values, norm_gain, upstream):
    unit, scale = norm_parts(values)
    inner = upstream * norm_gain
    back = scale * (inner - unit * jnp.mean(inner * unit, -1, keepdims=True))
    return back, jnp.sum(upstream * unit, 0, keepdims=True)


def hidden_block(rows):
    return 2 * D if rows <= 128 else D


def ffn_kernel(stream_ref, gain_ref, in_ref, down_ref, out_ref, inputs_ref, hidden_ref, slope_ref):
    step = pl.program_id(0)

    @pl.when(step == 0)
    def _():
        stream = stream_ref[...].astype(jnp.float32)
        out_ref[...] = stream
        inputs_ref[...] = (norm_parts(stream)[0] * gain_ref[...].astype(jnp.float32)).astype(BF)

    value, slope = gelu_parts(dot(inputs_ref[...], in_ref[...], NN))
    hidden = value.astype(BF)
    hidden_ref[...] = hidden
    slope_ref[...] = slope.astype(BF)
    out_ref[...] += dot(hidden, down_ref[...], NN)


def ffn(stream, norm_gain, weight_in, weight_down):
    rows = stream.shape[0]
    block = hidden_block(rows)
    still = lambda j: (0, 0)
    return pl.pallas_call(
        ffn_kernel,
        grid=(FF // block,),
        out_shape=[
            jax.ShapeDtypeStruct((rows, D), jnp.float32),
            jax.ShapeDtypeStruct((rows, D), BF),
            jax.ShapeDtypeStruct((rows, FF), BF),
            jax.ShapeDtypeStruct((rows, FF), BF),
        ],
        in_specs=[
            pl.BlockSpec((rows, D), still),
            pl.BlockSpec((1, D), still),
            pl.BlockSpec((D, block), lambda j: (0, j)),
            pl.BlockSpec((block, D), lambda j: (j, 0)),
        ],
        out_specs=[
            pl.BlockSpec((rows, D), still),
            pl.BlockSpec((rows, D), still),
            pl.BlockSpec((rows, block), lambda j: (0, j)),
            pl.BlockSpec((rows, block), lambda j: (0, j)),
        ],
        cost_estimate=pl.CostEstimate(
            flops=4 * rows * D * FF, bytes_accessed=4 * D * FF + 4 * rows * FF + 8 * rows * D, transcendentals=rows * FF
        ),
        name="ffn",
    )(stream, norm_gain, weight_in, weight_down)


def ffn_back_kernel(grad_ref, stream_ref, gain_ref, slope_ref, in_ref, down_ref, out_ref, low_ref, pre_ref, gain_out, total):
    step = pl.program_id(0)

    @pl.when(step == 0)
    def _():
        low_ref[...] = grad_ref[...].astype(BF)
        total[...] = jnp.zeros_like(total)

    pre = (dot(low_ref[...], down_ref[...], NT) * slope_ref[...].astype(jnp.float32)).astype(BF)
    pre_ref[...] = pre
    total[...] += dot(pre, in_ref[...], NT)

    @pl.when(step == pl.num_programs(0) - 1)
    def _():
        back, gain = norm_gradient(stream_ref[...].astype(jnp.float32), gain_ref[...].astype(jnp.float32), total[...])
        out_ref[...] = grad_ref[...].astype(jnp.float32) + back
        gain_out[...] = gain


def ffn_back(upstream, stream, norm_gain, slope, weight_in, weight_down):
    rows = stream.shape[0]
    block = hidden_block(rows)
    still = lambda j: (0, 0)
    return pl.pallas_call(
        ffn_back_kernel,
        grid=(FF // block,),
        out_shape=[
            jax.ShapeDtypeStruct((rows, D), jnp.float32),
            jax.ShapeDtypeStruct((rows, D), BF),
            jax.ShapeDtypeStruct((rows, FF), BF),
            jax.ShapeDtypeStruct((1, D), jnp.float32),
        ],
        in_specs=[
            pl.BlockSpec((rows, D), still),
            pl.BlockSpec((rows, D), still),
            pl.BlockSpec((1, D), still),
            pl.BlockSpec((rows, block), lambda j: (0, j)),
            pl.BlockSpec((D, block), lambda j: (0, j)),
            pl.BlockSpec((block, D), lambda j: (j, 0)),
        ],
        out_specs=[
            pl.BlockSpec((rows, D), still),
            pl.BlockSpec((rows, D), still),
            pl.BlockSpec((rows, block), lambda j: (0, j)),
            pl.BlockSpec((1, D), still),
        ],
        scratch_shapes=[pltpu.VMEM((rows, D), jnp.float32)],
        cost_estimate=pl.CostEstimate(
            flops=4 * rows * D * FF, bytes_accessed=4 * D * FF + 4 * rows * FF + 16 * rows * D, transcendentals=0
        ),
        name="ffn_back",
    )(upstream, stream, norm_gain, slope, weight_in, weight_down)


def shifted(x, axis, by):
    count = lax.axis_size(axis)
    pairs = [(i, i + by) for i in range(count) if 0 <= i + by < count]
    return lax.ppermute(x, axis, pairs)


def slab_term(left, right):
    return dot(left, right, TN)


def normed(values, norm_gain):
    return (norm_parts(values)[0] * norm_gain.astype(jnp.float32)).astype(BF)


def norm_back(values, norm_gain, upstream):
    return norm_gradient(values, norm_gain.astype(jnp.float32), upstream)


def self_forward(stream, norm_gain, weight_qkv, weight_out, bias):
    inputs = normed(stream, norm_gain)
    joined = dot(inputs, weight_qkv, NN).astype(BF)
    keys_vals = lax.all_gather(joined[:, D:], "seq", axis=0, tiled=True)
    mixed, log_total = attend(joined, keys_vals, bias)
    return stream + dot(mixed, weight_out, NN), (stream, inputs, joined, keys_vals, log_total, mixed)


def self_back(stored, norm_gain, weight_qkv, weight_out, bias, upstream):
    stream, inputs, joined, keys_vals, log_total, mixed = stored
    grad_low = upstream.astype(BF)
    grad_mixed = dot(grad_low, weight_out, NT).astype(BF)
    grad_queries, grad_pairs = attend_back(joined, keys_vals, bias, log_total, grad_mixed)
    own_pairs = lax.psum_scatter(grad_pairs, "seq", scatter_dimension=0, tiled=True)
    grad_joined = jnp.concatenate([grad_queries, own_pairs], -1)
    back, gain_grad = norm_back(stream, norm_gain, dot(grad_joined, weight_qkv, NT))
    return upstream + back, gain_grad, ((inputs, grad_joined), (mixed, grad_low))


def causal_bias(queries, keys):
    offset = lax.axis_index("seq") * queries
    key_place = lax.broadcasted_iota(jnp.int32, (keys, queries), 0)
    query_place = offset + lax.broadcasted_iota(jnp.int32, (keys, queries), 1)
    return jnp.where(key_place <= query_place, 0.0, MASKED_SCORE).astype(jnp.float32)


def span_bias(prior_flag, queries):
    spans = prior_flag.shape[0]
    keys = spans * NEIGH * RET
    key_span = lax.broadcasted_iota(jnp.int32, (keys, queries), 0) // (NEIGH * RET)
    query_span = lax.broadcasted_iota(jnp.int32, (keys, queries), 1) // SPAN
    allowed = jnp.repeat(prior_flag.reshape(-1), RET)[:, None] > 0.5
    return jnp.where(key_span == query_span, jnp.where(allowed, 0.0, MASKED_SCORE), 2 * MASKED_SCORE).astype(jnp.float32)


def row_gate(prior_flag):
    return jnp.repeat(jnp.max(prior_flag, -1).astype(jnp.float32), SPAN)[:, None]


def prior_spans(encoded, keep_flag):
    last_enc, last_flag = shifted((encoded[-1:], keep_flag[-1:]), "seq", 1)
    return jnp.concatenate([last_enc, encoded[:-1]], 0), jnp.concatenate([last_flag, keep_flag[:-1]], 0)


def cross_forward(stream, encoded, keep_flag, norm_gain, weight_q, weight_kv, weight_out):
    prior_enc, prior_flag = prior_spans(encoded, keep_flag)
    prior_enc = prior_enc.reshape(-1, D)
    inputs = normed(stream, norm_gain)
    queries = dot(inputs, weight_q, NN).astype(BF)
    keys_vals = jnp.concatenate([dot(prior_enc, side, NN).astype(BF) for side in weight_kv], 1)
    bias = span_bias(prior_flag, stream.shape[0])
    mixed, log_total = attend(queries, keys_vals, bias)
    branch = row_gate(prior_flag) * dot(mixed, weight_out, NN)
    return stream + branch, (stream, inputs, prior_enc, prior_flag, queries, keys_vals, bias, log_total, mixed)


def cross_back(stored, norm_gain, weight_q, weight_kv, weight_out, upstream):
    stream, inputs, prior_enc, prior_flag, queries, keys_vals, bias, log_total, mixed = stored
    grad_low = (upstream * row_gate(prior_flag)).astype(BF)
    grad_mixed = dot(grad_low, weight_out, NT).astype(BF)
    grad_queries, grad_pairs = attend_back(queries, keys_vals, bias, log_total, grad_mixed)
    grad_prior = dot(grad_pairs[:, :D], weight_kv[0], NT) + dot(grad_pairs[:, D:], weight_kv[1], NT)
    grad_prior = grad_prior.reshape(prior_flag.shape[0], NEIGH * RET, D)
    from_next = shifted(grad_prior[:1].astype(BF), "seq", -1).astype(jnp.float32)
    encoded_grad = jnp.concatenate([grad_prior[1:], from_next], 0).reshape(-1, D)
    back, gain_grad = norm_back(stream, norm_gain, dot(grad_queries, weight_q, NT))
    pairs = ((inputs, grad_queries), (prior_enc, grad_pairs), (mixed, grad_low))
    return upstream + back, gain_grad, pairs, encoded_grad


def on_device(
    tokens,
    retrieved,
    span_doc,
    neigh_doc,
    cotangent,
    dec_gain,
    dec_qkv,
    dec_out,
    dec_in,
    dec_down,
    cca_gain,
    cca_q,
    cca_kv,
    cca_out,
    enc_gain,
    enc_in,
    enc_down,
    enc_final,
):
    assert tokens.shape[0] == 1
    rows = cca_q.shape[0]
    own_gains = jnp.concatenate([dec_gain.reshape(4, rows), cca_gain[None], enc_gain, enc_final[None]], 0).T
    own_gains = jnp.pad(own_gains, ((0, 0), (0, 120)))
    full = gather_weights(enc_in, enc_down, dec_qkv, dec_out, dec_in, dec_down, cca_q, cca_kv, cca_out, own_gains)
    gains = full["gains"].T
    attn_gain, ffn_gain = (gains[0:1], gains[2:3]), (gains[1:2], gains[3:4])
    cross_gain, encode_gain, final_gain = gains[4:5], (gains[5:6], gains[6:7]), gains[7:8]
    cross_weights = (cross_gain, full["cca_q"], full["cca_kv"], full["cca_out"])
    queries = tokens.shape[1]
    bias = causal_bias(queries, queries * lax.axis_size("seq"))

    encoder = retrieved.reshape(-1, D)
    encoder_kept = []
    for layer in range(ENC_LAYERS):
        after, inputs, hidden, slope = ffn(encoder, encode_gain[layer], full["enc_in"][layer], full["enc_down"][layer])
        encoder_kept.append((encoder, inputs, hidden, slope))
        encoder = after
    encoded = normed(encoder, final_gain).reshape(span_doc.shape[1], NEIGH * RET, D)
    keep_flag = (neigh_doc[0] != span_doc[0][:, None]).astype(BF)

    stream = tokens[0].astype(jnp.float32)
    attn_kept, ffn_kept = [], []
    for layer in range(DEC_LAYERS):
        stream, kept = self_forward(stream, attn_gain[layer], full["dec_qkv"][layer], full["dec_out"][layer], bias)
        attn_kept.append(kept)
        if layer == 0:
            stream, cross_kept = cross_forward(stream, encoded, keep_flag, *cross_weights)
        before = stream
        stream, inputs, hidden, slope = ffn(before, ffn_gain[layer], full["dec_in"][layer], full["dec_down"][layer])
        ffn_kept.append((before, inputs, hidden, slope))
    result = stream.astype(BF)

    upstream = cotangent[0].astype(jnp.float32)
    attn_gain_g, ffn_gain_g = [None] * DEC_LAYERS, [None] * DEC_LAYERS
    attn_pairs, ffn_pairs = [None] * DEC_LAYERS, [None] * DEC_LAYERS
    for layer in reversed(range(DEC_LAYERS)):
        before, inputs, hidden, slope = ffn_kept[layer]
        upstream, grad_low, grad_pre, ffn_gain_g[layer] = ffn_back(
            upstream, before, ffn_gain[layer], slope, full["dec_in"][layer], full["dec_down"][layer]
        )
        ffn_pairs[layer] = ((inputs, grad_pre), (grad_low, hidden))
        if layer == 0:
            upstream, cross_gain_g, cross_pairs, encoded_grad = cross_back(cross_kept, *cross_weights, upstream)
        upstream, attn_gain_g[layer], attn_pairs[layer] = self_back(
            attn_kept[layer], attn_gain[layer], full["dec_qkv"][layer], full["dec_out"][layer], bias, upstream
        )

    enc_upstream, final_gain_g = norm_back(encoder, final_gain, encoded_grad)
    enc_gain_g, enc_pairs = [None] * ENC_LAYERS, [None] * ENC_LAYERS
    for layer in reversed(range(ENC_LAYERS)):
        before, inputs, hidden, slope = encoder_kept[layer]
        enc_upstream, grad_low, grad_pre, enc_gain_g[layer] = ffn_back(
            enc_upstream, before, encode_gain[layer], slope, full["enc_in"][layer], full["enc_down"][layer]
        )
        enc_pairs[layer] = ((inputs, grad_pre), (grad_low, hidden))

    pair_list = []
    for layer in range(DEC_LAYERS):
        pair_list += list(attn_pairs[layer]) + list(ffn_pairs[layer])
    pair_list += list(cross_pairs)
    for layer in range(ENC_LAYERS):
        pair_list += list(enc_pairs[layer])
    gain_list = []
    for layer in range(DEC_LAYERS):
        gain_list += [attn_gain_g[layer], ffn_gain_g[layer]]
    gain_list = [gain.reshape(D) for gain in gain_list + [cross_gain_g] + enc_gain_g + [final_gain_g]]

    grads = sum_gradients(pair_list, gain_list, rows)
    (enc_in_g, enc_down_g, dec_qkv_g, dec_out_g, dec_in_g, dec_down_g, cross_q_g, cross_kv_g, cross_out_g, gain_cols) = grads
    gain_rows = gain_cols[:, :8].T
    return (
        result[None],
        upstream[None],
        gain_rows[:4].reshape(2, 2, rows),
        dec_qkv_g,
        dec_out_g,
        dec_in_g,
        jnp.swapaxes(dec_down_g, 1, 2),
        gain_rows[4],
        cross_q_g,
        cross_kv_g,
        cross_out_g,
        gain_rows[5:7],
        enc_in_g,
        jnp.swapaxes(enc_down_g, 1, 2),
        gain_rows[7],
    )


def sum_plainly(pair_list, gain_list):
    blocks = [slab_term(left, right) for left, right in pair_list] + [vector[:, None] for vector in gain_list]
    owned = lax.psum_scatter(
        jnp.concatenate(blocks, 1).astype(BF), ("dp", "seq"), scatter_dimension=0, tiled=True
    ).astype(jnp.float32)
    pieces, cursor = [], 0
    for _, right in pair_list:
        pieces.append(owned[:, cursor : cursor + right.shape[-1]])
        cursor += right.shape[-1]
    two = lambda first, second: jnp.stack([pieces[first], pieces[second]])
    return [
        two(11, 13), two(12, 14), two(0, 4), two(1, 5), two(2, 6), two(3, 7), pieces[8], pieces[9], pieces[10], owned[:, cursor:]
    ]


def sum_gradients(pair_list, gain_list, rows):
    sizes = grid_sizes()
    if rows % 4 or sizes != (4, 2, 2, 2):
        return sum_plainly(pair_list, gain_list)
    operands = [x.reshape(-1, x.shape[-1]) for pair in pair_list for x in pair]
    gains = jnp.pad(jnp.stack(gain_list).astype(BF).T, ((0, 0), (0, 128 - len(gain_list))))
    return reduce_gradients(operands, gains, rows)


def solution(mesh):
    return jax.shard_map(
        on_device,
        mesh=mesh,
        in_specs=(
            P("dp", "seq", None),
            P("dp", "seq", None, None, None),
            P("dp", "seq"),
            P("dp", "seq", None),
            P("dp", "seq", None),
            P(None, None, ("dp", "seq")),
            P(None, ("dp", "seq"), None),
            P(None, ("dp", "seq"), None),
            P(None, ("dp", "seq"), None),
            P(None, ("dp", "seq"), None),
            P(("dp", "seq")),
            P(("dp", "seq"), None),
            P(("dp", "seq"), None),
            P(("dp", "seq"), None),
            P(None, ("dp", "seq")),
            P(None, ("dp", "seq"), None),
            P(None, ("dp", "seq"), None),
            P(("dp", "seq")),
        ),
        out_specs=(
            P("dp", "seq", None),
            P("dp", "seq", None),
            P(None, None, ("dp", "seq")),
            P(None, ("dp", "seq"), None),
            P(None, ("dp", "seq"), None),
            P(None, ("dp", "seq"), None),
            P(None, None, ("dp", "seq")),
            P(("dp", "seq")),
            P(("dp", "seq"), None),
            P(("dp", "seq"), None),
            P(("dp", "seq"), None),
            P(None, ("dp", "seq")),
            P(None, ("dp", "seq"), None),
            P(None, None, ("dp", "seq")),
            P(("dp", "seq")),
        ),
        check_vma=False,
    )
```

```python
import functools
import heapq
import jax
import jax.numpy as jnp
from jax import lax
from jax.experimental import pallas as pl
from jax.experimental.pallas import tpu as pltpu
from jax.sharding import PartitionSpec as P

D = 896
FF = 3584
HEADS = 14
HEAD = 64
SPAN = 64
NEIGH = 2
RET = 128
ENC_LAYERS = 2
DEC_LAYERS = 2
EPSILON = 1e-06
SCORE_SCALE = 0.125
MASKED_SCORE = -1000000000.0
BF = jnp.bfloat16
MESH_ID = pl.DeviceIdType.MESH
ANY = pl.BlockSpec(memory_space=pl.ANY)


def grid_sizes():
    return (lax.axis_size("dp"), lax.axis_size("seq") // 4, 2, 2)


def grid_place():
    seq = lax.axis_index("seq")
    return (lax.axis_index("dp"), seq // 4, (seq // 2) % 2, seq % 2)


def device_at(place):
    z, y, x, core = place
    return (z, (y * 2 + x) * 2 + core)


def moved(place, sizes, axis, by):
    size = sizes[axis]
    there = lax.rem(place[axis] + (by % size), size)
    return place[:axis] + (there,) + place[axis + 1 :]


def greet(place, sizes):
    barrier = pltpu.get_barrier_semaphore()
    for axis in range(4):
        size, here = sizes[axis], place[axis]
        for by in (1, -1):
            there = here + by

            @pl.when(inside(there, size))
            def _():
                other = place[:axis] + (jnp.clip(there, 0, size - 1),) + place[axis + 1 :]
                pl.semaphore_signal(barrier, inc=1, device_id=device_at(other), device_id_type=MESH_ID)

    count = 0
    for axis in range(4):
        for by in (1, -1):
            count = count + inside(place[axis] + by, sizes[axis]).astype(jnp.int32)
    pl.semaphore_wait(barrier, count)


class Hop:
    def __init__(self, copy, sends, receives):
        self.copy, self.sends, self.receives = copy, sends, receives

    def start(self):
        pl.when(self.sends)(self.copy[0].start)

    def wait(self):
        pl.when(self.sends)(self.copy[0].wait_send)
        pl.when(self.receives)(self.copy[1].wait_recv)


def inside(place, size):
    return jnp.logical_and(place >= 0, place < size)


ZYX, ZXY, YZX, XZY, YXZ, XYZ = (0, 1, 2), (0, 2, 1), (1, 0, 2), (2, 0, 1), (1, 2, 0), (2, 1, 0)
ROUTES = (ZXY, ZYX, ZXY, ZYX, ZXY, ZYX, ZYX, ZXY, XZY, ZXY, ZXY, YZX)
ROUTES += (XZY, YZX, XZY, ZYX, ZXY, YZX, ZYX, YZX, XZY, YXZ, YXZ)
UNIT_US, HOP_US, CORE_US = 2.2, 2.5, 0.17


def schedule(pieces, routes, sizes):
    chains = []
    for number, piece in enumerate(pieces):
        scale, held, chain = piece[3] / PIECE, 1, []
        for axis in routes[number]:
            chain += [(axis, held * UNIT_US * scale)] * (sizes[axis] - 1)
            held *= sizes[axis]
        chains.append(chain + [(3, held * CORE_US * scale)])
    free, flying, ready = [0.0] * 4, [0] * 4, [[] for _ in range(4)]
    for number, chain in enumerate(chains):
        heapq.heappush(ready[chain[0][0]], (number, number, 0))
    now, events, order = 0.0, [], []
    while True:
        for link in range(4):
            while ready[link] and flying[link] < 2:
                _, number, step = heapq.heappop(ready[link])
                free[link] = max(free[link], now) + chains[number][step][1]
                flying[link] += 1
                order.append(("start", number, step, now))
                heapq.heappush(events, (free[link] + HOP_US, number, step, link))
        if not events:
            return order
        now, number, step, link = heapq.heappop(events)
        flying[link] -= 1
        order.append(("wait", number, step, now))
        if step + 1 < len(chains[number]):
            heapq.heappush(ready[chains[number][step + 1][0]], (number + step + 1, number, step + 1))


PIECE = 896


def narrow_groups():
    qkv = 3 * D
    wide = FF // 2
    whole = lambda arg, layer: [[(arg, layer, 0, wide)], [(arg, layer, wide, wide)]]
    return [
        whole(0, 0),
        whole(0, 1),
        [
            [(7, None, 0, D), (6, None, 0, D), (2, 0, 0, qkv), (3, 0, 0, D)],
            [(7, None, D, D), (8, None, 0, D), (2, 1, 0, qkv), (3, 1, 0, D)],
        ],
        whole(4, 0),
        whole(4, 1),
        [[(9, None, 0, 128)], [(9, None, 0, 128)]],
    ]


def half_width(group):
    return sum(part[3] for part in group[0])


def gather_plan():
    groups = narrow_groups()
    starts, cursor = [], 0
    for group in groups:
        starts.append(cursor)
        cursor += half_width(group)
    pieces = []
    for kind, number in (("n", 5), ("n", 0), ("r", 0), ("n", 1), ("r", 1), ("n", 2), ("n", 3), ("r", 2), ("n", 4), ("r", 3)):
        if kind == "n":
            width = half_width(groups[number])
            for first in range(0, width, PIECE):
                pieces.append((kind, number, first, min(PIECE, width - first)))
        else:
            pieces.append((kind, number, 0, D))
            pieces.append((kind, number, 1, D))
    return groups, starts, cursor, pieces


N_GROUPS = 6


def gather_kernel(sizes, *refs):
    groups, starts, _, pieces = gather_plan()
    ins, neighbours = refs[:10], refs[10]
    outs, encoder_outs = refs[11 : 15 + N_GROUPS], refs[15 + N_GROUPS : 24 + N_GROUPS]
    halves, other, joined, own_rows, send_sem, recv_sem, load_sem, swap_sem = refs[24 + N_GROUPS : 32 + N_GROUPS]
    encoder_rooms = refs[32 + N_GROUPS :]
    place = grid_place()
    z, y, x, core = place
    sibling = device_at(moved(place, sizes, 3, 1))
    loads = []
    for number, group in enumerate(groups):
        for half in range(2):
            cursor = starts[number]
            for arg, layer, first, size in group[half]:
                source = ins[arg] if layer is None else ins[arg].at[layer]
                loads.append((source.at[:, pl.ds(first, size)], halves.at[half, :, pl.ds(cursor, size)]))
                cursor += size
    for number, (arg, layer) in enumerate(((1, 0), (1, 1), (5, 0), (5, 1))):
        for part in range(2):
            loads.append((ins[arg].at[layer, part], own_rows.at[2 * number + part]))
    started = []
    for k, (source, target) in enumerate(loads):
        copy = pltpu.make_async_copy(source, target, load_sem.at[k])
        copy.start()
        started.append(copy)
    greet(place, sizes)
    for copy in started:
        copy.wait()
    placed = []
    for number in range(4):
        for part in range(2):
            k = 2 * number + part
            target = outs[N_GROUPS + number].at[z, y, x, core, part]
            placed.append(pltpu.make_async_copy(own_rows.at[k], target, load_sem.at[len(loads) + len(groups) + k]))
            placed[-1].start()
    swaps = []
    for number, group in enumerate(groups):
        columns = pl.ds(starts[number], half_width(group))
        copy = pltpu.make_async_remote_copy(
            src_ref=halves.at[1 - core, :, columns],
            dst_ref=other.at[:, columns],
            send_sem=swap_sem.at[0, number],
            recv_sem=swap_sem.at[1, number],
            device_id=sibling,
            device_id_type=MESH_ID,
        )
        copy.start()
        swaps.append(copy)

    def view(piece, where):
        kind, number, first, size = piece
        iz, iy, ix = where[:3]
        if kind == "n":
            start = pl.multiple_of(core * half_width(groups[number]) + first, 128)
            return outs[number].at[iz, iy, ix, :, pl.ds(start, size)]
        return outs[N_GROUPS + number].at[iz, iy, ix, core, first]

    prepared = {}

    def prepare(piece):
        kind, number, first, size = piece
        if kind == "n" and number not in prepared:
            swaps[number].wait()
            group = groups[number]
            for begin in range(starts[number], starts[number] + half_width(group), 128):
                columns = pl.ds(begin, 128)
                mine = halves[core, :, columns].astype(jnp.float32)
                theirs = other[:, columns].astype(jnp.float32)
                both = [jnp.where(core == 0, mine, theirs), jnp.where(core == 0, theirs, mine)]
                joined[:, columns] = jnp.concatenate(both, 0).astype(BF)
            width = half_width(group)
            copy = pltpu.make_async_copy(
                joined.at[:, pl.ds(starts[number], width)],
                outs[number].at[z, y, x, :, pl.ds(pl.multiple_of(core * width, 128), width)],
                load_sem.at[len(loads) + number],
            )
            copy.start()
            copy.wait()
            prepared[number] = True
        elif kind == "r" and "r" not in prepared:
            for copy in placed:
                copy.wait()
            prepared["r"] = True

    semaphores = [0]

    def transfers(number):
        piece = pieces[number]
        steps, done = [], []
        for axis in routes[number] + (3,):
            size, here = sizes[axis], place[axis]

            def block(at):
                where = list(place)
                for old in done:
                    where[old] = slice(None)
                where[axis] = jnp.clip(at, 0, size - 1)
                return view(piece, where)

            for hop in range(1, size):
                hops = []
                for way in (1, -1):
                    ahead, behind = here + way, here - way
                    sent, got = here - way * (hop - 1), here - way * hop
                    if size == 2 and way == -1:
                        continue
                    if size == 2:
                        ahead, behind, got = 1 - here, 1 - here, 1 - here
                    pair = []
                    for at, other_end in ((sent, ahead), (got, behind)):
                        ref = block(at)
                        target = place[:axis] + (jnp.clip(other_end, 0, size - 1),) + place[axis + 1 :]
                        pair.append(
                            pltpu.make_async_remote_copy(
                                src_ref=ref,
                                dst_ref=ref,
                                send_sem=send_sem.at[semaphores[0]],
                                recv_sem=recv_sem.at[semaphores[0]],
                                device_id=device_at(target),
                                device_id_type=MESH_ID,
                            )
                        )
                    semaphores[0] += 1
                    sends = jnp.logical_and(inside(sent, size), inside(ahead, size))
                    hops.append(Hop(pair, sends, inside(got, size)))
                steps.append(hops)
            done.append(axis)
        return steps

    routes = [ROUTES[number % len(ROUTES)] for number in range(len(pieces))]
    running = [transfers(number) for number in range(len(pieces))]
    units = encoder_units(
        neighbours, outs[N_GROUPS - 1], (outs[0], outs[1]), (outs[N_GROUPS], outs[N_GROUPS + 1]), encoder_outs, encoder_rooms
    )
    needs = [{k for k, piece in enumerate(pieces) if piece[:2] in wanted} for wanted in UNIT_NEEDS]
    due, arrived = 0.0, set()
    for what, number, step, time in schedule(pieces, routes, sizes):
        if what == "wait":
            for copy in running[number][step]:
                copy.wait()
            if step + 1 == len(running[number]):
                arrived.add(number)
        else:
            prepare(pieces[number])
            for copy in running[number][step]:
                copy.start()
        if units and time >= due and needs[len(needs) - len(units)] <= arrived:
            units.pop(0)()
            due = time + UNIT_TIME
    for unit in units:
        unit()


HIDDEN_UNITS = 4
UNIT_TIME = 7.0
GAINS, FIRST, SECOND = {("n", 5)}, {("n", 0), ("r", 0)}, {("n", 1), ("r", 1)}
UNIT_NEEDS = [GAINS | FIRST] * (1 + HIDDEN_UNITS) + [SECOND] * (1 + HIDDEN_UNITS) + [set()]


def encoder_units(neighbours, gain_columns, weights_in, weights_down, outs, rooms):
    after, inputs_out, hidden_out, slope_out, encoded_out = outs[0:2], outs[2:4], outs[4:6], outs[6:8], outs[8]
    stream, inputs, columns, gain_rows, block_in, block_down, hidden, slope, sems = rooms
    block = FF // HIDDEN_UNITS

    def flat(values, rows):
        return values.astype(jnp.float32).reshape(rows, values.shape[-1])

    def weights(layer, k):
        slot = k % 2
        return [
            pltpu.make_async_copy(weights_in[layer].at[:, :, :, :, pl.ds(k * block, block)], block_in.at[slot], sems.at[0, slot]),
            pltpu.make_async_copy(weights_down[layer].at[k], block_down.at[slot], sems.at[1, slot]),
        ]

    def results(layer, k):
        slot = k % 2
        place = pl.ds(k * block, block)
        return [
            pltpu.make_async_copy(hidden.at[slot], hidden_out[layer].at[:, place], sems.at[2, slot]),
            pltpu.make_async_copy(slope.at[slot], slope_out[layer].at[:, place], sems.at[3, slot]),
        ]

    def stream_copy(layer):
        return pltpu.make_async_copy(stream, after[layer], sems.at[4, layer])

    def inputs_copy(layer):
        return pltpu.make_async_copy(inputs, (*inputs_out, encoded_out)[layer], sems.at[5, layer % 2])

    def norm_unit(layer):
        if layer == 0:
            first = pltpu.make_async_copy(neighbours, inputs, sems.at[6, 0])
            second = pltpu.make_async_copy(gain_columns.at[:, :, :, :, pl.ds(0, 128)], columns, sems.at[6, 1])
            first.start()
            second.start()
            first.wait()
            second.wait()
            gain_rows[...] = flat(columns[...], D).T
            stream[...] = inputs[...].astype(jnp.float32)
        else:
            for k in (HIDDEN_UNITS - 2, HIDDEN_UNITS - 1):
                for copy in results(layer - 1, k):
                    copy.wait()
            inputs_copy(layer - 1).wait()
            stream_copy(layer - 1).start()
        if layer < ENC_LAYERS:
            for copy in weights(layer, 0):
                copy.start()
        gain = gain_rows[5 + layer : 6 + layer, :]
        inputs[...] = (norm_parts(stream[...])[0] * gain).astype(BF)
        inputs_copy(layer).start()
        if layer == ENC_LAYERS:
            stream_copy(layer - 1).wait()
            inputs_copy(layer).wait()

    def hidden_unit(layer, k):
        slot = k % 2
        if k + 1 < HIDDEN_UNITS:
            for copy in weights(layer, k + 1):
                copy.start()
        for copy in weights(layer, k):
            copy.wait()
        if k >= 2:
            for copy in results(layer, k - 2):
                copy.wait()
        value, rate = gelu_parts(dot(inputs[...], flat(block_in[slot], D).astype(BF), NN))
        hidden[slot] = value.astype(BF)
        slope[slot] = rate.astype(BF)
        for copy in results(layer, k):
            copy.start()
        if k == 0 and layer > 0:
            stream_copy(layer - 1).wait()
        stream[...] += dot(hidden[slot], flat(block_down[slot], block).astype(BF), NN)

    units = []
    for layer in range(ENC_LAYERS):
        units.append(functools.partial(norm_unit, layer))
        for k in range(HIDDEN_UNITS):
            units.append(functools.partial(hidden_unit, layer, k))
    units.append(functools.partial(norm_unit, ENC_LAYERS))
    return units


def gather_plainly(neighbours, enc_in, enc_down, dec_qkv, dec_out, dec_in, dec_down, cca_q, cca_kv, cca_out, gains):
    get = lambda w: lax.all_gather(w, ("dp", "seq"), axis=w.ndim - 2, tiled=True)
    kv = get(cca_kv)
    enc_in, enc_down, columns = get(enc_in), get(enc_down), get(gains)[:, :8]
    stream, kept = neighbours, []
    for layer in range(ENC_LAYERS):
        gain = columns[:, 5 + layer][None]
        after, inputs, hidden, slope = ffn(stream, gain, enc_in[layer], enc_down[layer])
        kept.append((stream, inputs, hidden, slope))
        stream = after
    return dict(
        encoder=(stream, kept, normed(stream, columns[:, 7][None])),
        enc_in=enc_in, enc_down=enc_down, dec_in=get(dec_in), dec_down=get(dec_down), dec_qkv=get(dec_qkv),
        dec_out=get(dec_out), cca_kv=[kv[:, :D], kv[:, D:]], cca_q=get(cca_q), cca_out=get(cca_out), gains=columns,
    )


def gather_weights(neighbours, enc_in, enc_down, dec_qkv, dec_out, dec_in, dec_down, cca_q, cca_kv, cca_out, gains):
    sizes = grid_sizes()
    rows = cca_q.shape[0]
    groups, starts, total, pieces = gather_plan()
    part = enc_down.shape[1] // 2
    if rows % 4 or part % 8 or sizes != (HIDDEN_UNITS, 2, 2, 2):
        return gather_plainly(neighbours, enc_in, enc_down, dec_qkv, dec_out, dec_in, dec_down, cca_q, cca_kv, cca_out, gains)
    lead = sizes[:3]
    shapes = [lead + (2 * rows, 2 * half_width(group)) for group in groups] + [lead + (2, 2, part, D)] * 4
    out_shape = [jax.ShapeDtypeStruct(shape, BF) for shape in shapes]
    count = neighbours.shape[0]
    block = FF // HIDDEN_UNITS
    out_shape += [jax.ShapeDtypeStruct((count, D), jnp.float32)] * 2 + [jax.ShapeDtypeStruct((count, D), BF)] * 2
    out_shape += [jax.ShapeDtypeStruct((count, FF), BF)] * 4 + [jax.ShapeDtypeStruct((count, D), BF)]
    per_piece = sum((size - 1) * (1 if size == 2 else 2) for size in sizes)
    n_loads = sum(len(half) for group in groups for half in group) + 16 + len(groups)
    split = lambda w: w.reshape(w.shape[0], 2, part, D)
    outs = pl.pallas_call(
        functools.partial(gather_kernel, sizes),
        out_shape=out_shape,
        in_specs=[ANY] * 11,
        out_specs=[ANY] * len(out_shape),
        scratch_shapes=[
            pltpu.VMEM((2, rows, total), BF),
            pltpu.VMEM((rows, total), BF),
            pltpu.VMEM((2 * rows, total), BF),
            pltpu.VMEM((8, part, D), BF),
            pltpu.SemaphoreType.DMA((per_piece * len(pieces),)),
            pltpu.SemaphoreType.DMA((per_piece * len(pieces),)),
            pltpu.SemaphoreType.DMA((n_loads,)),
            pltpu.SemaphoreType.DMA((2, len(groups))),
            pltpu.VMEM((count, D), jnp.float32),
            pltpu.VMEM((count, D), BF),
            pltpu.VMEM(lead + (2 * rows, 128), BF),
            pltpu.VMEM((128, D), jnp.float32),
            pltpu.VMEM((2,) + lead + (2 * rows, block), BF),
            pltpu.VMEM((2,) + sizes[1:3] + (2, 2, part, D), BF),
            pltpu.VMEM((2, count, block), BF),
            pltpu.VMEM((2, count, block), BF),
            pltpu.SemaphoreType.DMA((7, 2)),
        ],
        compiler_params=pltpu.CompilerParams(collective_id=0, has_side_effects=True, vmem_limit_bytes=56 << 20),
        name="gather_weights",
    )(enc_in, split(enc_down), dec_qkv, dec_out, dec_in, split(dec_down), cca_q, cca_kv, cca_out, gains, neighbours)
    narrow = [out.reshape(D, out.shape[-1]) for out in outs[:N_GROUPS]]
    tall = [out.reshape(FF, D) for out in outs[N_GROUPS : N_GROUPS + 4]]
    first, second, inputs_0, inputs_1, hidden_0, hidden_1, slope_0, slope_1, encoded = outs[N_GROUPS + 4 :]
    kept = [(neighbours, inputs_0, hidden_0, slope_0), (first, inputs_1, hidden_1, slope_1)]
    mixed = narrow[2]
    half = mixed.shape[1] // 2
    sides = [mixed[:, :half], mixed[:, half:]]
    qkv = [side[:, 2 * D : 5 * D] for side in sides]
    out = [side[:, 5 * D : 6 * D] for side in sides]
    return dict(
        encoder=(second, kept, encoded),
        enc_in=narrow[:2], enc_down=tall[:2], dec_in=narrow[3:5], dec_down=tall[2:], dec_qkv=qkv, dec_out=out,
        cca_kv=[side[:, :D] for side in sides], cca_q=sides[0][:, D : 2 * D], cca_out=sides[1][:, D : 2 * D],
        gains=narrow[5][:, :8],
    )


ORDERS = ((1, False), (2, False), (1, True), (2, False), (1, False), (2, True))
CORE, HEAVY, ZED, PAIR, CORE_AGAIN, PER_PIECE = 0, 1, 2, 8, 9, 10
START = (0, 1, 4, 6, 7, 8, 9, 10, 11)
SLOTS = dict(part=2, whole=5, half=8, sibling=3, heavy=8, middle=8, last=8, zed=6, final=4)


def gradient_pieces():
    pieces = []
    both = lambda left, right, out, layer, k: tuple(
        (left, right, 2 * D * half + D * k, out, layer, 2 * D * half + D * k) for half in range(2)
    )
    for layer in reversed(range(2)):
        base = 8 * layer
        for k in range(2):
            pieces.append(both(base + 6, base + 7, 5, layer, k))
        for k in range(2):
            pieces.append(both(base + 4, base + 5, 4, layer, k))
    pieces.append(tuple((8 * layer + 2, 8 * layer + 3, 0, 3, layer, 0) for layer in range(2)))
    for k in range(3):
        pieces.append(tuple((8 * layer, 8 * layer + 1, D * k, 2, layer, D * k) for layer in range(2)))
    pieces.append(((16, 17, 0, 6, None, 0), (20, 21, 0, 8, None, 0)))
    pieces.append(tuple((18, 19, D * half, 7, None, D * half) for half in range(2)))
    for layer in reversed(range(2)):
        base = 22 + 4 * layer
        for k in range(2):
            pieces.append(both(base + 2, base + 3, 1, layer, k))
        for k in range(2):
            pieces.append(both(base, base + 1, 0, layer, k))
    return pieces


N_OPERANDS = 30


class Sums:
    def __init__(self, place, sizes, sems, buffers, slots, width):
        self.place, self.sizes, self.width = place, sizes, width
        self.send_sem, self.recv_sem = sems
        self.part, self.whole, self.half, self.sibling, self.heavy, self.middle, self.last, self.zed, self.final = buffers
        self.slots = slots

    def slot(self, name, number):
        return lax.rem(number, self.slots[name])

    def copy(self, number, which, source, target, device):
        index = number * PER_PIECE + which
        return pltpu.make_async_remote_copy(
            src_ref=source,
            dst_ref=target,
            send_sem=self.send_sem.at[index],
            recv_sem=self.recv_sem.at[index],
            device_id=device_at(device),
            device_id_type=MESH_ID,
        )

    def core_copy(self, number):
        return self.copy(
            number,
            CORE,
            self.part.at[self.slot("part", number)],
            self.sibling.at[self.slot("sibling", number)],
            self.swapped(3),
        )

    def swapped(self, axis):
        return self.place[:axis] + (1 - self.place[axis],) + self.place[axis + 1 :]

    def heavy_copy(self, number, axis):
        whole = self.whole.at[self.slot("whole", number)]
        there = 1 - self.place[axis]
        source = whole.at[:, there] if axis == 1 else whole.at[:, :, there]
        return self.copy(number, HEAVY, source, self.heavy.at[self.slot("heavy", number)], self.swapped(axis))

    def pair_copy(self, number, axis, early):
        half = self.half.at[self.slot("half", number)]
        there = 1 - self.place[axis]
        if early:
            source, target = half.at[:, there], self.middle.at[self.slot("middle", number)]
        else:
            source, target = half.at[self.place[0], there], self.last.at[self.slot("last", number)]
        return self.copy(number, PAIR, source, target, self.swapped(axis))

    def zed_block(self, number, axis, early, at):
        half = self.half.at[self.slot("half", number)]
        at = jnp.clip(at, 0, self.sizes[0] - 1)
        return half.at[at, pl.ds(self.place[axis], 1)] if early else half.at[at]

    def zed_room(self, number, early, hop, way):
        room = self.zed.at[self.slot("zed", number), hop - 1, way]
        return room.at[pl.ds(0, 1)] if early else room

    def zed_hops(self, number, axis, early, hop):
        z, size = self.place[0], self.sizes[0]
        found = []
        for way, by in enumerate((-1, 1)):
            sent, ahead = z + by * hop, z + by
            behind, got = z - by, z - by + by * hop
            room = self.zed_room(number, early, hop, way)
            device = (jnp.clip(ahead, 0, size - 1),) + self.place[1:]
            copy = self.copy(number, ZED + 2 * (hop - 1) + way, self.zed_block(number, axis, early, sent), room, device)
            sends = jnp.logical_and(inside(sent, size), inside(ahead, size))
            receives = jnp.logical_and(inside(got, size), inside(behind, size))
            found.append((copy, sends, receives, self.zed_block(number, axis, early, got), room))
        return found

    def start_zed(self, number, axis, early, hop):
        for copy, sends, _, _, _ in self.zed_hops(number, axis, early, hop):
            pl.when(sends)(copy.start)

    def finish_zed(self, number, axis, early, hop):
        for copy, sends, receives, block, room in self.zed_hops(number, axis, early, hop):
            pl.when(sends)(copy.wait_send)

            @pl.when(receives)
            def _():
                copy.wait_recv()
                for k in range(1 if early else 2):
                    block[k] = block[k] + room[k]

    def add_core(self, number):
        self.core_copy(number).wait()
        whole, sibling = self.slot("whole", number), self.slot("sibling", number)

        def one(k, _):
            at = (k // 4, (k // 2) % 2, k % 2)
            self.whole[(whole, *at)] = self.whole[(whole, *at)] + self.sibling[(sibling, *at)]
            return 0

        lax.fori_loop(0, 4 * self.sizes[0], one, 0)

    def add_heavy(self, number, axis):
        self.heavy_copy(number, axis).wait()
        whole, half, heavy = (self.slot(name, number) for name in ("whole", "half", "heavy"))

        def one(k, _):
            z, o = k // 2, k % 2
            at = (z, self.place[1], o) if axis == 1 else (z, o, self.place[2])
            self.half[half, z, o] = self.whole[(whole, *at)] + self.heavy[heavy, z, o]
            return 0

        lax.fori_loop(0, 2 * self.sizes[0], one, 0)

    def add_pair(self, number, axis, early):
        self.pair_copy(number, axis, early).wait()
        half, here = self.slot("half", number), self.place[axis]
        if early:
            for z in range(self.sizes[0]):
                self.half[half, z, here] = self.half[half, z, here] + self.middle[self.slot("middle", number), z]
        else:
            z = self.place[0]
            self.half[half, z, here] = self.half[half, z, here] + self.last[self.slot("last", number)]

    def split_rows(self, number, axis):
        half, final = self.slot("half", number), self.slot("final", number)
        rows = self.half[half, self.place[0], self.place[axis]].astype(jnp.float32)
        count = rows.shape[0] // 2
        first, second = rows[:count], rows[count:]
        self.final[final, 0] = jnp.where(self.place[3] == 0, first, second)
        self.final[final, 2] = jnp.where(self.place[3] == 0, second, first)

    def final_copy(self, number):
        final = self.slot("final", number)
        return self.copy(number, CORE_AGAIN, self.final.at[final, 2], self.final.at[final, 1], self.swapped(3))

    def step(self, step, number, first, early):
        other = 3 - first
        sequence = [("pair", 0), ("zed", 3), ("zed", 2), ("zed", 1)] if early else [("zed", 3), ("zed", 2), ("zed", 1), ("pair", 0)]
        if step == 1:
            self.heavy_copy(number, first).start()
            return
        if step == 2:
            self.add_heavy(number, first)
        else:
            kind, hop = sequence[step - 3]
            if kind == "pair":
                self.add_pair(number, other, early)
            else:
                self.finish_zed(number, other, early, hop)
        if step < 6:
            kind, hop = sequence[step - 2]
            if kind == "pair":
                self.pair_copy(number, other, early).start()
            else:
                self.start_zed(number, other, early, hop)
        else:
            self.split_rows(number, other)
            self.final_copy(number).start()


def reduce_kernel(sizes, tall, *refs):
    pieces = gradient_pieces()
    operands, gains = refs[:N_OPERANDS], refs[N_OPERANDS]
    outs = refs[N_OPERANDS + 1 : N_OPERANDS + 11]
    scratch = refs[N_OPERANDS + 11 :]
    left, right, product = scratch[:3]
    buffers, small = scratch[3:12], scratch[12:21]
    send_sem, recv_sem, small_send, small_recv, load_sem, out_sem = scratch[21:]
    place = grid_place()
    core = place[3]
    count = len(pieces)
    sums = Sums(place, sizes, (send_sem, recv_sem), buffers, SLOTS, D)
    once = Sums(place, sizes, (small_send, small_recv), small, {name: 1 for name in SLOTS}, 128)
    is_tall = [tall[piece[0][0]] for piece in pieces]
    first_tall = is_tall.index(True)
    long_rows, short_rows = left.shape[2], None

    def rows_of(k):
        return operands[pieces[k][0][0]].shape[0]

    def loads(k, slot):
        rows = rows_of(k)
        found = []
        for half in range(2):
            l, r, column, _, _, _ = pieces[k][half]
            mine = jnp.where(core == half, 1, 0)
            found.append((operands[l], left.at[slot, mine, pl.ds(0, rows)], load_sem.at[slot, half]))
            found.append((operands[r].at[:, pl.ds(column, D)], right.at[slot, mine, pl.ds(0, rows)], load_sem.at[slot, 2 + half]))
        return [pltpu.make_async_copy(*args) for args in found]

    def start_loads(number):
        for k in range(count):

            @pl.when(number == k)
            def _():
                for copy in loads(k, k % 2):
                    copy.start()

    def multiply(number, which, rows):
        slot = lax.rem(number, 2)

        def block(k, _):
            columns = pl.ds(pl.multiple_of(k * 128, 128), 128)
            product[pl.ds(pl.multiple_of(k * 128, 128), 128), :] = lax.dot_general(
                left[slot, which, pl.ds(0, rows), columns],
                right[slot, which, pl.ds(0, rows), :],
                (((0,), (0,)), ((), ())),
                preferred_element_type=jnp.float32,
            )
            return 0

        lax.fori_loop(0, D // 128, block, 0)
        chunk = sums.whole.shape[4]

        def store(k, _):
            values = product[pl.ds(pl.multiple_of(k * chunk, 8), chunk), :].astype(BF)
            at = (k // 4, (k // 2) % 2, k % 2)
            if which == 0:
                sums.part[(sums.slot("part", number), *at)] = values
            else:
                sums.whole[(sums.slot("whole", number), *at)] = values
            return 0

        lax.fori_loop(0, D // chunk, store, 0)

    def compute(number):
        for flag in sorted(set(is_tall)):
            wanted = jnp.logical_and(number >= first_tall, flag) if flag else number < first_tall
            k = first_tall if flag else 0

            @pl.when(wanted)
            def _():
                for copy in loads(k, lax.rem(number, 2)):
                    copy.wait()
                multiply(number, 0, rows_of(k))
                sums.core_copy(number).start()
                multiply(number, 1, rows_of(k))

    def out_copies(k):
        slot = k % SLOTS["final"]
        found = []
        for half in range(2):
            _, _, _, out, layer, column = pieces[k][half]
            target = outs[out] if layer is None else outs[out].at[layer]
            source = sums.final.at[slot, jnp.where(core == half, 0, 1)]
            found.append(pltpu.make_async_copy(source, target.at[:, pl.ds(column, D)], out_sem.at[slot, half]))
        return found

    greet(place, sizes)
    small_loads = []
    for k, target in enumerate((once.part.at[0], once.whole.at[0])):
        copy = pltpu.make_async_copy(gains, target, out_sem.at[SLOTS["final"], k])
        copy.start()
        small_loads.append(copy)
    start_loads(0)

    def tick(time, _):
        for step in reversed(range(8)):

            @pl.when(time == START[step])
            def _():
                if step == 0:
                    for copy in small_loads:
                        copy.wait()
                    once.core_copy(0).start()
                elif step == 7:
                    once.final_copy(0).wait()
                    copy = pltpu.make_async_copy(once.final.at[0, 0], outs[9], out_sem.at[SLOTS["final"], 0])
                    copy.start()
                    copy.wait()
                else:
                    if step == 1:
                        once.add_core(0)
                    once.step(step, 0, *ORDERS[-1])

        for step in reversed(range(9)):
            number = time - START[step]

            @pl.when(jnp.logical_and(number >= 0, number < count))
            def _():
                if step == 0:
                    start_loads(number + 1)
                    compute(number)
                elif step == 8:
                    for copy in out_copies_at(number):
                        copy.wait()
                elif step == 7:
                    sums.final_copy(number).wait()
                    for k in range(count):

                        @pl.when(number == k)
                        def _():
                            for copy in out_copies(k):
                                copy.start()

                else:
                    if step == 1:
                        sums.add_core(number)
                    turn = lax.rem(number, len(ORDERS))
                    for order in sorted(set(ORDERS)):
                        here = functools.reduce(jnp.logical_or, [turn == k for k, one in enumerate(ORDERS) if one == order])

                        @pl.when(here)
                        def _():
                            sums.step(step, number, *order)

        return 0

    def out_copies_at(number):
        slot = lax.rem(number, SLOTS["final"])
        return [
            pltpu.make_async_copy(sums.final.at[slot, 0], outs[3].at[0, :, pl.ds(0, D)], out_sem.at[slot, half])
            for half in range(2)
        ]

    lax.fori_loop(0, count + START[8], tick, 0)


def reduce_gradients(operands, gains, layers_rows):
    sizes = grid_sizes()
    rows = layers_rows
    chunk = 2 * rows
    lead = sizes[:3] + (chunk,)
    longest = max(x.shape[0] for x in operands)
    shortest = min(x.shape[0] for x in operands)
    tall = tuple(x.shape[0] == longest for x in operands)
    f32 = jnp.float32
    shapes = [(2, rows, FF), (2, rows, FF), (2, rows, 3 * D), (2, rows, D), (2, rows, FF), (2, rows, FF)]
    shapes += [(rows, D), (rows, 2 * D), (rows, D), (rows, 128)]

    def rooms(slots, width):
        z = sizes[0]
        return [
            pltpu.VMEM((slots["part"],) + lead + (width,), BF),
            pltpu.VMEM((slots["whole"],) + lead + (width,), BF),
            pltpu.VMEM((slots["half"], z, 2, chunk, width), BF),
            pltpu.VMEM((slots["sibling"],) + lead + (width,), BF),
            pltpu.VMEM((slots["heavy"], z, 2, chunk, width), BF),
            pltpu.VMEM((slots["middle"], z, chunk, width), BF),
            pltpu.VMEM((slots["last"], chunk, width), BF),
            pltpu.VMEM((slots["zed"], z - 1, 2, 2, chunk, width), BF),
            pltpu.VMEM((slots["final"], 3, rows, width), f32),
        ]

    count = len(gradient_pieces())
    return pl.pallas_call(
        functools.partial(reduce_kernel, sizes, tall),
        out_shape=[jax.ShapeDtypeStruct(shape, f32) for shape in shapes],
        in_specs=[ANY] * (N_OPERANDS + 1),
        out_specs=[ANY] * 10,
        scratch_shapes=[
            pltpu.VMEM((2, 2, longest, D), BF),
            pltpu.VMEM((2, 2, longest, D), BF),
            pltpu.VMEM((D, D), f32),
            *rooms(SLOTS, D),
            *rooms({name: 1 for name in SLOTS}, 128),
            pltpu.SemaphoreType.DMA((PER_PIECE * count,)),
            pltpu.SemaphoreType.DMA((PER_PIECE * count,)),
            pltpu.SemaphoreType.DMA((PER_PIECE,)),
            pltpu.SemaphoreType.DMA((PER_PIECE,)),
            pltpu.SemaphoreType.DMA((2, 4)),
            pltpu.SemaphoreType.DMA((SLOTS["final"] + 1, 2)),
        ],
        compiler_params=pltpu.CompilerParams(collective_id=1, has_side_effects=True, vmem_limit_bytes=62 << 20),
        name="reduce_gradients",
    )(*operands, gains.reshape(lead + (128,)))


NN = (((1,), (0,)), ((), ()))
NT = (((1,), (1,)), ((), ()))
TN = (((0,), (0,)), ((), ()))


def dot(left, right, dims):
    return lax.dot_general(left, right, dims, preferred_element_type=jnp.float32)


def head_sides(values):
    lane = lax.broadcasted_iota(jnp.int32, values.shape, 1)
    zero = jnp.zeros_like(values)
    return [jnp.where(lane < HEAD, values, zero), jnp.where(lane >= HEAD, values, zero)]


def attend_kernel(q_ref, k_ref, v_ref, bias_ref, out_ref, total_ref):
    keys, vals = k_ref[...], v_ref[...]
    outs = []
    for side, queries in enumerate(head_sides(q_ref[...])):
        scores = dot(keys, queries, NT) * SCORE_SCALE + bias_ref[...]
        peak = jnp.max(scores, 0, keepdims=True)
        powers = jnp.exp(scores - peak)
        total = jnp.sum(powers, 0, keepdims=True)
        total_ref[0, side : side + 1, :] = peak + jnp.log(total)
        probs = (powers * (1.0 / total)).astype(BF)
        outs.append(dot(probs, vals, TN))
    lane = lax.broadcasted_iota(jnp.int32, outs[0].shape, 1)
    out_ref[...] = jnp.where(lane < HEAD, outs[0], outs[1]).astype(BF)


def attend(joined, keys_vals, bias):
    queries, keys = joined.shape[0], keys_vals.shape[0]
    pairs = D // 128
    return pl.pallas_call(
        attend_kernel,
        grid=(pairs,),
        out_shape=[jax.ShapeDtypeStruct((queries, D), BF), jax.ShapeDtypeStruct((pairs, 2, queries), jnp.float32)],
        in_specs=[
            pl.BlockSpec((queries, 128), lambda p: (0, p)),
            pl.BlockSpec((keys, 128), lambda p: (0, p)),
            pl.BlockSpec((keys, 128), lambda p: (0, pairs + p)),
            pl.BlockSpec((keys, queries), lambda p: (0, 0)),
        ],
        out_specs=[pl.BlockSpec((queries, 128), lambda p: (0, p)), pl.BlockSpec((1, 2, queries), lambda p: (p, 0, 0))],
        cost_estimate=pl.CostEstimate(
            flops=4 * queries * keys * D * 2, bytes_accessed=2 * keys * 2 * D, transcendentals=14 * queries * keys
        ),
        name="attend",
    )(joined, keys_vals, keys_vals, bias)


def attend_back_kernel(q_ref, k_ref, v_ref, bias_ref, total_ref, grad_ref, gq_ref, gkv_ref):
    pair = pl.program_id(0)
    keys, vals = k_ref[...], v_ref[...]
    q_sides, g_sides = head_sides(q_ref[...]), head_sides(grad_ref[...])
    grad_q, grad_k, grad_v = [], 0.0, 0.0
    for side in range(2):
        scores = dot(keys, q_sides[side], NT) * SCORE_SCALE + bias_ref[...]
        probs = jnp.exp(scores - total_ref[0, side : side + 1, :])
        grad_probs = dot(vals, g_sides[side], NT)
        delta = jnp.sum(probs * grad_probs, 0, keepdims=True)
        grad_scores = (probs * (grad_probs - delta)).astype(BF)
        grad_v = grad_v + dot(probs.astype(BF), g_sides[side], NN)
        grad_k = grad_k + dot(grad_scores, q_sides[side], NN)
        grad_q.append(dot(grad_scores, keys, TN))
    lane = lax.broadcasted_iota(jnp.int32, grad_q[0].shape, 1)
    gq_ref[...] = (jnp.where(lane < HEAD, grad_q[0], grad_q[1]) * SCORE_SCALE).astype(BF)
    gkv_ref[:, pl.ds(pl.multiple_of(pair * 128, 128), 128)] = (grad_k * SCORE_SCALE).astype(BF)
    gkv_ref[:, pl.ds(pl.multiple_of(D + pair * 128, 128), 128)] = grad_v.astype(BF)


def attend_back(joined, keys_vals, bias, log_total, grad_mixed):
    queries, keys = joined.shape[0], keys_vals.shape[0]
    pairs = D // 128
    return pl.pallas_call(
        attend_back_kernel,
        grid=(pairs,),
        out_shape=[jax.ShapeDtypeStruct((queries, D), BF), jax.ShapeDtypeStruct((keys, 2 * D), BF)],
        in_specs=[
            pl.BlockSpec((queries, 128), lambda p: (0, p)),
            pl.BlockSpec((keys, 128), lambda p: (0, p)),
            pl.BlockSpec((keys, 128), lambda p: (0, pairs + p)),
            pl.BlockSpec((keys, queries), lambda p: (0, 0)),
            pl.BlockSpec((1, 2, queries), lambda p: (p, 0, 0)),
            pl.BlockSpec((queries, 128), lambda p: (0, p)),
        ],
        out_specs=[pl.BlockSpec((queries, 128), lambda p: (0, p)), pl.BlockSpec((keys, 2 * D), lambda p: (0, 0))],
        cost_estimate=pl.CostEstimate(
            flops=10 * queries * keys * D * 2, bytes_accessed=4 * keys * 2 * D, transcendentals=14 * queries * keys
        ),
        name="attend_back",
    )(joined, keys_vals, keys_vals, bias, log_total, grad_mixed)


def gelu_parts(values):
    size = jnp.abs(values)
    bell = jnp.exp(-0.5 * size * size)
    t = 1.0 / (1.0 + (0.3275911 * 0.7071067811865476) * size)
    tail = t * (0.127414796 + t * (-0.142248368 + t * (0.7107068705 + t * (-0.7265760135 + t * 0.5307027145)))) * bell
    share = jnp.where(values >= 0, 1.0 - tail, tail)
    return values * share, share + values * (0.3989422804014327 * bell)


def norm_parts(values):
    scale = lax.rsqrt(jnp.mean(values * values, -1, keepdims=True) + EPSILON)
    return values * scale, scale


def norm_gradient(values, norm_gain, upstream):
    unit, scale = norm_parts(values)
    inner = upstream * norm_gain
    back = scale * (inner - unit * jnp.mean(inner * unit, -1, keepdims=True))
    return back, jnp.sum(upstream * unit, 0, keepdims=True)


def hidden_block(rows):
    return 2 * D if rows <= 128 else D


def ffn_kernel(stream_ref, gain_ref, in_ref, down_ref, out_ref, inputs_ref, hidden_ref, slope_ref):
    step = pl.program_id(0)

    @pl.when(step == 0)
    def _():
        stream = stream_ref[...].astype(jnp.float32)
        out_ref[...] = stream
        inputs_ref[...] = (norm_parts(stream)[0] * gain_ref[...].astype(jnp.float32)).astype(BF)

    value, slope = gelu_parts(dot(inputs_ref[...], in_ref[...], NN))
    hidden = value.astype(BF)
    hidden_ref[...] = hidden
    slope_ref[...] = slope.astype(BF)
    out_ref[...] += dot(hidden, down_ref[...], NN)


def ffn(stream, norm_gain, weight_in, weight_down):
    rows = stream.shape[0]
    block = hidden_block(rows)
    still = lambda j: (0, 0)
    return pl.pallas_call(
        ffn_kernel,
        grid=(FF // block,),
        out_shape=[
            jax.ShapeDtypeStruct((rows, D), jnp.float32),
            jax.ShapeDtypeStruct((rows, D), BF),
            jax.ShapeDtypeStruct((rows, FF), BF),
            jax.ShapeDtypeStruct((rows, FF), BF),
        ],
        in_specs=[
            pl.BlockSpec((rows, D), still),
            pl.BlockSpec((1, D), still),
            pl.BlockSpec((D, block), lambda j: (0, j)),
            pl.BlockSpec((block, D), lambda j: (j, 0)),
        ],
        out_specs=[
            pl.BlockSpec((rows, D), still),
            pl.BlockSpec((rows, D), still),
            pl.BlockSpec((rows, block), lambda j: (0, j)),
            pl.BlockSpec((rows, block), lambda j: (0, j)),
        ],
        cost_estimate=pl.CostEstimate(
            flops=4 * rows * D * FF, bytes_accessed=4 * D * FF + 4 * rows * FF + 8 * rows * D, transcendentals=rows * FF
        ),
        name="ffn",
    )(stream, norm_gain, weight_in, weight_down)


def ffn_back_kernel(grad_ref, stream_ref, gain_ref, slope_ref, in_ref, down_ref, out_ref, low_ref, pre_ref, gain_out, total):
    step = pl.program_id(0)

    @pl.when(step == 0)
    def _():
        low_ref[...] = grad_ref[...].astype(BF)
        total[...] = jnp.zeros_like(total)

    pre = (dot(low_ref[...], down_ref[...], NT) * slope_ref[...].astype(jnp.float32)).astype(BF)
    pre_ref[...] = pre
    total[...] += dot(pre, in_ref[...], NT)

    @pl.when(step == pl.num_programs(0) - 1)
    def _():
        back, gain = norm_gradient(stream_ref[...].astype(jnp.float32), gain_ref[...].astype(jnp.float32), total[...])
        out_ref[...] = grad_ref[...].astype(jnp.float32) + back
        gain_out[...] = gain


def ffn_back(upstream, stream, norm_gain, slope, weight_in, weight_down):
    rows = stream.shape[0]
    block = hidden_block(rows)
    still = lambda j: (0, 0)
    return pl.pallas_call(
        ffn_back_kernel,
        grid=(FF // block,),
        out_shape=[
            jax.ShapeDtypeStruct((rows, D), jnp.float32),
            jax.ShapeDtypeStruct((rows, D), BF),
            jax.ShapeDtypeStruct((rows, FF), BF),
            jax.ShapeDtypeStruct((1, D), jnp.float32),
        ],
        in_specs=[
            pl.BlockSpec((rows, D), still),
            pl.BlockSpec((rows, D), still),
            pl.BlockSpec((1, D), still),
            pl.BlockSpec((rows, block), lambda j: (0, j)),
            pl.BlockSpec((D, block), lambda j: (0, j)),
            pl.BlockSpec((block, D), lambda j: (j, 0)),
        ],
        out_specs=[
            pl.BlockSpec((rows, D), still),
            pl.BlockSpec((rows, D), still),
            pl.BlockSpec((rows, block), lambda j: (0, j)),
            pl.BlockSpec((1, D), still),
        ],
        scratch_shapes=[pltpu.VMEM((rows, D), jnp.float32)],
        cost_estimate=pl.CostEstimate(
            flops=4 * rows * D * FF, bytes_accessed=4 * D * FF + 4 * rows * FF + 16 * rows * D, transcendentals=0
        ),
        name="ffn_back",
    )(upstream, stream, norm_gain, slope, weight_in, weight_down)


def shifted(x, axis, by):
    count = lax.axis_size(axis)
    pairs = [(i, i + by) for i in range(count) if 0 <= i + by < count]
    return lax.ppermute(x, axis, pairs)


def slab_term(left, right):
    return dot(left, right, TN)


def normed(values, norm_gain):
    return (norm_parts(values)[0] * norm_gain.astype(jnp.float32)).astype(BF)


def norm_back(values, norm_gain, upstream):
    return norm_gradient(values, norm_gain.astype(jnp.float32), upstream)


def self_forward(stream, norm_gain, weight_qkv, weight_out, bias):
    inputs = normed(stream, norm_gain)
    joined = dot(inputs, weight_qkv, NN).astype(BF)
    keys_vals = lax.all_gather(joined[:, D:], "seq", axis=0, tiled=True)
    mixed, log_total = attend(joined, keys_vals, bias)
    return stream + dot(mixed, weight_out, NN), (stream, inputs, joined, keys_vals, log_total, mixed)


def self_back(stored, norm_gain, weight_qkv, weight_out, bias, upstream):
    stream, inputs, joined, keys_vals, log_total, mixed = stored
    grad_low = upstream.astype(BF)
    grad_mixed = dot(grad_low, weight_out, NT).astype(BF)
    grad_queries, grad_pairs = attend_back(joined, keys_vals, bias, log_total, grad_mixed)
    own_pairs = lax.psum_scatter(grad_pairs, "seq", scatter_dimension=0, tiled=True)
    grad_joined = jnp.concatenate([grad_queries, own_pairs], -1)
    back, gain_grad = norm_back(stream, norm_gain, dot(grad_joined, weight_qkv, NT))
    return upstream + back, gain_grad, ((inputs, grad_joined), (mixed, grad_low))


def causal_bias(queries, keys):
    offset = lax.axis_index("seq") * queries
    key_place = lax.broadcasted_iota(jnp.int32, (keys, queries), 0)
    query_place = offset + lax.broadcasted_iota(jnp.int32, (keys, queries), 1)
    return jnp.where(key_place <= query_place, 0.0, MASKED_SCORE).astype(jnp.float32)


def span_bias(prior_flag, queries):
    spans = prior_flag.shape[0]
    keys = spans * NEIGH * RET
    key_span = lax.broadcasted_iota(jnp.int32, (keys, queries), 0) // (NEIGH * RET)
    query_span = lax.broadcasted_iota(jnp.int32, (keys, queries), 1) // SPAN
    allowed = jnp.repeat(prior_flag.reshape(-1), RET)[:, None] > 0.5
    return jnp.where(key_span == query_span, jnp.where(allowed, 0.0, MASKED_SCORE), 2 * MASKED_SCORE).astype(jnp.float32)


def row_gate(prior_flag):
    return jnp.repeat(jnp.max(prior_flag, -1).astype(jnp.float32), SPAN)[:, None]


def prior_spans(encoded, keep_flag):
    last_enc, last_flag = shifted((encoded[-1:], keep_flag[-1:]), "seq", 1)
    return jnp.concatenate([last_enc, encoded[:-1]], 0), jnp.concatenate([last_flag, keep_flag[:-1]], 0)


def cross_forward(stream, encoded, keep_flag, norm_gain, weight_q, weight_kv, weight_out):
    prior_enc, prior_flag = prior_spans(encoded, keep_flag)
    prior_enc = prior_enc.reshape(-1, D)
    inputs = normed(stream, norm_gain)
    queries = dot(inputs, weight_q, NN).astype(BF)
    keys_vals = jnp.concatenate([dot(prior_enc, side, NN).astype(BF) for side in weight_kv], 1)
    bias = span_bias(prior_flag, stream.shape[0])
    mixed, log_total = attend(queries, keys_vals, bias)
    branch = row_gate(prior_flag) * dot(mixed, weight_out, NN)
    return stream + branch, (stream, inputs, prior_enc, prior_flag, queries, keys_vals, bias, log_total, mixed)


def cross_back(stored, norm_gain, weight_q, weight_kv, weight_out, upstream):
    stream, inputs, prior_enc, prior_flag, queries, keys_vals, bias, log_total, mixed = stored
    grad_low = (upstream * row_gate(prior_flag)).astype(BF)
    grad_mixed = dot(grad_low, weight_out, NT).astype(BF)
    grad_queries, grad_pairs = attend_back(queries, keys_vals, bias, log_total, grad_mixed)
    grad_prior = dot(grad_pairs[:, :D], weight_kv[0], NT) + dot(grad_pairs[:, D:], weight_kv[1], NT)
    grad_prior = grad_prior.reshape(prior_flag.shape[0], NEIGH * RET, D)
    from_next = shifted(grad_prior[:1].astype(BF), "seq", -1).astype(jnp.float32)
    encoded_grad = jnp.concatenate([grad_prior[1:], from_next], 0).reshape(-1, D)
    back, gain_grad = norm_back(stream, norm_gain, dot(grad_queries, weight_q, NT))
    pairs = ((inputs, grad_queries), (prior_enc, grad_pairs), (mixed, grad_low))
    return upstream + back, gain_grad, pairs, encoded_grad


def on_device(
    tokens,
    retrieved,
    span_doc,
    neigh_doc,
    cotangent,
    dec_gain,
    dec_qkv,
    dec_out,
    dec_in,
    dec_down,
    cca_gain,
    cca_q,
    cca_kv,
    cca_out,
    enc_gain,
    enc_in,
    enc_down,
    enc_final,
):
    assert tokens.shape[0] == 1
    rows = cca_q.shape[0]
    own_gains = jnp.concatenate([dec_gain.reshape(4, rows), cca_gain[None], enc_gain, enc_final[None]], 0).T
    own_gains = jnp.pad(own_gains, ((0, 0), (0, 120)))
    neighbours = retrieved.reshape(-1, D)
    full = gather_weights(
        neighbours, enc_in, enc_down, dec_qkv, dec_out, dec_in, dec_down, cca_q, cca_kv, cca_out, own_gains
    )
    gains = full["gains"].T
    attn_gain, ffn_gain = (gains[0:1], gains[2:3]), (gains[1:2], gains[3:4])
    cross_gain, encode_gain, final_gain = gains[4:5], (gains[5:6], gains[6:7]), gains[7:8]
    cross_weights = (cross_gain, full["cca_q"], full["cca_kv"], full["cca_out"])
    queries = tokens.shape[1]
    bias = causal_bias(queries, queries * lax.axis_size("seq"))

    encoder, encoder_kept, encoded = full["encoder"]
    encoded = encoded.reshape(span_doc.shape[1], NEIGH * RET, D)
    keep_flag = (neigh_doc[0] != span_doc[0][:, None]).astype(BF)

    stream = tokens[0].astype(jnp.float32)
    attn_kept, ffn_kept = [], []
    for layer in range(DEC_LAYERS):
        stream, kept = self_forward(stream, attn_gain[layer], full["dec_qkv"][layer], full["dec_out"][layer], bias)
        attn_kept.append(kept)
        if layer == 0:
            stream, cross_kept = cross_forward(stream, encoded, keep_flag, *cross_weights)
        before = stream
        stream, inputs, hidden, slope = ffn(before, ffn_gain[layer], full["dec_in"][layer], full["dec_down"][layer])
        ffn_kept.append((before, inputs, hidden, slope))
    result = stream.astype(BF)

    upstream = cotangent[0].astype(jnp.float32)
    attn_gain_g, ffn_gain_g = [None] * DEC_LAYERS, [None] * DEC_LAYERS
    attn_pairs, ffn_pairs = [None] * DEC_LAYERS, [None] * DEC_LAYERS
    for layer in reversed(range(DEC_LAYERS)):
        before, inputs, hidden, slope = ffn_kept[layer]
        upstream, grad_low, grad_pre, ffn_gain_g[layer] = ffn_back(
            upstream, before, ffn_gain[layer], slope, full["dec_in"][layer], full["dec_down"][layer]
        )
        ffn_pairs[layer] = ((inputs, grad_pre), (grad_low, hidden))
        if layer == 0:
            upstream, cross_gain_g, cross_pairs, encoded_grad = cross_back(cross_kept, *cross_weights, upstream)
        upstream, attn_gain_g[layer], attn_pairs[layer] = self_back(
            attn_kept[layer], attn_gain[layer], full["dec_qkv"][layer], full["dec_out"][layer], bias, upstream
        )

    enc_upstream, final_gain_g = norm_back(encoder, final_gain, encoded_grad)
    enc_gain_g, enc_pairs = [None] * ENC_LAYERS, [None] * ENC_LAYERS
    for layer in reversed(range(ENC_LAYERS)):
        before, inputs, hidden, slope = encoder_kept[layer]
        enc_upstream, grad_low, grad_pre, enc_gain_g[layer] = ffn_back(
            enc_upstream, before, encode_gain[layer], slope, full["enc_in"][layer], full["enc_down"][layer]
        )
        enc_pairs[layer] = ((inputs, grad_pre), (grad_low, hidden))

    pair_list = []
    for layer in range(DEC_LAYERS):
        pair_list += list(attn_pairs[layer]) + list(ffn_pairs[layer])
    pair_list += list(cross_pairs)
    for layer in range(ENC_LAYERS):
        pair_list += list(enc_pairs[layer])
    gain_list = []
    for layer in range(DEC_LAYERS):
        gain_list += [attn_gain_g[layer], ffn_gain_g[layer]]
    gain_list = [gain.reshape(D) for gain in gain_list + [cross_gain_g] + enc_gain_g + [final_gain_g]]

    grads = sum_gradients(pair_list, gain_list, rows)
    (enc_in_g, enc_down_g, dec_qkv_g, dec_out_g, dec_in_g, dec_down_g, cross_q_g, cross_kv_g, cross_out_g, gain_cols) = grads
    gain_rows = gain_cols[:, :8].T
    return (
        result[None],
        upstream[None],
        gain_rows[:4].reshape(2, 2, rows),
        dec_qkv_g,
        dec_out_g,
        dec_in_g,
        jnp.swapaxes(dec_down_g, 1, 2),
        gain_rows[4],
        cross_q_g,
        cross_kv_g,
        cross_out_g,
        gain_rows[5:7],
        enc_in_g,
        jnp.swapaxes(enc_down_g, 1, 2),
        gain_rows[7],
    )


def sum_plainly(pair_list, gain_list):
    blocks = [slab_term(left, right) for left, right in pair_list] + [vector[:, None] for vector in gain_list]
    owned = lax.psum_scatter(
        jnp.concatenate(blocks, 1).astype(BF), ("dp", "seq"), scatter_dimension=0, tiled=True
    ).astype(jnp.float32)
    pieces, cursor = [], 0
    for _, right in pair_list:
        pieces.append(owned[:, cursor : cursor + right.shape[-1]])
        cursor += right.shape[-1]
    two = lambda first, second: jnp.stack([pieces[first], pieces[second]])
    return [
        two(11, 13), two(12, 14), two(0, 4), two(1, 5), two(2, 6), two(3, 7), pieces[8], pieces[9], pieces[10], owned[:, cursor:]
    ]


def sum_gradients(pair_list, gain_list, rows):
    sizes = grid_sizes()
    if rows % 4 or sizes != (4, 2, 2, 2):
        return sum_plainly(pair_list, gain_list)
    operands = [x.reshape(-1, x.shape[-1]) for pair in pair_list for x in pair]
    gains = jnp.pad(jnp.stack(gain_list).astype(BF).T, ((0, 0), (0, 128 - len(gain_list))))
    return reduce_gradients(operands, gains, rows)


def solution(mesh):
    return jax.shard_map(
        on_device,
        mesh=mesh,
        in_specs=(
            P("dp", "seq", None),
            P("dp", "seq", None, None, None),
            P("dp", "seq"),
            P("dp", "seq", None),
            P("dp", "seq", None),
            P(None, None, ("dp", "seq")),
            P(None, ("dp", "seq"), None),
            P(None, ("dp", "seq"), None),
            P(None, ("dp", "seq"), None),
            P(None, ("dp", "seq"), None),
            P(("dp", "seq")),
            P(("dp", "seq"), None),
            P(("dp", "seq"), None),
            P(("dp", "seq"), None),
            P(None, ("dp", "seq")),
            P(None, ("dp", "seq"), None),
            P(None, ("dp", "seq"), None),
            P(("dp", "seq")),
        ),
        out_specs=(
            P("dp", "seq", None),
            P("dp", "seq", None),
            P(None, None, ("dp", "seq")),
            P(None, ("dp", "seq"), None),
            P(None, ("dp", "seq"), None),
            P(None, ("dp", "seq"), None),
            P(None, None, ("dp", "seq")),
            P(("dp", "seq")),
            P(("dp", "seq"), None),
            P(("dp", "seq"), None),
            P(("dp", "seq"), None),
            P(None, ("dp", "seq")),
            P(None, ("dp", "seq"), None),
            P(None, None, ("dp", "seq")),
            P(("dp", "seq")),
        ),
        check_vma=False,
    )
```

```python
import functools
import heapq
import jax
import jax.numpy as jnp
from jax import lax
from jax.experimental import pallas as pl
from jax.experimental.pallas import tpu as pltpu
from jax.sharding import PartitionSpec as P

D = 896
FF = 3584
HEADS = 14
HEAD = 64
SPAN = 64
NEIGH = 2
RET = 128
ENC_LAYERS = 2
DEC_LAYERS = 2
EPSILON = 1e-06
SCORE_SCALE = 0.125
MASKED_SCORE = -1000000000.0
BF = jnp.bfloat16
MESH_ID = pl.DeviceIdType.MESH
ANY = pl.BlockSpec(memory_space=pl.ANY)


def grid_sizes():
    return (lax.axis_size("dp"), lax.axis_size("seq") // 4, 2, 2)


def grid_place():
    seq = lax.axis_index("seq")
    return (lax.axis_index("dp"), seq // 4, (seq // 2) % 2, seq % 2)


def device_at(place):
    z, y, x, core = place
    return (z, (y * 2 + x) * 2 + core)


def moved(place, sizes, axis, by):
    size = sizes[axis]
    there = lax.rem(place[axis] + (by % size), size)
    return place[:axis] + (there,) + place[axis + 1 :]


def greet(place, sizes):
    barrier = pltpu.get_barrier_semaphore()
    for axis in range(4):
        size, here = sizes[axis], place[axis]
        for by in (1, -1):
            there = here + by

            @pl.when(inside(there, size))
            def _():
                other = place[:axis] + (jnp.clip(there, 0, size - 1),) + place[axis + 1 :]
                pl.semaphore_signal(barrier, inc=1, device_id=device_at(other), device_id_type=MESH_ID)

    count = 0
    for axis in range(4):
        for by in (1, -1):
            count = count + inside(place[axis] + by, sizes[axis]).astype(jnp.int32)
    pl.semaphore_wait(barrier, count)


class Hop:
    def __init__(self, copy, sends, receives):
        self.copy, self.sends, self.receives = copy, sends, receives

    def start(self):
        pl.when(self.sends)(self.copy[0].start)

    def wait(self):
        pl.when(self.sends)(self.copy[0].wait_send)
        pl.when(self.receives)(self.copy[1].wait_recv)


def inside(place, size):
    return jnp.logical_and(place >= 0, place < size)


ZYX, ZXY, YZX, XZY, YXZ, XYZ = (0, 1, 2), (0, 2, 1), (1, 0, 2), (2, 0, 1), (1, 2, 0), (2, 1, 0)
ROUTES = (YXZ, ZYX, ZXY, ZYX, ZXY, ZXY, YZX, ZXY, ZYX, ZYX)
ROUTES += (ZXY, XZY, ZYX, YZX, XZY, XZY, YZX, YXZ, XYZ)
UNIT_US, HOP_US, CORE_US = 2.2, 2.5, 0.17


def schedule(pieces, routes, sizes):
    chains = []
    for number, piece in enumerate(pieces):
        scale, held, chain = piece[3] / PIECE, 1, []
        for axis in routes[number]:
            chain += [(axis, held * UNIT_US * scale)] * (sizes[axis] - 1)
            held *= sizes[axis]
        chains.append(chain + [(3, held * CORE_US * scale)])
    free, flying, ready = [0.0] * 4, [0] * 4, [[] for _ in range(4)]
    for number, chain in enumerate(chains):
        heapq.heappush(ready[chain[0][0]], (number, number, 0))
    now, events, order = 0.0, [], []
    while True:
        for link in range(4):
            while ready[link] and flying[link] < 2:
                _, number, step = heapq.heappop(ready[link])
                free[link] = max(free[link], now) + chains[number][step][1]
                flying[link] += 1
                order.append(("start", number, step, now))
                heapq.heappush(events, (free[link] + HOP_US, number, step, link))
        if not events:
            return order
        now, number, step, link = heapq.heappop(events)
        flying[link] -= 1
        order.append(("wait", number, step, now))
        if step + 1 < len(chains[number]):
            heapq.heappush(ready[chains[number][step + 1][0]], (number, number, step + 1))


PIECE = 896


def narrow_groups():
    qkv = 3 * D
    wide = FF // 2
    whole = lambda arg, layer: [[(arg, layer, 0, wide)], [(arg, layer, wide, wide)]]
    return [
        whole(0, 0),
        whole(0, 1),
        [
            [(7, None, 0, D), (6, None, 0, D), (2, 0, 0, qkv), (3, 0, 0, D)],
            [(7, None, D, D), (8, None, 0, D), (2, 1, 0, qkv), (3, 1, 0, D)],
        ],
        whole(4, 0),
        [[(9, None, 0, 128)], [(9, None, 0, 128)]],
    ]


def half_width(group):
    return sum(part[3] for part in group[0])


def gather_plan():
    groups = narrow_groups()
    starts, cursor = [], 0
    for group in groups:
        starts.append(cursor)
        cursor += half_width(group)
    pieces = []
    for kind, number in (("n", 4), ("n", 0), ("r", 0), ("n", 1), ("r", 1), ("n", 2), ("n", 3), ("r", 2)):
        if kind == "n":
            width = half_width(groups[number])
            for first in range(0, width, PIECE):
                pieces.append((kind, number, first, min(PIECE, width - first)))
        else:
            pieces.append((kind, number, 0, D))
            pieces.append((kind, number, 1, D))
    return groups, starts, cursor, pieces


N_GROUPS = 5
N_TALL = 3


def gather_kernel(sizes, *refs):
    groups, starts, _, pieces = gather_plan()
    ins, neighbours = refs[:10], refs[10]
    n_outs = N_GROUPS + N_TALL
    outs, encoder_outs, late_out = refs[11 : 11 + n_outs], refs[11 + n_outs : 20 + n_outs], refs[20 + n_outs]
    halves, other, joined, own_rows, send_sem, recv_sem, load_sem, swap_sem = refs[21 + n_outs : 29 + n_outs]
    late_in, late_down, late, late_sem = refs[29 + n_outs : 33 + n_outs]
    encoder_rooms = refs[33 + n_outs :]
    place = grid_place()
    z, y, x, core = place
    sibling = device_at(moved(place, sizes, 3, 1))
    loads = []
    for number, group in enumerate(groups):
        for half in range(2):
            cursor = starts[number]
            for arg, layer, first, size in group[half]:
                source = ins[arg] if layer is None else ins[arg].at[layer]
                loads.append((source.at[:, pl.ds(first, size)], halves.at[half, :, pl.ds(cursor, size)]))
                cursor += size
    for number, (arg, layer) in enumerate(((1, 0), (1, 1), (5, 0))):
        for part in range(2):
            loads.append((ins[arg].at[layer, part], own_rows.at[2 * number + part]))
    late_loads = [
        pltpu.make_async_copy(ins[4].at[1], late_in, late_sem.at[0]),
        pltpu.make_async_copy(ins[5].at[1], late_down, late_sem.at[1]),
    ]
    late_store = pltpu.make_async_copy(late, late_out, late_sem.at[2])

    def late_unit():
        for copy in late_loads:
            copy.wait()
        down = late_down[...].astype(jnp.float32).reshape(-1, D)
        fill = jnp.zeros((4 * ROOM - down.shape[0], D), jnp.float32)
        late[pl.ds(0, 4 * ROOM), :] = jnp.concatenate([down, fill], 0).astype(BF)
        fill = jnp.zeros((ROOM - late_in.shape[0], D), jnp.float32)
        for k in range(FF // D):
            rows = late_in[:, pl.ds(k * D, D)].astype(jnp.float32)
            late[pl.ds((4 + k) * ROOM, ROOM), :] = jnp.concatenate([rows, fill], 0).astype(BF)
        late_store.start()

    started = []
    for copy in late_loads:
        copy.start()
    for k, (source, target) in enumerate(loads):
        copy = pltpu.make_async_copy(source, target, load_sem.at[k])
        copy.start()
        started.append(copy)
    greet(place, sizes)
    for copy in started:
        copy.wait()
    placed = []
    for number in range(N_TALL):
        for part in range(2):
            k = 2 * number + part
            target = outs[N_GROUPS + number].at[z, y, x, core, part]
            placed.append(pltpu.make_async_copy(own_rows.at[k], target, load_sem.at[len(loads) + len(groups) + k]))
            placed[-1].start()
    swaps = []
    for number, group in enumerate(groups):
        columns = pl.ds(starts[number], half_width(group))
        copy = pltpu.make_async_remote_copy(
            src_ref=halves.at[1 - core, :, columns],
            dst_ref=other.at[:, columns],
            send_sem=swap_sem.at[0, number],
            recv_sem=swap_sem.at[1, number],
            device_id=sibling,
            device_id_type=MESH_ID,
        )
        copy.start()
        swaps.append(copy)

    def view(piece, where):
        kind, number, first, size = piece
        iz, iy, ix = where[:3]
        if kind == "n":
            start = pl.multiple_of(core * half_width(groups[number]) + first, 128)
            return outs[number].at[iz, iy, ix, :, pl.ds(start, size)]
        return outs[N_GROUPS + number].at[iz, iy, ix, core, first]

    prepared = {}

    def prepare(piece):
        kind, number, first, size = piece
        if kind == "n" and number not in prepared:
            swaps[number].wait()
            group = groups[number]
            for begin in range(starts[number], starts[number] + half_width(group), 128):
                columns = pl.ds(begin, 128)
                mine = halves[core, :, columns].astype(jnp.float32)
                theirs = other[:, columns].astype(jnp.float32)
                both = [jnp.where(core == 0, mine, theirs), jnp.where(core == 0, theirs, mine)]
                joined[:, columns] = jnp.concatenate(both, 0).astype(BF)
            width = half_width(group)
            copy = pltpu.make_async_copy(
                joined.at[:, pl.ds(starts[number], width)],
                outs[number].at[z, y, x, :, pl.ds(pl.multiple_of(core * width, 128), width)],
                load_sem.at[len(loads) + number],
            )
            copy.start()
            copy.wait()
            prepared[number] = True
        elif kind == "r" and "r" not in prepared:
            for copy in placed:
                copy.wait()
            prepared["r"] = True

    semaphores = [0]

    def transfers(number):
        piece = pieces[number]
        steps, done = [], []
        for axis in routes[number] + (3,):
            size, here = sizes[axis], place[axis]

            def block(at):
                where = list(place)
                for old in done:
                    where[old] = slice(None)
                where[axis] = jnp.clip(at, 0, size - 1)
                return view(piece, where)

            for hop in range(1, size):
                hops = []
                for way in (1, -1):
                    ahead, behind = here + way, here - way
                    sent, got = here - way * (hop - 1), here - way * hop
                    if size == 2 and way == -1:
                        continue
                    if size == 2:
                        ahead, behind, got = 1 - here, 1 - here, 1 - here
                    pair = []
                    for at, other_end in ((sent, ahead), (got, behind)):
                        ref = block(at)
                        target = place[:axis] + (jnp.clip(other_end, 0, size - 1),) + place[axis + 1 :]
                        pair.append(
                            pltpu.make_async_remote_copy(
                                src_ref=ref,
                                dst_ref=ref,
                                send_sem=send_sem.at[semaphores[0]],
                                recv_sem=recv_sem.at[semaphores[0]],
                                device_id=device_at(target),
                                device_id_type=MESH_ID,
                            )
                        )
                    semaphores[0] += 1
                    sends = jnp.logical_and(inside(sent, size), inside(ahead, size))
                    hops.append(Hop(pair, sends, inside(got, size)))
                steps.append(hops)
            done.append(axis)
        return steps

    routes = [ROUTES[number % len(ROUTES)] for number in range(len(pieces))]
    running = [transfers(number) for number in range(len(pieces))]
    units = encoder_units(
        neighbours, outs[N_GROUPS - 1], (outs[0], outs[1]), (outs[N_GROUPS], outs[N_GROUPS + 1]), encoder_outs, encoder_rooms
    )
    units.insert(0, late_unit)
    needs = [{k for k, piece in enumerate(pieces) if piece[:2] in wanted} for wanted in [set()] + UNIT_NEEDS]
    due, arrived = 0.0, set()
    for what, number, step, time in schedule(pieces, routes, sizes):
        if what == "wait":
            for copy in running[number][step]:
                copy.wait()
            if step + 1 == len(running[number]):
                arrived.add(number)
        else:
            prepare(pieces[number])
            for copy in running[number][step]:
                copy.start()
        if units and time >= due and needs[len(needs) - len(units)] <= arrived:
            units.pop(0)()
            due = time + UNIT_TIME
    for unit in units:
        unit()
    late_store.wait()


ROOM = 32


HIDDEN_UNITS = 4
UNIT_TIME = 7.0
GAINS, FIRST, SECOND = {("n", 4)}, {("n", 0), ("r", 0)}, {("n", 1), ("r", 1)}
UNIT_NEEDS = [GAINS | FIRST] * (1 + HIDDEN_UNITS) + [SECOND] * (1 + HIDDEN_UNITS) + [set()]


def encoder_units(neighbours, gain_columns, weights_in, weights_down, outs, rooms):
    after, inputs_out, hidden_out, slope_out, encoded_out = outs[0:2], outs[2:4], outs[4:6], outs[6:8], outs[8]
    stream, inputs, columns, gain_rows, block_in, block_down, hidden, slope, sems = rooms
    block = FF // HIDDEN_UNITS

    def flat(values, rows):
        return values.astype(jnp.float32).reshape(rows, values.shape[-1])

    def weights(layer, k):
        slot = k % 2
        return [
            pltpu.make_async_copy(weights_in[layer].at[:, :, :, :, pl.ds(k * block, block)], block_in.at[slot], sems.at[0, slot]),
            pltpu.make_async_copy(weights_down[layer].at[k], block_down.at[slot], sems.at[1, slot]),
        ]

    def results(layer, k):
        slot = k % 2
        place = pl.ds(k * block, block)
        return [
            pltpu.make_async_copy(hidden.at[slot], hidden_out[layer].at[:, place], sems.at[2, slot]),
            pltpu.make_async_copy(slope.at[slot], slope_out[layer].at[:, place], sems.at[3, slot]),
        ]

    def stream_copy(layer):
        return pltpu.make_async_copy(stream, after[layer], sems.at[4, layer])

    def inputs_copy(layer):
        return pltpu.make_async_copy(inputs, (*inputs_out, encoded_out)[layer], sems.at[5, layer % 2])

    def norm_unit(layer):
        if layer == 0:
            first = pltpu.make_async_copy(neighbours, inputs, sems.at[6, 0])
            second = pltpu.make_async_copy(gain_columns.at[:, :, :, :, pl.ds(0, 128)], columns, sems.at[6, 1])
            first.start()
            second.start()
            first.wait()
            second.wait()
            gain_rows[...] = flat(columns[...], D).T
            stream[...] = inputs[...].astype(jnp.float32)
        else:
            for k in (HIDDEN_UNITS - 2, HIDDEN_UNITS - 1):
                for copy in results(layer - 1, k):
                    copy.wait()
            inputs_copy(layer - 1).wait()
            stream_copy(layer - 1).start()
        if layer < ENC_LAYERS:
            for copy in weights(layer, 0):
                copy.start()
        gain = gain_rows[5 + layer : 6 + layer, :]
        inputs[...] = (norm_parts(stream[...])[0] * gain).astype(BF)
        inputs_copy(layer).start()
        if layer == ENC_LAYERS:
            stream_copy(layer - 1).wait()
            inputs_copy(layer).wait()

    def hidden_unit(layer, k):
        slot = k % 2
        if k + 1 < HIDDEN_UNITS:
            for copy in weights(layer, k + 1):
                copy.start()
        for copy in weights(layer, k):
            copy.wait()
        if k >= 2:
            for copy in results(layer, k - 2):
                copy.wait()
        value, rate = gelu_parts(dot(inputs[...], flat(block_in[slot], D).astype(BF), NN))
        hidden[slot] = value.astype(BF)
        slope[slot] = rate.astype(BF)
        for copy in results(layer, k):
            copy.start()
        if k == 0 and layer > 0:
            stream_copy(layer - 1).wait()
        stream[...] += dot(hidden[slot], flat(block_down[slot], block).astype(BF), NN)

    units = []
    for layer in range(ENC_LAYERS):
        units.append(functools.partial(norm_unit, layer))
        for k in range(HIDDEN_UNITS):
            units.append(functools.partial(hidden_unit, layer, k))
    units.append(functools.partial(norm_unit, ENC_LAYERS))
    return units


def gather_plainly(neighbours, enc_in, enc_down, dec_qkv, dec_out, dec_in, dec_down, cca_q, cca_kv, cca_out, gains):
    get = lambda w: lax.all_gather(w, ("dp", "seq"), axis=w.ndim - 2, tiled=True)
    kv = get(cca_kv)
    enc_in, enc_down, columns = get(enc_in), get(enc_down), get(gains)[:, :8]
    stream, kept = neighbours, []
    for layer in range(ENC_LAYERS):
        gain = columns[:, 5 + layer][None]
        after, inputs, hidden, slope = ffn(stream, gain, enc_in[layer], enc_down[layer])
        kept.append((stream, inputs, hidden, slope))
        stream = after
    return dict(
        encoder=(stream, kept, normed(stream, columns[:, 7][None])),
        enc_in=enc_in, enc_down=enc_down, dec_in=get(dec_in), dec_down=get(dec_down), dec_qkv=get(dec_qkv),
        dec_out=get(dec_out), cca_kv=[kv[:, :D], kv[:, D:]], cca_q=get(cca_q), cca_out=get(cca_out), gains=columns,
    )


def gather_weights(neighbours, enc_in, enc_down, dec_qkv, dec_out, dec_in, dec_down, cca_q, cca_kv, cca_out, gains):
    sizes = grid_sizes()
    rows = cca_q.shape[0]
    groups, starts, total, pieces = gather_plan()
    part = enc_down.shape[1] // 2
    if rows % 4 or part % 8 or sizes != (HIDDEN_UNITS, 2, 2, 2):
        return gather_plainly(neighbours, enc_in, enc_down, dec_qkv, dec_out, dec_in, dec_down, cca_q, cca_kv, cca_out, gains)
    lead = sizes[:3]
    shapes = [lead + (2 * rows, 2 * half_width(group)) for group in groups] + [lead + (2, 2, part, D)] * N_TALL
    out_shape = [jax.ShapeDtypeStruct(shape, BF) for shape in shapes]
    count = neighbours.shape[0]
    block = FF // HIDDEN_UNITS
    out_shape += [jax.ShapeDtypeStruct((count, D), jnp.float32)] * 2 + [jax.ShapeDtypeStruct((count, D), BF)] * 2
    out_shape += [jax.ShapeDtypeStruct((count, FF), BF)] * 4 + [jax.ShapeDtypeStruct((count, D), BF)]
    out_shape += [jax.ShapeDtypeStruct((8 * ROOM, D), BF)]
    per_piece = sum((size - 1) * (1 if size == 2 else 2) for size in sizes)
    n_loads = sum(len(half) for group in groups for half in group) + 4 * N_TALL + len(groups)
    split = lambda w: w.reshape(w.shape[0], 2, part, D)
    outs = pl.pallas_call(
        functools.partial(gather_kernel, sizes),
        out_shape=out_shape,
        in_specs=[ANY] * 11,
        out_specs=[ANY] * len(out_shape),
        scratch_shapes=[
            pltpu.VMEM((2, rows, total), BF),
            pltpu.VMEM((rows, total), BF),
            pltpu.VMEM((2 * rows, total), BF),
            pltpu.VMEM((2 * N_TALL, part, D), BF),
            pltpu.SemaphoreType.DMA((per_piece * len(pieces),)),
            pltpu.SemaphoreType.DMA((per_piece * len(pieces),)),
            pltpu.SemaphoreType.DMA((n_loads,)),
            pltpu.SemaphoreType.DMA((2, len(groups))),
            pltpu.VMEM((rows, FF), BF),
            pltpu.VMEM((2, part, D), BF),
            pltpu.VMEM((8 * ROOM, D), BF),
            pltpu.SemaphoreType.DMA((3,)),
            pltpu.VMEM((count, D), jnp.float32),
            pltpu.VMEM((count, D), BF),
            pltpu.VMEM(lead + (2 * rows, 128), BF),
            pltpu.VMEM((128, D), jnp.float32),
            pltpu.VMEM((2,) + lead + (2 * rows, block), BF),
            pltpu.VMEM((2,) + sizes[1:3] + (2, 2, part, D), BF),
            pltpu.VMEM((2, count, block), BF),
            pltpu.VMEM((2, count, block), BF),
            pltpu.SemaphoreType.DMA((7, 2)),
        ],
        compiler_params=pltpu.CompilerParams(collective_id=0, has_side_effects=True, vmem_limit_bytes=56 << 20),
        name="gather_weights",
    )(enc_in, split(enc_down), dec_qkv, dec_out, dec_in, split(dec_down), cca_q, cca_kv, cca_out, gains, neighbours)
    narrow = [out.reshape(D, out.shape[-1]) for out in outs[:N_GROUPS]]
    tall = [out.reshape(FF, D) for out in outs[N_GROUPS : N_GROUPS + N_TALL]]
    first, second, inputs_0, inputs_1, hidden_0, hidden_1, slope_0, slope_1, encoded, late = outs[N_GROUPS + N_TALL :]
    late = lax.all_gather(late, ("dp", "seq"), axis=0, tiled=False)
    kept = [(neighbours, inputs_0, hidden_0, slope_0), (first, inputs_1, hidden_1, slope_1)]
    mixed = narrow[2]
    half = mixed.shape[1] // 2
    sides = [mixed[:, :half], mixed[:, half:]]
    qkv = [side[:, 2 * D : 5 * D] for side in sides]
    out = [side[:, 5 * D : 6 * D] for side in sides]
    return dict(
        encoder=(second, kept, encoded),
        enc_in=narrow[:2], enc_down=tall[:2], dec_in=[narrow[3], None], dec_down=[tall[2], late], dec_qkv=qkv, dec_out=out,
        cca_kv=[side[:, :D] for side in sides], cca_q=sides[0][:, D : 2 * D], cca_out=sides[1][:, D : 2 * D],
        gains=narrow[4][:, :8],
    )


ORDERS = ((1, False), (2, False), (1, True), (2, False), (1, False), (2, True))
CORE, HEAVY, ZED, PAIR, CORE_AGAIN, PER_PIECE = 0, 1, 2, 8, 9, 10
START = (0, 1, 4, 6, 7, 8, 9, 10, 11)
SLOTS = dict(part=2, whole=5, half=8, sibling=3, heavy=8, middle=8, last=8, zed=6, final=4)


def gradient_pieces():
    pieces = []
    both = lambda left, right, out, layer, k: tuple(
        (left, right, 2 * D * half + D * k, out, layer, 2 * D * half + D * k) for half in range(2)
    )
    for layer in reversed(range(2)):
        base = 8 * layer
        for k in range(2):
            pieces.append(both(base + 6, base + 7, 5, layer, k))
        for k in range(2):
            pieces.append(both(base + 4, base + 5, 4, layer, k))
    pieces.append(tuple((8 * layer + 2, 8 * layer + 3, 0, 3, layer, 0) for layer in range(2)))
    for k in range(3):
        pieces.append(tuple((8 * layer, 8 * layer + 1, D * k, 2, layer, D * k) for layer in range(2)))
    pieces.append(((16, 17, 0, 6, None, 0), (20, 21, 0, 8, None, 0)))
    pieces.append(tuple((18, 19, D * half, 7, None, D * half) for half in range(2)))
    for layer in reversed(range(2)):
        base = 22 + 4 * layer
        for k in range(2):
            pieces.append(both(base + 2, base + 3, 1, layer, k))
        for k in range(2):
            pieces.append(both(base, base + 1, 0, layer, k))
    return pieces


N_OPERANDS = 30


class Sums:
    def __init__(self, place, sizes, sems, buffers, slots, width):
        self.place, self.sizes, self.width = place, sizes, width
        self.send_sem, self.recv_sem = sems
        self.part, self.whole, self.half, self.sibling, self.heavy, self.middle, self.last, self.zed, self.final = buffers
        self.slots = slots

    def slot(self, name, number):
        return lax.rem(number, self.slots[name])

    def copy(self, number, which, source, target, device):
        index = number * PER_PIECE + which
        return pltpu.make_async_remote_copy(
            src_ref=source,
            dst_ref=target,
            send_sem=self.send_sem.at[index],
            recv_sem=self.recv_sem.at[index],
            device_id=device_at(device),
            device_id_type=MESH_ID,
        )

    def core_copy(self, number):
        return self.copy(
            number,
            CORE,
            self.part.at[self.slot("part", number)],
            self.sibling.at[self.slot("sibling", number)],
            self.swapped(3),
        )

    def swapped(self, axis):
        return self.place[:axis] + (1 - self.place[axis],) + self.place[axis + 1 :]

    def heavy_copy(self, number, axis):
        whole = self.whole.at[self.slot("whole", number)]
        there = 1 - self.place[axis]
        source = whole.at[:, there] if axis == 1 else whole.at[:, :, there]
        return self.copy(number, HEAVY, source, self.heavy.at[self.slot("heavy", number)], self.swapped(axis))

    def pair_copy(self, number, axis, early):
        half = self.half.at[self.slot("half", number)]
        there = 1 - self.place[axis]
        if early:
            source, target = half.at[:, there], self.middle.at[self.slot("middle", number)]
        else:
            source, target = half.at[self.place[0], there], self.last.at[self.slot("last", number)]
        return self.copy(number, PAIR, source, target, self.swapped(axis))

    def zed_block(self, number, axis, early, at):
        half = self.half.at[self.slot("half", number)]
        at = jnp.clip(at, 0, self.sizes[0] - 1)
        return half.at[at, pl.ds(self.place[axis], 1)] if early else half.at[at]

    def zed_room(self, number, early, hop, way):
        room = self.zed.at[self.slot("zed", number), hop - 1, way]
        return room.at[pl.ds(0, 1)] if early else room

    def zed_hops(self, number, axis, early, hop):
        z, size = self.place[0], self.sizes[0]
        found = []
        for way, by in enumerate((-1, 1)):
            sent, ahead = z + by * hop, z + by
            behind, got = z - by, z - by + by * hop
            room = self.zed_room(number, early, hop, way)
            device = (jnp.clip(ahead, 0, size - 1),) + self.place[1:]
            copy = self.copy(number, ZED + 2 * (hop - 1) + way, self.zed_block(number, axis, early, sent), room, device)
            sends = jnp.logical_and(inside(sent, size), inside(ahead, size))
            receives = jnp.logical_and(inside(got, size), inside(behind, size))
            found.append((copy, sends, receives, self.zed_block(number, axis, early, got), room))
        return found

    def start_zed(self, number, axis, early, hop):
        for copy, sends, _, _, _ in self.zed_hops(number, axis, early, hop):
            pl.when(sends)(copy.start)

    def finish_zed(self, number, axis, early, hop):
        for copy, sends, receives, block, room in self.zed_hops(number, axis, early, hop):
            pl.when(sends)(copy.wait_send)

            @pl.when(receives)
            def _():
                copy.wait_recv()
                for k in range(1 if early else 2):
                    block[k] = block[k] + room[k]

    def add_core(self, number):
        self.core_copy(number).wait()
        whole, sibling = self.slot("whole", number), self.slot("sibling", number)

        def one(k, _):
            at = (k // 4, (k // 2) % 2, k % 2)
            self.whole[(whole, *at)] = self.whole[(whole, *at)] + self.sibling[(sibling, *at)]
            return 0

        lax.fori_loop(0, 4 * self.sizes[0], one, 0)

    def add_heavy(self, number, axis):
        self.heavy_copy(number, axis).wait()
        whole, half, heavy = (self.slot(name, number) for name in ("whole", "half", "heavy"))

        def one(k, _):
            z, o = k // 2, k % 2
            at = (z, self.place[1], o) if axis == 1 else (z, o, self.place[2])
            self.half[half, z, o] = self.whole[(whole, *at)] + self.heavy[heavy, z, o]
            return 0

        lax.fori_loop(0, 2 * self.sizes[0], one, 0)

    def add_pair(self, number, axis, early):
        self.pair_copy(number, axis, early).wait()
        half, here = self.slot("half", number), self.place[axis]
        if early:
            for z in range(self.sizes[0]):
                self.half[half, z, here] = self.half[half, z, here] + self.middle[self.slot("middle", number), z]
        else:
            z = self.place[0]
            self.half[half, z, here] = self.half[half, z, here] + self.last[self.slot("last", number)]

    def split_rows(self, number, axis):
        half, final = self.slot("half", number), self.slot("final", number)
        rows = self.half[half, self.place[0], self.place[axis]].astype(jnp.float32)
        count = rows.shape[0] // 2
        first, second = rows[:count], rows[count:]
        self.final[final, 0] = jnp.where(self.place[3] == 0, first, second)
        self.final[final, 2] = jnp.where(self.place[3] == 0, second, first)

    def final_copy(self, number):
        final = self.slot("final", number)
        return self.copy(number, CORE_AGAIN, self.final.at[final, 2], self.final.at[final, 1], self.swapped(3))

    def step(self, step, number, first, early):
        other = 3 - first
        sequence = [("pair", 0), ("zed", 3), ("zed", 2), ("zed", 1)] if early else [("zed", 3), ("zed", 2), ("zed", 1), ("pair", 0)]
        if step == 1:
            self.heavy_copy(number, first).start()
            return
        if step == 2:
            self.add_heavy(number, first)
        else:
            kind, hop = sequence[step - 3]
            if kind == "pair":
                self.add_pair(number, other, early)
            else:
                self.finish_zed(number, other, early, hop)
        if step < 6:
            kind, hop = sequence[step - 2]
            if kind == "pair":
                self.pair_copy(number, other, early).start()
            else:
                self.start_zed(number, other, early, hop)
        else:
            self.split_rows(number, other)
            self.final_copy(number).start()


def reduce_kernel(sizes, tall, *refs):
    pieces = gradient_pieces()
    operands, gains = refs[:N_OPERANDS], refs[N_OPERANDS]
    outs = refs[N_OPERANDS + 1 : N_OPERANDS + 11]
    scratch = refs[N_OPERANDS + 11 :]
    left, right, product = scratch[:3]
    buffers, small = scratch[3:12], scratch[12:21]
    send_sem, recv_sem, small_send, small_recv, load_sem, out_sem = scratch[21:]
    place = grid_place()
    core = place[3]
    count = len(pieces)
    sums = Sums(place, sizes, (send_sem, recv_sem), buffers, SLOTS, D)
    once = Sums(place, sizes, (small_send, small_recv), small, {name: 1 for name in SLOTS}, 128)
    is_tall = [tall[piece[0][0]] for piece in pieces]
    first_tall = is_tall.index(True)
    long_rows, short_rows = left.shape[2], None

    def rows_of(k):
        return operands[pieces[k][0][0]].shape[0]

    def loads(k, slot):
        rows = rows_of(k)
        found = []
        for half in range(2):
            l, r, column, _, _, _ = pieces[k][half]
            mine = jnp.where(core == half, 1, 0)
            found.append((operands[l], left.at[slot, mine, pl.ds(0, rows)], load_sem.at[slot, half]))
            found.append((operands[r].at[:, pl.ds(column, D)], right.at[slot, mine, pl.ds(0, rows)], load_sem.at[slot, 2 + half]))
        return [pltpu.make_async_copy(*args) for args in found]

    def start_loads(number):
        for k in range(count):

            @pl.when(number == k)
            def _():
                for copy in loads(k, k % 2):
                    copy.start()

    def multiply(number, which, rows):
        slot = lax.rem(number, 2)

        def block(k, _):
            columns = pl.ds(pl.multiple_of(k * 128, 128), 128)
            product[pl.ds(pl.multiple_of(k * 128, 128), 128), :] = lax.dot_general(
                left[slot, which, pl.ds(0, rows), columns],
                right[slot, which, pl.ds(0, rows), :],
                (((0,), (0,)), ((), ())),
                preferred_element_type=jnp.float32,
            )
            return 0

        lax.fori_loop(0, D // 128, block, 0)
        chunk = sums.whole.shape[4]

        def store(k, _):
            values = product[pl.ds(pl.multiple_of(k * chunk, 8), chunk), :].astype(BF)
            at = (k // 4, (k // 2) % 2, k % 2)
            if which == 0:
                sums.part[(sums.slot("part", number), *at)] = values
            else:
                sums.whole[(sums.slot("whole", number), *at)] = values
            return 0

        lax.fori_loop(0, D // chunk, store, 0)

    def compute(number):
        for flag in sorted(set(is_tall)):
            wanted = jnp.logical_and(number >= first_tall, flag) if flag else number < first_tall
            k = first_tall if flag else 0

            @pl.when(wanted)
            def _():
                for copy in loads(k, lax.rem(number, 2)):
                    copy.wait()
                multiply(number, 0, rows_of(k))
                sums.core_copy(number).start()
                multiply(number, 1, rows_of(k))

    def out_copies(k):
        slot = k % SLOTS["final"]
        found = []
        for half in range(2):
            _, _, _, out, layer, column = pieces[k][half]
            target = outs[out] if layer is None else outs[out].at[layer]
            source = sums.final.at[slot, jnp.where(core == half, 0, 1)]
            found.append(pltpu.make_async_copy(source, target.at[:, pl.ds(column, D)], out_sem.at[slot, half]))
        return found

    greet(place, sizes)
    small_loads = []
    for k, target in enumerate((once.part.at[0], once.whole.at[0])):
        copy = pltpu.make_async_copy(gains, target, out_sem.at[SLOTS["final"], k])
        copy.start()
        small_loads.append(copy)
    start_loads(0)

    def tick(time, _):
        for step in reversed(range(8)):

            @pl.when(time == START[step])
            def _():
                if step == 0:
                    for copy in small_loads:
                        copy.wait()
                    once.core_copy(0).start()
                elif step == 7:
                    once.final_copy(0).wait()
                    copy = pltpu.make_async_copy(once.final.at[0, 0], outs[9], out_sem.at[SLOTS["final"], 0])
                    copy.start()
                    copy.wait()
                else:
                    if step == 1:
                        once.add_core(0)
                    once.step(step, 0, *ORDERS[-1])

        for step in reversed(range(9)):
            number = time - START[step]

            @pl.when(jnp.logical_and(number >= 0, number < count))
            def _():
                if step == 0:
                    start_loads(number + 1)
                    compute(number)
                elif step == 8:
                    for copy in out_copies_at(number):
                        copy.wait()
                elif step == 7:
                    sums.final_copy(number).wait()
                    for k in range(count):

                        @pl.when(number == k)
                        def _():
                            for copy in out_copies(k):
                                copy.start()

                else:
                    if step == 1:
                        sums.add_core(number)
                    turn = lax.rem(number, len(ORDERS))
                    for order in sorted(set(ORDERS)):
                        here = functools.reduce(jnp.logical_or, [turn == k for k, one in enumerate(ORDERS) if one == order])

                        @pl.when(here)
                        def _():
                            sums.step(step, number, *order)

        return 0

    def out_copies_at(number):
        slot = lax.rem(number, SLOTS["final"])
        return [
            pltpu.make_async_copy(sums.final.at[slot, 0], outs[3].at[0, :, pl.ds(0, D)], out_sem.at[slot, half])
            for half in range(2)
        ]

    lax.fori_loop(0, count + START[8], tick, 0)


def reduce_gradients(operands, gains, layers_rows):
    sizes = grid_sizes()
    rows = layers_rows
    chunk = 2 * rows
    lead = sizes[:3] + (chunk,)
    longest = max(x.shape[0] for x in operands)
    shortest = min(x.shape[0] for x in operands)
    tall = tuple(x.shape[0] == longest for x in operands)
    f32 = jnp.float32
    shapes = [(2, rows, FF), (2, rows, FF), (2, rows, 3 * D), (2, rows, D), (2, rows, FF), (2, rows, FF)]
    shapes += [(rows, D), (rows, 2 * D), (rows, D), (rows, 128)]

    def rooms(slots, width):
        z = sizes[0]
        return [
            pltpu.VMEM((slots["part"],) + lead + (width,), BF),
            pltpu.VMEM((slots["whole"],) + lead + (width,), BF),
            pltpu.VMEM((slots["half"], z, 2, chunk, width), BF),
            pltpu.VMEM((slots["sibling"],) + lead + (width,), BF),
            pltpu.VMEM((slots["heavy"], z, 2, chunk, width), BF),
            pltpu.VMEM((slots["middle"], z, chunk, width), BF),
            pltpu.VMEM((slots["last"], chunk, width), BF),
            pltpu.VMEM((slots["zed"], z - 1, 2, 2, chunk, width), BF),
            pltpu.VMEM((slots["final"], 3, rows, width), f32),
        ]

    count = len(gradient_pieces())
    return pl.pallas_call(
        functools.partial(reduce_kernel, sizes, tall),
        out_shape=[jax.ShapeDtypeStruct(shape, f32) for shape in shapes],
        in_specs=[ANY] * (N_OPERANDS + 1),
        out_specs=[ANY] * 10,
        scratch_shapes=[
            pltpu.VMEM((2, 2, longest, D), BF),
            pltpu.VMEM((2, 2, longest, D), BF),
            pltpu.VMEM((D, D), f32),
            *rooms(SLOTS, D),
            *rooms({name: 1 for name in SLOTS}, 128),
            pltpu.SemaphoreType.DMA((PER_PIECE * count,)),
            pltpu.SemaphoreType.DMA((PER_PIECE * count,)),
            pltpu.SemaphoreType.DMA((PER_PIECE,)),
            pltpu.SemaphoreType.DMA((PER_PIECE,)),
            pltpu.SemaphoreType.DMA((2, 4)),
            pltpu.SemaphoreType.DMA((SLOTS["final"] + 1, 2)),
        ],
        compiler_params=pltpu.CompilerParams(collective_id=1, has_side_effects=True, vmem_limit_bytes=62 << 20),
        name="reduce_gradients",
    )(*operands, gains.reshape(lead + (128,)))


NN = (((1,), (0,)), ((), ()))
NT = (((1,), (1,)), ((), ()))
TN = (((0,), (0,)), ((), ()))


def dot(left, right, dims):
    return lax.dot_general(left, right, dims, preferred_element_type=jnp.float32)


def head_sides(values):
    lane = lax.broadcasted_iota(jnp.int32, values.shape, 1)
    zero = jnp.zeros_like(values)
    return [jnp.where(lane < HEAD, values, zero), jnp.where(lane >= HEAD, values, zero)]


def attend_kernel(q_ref, k_ref, v_ref, bias_ref, out_ref, total_ref):
    keys, vals = k_ref[...], v_ref[...]
    outs = []
    for side, queries in enumerate(head_sides(q_ref[...])):
        scores = dot(keys, queries, NT) * SCORE_SCALE + bias_ref[...]
        peak = jnp.max(scores, 0, keepdims=True)
        powers = jnp.exp(scores - peak)
        total = jnp.sum(powers, 0, keepdims=True)
        total_ref[0, side : side + 1, :] = peak + jnp.log(total)
        probs = (powers * (1.0 / total)).astype(BF)
        outs.append(dot(probs, vals, TN))
    lane = lax.broadcasted_iota(jnp.int32, outs[0].shape, 1)
    out_ref[...] = jnp.where(lane < HEAD, outs[0], outs[1]).astype(BF)


def attend(joined, keys_vals, bias):
    queries, keys = joined.shape[0], keys_vals.shape[0]
    pairs = D // 128
    return pl.pallas_call(
        attend_kernel,
        grid=(pairs,),
        out_shape=[jax.ShapeDtypeStruct((queries, D), BF), jax.ShapeDtypeStruct((pairs, 2, queries), jnp.float32)],
        in_specs=[
            pl.BlockSpec((queries, 128), lambda p: (0, p)),
            pl.BlockSpec((keys, 128), lambda p: (0, p)),
            pl.BlockSpec((keys, 128), lambda p: (0, pairs + p)),
            pl.BlockSpec((keys, queries), lambda p: (0, 0)),
        ],
        out_specs=[pl.BlockSpec((queries, 128), lambda p: (0, p)), pl.BlockSpec((1, 2, queries), lambda p: (p, 0, 0))],
        cost_estimate=pl.CostEstimate(
            flops=4 * queries * keys * D * 2, bytes_accessed=2 * keys * 2 * D, transcendentals=14 * queries * keys
        ),
        name="attend",
    )(joined, keys_vals, keys_vals, bias)


def attend_back_kernel(q_ref, k_ref, v_ref, bias_ref, total_ref, grad_ref, gq_ref, gkv_ref):
    pair = pl.program_id(0)
    keys, vals = k_ref[...], v_ref[...]
    q_sides, g_sides = head_sides(q_ref[...]), head_sides(grad_ref[...])
    grad_q, grad_k, grad_v = [], 0.0, 0.0
    for side in range(2):
        scores = dot(keys, q_sides[side], NT) * SCORE_SCALE + bias_ref[...]
        probs = jnp.exp(scores - total_ref[0, side : side + 1, :])
        grad_probs = dot(vals, g_sides[side], NT)
        delta = jnp.sum(probs * grad_probs, 0, keepdims=True)
        grad_scores = (probs * (grad_probs - delta)).astype(BF)
        grad_v = grad_v + dot(probs.astype(BF), g_sides[side], NN)
        grad_k = grad_k + dot(grad_scores, q_sides[side], NN)
        grad_q.append(dot(grad_scores, keys, TN))
    lane = lax.broadcasted_iota(jnp.int32, grad_q[0].shape, 1)
    gq_ref[...] = (jnp.where(lane < HEAD, grad_q[0], grad_q[1]) * SCORE_SCALE).astype(BF)
    gkv_ref[:, pl.ds(pl.multiple_of(pair * 128, 128), 128)] = (grad_k * SCORE_SCALE).astype(BF)
    gkv_ref[:, pl.ds(pl.multiple_of(D + pair * 128, 128), 128)] = grad_v.astype(BF)


def attend_back(joined, keys_vals, bias, log_total, grad_mixed):
    queries, keys = joined.shape[0], keys_vals.shape[0]
    pairs = D // 128
    return pl.pallas_call(
        attend_back_kernel,
        grid=(pairs,),
        out_shape=[jax.ShapeDtypeStruct((queries, D), BF), jax.ShapeDtypeStruct((keys, 2 * D), BF)],
        in_specs=[
            pl.BlockSpec((queries, 128), lambda p: (0, p)),
            pl.BlockSpec((keys, 128), lambda p: (0, p)),
            pl.BlockSpec((keys, 128), lambda p: (0, pairs + p)),
            pl.BlockSpec((keys, queries), lambda p: (0, 0)),
            pl.BlockSpec((1, 2, queries), lambda p: (p, 0, 0)),
            pl.BlockSpec((queries, 128), lambda p: (0, p)),
        ],
        out_specs=[pl.BlockSpec((queries, 128), lambda p: (0, p)), pl.BlockSpec((keys, 2 * D), lambda p: (0, 0))],
        cost_estimate=pl.CostEstimate(
            flops=10 * queries * keys * D * 2, bytes_accessed=4 * keys * 2 * D, transcendentals=14 * queries * keys
        ),
        name="attend_back",
    )(joined, keys_vals, keys_vals, bias, log_total, grad_mixed)


PAIR_GROUPS = (((0, 1), (2, 1)), ((2, 3), (1, 2)), ((4, 5), (2, 1)), ((6,), (1, 2)))
BACK_GROUPS = tuple(((pair,), ((2, 1), (1, 2))[pair % 2]) for pair in range(7))
BACK_LAGS = (2, 5, 7)


def greet_plane(place):
    barrier = pltpu.get_barrier_semaphore()
    for axis in (1, 2, 3):
        other = place[:axis] + (1 - place[axis],) + place[axis + 1 :]
        pl.semaphore_signal(barrier, inc=1, device_id=device_at(other), device_id_type=MESH_ID)
    pl.semaphore_wait(barrier, 3)


def group_columns(pairs):
    return [pl.ds(side * D + 128 * pairs[0], 128 * len(pairs)) for side in range(2)]


def plane_copies(place, axis, sources, targets, send_sem, recv_sem, index):
    device = place[:axis] + (1 - place[axis],) + place[axis + 1 :]
    return [
        pltpu.make_async_remote_copy(
            src_ref=source,
            dst_ref=target,
            send_sem=send_sem.at[index, k],
            recv_sem=recv_sem.at[index, k],
            device_id=device_at(device),
            device_id_type=MESH_ID,
        )
        for k, (source, target) in enumerate(zip(sources, targets))
    ]


def start_all(copies):
    for copy in copies:
        copy.start()


def wait_all(copies):
    for copy in copies:
        copy.wait()


def attend_gather_kernel(joined_ref, bias_ref, out_ref, total_ref, kept_ref, held, queries, send_sem, recv_sem, load_sem):
    place = grid_place()
    _, y, x, core = place
    loads = [
        pltpu.make_async_copy(joined_ref.at[:, pl.ds(D, 2 * D)], held.at[y, x, core], load_sem.at[0]),
        pltpu.make_async_copy(joined_ref.at[:, pl.ds(0, D)], queries, load_sem.at[1]),
    ]
    start_all(loads)
    greet_plane(place)
    wait_all(loads)

    def step(number, k):
        pairs, route = PAIR_GROUPS[number]
        if k == 0:
            views = [held.at[y, x, core, :, columns] for columns in group_columns(pairs)]
            axis = route[0]
        elif k == 1:
            axis = route[1]
            views = [(held.at[y, :, core, :, c] if axis == 1 else held.at[:, x, core, :, c]) for c in group_columns(pairs)]
        else:
            axis = 3
            views = [held.at[:, :, core, :, c] for c in group_columns(pairs)]
        return plane_copies(place, axis, views, views, send_sem, recv_sem, 3 * number + k)

    lane = lax.broadcasted_iota(jnp.int32, (queries.shape[0], 128), 1)
    rows = bias_ref.shape[0]

    def compute(number):
        for pair in PAIR_GROUPS[number][0]:
            keys = held[:, :, :, :, pl.ds(128 * pair, 128)].reshape(rows, 128)
            vals = held[:, :, :, :, pl.ds(D + 128 * pair, 128)].reshape(rows, 128)
            outs = []
            for side, sided in enumerate(head_sides(queries[:, pl.ds(128 * pair, 128)])):
                scores = dot(keys, sided, NT) * SCORE_SCALE + bias_ref[...]
                peak = jnp.max(scores, 0, keepdims=True)
                powers = jnp.exp(scores - peak)
                total = jnp.sum(powers, 0, keepdims=True)
                total_ref[pair, side : side + 1, :] = peak + jnp.log(total)
                outs.append(dot((powers * (1.0 / total)).astype(BF), vals, TN))
            out_ref[:, pl.ds(128 * pair, 128)] = jnp.where(lane < HEAD, outs[0], outs[1]).astype(BF)

    count = len(PAIR_GROUPS)
    for number in range(count):
        start_all(step(number, 0))
    for number in range(count):
        wait_all(step(number, 0))
        start_all(step(number, 1))
    for number in range(count):
        wait_all(step(number, 1))
        start_all(step(number, 2))
        if number > 0:
            wait_all(step(number - 1, 2))
            if number < count - 1:
                compute(number - 1)
    wait_all(step(count - 1, 2))
    keep = pltpu.make_async_copy(held, kept_ref, load_sem.at[0])
    keep.start()
    compute(count - 2)
    compute(count - 1)
    keep.wait()


def whole_block(shape):
    return pl.BlockSpec(shape, lambda: (0,) * len(shape))


def attend_gather(joined, bias):
    rows = joined.shape[0]
    _, n_y, n_x, n_core = grid_sizes()
    lead = (n_y, n_x, n_core)
    pairs, count = D // 128, len(PAIR_GROUPS)
    mixed, log_total, kept = pl.pallas_call(
        attend_gather_kernel,
        out_shape=[
            jax.ShapeDtypeStruct((rows, D), BF),
            jax.ShapeDtypeStruct((pairs, 2, rows), jnp.float32),
            jax.ShapeDtypeStruct(lead + (rows, 2 * D), BF),
        ],
        in_specs=[ANY, whole_block(bias.shape)],
        out_specs=[whole_block((rows, D)), whole_block((pairs, 2, rows)), ANY],
        scratch_shapes=[
            pltpu.VMEM(lead + (rows, 2 * D), BF),
            pltpu.VMEM((rows, D), BF),
            pltpu.SemaphoreType.DMA((3 * count, 2)),
            pltpu.SemaphoreType.DMA((3 * count, 2)),
            pltpu.SemaphoreType.DMA((2,)),
        ],
        compiler_params=pltpu.CompilerParams(collective_id=2, has_side_effects=True, vmem_limit_bytes=32 << 20),
        name="attend_gather",
    )(joined, bias)
    return mixed, log_total, kept.reshape(-1, 2 * D)


def attend_scatter_kernel(joined_ref, held_ref, bias_ref, total_ref, grad_ref, gq_ref, own_ref, *scratch):
    queries, part, from_core, from_first, from_second, send_sem, recv_sem, load_sem = scratch
    place = grid_place()
    _, y, x, core = place
    load = pltpu.make_async_copy(joined_ref.at[:, pl.ds(0, D)], queries, load_sem.at[0])
    load.start()
    greet_plane(place)
    load.wait()
    rows = bias_ref.shape[0]
    lane = lax.broadcasted_iota(jnp.int32, (queries.shape[0], 128), 1)

    def compute(number):
        for pair in BACK_GROUPS[number][0]:
            columns, beside = pl.ds(128 * pair, 128), pl.ds(D + 128 * pair, 128)
            keys = held_ref[:, :, :, :, columns].reshape(rows, 128)
            vals = held_ref[:, :, :, :, beside].reshape(rows, 128)
            q_sides, g_sides = head_sides(queries[:, columns]), head_sides(grad_ref[:, columns])
            grad_q, grad_k, grad_v = [], 0.0, 0.0
            for side in range(2):
                scores = dot(keys, q_sides[side], NT) * SCORE_SCALE + bias_ref[...]
                probs = jnp.exp(scores - total_ref[pair, side : side + 1, :])
                grad_probs = dot(vals, g_sides[side], NT)
                delta = jnp.sum(probs * grad_probs, 0, keepdims=True)
                grad_scores = (probs * (grad_probs - delta)).astype(BF)
                grad_v = grad_v + dot(probs.astype(BF), g_sides[side], NN)
                grad_k = grad_k + dot(grad_scores, q_sides[side], NN)
                grad_q.append(dot(grad_scores, keys, TN))
            gq_ref[:, columns] = (jnp.where(lane < HEAD, grad_q[0], grad_q[1]) * SCORE_SCALE).astype(BF)
            shape = part.shape[:4] + (128,)
            part[:, :, :, :, columns] = (grad_k * SCORE_SCALE).astype(BF).reshape(shape)
            part[:, :, :, :, beside] = grad_v.astype(BF).reshape(shape)

    def step(number, k):
        pairs, route = BACK_GROUPS[number]
        columns = group_columns(pairs)
        if k == 0:
            axis = 3
            sources = [part.at[:, :, 1 - core, :, c] for c in columns]
            targets = [from_core.at[:, :, :, c] for c in columns]
        elif k == 1:
            axis = route[1]
            sources = [(part.at[1 - y, :, core, :, c] if axis == 1 else part.at[:, 1 - x, core, :, c]) for c in columns]
            targets = [from_first.at[:, :, c] for c in columns]
        else:
            axis = route[0]
            sources = [(part.at[1 - y, x, core, :, c] if axis == 1 else part.at[y, 1 - x, core, :, c]) for c in columns]
            targets = [from_second.at[:, c] for c in columns]
        return plane_copies(place, axis, sources, targets, send_sem, recv_sem, 3 * number + k)

    def add(number, k):
        pairs, route = BACK_GROUPS[number]
        wait_all(step(number, k))
        for c in group_columns(pairs):
            if k == 0:
                part[:, :, core, :, c] = part[:, :, core, :, c] + from_core[:, :, :, c]
            elif k == 1 and route[1] == 1:
                part[y, :, core, :, c] = part[y, :, core, :, c] + from_first[:, :, c]
            elif k == 1:
                part[:, x, core, :, c] = part[:, x, core, :, c] + from_first[:, :, c]
            else:
                own_ref[:, c] = part[y, x, core, :, c] + from_second[:, c]

    count = len(BACK_GROUPS)
    for time in range(count + BACK_LAGS[-1]):
        if time < count:
            compute(time)
            start_all(step(time, 0))
        for k, lag in enumerate(BACK_LAGS):
            number = time - lag
            if 0 <= number < count:
                add(number, k)
                if k < 2:
                    start_all(step(number, k + 1))


def attend_scatter(joined, keys_vals, bias, log_total, grad_mixed):
    rows = joined.shape[0]
    _, n_y, n_x, n_core = grid_sizes()
    lead = (n_y, n_x, n_core)
    count = len(BACK_GROUPS)
    held = keys_vals.reshape(lead + (rows, 2 * D))
    return pl.pallas_call(
        attend_scatter_kernel,
        out_shape=[jax.ShapeDtypeStruct((rows, D), BF), jax.ShapeDtypeStruct((rows, 2 * D), BF)],
        in_specs=[ANY] + [whole_block(v.shape) for v in (held, bias, log_total, grad_mixed)],
        out_specs=[whole_block((rows, D)), whole_block((rows, 2 * D))],
        scratch_shapes=[
            pltpu.VMEM((rows, D), BF),
            pltpu.VMEM(lead + (rows, 2 * D), BF),
            pltpu.VMEM((n_y, n_x, rows, 2 * D), BF),
            pltpu.VMEM((2, rows, 2 * D), BF),
            pltpu.VMEM((rows, 2 * D), BF),
            pltpu.SemaphoreType.DMA((3 * count, 2)),
            pltpu.SemaphoreType.DMA((3 * count, 2)),
            pltpu.SemaphoreType.DMA((1,)),
        ],
        compiler_params=pltpu.CompilerParams(collective_id=3, has_side_effects=True, vmem_limit_bytes=40 << 20),
        name="attend_scatter",
    )(joined, held, bias, log_total, grad_mixed)


def gelu_parts(values):
    size = jnp.abs(values)
    bell = jnp.exp(-0.5 * size * size)
    t = 1.0 / (1.0 + (0.3275911 * 0.7071067811865476) * size)
    tail = t * (0.127414796 + t * (-0.142248368 + t * (0.7107068705 + t * (-0.7265760135 + t * 0.5307027145)))) * bell
    share = jnp.where(values >= 0, 1.0 - tail, tail)
    return values * share, share + values * (0.3989422804014327 * bell)


def norm_parts(values):
    scale = lax.rsqrt(jnp.mean(values * values, -1, keepdims=True) + EPSILON)
    return values * scale, scale


def norm_gradient(values, norm_gain, upstream):
    unit, scale = norm_parts(values)
    inner = upstream * norm_gain
    back = scale * (inner - unit * jnp.mean(inner * unit, -1, keepdims=True))
    return back, jnp.sum(upstream * unit, 0, keepdims=True)


def hidden_block(rows):
    return 2 * D if rows <= 128 else D


def ffn_kernel(stream_ref, gain_ref, in_ref, down_ref, out_ref, inputs_ref, hidden_ref, slope_ref):
    step = pl.program_id(0)

    @pl.when(step == 0)
    def _():
        stream = stream_ref[...].astype(jnp.float32)
        out_ref[...] = stream
        inputs_ref[...] = (norm_parts(stream)[0] * gain_ref[...].astype(jnp.float32)).astype(BF)

    value, slope = gelu_parts(dot(inputs_ref[...], in_ref[...], NN))
    hidden = value.astype(BF)
    hidden_ref[...] = hidden
    slope_ref[...] = slope.astype(BF)
    out_ref[...] += dot(hidden, down_ref[...], NN)


def ffn(stream, norm_gain, weight_in, weight_down):
    rows = stream.shape[0]
    block = hidden_block(rows)
    still = lambda j: (0, 0)
    return pl.pallas_call(
        ffn_kernel,
        grid=(FF // block,),
        out_shape=[
            jax.ShapeDtypeStruct((rows, D), jnp.float32),
            jax.ShapeDtypeStruct((rows, D), BF),
            jax.ShapeDtypeStruct((rows, FF), BF),
            jax.ShapeDtypeStruct((rows, FF), BF),
        ],
        in_specs=[
            pl.BlockSpec((rows, D), still),
            pl.BlockSpec((1, D), still),
            pl.BlockSpec((D, block), lambda j: (0, j)),
            pl.BlockSpec((block, D), lambda j: (j, 0)),
        ],
        out_specs=[
            pl.BlockSpec((rows, D), still),
            pl.BlockSpec((rows, D), still),
            pl.BlockSpec((rows, block), lambda j: (0, j)),
            pl.BlockSpec((rows, block), lambda j: (0, j)),
        ],
        cost_estimate=pl.CostEstimate(
            flops=4 * rows * D * FF, bytes_accessed=4 * D * FF + 4 * rows * FF + 8 * rows * D, transcendentals=rows * FF
        ),
        name="ffn",
    )(stream, norm_gain, weight_in, weight_down)


def ffn_back_kernel(grad_ref, stream_ref, gain_ref, slope_ref, in_ref, down_ref, out_ref, low_ref, pre_ref, gain_out, total):
    step = pl.program_id(0)

    @pl.when(step == 0)
    def _():
        low_ref[...] = grad_ref[...].astype(BF)
        total[...] = jnp.zeros_like(total)

    pre = (dot(low_ref[...], down_ref[...], NT) * slope_ref[...].astype(jnp.float32)).astype(BF)
    pre_ref[...] = pre
    total[...] += dot(pre, in_ref[...], NT)

    @pl.when(step == pl.num_programs(0) - 1)
    def _():
        back, gain = norm_gradient(stream_ref[...].astype(jnp.float32), gain_ref[...].astype(jnp.float32), total[...])
        out_ref[...] = grad_ref[...].astype(jnp.float32) + back
        gain_out[...] = gain


def ffn_back(upstream, stream, norm_gain, slope, weight_in, weight_down):
    rows = stream.shape[0]
    block = hidden_block(rows)
    still = lambda j: (0, 0)
    return pl.pallas_call(
        ffn_back_kernel,
        grid=(FF // block,),
        out_shape=[
            jax.ShapeDtypeStruct((rows, D), jnp.float32),
            jax.ShapeDtypeStruct((rows, D), BF),
            jax.ShapeDtypeStruct((rows, FF), BF),
            jax.ShapeDtypeStruct((1, D), jnp.float32),
        ],
        in_specs=[
            pl.BlockSpec((rows, D), still),
            pl.BlockSpec((rows, D), still),
            pl.BlockSpec((1, D), still),
            pl.BlockSpec((rows, block), lambda j: (0, j)),
            pl.BlockSpec((D, block), lambda j: (0, j)),
            pl.BlockSpec((block, D), lambda j: (j, 0)),
        ],
        out_specs=[
            pl.BlockSpec((rows, D), still),
            pl.BlockSpec((rows, D), still),
            pl.BlockSpec((rows, block), lambda j: (0, j)),
            pl.BlockSpec((1, D), still),
        ],
        scratch_shapes=[pltpu.VMEM((rows, D), jnp.float32)],
        cost_estimate=pl.CostEstimate(
            flops=4 * rows * D * FF, bytes_accessed=4 * D * FF + 4 * rows * FF + 16 * rows * D, transcendentals=0
        ),
        name="ffn_back",
    )(upstream, stream, norm_gain, slope, weight_in, weight_down)


def spread_matrix(devices):
    rows = D // devices
    source = lax.broadcasted_iota(jnp.int32, (D, devices * ROOM), 0)
    target = lax.broadcasted_iota(jnp.int32, (D, devices * ROOM), 1)
    return jnp.where((target // ROOM * rows + target % ROOM == source) & (target % ROOM < rows), 1.0, 0.0).astype(BF)


def late_blocks(late, tall):
    devices = late.shape[0]
    per_block = D // tall
    return [
        pl.BlockSpec((devices, ROOM, D), lambda j: (0, 4 + j, 0)),
        pl.BlockSpec((per_block, 4 * ROOM, D), lambda j: (j, 0, 0)),
    ]


def late_in_block(ref):
    return ref[...].reshape(-1, D)


def late_down_block(ref):
    values = ref[...]
    return values[:, : D // values.shape[0]].reshape(D, D)


def late_ffn_kernel(stream_ref, gain_ref, spread_ref, in_ref, down_ref, out_ref, inputs_ref, hidden_ref, slope_ref, spread):
    step = pl.program_id(0)

    @pl.when(step == 0)
    def _():
        stream = stream_ref[...].astype(jnp.float32)
        out_ref[...] = stream
        inputs = (norm_parts(stream)[0] * gain_ref[...].astype(jnp.float32)).astype(BF)
        inputs_ref[...] = inputs
        spread[...] = dot(inputs, spread_ref[...], NN).astype(BF)

    value, slope = gelu_parts(dot(spread[...], late_in_block(in_ref), NN))
    hidden = value.astype(BF)
    hidden_ref[...] = hidden
    slope_ref[...] = slope.astype(BF)
    out_ref[...] += dot(hidden, late_down_block(down_ref), NN)


def late_ffn(stream, norm_gain, spread, late, tall):
    rows = stream.shape[0]
    still = lambda j: (0, 0)
    return pl.pallas_call(
        late_ffn_kernel,
        grid=(FF // D,),
        out_shape=[
            jax.ShapeDtypeStruct((rows, D), jnp.float32),
            jax.ShapeDtypeStruct((rows, D), BF),
            jax.ShapeDtypeStruct((rows, FF), BF),
            jax.ShapeDtypeStruct((rows, FF), BF),
        ],
        in_specs=[pl.BlockSpec((rows, D), still), pl.BlockSpec((1, D), still), pl.BlockSpec(spread.shape, still)]
        + late_blocks(late, tall),
        out_specs=[
            pl.BlockSpec((rows, D), still),
            pl.BlockSpec((rows, D), still),
            pl.BlockSpec((rows, D), lambda j: (0, j)),
            pl.BlockSpec((rows, D), lambda j: (0, j)),
        ],
        scratch_shapes=[pltpu.VMEM((rows, spread.shape[1]), BF)],
        cost_estimate=pl.CostEstimate(flops=4 * rows * D * FF, bytes_accessed=5 * D * FF, transcendentals=rows * FF),
        name="late_ffn",
    )(stream, norm_gain, spread, late, late)


def late_back_kernel(grad_ref, stream_ref, gain_ref, spread_ref, slope_ref, in_ref, down_ref, out_ref, low_ref, pre_ref, gain_out, total):
    step = pl.program_id(0)

    @pl.when(step == 0)
    def _():
        low_ref[...] = grad_ref[...].astype(BF)
        total[...] = jnp.zeros_like(total)

    pre = (dot(low_ref[...], late_down_block(down_ref), NT) * slope_ref[...].astype(jnp.float32)).astype(BF)
    pre_ref[...] = pre
    total[...] += dot(pre, late_in_block(in_ref), NT)

    @pl.when(step == pl.num_programs(0) - 1)
    def _():
        whole = total[...]
        high = whole.astype(BF)
        rest = (whole - high.astype(jnp.float32)).astype(BF)
        inner = dot(high, spread_ref[...], NT) + dot(rest, spread_ref[...], NT)
        back, gain = norm_gradient(stream_ref[...].astype(jnp.float32), gain_ref[...].astype(jnp.float32), inner)
        out_ref[...] = grad_ref[...].astype(jnp.float32) + back
        gain_out[...] = gain


def late_ffn_back(upstream, stream, norm_gain, slope, spread, late, tall):
    rows = stream.shape[0]
    still = lambda j: (0, 0)
    return pl.pallas_call(
        late_back_kernel,
        grid=(FF // D,),
        out_shape=[
            jax.ShapeDtypeStruct((rows, D), jnp.float32),
            jax.ShapeDtypeStruct((rows, D), BF),
            jax.ShapeDtypeStruct((rows, FF), BF),
            jax.ShapeDtypeStruct((1, D), jnp.float32),
        ],
        in_specs=[
            pl.BlockSpec((rows, D), still),
            pl.BlockSpec((rows, D), still),
            pl.BlockSpec((1, D), still),
            pl.BlockSpec(spread.shape, still),
            pl.BlockSpec((rows, D), lambda j: (0, j)),
        ]
        + late_blocks(late, tall),
        out_specs=[
            pl.BlockSpec((rows, D), still),
            pl.BlockSpec((rows, D), still),
            pl.BlockSpec((rows, D), lambda j: (0, j)),
            pl.BlockSpec((1, D), still),
        ],
        scratch_shapes=[pltpu.VMEM((rows, spread.shape[1]), jnp.float32)],
        cost_estimate=pl.CostEstimate(flops=4 * rows * D * FF, bytes_accessed=5 * D * FF, transcendentals=0),
        name="late_ffn_back",
    )(upstream, stream, norm_gain, spread, slope, late, late)


def shifted(x, axis, by):
    count = lax.axis_size(axis)
    pairs = [(i, i + by) for i in range(count) if 0 <= i + by < count]
    return lax.ppermute(x, axis, pairs)


def slab_term(left, right):
    return dot(left, right, TN)


def normed(values, norm_gain):
    return (norm_parts(values)[0] * norm_gain.astype(jnp.float32)).astype(BF)


def norm_back(values, norm_gain, upstream):
    return norm_gradient(values, norm_gain.astype(jnp.float32), upstream)


def self_forward(stream, norm_gain, weight_qkv, weight_out, bias):
    inputs = normed(stream, norm_gain)
    joined = dot(inputs, weight_qkv, NN).astype(BF)
    if grid_sizes() == (4, 2, 2, 2):
        mixed, log_total, keys_vals = attend_gather(joined, bias)
    else:
        keys_vals = lax.all_gather(joined[:, D:], "seq", axis=0, tiled=True)
        mixed, log_total = attend(joined, keys_vals, bias)
    return stream + dot(mixed, weight_out, NN), (stream, inputs, joined, keys_vals, log_total, mixed)


def self_back(stored, norm_gain, weight_qkv, weight_out, bias, upstream, covered):
    stream, inputs, joined, keys_vals, log_total, mixed = stored
    grad_low = upstream.astype(BF)
    grad_mixed = dot(grad_low, weight_out, NT).astype(BF)
    if grid_sizes() == (4, 2, 2, 2) and not covered:
        grad_queries, own_pairs = attend_scatter(joined, keys_vals, bias, log_total, grad_mixed)
    else:
        grad_queries, grad_pairs = attend_back(joined, keys_vals, bias, log_total, grad_mixed)
        own_pairs = lax.psum_scatter(grad_pairs, "seq", scatter_dimension=0, tiled=True)
    grad_joined = jnp.concatenate([grad_queries, own_pairs], -1)
    back, gain_grad = norm_back(stream, norm_gain, dot(grad_joined, weight_qkv, NT))
    return upstream + back, gain_grad, ((inputs, grad_joined), (mixed, grad_low))


def causal_bias(queries, keys):
    offset = lax.axis_index("seq") * queries
    key_place = lax.broadcasted_iota(jnp.int32, (keys, queries), 0)
    query_place = offset + lax.broadcasted_iota(jnp.int32, (keys, queries), 1)
    return jnp.where(key_place <= query_place, 0.0, MASKED_SCORE).astype(jnp.float32)


def span_bias(prior_flag, queries):
    spans = prior_flag.shape[0]
    keys = spans * NEIGH * RET
    key_span = lax.broadcasted_iota(jnp.int32, (keys, queries), 0) // (NEIGH * RET)
    query_span = lax.broadcasted_iota(jnp.int32, (keys, queries), 1) // SPAN
    allowed = jnp.repeat(prior_flag.reshape(-1), RET)[:, None] > 0.5
    return jnp.where(key_span == query_span, jnp.where(allowed, 0.0, MASKED_SCORE), 2 * MASKED_SCORE).astype(jnp.float32)


def row_gate(prior_flag):
    return jnp.repeat(jnp.max(prior_flag, -1).astype(jnp.float32), SPAN)[:, None]


def prior_spans(encoded, keep_flag):
    last_enc, last_flag = shifted((encoded[-1:], keep_flag[-1:]), "seq", 1)
    return jnp.concatenate([last_enc, encoded[:-1]], 0), jnp.concatenate([last_flag, keep_flag[:-1]], 0)


def cross_forward(stream, encoded, keep_flag, norm_gain, weight_q, weight_kv, weight_out):
    prior_enc, prior_flag = prior_spans(encoded, keep_flag)
    prior_enc = prior_enc.reshape(-1, D)
    inputs = normed(stream, norm_gain)
    queries = dot(inputs, weight_q, NN).astype(BF)
    keys_vals = jnp.concatenate([dot(prior_enc, side, NN).astype(BF) for side in weight_kv], 1)
    bias = span_bias(prior_flag, stream.shape[0])
    mixed, log_total = attend(queries, keys_vals, bias)
    branch = row_gate(prior_flag) * dot(mixed, weight_out, NN)
    return stream + branch, (stream, inputs, prior_enc, prior_flag, queries, keys_vals, bias, log_total, mixed)


def cross_back(stored, norm_gain, weight_q, weight_kv, weight_out, upstream):
    stream, inputs, prior_enc, prior_flag, queries, keys_vals, bias, log_total, mixed = stored
    grad_low = (upstream * row_gate(prior_flag)).astype(BF)
    grad_mixed = dot(grad_low, weight_out, NT).astype(BF)
    grad_queries, grad_pairs = attend_back(queries, keys_vals, bias, log_total, grad_mixed)
    grad_prior = dot(grad_pairs[:, :D], weight_kv[0], NT) + dot(grad_pairs[:, D:], weight_kv[1], NT)
    grad_prior = grad_prior.reshape(prior_flag.shape[0], NEIGH * RET, D)
    from_next = shifted(grad_prior[:1].astype(BF), "seq", -1).astype(jnp.float32)
    encoded_grad = jnp.concatenate([grad_prior[1:], from_next], 0).reshape(-1, D)
    back, gain_grad = norm_back(stream, norm_gain, dot(grad_queries, weight_q, NT))
    pairs = ((inputs, grad_queries), (prior_enc, grad_pairs), (mixed, grad_low))
    return upstream + back, gain_grad, pairs, encoded_grad


def on_device(
    tokens,
    retrieved,
    span_doc,
    neigh_doc,
    cotangent,
    dec_gain,
    dec_qkv,
    dec_out,
    dec_in,
    dec_down,
    cca_gain,
    cca_q,
    cca_kv,
    cca_out,
    enc_gain,
    enc_in,
    enc_down,
    enc_final,
):
    assert tokens.shape[0] == 1
    rows = cca_q.shape[0]
    own_gains = jnp.concatenate([dec_gain.reshape(4, rows), cca_gain[None], enc_gain, enc_final[None]], 0).T
    own_gains = jnp.pad(own_gains, ((0, 0), (0, 120)))
    neighbours = retrieved.reshape(-1, D)
    full = gather_weights(
        neighbours, enc_in, enc_down, dec_qkv, dec_out, dec_in, dec_down, cca_q, cca_kv, cca_out, own_gains
    )
    gains = full["gains"].T
    attn_gain, ffn_gain = (gains[0:1], gains[2:3]), (gains[1:2], gains[3:4])
    cross_gain, encode_gain, final_gain = gains[4:5], (gains[5:6], gains[6:7]), gains[7:8]
    cross_weights = (cross_gain, full["cca_q"], full["cca_kv"], full["cca_out"])
    queries = tokens.shape[1]
    bias = causal_bias(queries, queries * lax.axis_size("seq"))

    encoder, encoder_kept, encoded = full["encoder"]
    encoded = encoded.reshape(span_doc.shape[1], NEIGH * RET, D)
    keep_flag = (neigh_doc[0] != span_doc[0][:, None]).astype(BF)

    stream = tokens[0].astype(jnp.float32)
    attn_kept, ffn_kept = [], []
    for layer in range(DEC_LAYERS):
        stream, kept = self_forward(stream, attn_gain[layer], full["dec_qkv"][layer], full["dec_out"][layer], bias)
        attn_kept.append(kept)
        if layer == 0:
            stream, cross_kept = cross_forward(stream, encoded, keep_flag, *cross_weights)
        before = stream
        if full["dec_in"][layer] is None:
            late, tall = full["dec_down"][layer], dec_down.shape[1]
            spread = spread_matrix(late.shape[0])
            stream, inputs, hidden, slope = late_ffn(before, ffn_gain[layer], spread, late, tall)
        else:
            stream, inputs, hidden, slope = ffn(before, ffn_gain[layer], full["dec_in"][layer], full["dec_down"][layer])
        ffn_kept.append((before, inputs, hidden, slope))
    result = stream.astype(BF)

    upstream = cotangent[0].astype(jnp.float32)
    attn_gain_g, ffn_gain_g = [None] * DEC_LAYERS, [None] * DEC_LAYERS
    attn_pairs, ffn_pairs = [None] * DEC_LAYERS, [None] * DEC_LAYERS
    for layer in reversed(range(DEC_LAYERS)):
        before, inputs, hidden, slope = ffn_kept[layer]
        if full["dec_in"][layer] is None:
            back = late_ffn_back(upstream, before, ffn_gain[layer], slope, spread, late, tall)
        else:
            back = ffn_back(upstream, before, ffn_gain[layer], slope, full["dec_in"][layer], full["dec_down"][layer])
        upstream, grad_low, grad_pre, ffn_gain_g[layer] = back
        ffn_pairs[layer] = ((inputs, grad_pre), (grad_low, hidden))
        if layer == 0:
            upstream, cross_gain_g, cross_pairs, encoded_grad = cross_back(cross_kept, *cross_weights, upstream)
        upstream, attn_gain_g[layer], attn_pairs[layer] = self_back(
            attn_kept[layer], attn_gain[layer], full["dec_qkv"][layer], full["dec_out"][layer], bias, upstream, layer == 0
        )

    enc_upstream, final_gain_g = norm_back(encoder, final_gain, encoded_grad)
    enc_gain_g, enc_pairs = [None] * ENC_LAYERS, [None] * ENC_LAYERS
    for layer in reversed(range(ENC_LAYERS)):
        before, inputs, hidden, slope = encoder_kept[layer]
        enc_upstream, grad_low, grad_pre, enc_gain_g[layer] = ffn_back(
            enc_upstream, before, encode_gain[layer], slope, full["enc_in"][layer], full["enc_down"][layer]
        )
        enc_pairs[layer] = ((inputs, grad_pre), (grad_low, hidden))

    pair_list = []
    for layer in range(DEC_LAYERS):
        pair_list += list(attn_pairs[layer]) + list(ffn_pairs[layer])
    pair_list += list(cross_pairs)
    for layer in range(ENC_LAYERS):
        pair_list += list(enc_pairs[layer])
    gain_list = []
    for layer in range(DEC_LAYERS):
        gain_list += [attn_gain_g[layer], ffn_gain_g[layer]]
    gain_list = [gain.reshape(D) for gain in gain_list + [cross_gain_g] + enc_gain_g + [final_gain_g]]

    grads = sum_gradients(pair_list, gain_list, rows)
    (enc_in_g, enc_down_g, dec_qkv_g, dec_out_g, dec_in_g, dec_down_g, cross_q_g, cross_kv_g, cross_out_g, gain_cols) = grads
    gain_rows = gain_cols[:, :8].T
    return (
        result[None],
        upstream[None],
        gain_rows[:4].reshape(2, 2, rows),
        dec_qkv_g,
        dec_out_g,
        dec_in_g,
        jnp.swapaxes(dec_down_g, 1, 2),
        gain_rows[4],
        cross_q_g,
        cross_kv_g,
        cross_out_g,
        gain_rows[5:7],
        enc_in_g,
        jnp.swapaxes(enc_down_g, 1, 2),
        gain_rows[7],
    )


def sum_plainly(pair_list, gain_list):
    blocks = [slab_term(left, right) for left, right in pair_list] + [vector[:, None] for vector in gain_list]
    owned = lax.psum_scatter(
        jnp.concatenate(blocks, 1).astype(BF), ("dp", "seq"), scatter_dimension=0, tiled=True
    ).astype(jnp.float32)
    pieces, cursor = [], 0
    for _, right in pair_list:
        pieces.append(owned[:, cursor : cursor + right.shape[-1]])
        cursor += right.shape[-1]
    two = lambda first, second: jnp.stack([pieces[first], pieces[second]])
    return [
        two(11, 13), two(12, 14), two(0, 4), two(1, 5), two(2, 6), two(3, 7), pieces[8], pieces[9], pieces[10], owned[:, cursor:]
    ]


def sum_gradients(pair_list, gain_list, rows):
    sizes = grid_sizes()
    if rows % 4 or sizes != (4, 2, 2, 2):
        return sum_plainly(pair_list, gain_list)
    operands = [x.reshape(-1, x.shape[-1]) for pair in pair_list for x in pair]
    gains = jnp.pad(jnp.stack(gain_list).astype(BF).T, ((0, 0), (0, 128 - len(gain_list))))
    return reduce_gradients(operands, gains, rows)


def solution(mesh):
    return jax.shard_map(
        on_device,
        mesh=mesh,
        in_specs=(
            P("dp", "seq", None),
            P("dp", "seq", None, None, None),
            P("dp", "seq"),
            P("dp", "seq", None),
            P("dp", "seq", None),
            P(None, None, ("dp", "seq")),
            P(None, ("dp", "seq"), None),
            P(None, ("dp", "seq"), None),
            P(None, ("dp", "seq"), None),
            P(None, ("dp", "seq"), None),
            P(("dp", "seq")),
            P(("dp", "seq"), None),
            P(("dp", "seq"), None),
            P(("dp", "seq"), None),
            P(None, ("dp", "seq")),
            P(None, ("dp", "seq"), None),
            P(None, ("dp", "seq"), None),
            P(("dp", "seq")),
        ),
        out_specs=(
            P("dp", "seq", None),
            P("dp", "seq", None),
            P(None, None, ("dp", "seq")),
            P(None, ("dp", "seq"), None),
            P(None, ("dp", "seq"), None),
            P(None, ("dp", "seq"), None),
            P(None, None, ("dp", "seq")),
            P(("dp", "seq")),
            P(("dp", "seq"), None),
            P(("dp", "seq"), None),
            P(("dp", "seq"), None),
            P(None, ("dp", "seq")),
            P(None, ("dp", "seq"), None),
            P(None, None, ("dp", "seq")),
            P(("dp", "seq")),
        ),
        check_vma=False,
    )
```

```python
import functools
import heapq
import jax
import jax.numpy as jnp
from jax import lax
from jax.experimental import pallas as pl
from jax.experimental.pallas import tpu as pltpu
from jax.sharding import PartitionSpec as P

D = 896
FF = 3584
HEADS = 14
HEAD = 64
SPAN = 64
NEIGH = 2
RET = 128
ENC_LAYERS = 2
DEC_LAYERS = 2
EPSILON = 1e-06
SCORE_SCALE = 0.125
MASKED_SCORE = -1000000000.0
BF = jnp.bfloat16
MESH_ID = pl.DeviceIdType.MESH
ANY = pl.BlockSpec(memory_space=pl.ANY)


def grid_sizes():
    return (lax.axis_size("dp"), lax.axis_size("seq") // 4, 2, 2)


def grid_place():
    seq = lax.axis_index("seq")
    return (lax.axis_index("dp"), seq // 4, (seq // 2) % 2, seq % 2)


def device_at(place):
    z, y, x, core = place
    return (z, (y * 2 + x) * 2 + core)


def moved(place, sizes, axis, by):
    size = sizes[axis]
    there = lax.rem(place[axis] + (by % size), size)
    return place[:axis] + (there,) + place[axis + 1 :]


def greet(place, sizes):
    barrier = pltpu.get_barrier_semaphore()
    for axis in range(4):
        size, here = sizes[axis], place[axis]
        for by in (1, -1):
            there = here + by

            @pl.when(inside(there, size))
            def _():
                other = place[:axis] + (jnp.clip(there, 0, size - 1),) + place[axis + 1 :]
                pl.semaphore_signal(barrier, inc=1, device_id=device_at(other), device_id_type=MESH_ID)

    count = 0
    for axis in range(4):
        for by in (1, -1):
            count = count + inside(place[axis] + by, sizes[axis]).astype(jnp.int32)
    pl.semaphore_wait(barrier, count)


class Hop:
    def __init__(self, copy, sends, receives):
        self.copy, self.sends, self.receives = copy, sends, receives

    def start(self):
        pl.when(self.sends)(self.copy[0].start)

    def wait(self):
        pl.when(self.sends)(self.copy[0].wait_send)
        pl.when(self.receives)(self.copy[1].wait_recv)


def inside(place, size):
    return jnp.logical_and(place >= 0, place < size)


ZYX, ZXY, YZX, XZY, YXZ, XYZ = (0, 1, 2), (0, 2, 1), (1, 0, 2), (2, 0, 1), (1, 2, 0), (2, 1, 0)
ROUTES = (YXZ, ZYX, ZXY, ZYX, ZXY, ZXY, YZX, ZXY, ZYX, ZYX)
ROUTES += (ZXY, XZY, ZYX, YZX, XZY, XZY, YZX, YXZ, XYZ)
UNIT_US, HOP_US, CORE_US = 2.2, 2.5, 0.17


def schedule(pieces, routes, sizes):
    chains = []
    for number, piece in enumerate(pieces):
        scale, held, chain = piece[3] / PIECE, 1, []
        for axis in routes[number]:
            chain += [(axis, held * UNIT_US * scale)] * (sizes[axis] - 1)
            held *= sizes[axis]
        chains.append(chain + [(3, held * CORE_US * scale)])
    free, flying, ready = [0.0] * 4, [0] * 4, [[] for _ in range(4)]
    for number, chain in enumerate(chains):
        heapq.heappush(ready[chain[0][0]], (number, number, 0))
    now, events, order = 0.0, [], []
    while True:
        for link in range(4):
            while ready[link] and flying[link] < 2:
                _, number, step = heapq.heappop(ready[link])
                free[link] = max(free[link], now) + chains[number][step][1]
                flying[link] += 1
                order.append(("start", number, step, now))
                heapq.heappush(events, (free[link] + HOP_US, number, step, link))
        if not events:
            return order
        now, number, step, link = heapq.heappop(events)
        flying[link] -= 1
        order.append(("wait", number, step, now))
        if step + 1 < len(chains[number]):
            heapq.heappush(ready[chains[number][step + 1][0]], (number, number, step + 1))


PIECE = 896


def narrow_groups():
    qkv = 3 * D
    wide = FF // 2
    whole = lambda arg, layer: [[(arg, layer, 0, wide)], [(arg, layer, wide, wide)]]
    return [
        whole(0, 0),
        whole(0, 1),
        [
            [(7, None, 0, D), (6, None, 0, D), (2, 0, 0, qkv), (3, 0, 0, D)],
            [(7, None, D, D), (8, None, 0, D), (2, 1, 0, qkv), (3, 1, 0, D)],
        ],
        whole(4, 0),
        [[(9, None, 0, 128)], [(9, None, 0, 128)]],
    ]


def half_width(group):
    return sum(part[3] for part in group[0])


def gather_plan():
    groups = narrow_groups()
    starts, cursor = [], 0
    for group in groups:
        starts.append(cursor)
        cursor += half_width(group)
    pieces = []
    for kind, number in (("n", 4), ("n", 0), ("r", 0), ("n", 1), ("r", 1), ("n", 2), ("n", 3), ("r", 2)):
        if kind == "n":
            width = half_width(groups[number])
            for first in range(0, width, PIECE):
                pieces.append((kind, number, first, min(PIECE, width - first)))
        else:
            pieces.append((kind, number, 0, D))
            pieces.append((kind, number, 1, D))
    return groups, starts, cursor, pieces


N_GROUPS = 5
N_TALL = 3


def gather_kernel(sizes, *refs):
    groups, starts, _, pieces = gather_plan()
    ins, neighbours = refs[:10], refs[10]
    n_outs = N_GROUPS + N_TALL
    outs, encoder_outs, late_out = refs[11 : 11 + n_outs], refs[11 + n_outs : 20 + n_outs], refs[20 + n_outs]
    halves, other, joined, own_rows, send_sem, recv_sem, load_sem, swap_sem = refs[21 + n_outs : 29 + n_outs]
    late_in, late_down, late, late_sem = refs[29 + n_outs : 33 + n_outs]
    encoder_rooms = refs[33 + n_outs :]
    place = grid_place()
    z, y, x, core = place
    sibling = device_at(moved(place, sizes, 3, 1))
    loads = []
    for number, group in enumerate(groups):
        for half in range(2):
            cursor = starts[number]
            for arg, layer, first, size in group[half]:
                source = ins[arg] if layer is None else ins[arg].at[layer]
                loads.append((source.at[:, pl.ds(first, size)], halves.at[half, :, pl.ds(cursor, size)]))
                cursor += size
    for number, (arg, layer) in enumerate(((1, 0), (1, 1), (5, 0))):
        for part in range(2):
            loads.append((ins[arg].at[layer, part], own_rows.at[2 * number + part]))
    late_loads = [
        pltpu.make_async_copy(ins[4].at[1], late_in, late_sem.at[0]),
        pltpu.make_async_copy(ins[5].at[1], late_down, late_sem.at[1]),
    ]
    late_store = pltpu.make_async_copy(late, late_out, late_sem.at[2])

    def late_unit():
        for copy in late_loads:
            copy.wait()
        down = late_down[...].astype(jnp.float32).reshape(-1, D)
        fill = jnp.zeros((4 * ROOM - down.shape[0], D), jnp.float32)
        late[pl.ds(0, 4 * ROOM), :] = jnp.concatenate([down, fill], 0).astype(BF)
        fill = jnp.zeros((ROOM - late_in.shape[0], D), jnp.float32)
        for k in range(FF // D):
            rows = late_in[:, pl.ds(k * D, D)].astype(jnp.float32)
            late[pl.ds((4 + k) * ROOM, ROOM), :] = jnp.concatenate([rows, fill], 0).astype(BF)
        late_store.start()

    started = []
    for copy in late_loads:
        copy.start()
    for k, (source, target) in enumerate(loads):
        copy = pltpu.make_async_copy(source, target, load_sem.at[k])
        copy.start()
        started.append(copy)
    greet(place, sizes)
    for copy in started:
        copy.wait()
    placed = []
    for number in range(N_TALL):
        for part in range(2):
            k = 2 * number + part
            target = outs[N_GROUPS + number].at[z, y, x, core, part]
            placed.append(pltpu.make_async_copy(own_rows.at[k], target, load_sem.at[len(loads) + len(groups) + k]))
            placed[-1].start()
    swaps = []
    for number, group in enumerate(groups):
        columns = pl.ds(starts[number], half_width(group))
        copy = pltpu.make_async_remote_copy(
            src_ref=halves.at[1 - core, :, columns],
            dst_ref=other.at[:, columns],
            send_sem=swap_sem.at[0, number],
            recv_sem=swap_sem.at[1, number],
            device_id=sibling,
            device_id_type=MESH_ID,
        )
        copy.start()
        swaps.append(copy)

    def view(piece, where):
        kind, number, first, size = piece
        iz, iy, ix = where[:3]
        if kind == "n":
            start = pl.multiple_of(core * half_width(groups[number]) + first, 128)
            return outs[number].at[iz, iy, ix, :, pl.ds(start, size)]
        return outs[N_GROUPS + number].at[iz, iy, ix, core, first]

    prepared = {}

    def prepare(piece):
        kind, number, first, size = piece
        if kind == "n" and number not in prepared:
            swaps[number].wait()
            group = groups[number]
            for begin in range(starts[number], starts[number] + half_width(group), 128):
                columns = pl.ds(begin, 128)
                mine = halves[core, :, columns].astype(jnp.float32)
                theirs = other[:, columns].astype(jnp.float32)
                both = [jnp.where(core == 0, mine, theirs), jnp.where(core == 0, theirs, mine)]
                joined[:, columns] = jnp.concatenate(both, 0).astype(BF)
            width = half_width(group)
            copy = pltpu.make_async_copy(
                joined.at[:, pl.ds(starts[number], width)],
                outs[number].at[z, y, x, :, pl.ds(pl.multiple_of(core * width, 128), width)],
                load_sem.at[len(loads) + number],
            )
            copy.start()
            copy.wait()
            prepared[number] = True
        elif kind == "r" and "r" not in prepared:
            for copy in placed:
                copy.wait()
            prepared["r"] = True

    semaphores = [0]

    def transfers(number):
        piece = pieces[number]
        steps, done = [], []
        for axis in routes[number] + (3,):
            size, here = sizes[axis], place[axis]

            def block(at):
                where = list(place)
                for old in done:
                    where[old] = slice(None)
                where[axis] = jnp.clip(at, 0, size - 1)
                return view(piece, where)

            for hop in range(1, size):
                hops = []
                for way in (1, -1):
                    ahead, behind = here + way, here - way
                    sent, got = here - way * (hop - 1), here - way * hop
                    if size == 2 and way == -1:
                        continue
                    if size == 2:
                        ahead, behind, got = 1 - here, 1 - here, 1 - here
                    pair = []
                    for at, other_end in ((sent, ahead), (got, behind)):
                        ref = block(at)
                        target = place[:axis] + (jnp.clip(other_end, 0, size - 1),) + place[axis + 1 :]
                        pair.append(
                            pltpu.make_async_remote_copy(
                                src_ref=ref,
                                dst_ref=ref,
                                send_sem=send_sem.at[semaphores[0]],
                                recv_sem=recv_sem.at[semaphores[0]],
                                device_id=device_at(target),
                                device_id_type=MESH_ID,
                            )
                        )
                    semaphores[0] += 1
                    sends = jnp.logical_and(inside(sent, size), inside(ahead, size))
                    hops.append(Hop(pair, sends, inside(got, size)))
                steps.append(hops)
            done.append(axis)
        return steps

    routes = [ROUTES[number % len(ROUTES)] for number in range(len(pieces))]
    running = [transfers(number) for number in range(len(pieces))]
    units = encoder_units(
        neighbours, outs[N_GROUPS - 1], (outs[0], outs[1]), (outs[N_GROUPS], outs[N_GROUPS + 1]), encoder_outs, encoder_rooms
    )
    units.insert(0, late_unit)
    needs = [{k for k, piece in enumerate(pieces) if piece[:2] in wanted} for wanted in [set()] + UNIT_NEEDS]
    due, arrived = 0.0, set()
    for what, number, step, time in schedule(pieces, routes, sizes):
        if what == "wait":
            for copy in running[number][step]:
                copy.wait()
            if step + 1 == len(running[number]):
                arrived.add(number)
        else:
            prepare(pieces[number])
            for copy in running[number][step]:
                copy.start()
        if units and time >= due and needs[len(needs) - len(units)] <= arrived:
            units.pop(0)()
            due = time + UNIT_TIME
    for unit in units:
        unit()
    late_store.wait()


ROOM = 32


HIDDEN_UNITS = 4
UNIT_TIME = 7.0
GAINS, FIRST, SECOND = {("n", 4)}, {("n", 0), ("r", 0)}, {("n", 1), ("r", 1)}
UNIT_NEEDS = [GAINS | FIRST] * (1 + HIDDEN_UNITS) + [SECOND] * (1 + HIDDEN_UNITS) + [set()]


def encoder_units(neighbours, gain_columns, weights_in, weights_down, outs, rooms):
    after, inputs_out, hidden_out, slope_out, encoded_out = outs[0:2], outs[2:4], outs[4:6], outs[6:8], outs[8]
    stream, inputs, columns, gain_rows, block_in, block_down, hidden, slope, sems = rooms
    block = FF // HIDDEN_UNITS

    def flat(values, rows):
        return values.astype(jnp.float32).reshape(rows, values.shape[-1])

    def weights(layer, k):
        slot = k % 2
        return [
            pltpu.make_async_copy(weights_in[layer].at[:, :, :, :, pl.ds(k * block, block)], block_in.at[slot], sems.at[0, slot]),
            pltpu.make_async_copy(weights_down[layer].at[k], block_down.at[slot], sems.at[1, slot]),
        ]

    def results(layer, k):
        slot = k % 2
        place = pl.ds(k * block, block)
        return [
            pltpu.make_async_copy(hidden.at[slot], hidden_out[layer].at[:, place], sems.at[2, slot]),
            pltpu.make_async_copy(slope.at[slot], slope_out[layer].at[:, place], sems.at[3, slot]),
        ]

    def stream_copy(layer):
        return pltpu.make_async_copy(stream, after[layer], sems.at[4, layer])

    def inputs_copy(layer):
        return pltpu.make_async_copy(inputs, (*inputs_out, encoded_out)[layer], sems.at[5, layer % 2])

    def norm_unit(layer):
        if layer == 0:
            first = pltpu.make_async_copy(neighbours, inputs, sems.at[6, 0])
            second = pltpu.make_async_copy(gain_columns.at[:, :, :, :, pl.ds(0, 128)], columns, sems.at[6, 1])
            first.start()
            second.start()
            first.wait()
            second.wait()
            gain_rows[...] = flat(columns[...], D).T
            stream[...] = inputs[...].astype(jnp.float32)
        else:
            for k in (HIDDEN_UNITS - 2, HIDDEN_UNITS - 1):
                for copy in results(layer - 1, k):
                    copy.wait()
            inputs_copy(layer - 1).wait()
            stream_copy(layer - 1).start()
        if layer < ENC_LAYERS:
            for copy in weights(layer, 0):
                copy.start()
        gain = gain_rows[5 + layer : 6 + layer, :]
        inputs[...] = (norm_parts(stream[...])[0] * gain).astype(BF)
        inputs_copy(layer).start()
        if layer == ENC_LAYERS:
            stream_copy(layer - 1).wait()
            inputs_copy(layer).wait()

    def hidden_unit(layer, k):
        slot = k % 2
        if k + 1 < HIDDEN_UNITS:
            for copy in weights(layer, k + 1):
                copy.start()
        for copy in weights(layer, k):
            copy.wait()
        if k >= 2:
            for copy in results(layer, k - 2):
                copy.wait()
        value, rate = gelu_parts(dot(inputs[...], flat(block_in[slot], D).astype(BF), NN))
        hidden[slot] = value.astype(BF)
        slope[slot] = rate.astype(BF)
        for copy in results(layer, k):
            copy.start()
        if k == 0 and layer > 0:
            stream_copy(layer - 1).wait()
        stream[...] += dot(hidden[slot], flat(block_down[slot], block).astype(BF), NN)

    units = []
    for layer in range(ENC_LAYERS):
        units.append(functools.partial(norm_unit, layer))
        for k in range(HIDDEN_UNITS):
            units.append(functools.partial(hidden_unit, layer, k))
    units.append(functools.partial(norm_unit, ENC_LAYERS))
    return units


def gather_plainly(neighbours, enc_in, enc_down, dec_qkv, dec_out, dec_in, dec_down, cca_q, cca_kv, cca_out, gains):
    get = lambda w: lax.all_gather(w, ("dp", "seq"), axis=w.ndim - 2, tiled=True)
    kv = get(cca_kv)
    enc_in, enc_down, columns = get(enc_in), get(enc_down), get(gains)[:, :8]
    stream, kept = neighbours, []
    for layer in range(ENC_LAYERS):
        gain = columns[:, 5 + layer][None]
        after, inputs, hidden, slope = ffn(stream, gain, enc_in[layer], enc_down[layer])
        kept.append((stream, inputs, hidden, slope))
        stream = after
    return dict(
        encoder=(stream, kept, normed(stream, columns[:, 7][None])),
        enc_in=enc_in, enc_down=enc_down, dec_in=get(dec_in), dec_down=get(dec_down), dec_qkv=get(dec_qkv),
        dec_out=get(dec_out), cca_kv=[kv[:, :D], kv[:, D:]], cca_q=get(cca_q), cca_out=get(cca_out), gains=columns,
    )


def gather_weights(neighbours, enc_in, enc_down, dec_qkv, dec_out, dec_in, dec_down, cca_q, cca_kv, cca_out, gains):
    sizes = grid_sizes()
    rows = cca_q.shape[0]
    groups, starts, total, pieces = gather_plan()
    part = enc_down.shape[1] // 2
    if rows % 4 or part % 8 or sizes != (HIDDEN_UNITS, 2, 2, 2):
        return gather_plainly(neighbours, enc_in, enc_down, dec_qkv, dec_out, dec_in, dec_down, cca_q, cca_kv, cca_out, gains)
    lead = sizes[:3]
    shapes = [lead + (2 * rows, 2 * half_width(group)) for group in groups] + [lead + (2, 2, part, D)] * N_TALL
    out_shape = [jax.ShapeDtypeStruct(shape, BF) for shape in shapes]
    count = neighbours.shape[0]
    block = FF // HIDDEN_UNITS
    out_shape += [jax.ShapeDtypeStruct((count, D), jnp.float32)] * 2 + [jax.ShapeDtypeStruct((count, D), BF)] * 2
    out_shape += [jax.ShapeDtypeStruct((count, FF), BF)] * 4 + [jax.ShapeDtypeStruct((count, D), BF)]
    out_shape += [jax.ShapeDtypeStruct((8 * ROOM, D), BF)]
    per_piece = sum((size - 1) * (1 if size == 2 else 2) for size in sizes)
    n_loads = sum(len(half) for group in groups for half in group) + 4 * N_TALL + len(groups)
    split = lambda w: w.reshape(w.shape[0], 2, part, D)
    outs = pl.pallas_call(
        functools.partial(gather_kernel, sizes),
        out_shape=out_shape,
        in_specs=[ANY] * 11,
        out_specs=[ANY] * len(out_shape),
        scratch_shapes=[
            pltpu.VMEM((2, rows, total), BF),
            pltpu.VMEM((rows, total), BF),
            pltpu.VMEM((2 * rows, total), BF),
            pltpu.VMEM((2 * N_TALL, part, D), BF),
            pltpu.SemaphoreType.DMA((per_piece * len(pieces),)),
            pltpu.SemaphoreType.DMA((per_piece * len(pieces),)),
            pltpu.SemaphoreType.DMA((n_loads,)),
            pltpu.SemaphoreType.DMA((2, len(groups))),
            pltpu.VMEM((rows, FF), BF),
            pltpu.VMEM((2, part, D), BF),
            pltpu.VMEM((8 * ROOM, D), BF),
            pltpu.SemaphoreType.DMA((3,)),
            pltpu.VMEM((count, D), jnp.float32),
            pltpu.VMEM((count, D), BF),
            pltpu.VMEM(lead + (2 * rows, 128), BF),
            pltpu.VMEM((128, D), jnp.float32),
            pltpu.VMEM((2,) + lead + (2 * rows, block), BF),
            pltpu.VMEM((2,) + sizes[1:3] + (2, 2, part, D), BF),
            pltpu.VMEM((2, count, block), BF),
            pltpu.VMEM((2, count, block), BF),
            pltpu.SemaphoreType.DMA((7, 2)),
        ],
        compiler_params=pltpu.CompilerParams(collective_id=0, has_side_effects=True, vmem_limit_bytes=56 << 20),
        name="gather_weights",
    )(enc_in, split(enc_down), dec_qkv, dec_out, dec_in, split(dec_down), cca_q, cca_kv, cca_out, gains, neighbours)
    narrow = [out.reshape(D, out.shape[-1]) for out in outs[:N_GROUPS]]
    tall = [out.reshape(FF, D) for out in outs[N_GROUPS : N_GROUPS + N_TALL]]
    first, second, inputs_0, inputs_1, hidden_0, hidden_1, slope_0, slope_1, encoded, late = outs[N_GROUPS + N_TALL :]
    late = lax.all_gather(late, ("dp", "seq"), axis=0, tiled=False)
    kept = [(neighbours, inputs_0, hidden_0, slope_0), (first, inputs_1, hidden_1, slope_1)]
    mixed = narrow[2]
    half = mixed.shape[1] // 2
    sides = [mixed[:, :half], mixed[:, half:]]
    qkv = [side[:, 2 * D : 5 * D] for side in sides]
    out = [side[:, 5 * D : 6 * D] for side in sides]
    return dict(
        encoder=(second, kept, encoded),
        enc_in=narrow[:2], enc_down=tall[:2], dec_in=[narrow[3], None], dec_down=[tall[2], late], dec_qkv=qkv, dec_out=out,
        cca_kv=[side[:, :D] for side in sides], cca_q=sides[0][:, D : 2 * D], cca_out=sides[1][:, D : 2 * D],
        gains=narrow[4][:, :8],
    )


YZX_SUM, XZY_SUM, YXZ_SUM, XYZ_SUM = (1, False), (2, False), (1, True), (2, True)
ORDERS = (YZX_SUM, XZY_SUM, YZX_SUM, XZY_SUM, YXZ_SUM, XZY_SUM, YZX_SUM, XYZ_SUM, YZX_SUM, XZY_SUM, YXZ_SUM)
ORDERS += (XZY_SUM, YZX_SUM, XYZ_SUM, YZX_SUM, XZY_SUM, YXZ_SUM, XYZ_SUM, YZX_SUM, XYZ_SUM, YXZ_SUM, XYZ_SUM)
CORE, HEAVY, ZED, PAIR, CORE_AGAIN, PER_PIECE = 0, 1, 2, 8, 9, 10
START = (0, 1, 4, 6, 7, 8, 10, 11, 12)
SLOTS = dict(part=2, whole=5, half=8, sibling=3, heavy=8, middle=8, last=8, zed=7, final=4)


def gradient_pieces():
    pieces = []
    both = lambda left, right, out, layer, k: tuple(
        (left, right, 2 * D * half + D * k, out, layer, 2 * D * half + D * k) for half in range(2)
    )
    for layer in reversed(range(2)):
        base = 8 * layer
        for k in range(2):
            pieces.append(both(base + 6, base + 7, 5, layer, k))
        for k in range(2):
            pieces.append(both(base + 4, base + 5, 4, layer, k))
    pieces.append(tuple((8 * layer + 2, 8 * layer + 3, 0, 3, layer, 0) for layer in range(2)))
    for k in range(3):
        pieces.append(tuple((8 * layer, 8 * layer + 1, D * k, 2, layer, D * k) for layer in range(2)))
    pieces.append(((16, 17, 0, 6, None, 0), (20, 21, 0, 8, None, 0)))
    pieces.append(tuple((18, 19, D * half, 7, None, D * half) for half in range(2)))
    for layer in reversed(range(2)):
        base = 22 + 4 * layer
        for k in range(2):
            pieces.append(both(base + 2, base + 3, 1, layer, k))
        for k in range(2):
            pieces.append(both(base, base + 1, 0, layer, k))
    return pieces


N_OPERANDS = 30


class Sums:
    def __init__(self, place, sizes, sems, buffers, slots, width):
        self.place, self.sizes, self.width = place, sizes, width
        self.send_sem, self.recv_sem = sems
        self.part, self.whole, self.half, self.sibling, self.heavy, self.middle, self.last, self.zed, self.final = buffers
        self.slots = slots

    def slot(self, name, number):
        return lax.rem(number, self.slots[name])

    def copy(self, number, which, source, target, device):
        index = number * PER_PIECE + which
        return pltpu.make_async_remote_copy(
            src_ref=source,
            dst_ref=target,
            send_sem=self.send_sem.at[index],
            recv_sem=self.recv_sem.at[index],
            device_id=device_at(device),
            device_id_type=MESH_ID,
        )

    def core_copy(self, number):
        return self.copy(
            number,
            CORE,
            self.part.at[self.slot("part", number)],
            self.sibling.at[self.slot("sibling", number)],
            self.swapped(3),
        )

    def swapped(self, axis):
        return self.place[:axis] + (1 - self.place[axis],) + self.place[axis + 1 :]

    def heavy_copy(self, number, axis):
        whole = self.whole.at[self.slot("whole", number)]
        there = 1 - self.place[axis]
        source = whole.at[:, there] if axis == 1 else whole.at[:, :, there]
        return self.copy(number, HEAVY, source, self.heavy.at[self.slot("heavy", number)], self.swapped(axis))

    def pair_copy(self, number, axis, early):
        half = self.half.at[self.slot("half", number)]
        there = 1 - self.place[axis]
        if early:
            source, target = half.at[:, there], self.middle.at[self.slot("middle", number)]
        else:
            source, target = half.at[self.place[0], there], self.last.at[self.slot("last", number)]
        return self.copy(number, PAIR, source, target, self.swapped(axis))

    def zed_block(self, number, axis, early, at):
        half = self.half.at[self.slot("half", number)]
        at = jnp.clip(at, 0, self.sizes[0] - 1)
        return half.at[at, pl.ds(self.place[axis], 1)] if early else half.at[at]

    def zed_room(self, number, early, hop, way):
        room = self.zed.at[self.slot("zed", number), hop - 1, way]
        return room.at[pl.ds(0, 1)] if early else room

    def zed_hops(self, number, axis, early, hop):
        z, size = self.place[0], self.sizes[0]
        found = []
        for way, by in enumerate((-1, 1)):
            sent, ahead = z + by * hop, z + by
            behind, got = z - by, z - by + by * hop
            room = self.zed_room(number, early, hop, way)
            device = (jnp.clip(ahead, 0, size - 1),) + self.place[1:]
            copy = self.copy(number, ZED + 2 * (hop - 1) + way, self.zed_block(number, axis, early, sent), room, device)
            sends = jnp.logical_and(inside(sent, size), inside(ahead, size))
            receives = jnp.logical_and(inside(got, size), inside(behind, size))
            found.append((copy, sends, receives, self.zed_block(number, axis, early, got), room))
        return found

    def start_zed(self, number, axis, early, hop):
        for copy, sends, _, _, _ in self.zed_hops(number, axis, early, hop):
            pl.when(sends)(copy.start)

    def finish_zed(self, number, axis, early, hop):
        for copy, sends, receives, block, room in self.zed_hops(number, axis, early, hop):
            pl.when(sends)(copy.wait_send)

            @pl.when(receives)
            def _():
                copy.wait_recv()
                for k in range(1 if early else 2):
                    block[k] = block[k] + room[k]

    def add_core(self, number):
        self.core_copy(number).wait()
        whole, sibling = self.slot("whole", number), self.slot("sibling", number)

        def one(k, _):
            at = (k // 4, (k // 2) % 2, k % 2)
            self.whole[(whole, *at)] = self.whole[(whole, *at)] + self.sibling[(sibling, *at)]
            return 0

        lax.fori_loop(0, 4 * self.sizes[0], one, 0)

    def add_heavy(self, number, axis):
        self.heavy_copy(number, axis).wait()
        whole, half, heavy = (self.slot(name, number) for name in ("whole", "half", "heavy"))

        def one(k, _):
            z, o = k // 2, k % 2
            at = (z, self.place[1], o) if axis == 1 else (z, o, self.place[2])
            self.half[half, z, o] = self.whole[(whole, *at)] + self.heavy[heavy, z, o]
            return 0

        lax.fori_loop(0, 2 * self.sizes[0], one, 0)

    def add_pair(self, number, axis, early):
        self.pair_copy(number, axis, early).wait()
        half, here = self.slot("half", number), self.place[axis]
        if early:
            for z in range(self.sizes[0]):
                self.half[half, z, here] = self.half[half, z, here] + self.middle[self.slot("middle", number), z]
        else:
            z = self.place[0]
            self.half[half, z, here] = self.half[half, z, here] + self.last[self.slot("last", number)]

    def split_rows(self, number, axis):
        half, final = self.slot("half", number), self.slot("final", number)
        rows = self.half[half, self.place[0], self.place[axis]].astype(jnp.float32)
        count = rows.shape[0] // 2
        first, second = rows[:count], rows[count:]
        self.final[final, 0] = jnp.where(self.place[3] == 0, first, second)
        self.final[final, 2] = jnp.where(self.place[3] == 0, second, first)

    def final_copy(self, number):
        final = self.slot("final", number)
        return self.copy(number, CORE_AGAIN, self.final.at[final, 2], self.final.at[final, 1], self.swapped(3))

    def step(self, step, number, first, early):
        other = 3 - first
        sequence = [("pair", 0), ("zed", 3), ("zed", 2), ("zed", 1)] if early else [("zed", 3), ("zed", 2), ("zed", 1), ("pair", 0)]
        if step == 1:
            self.heavy_copy(number, first).start()
            return
        if step == 2:
            self.add_heavy(number, first)
        else:
            kind, hop = sequence[step - 3]
            if kind == "pair":
                self.add_pair(number, other, early)
            else:
                self.finish_zed(number, other, early, hop)
        if step < 6:
            kind, hop = sequence[step - 2]
            if kind == "pair":
                self.pair_copy(number, other, early).start()
            else:
                self.start_zed(number, other, early, hop)
        else:
            self.split_rows(number, other)
            self.final_copy(number).start()


def reduce_kernel(sizes, tall, *refs):
    pieces = gradient_pieces()
    operands, gains = refs[:N_OPERANDS], refs[N_OPERANDS]
    outs = refs[N_OPERANDS + 1 : N_OPERANDS + 11]
    scratch = refs[N_OPERANDS + 11 :]
    left, right, product = scratch[:3]
    buffers, small = scratch[3:12], scratch[12:21]
    send_sem, recv_sem, small_send, small_recv, load_sem, out_sem = scratch[21:]
    place = grid_place()
    core = place[3]
    count = len(pieces)
    sums = Sums(place, sizes, (send_sem, recv_sem), buffers, SLOTS, D)
    once = Sums(place, sizes, (small_send, small_recv), small, {name: 1 for name in SLOTS}, 128)
    is_tall = [tall[piece[0][0]] for piece in pieces]
    first_tall = is_tall.index(True)
    long_rows, short_rows = left.shape[2], None

    def rows_of(k):
        return operands[pieces[k][0][0]].shape[0]

    def loads(k, slot):
        rows = rows_of(k)
        found = []
        for half in range(2):
            l, r, column, _, _, _ = pieces[k][half]
            mine = jnp.where(core == half, 1, 0)
            found.append((operands[l], left.at[slot, mine, pl.ds(0, rows)], load_sem.at[slot, half]))
            found.append((operands[r].at[:, pl.ds(column, D)], right.at[slot, mine, pl.ds(0, rows)], load_sem.at[slot, 2 + half]))
        return [pltpu.make_async_copy(*args) for args in found]

    def start_loads(number):
        for k in range(count):

            @pl.when(number == k)
            def _():
                for copy in loads(k, k % 2):
                    copy.start()

    def multiply(number, which, rows):
        slot = lax.rem(number, 2)

        def block(k, _):
            columns = pl.ds(pl.multiple_of(k * 128, 128), 128)
            product[pl.ds(pl.multiple_of(k * 128, 128), 128), :] = lax.dot_general(
                left[slot, which, pl.ds(0, rows), columns],
                right[slot, which, pl.ds(0, rows), :],
                (((0,), (0,)), ((), ())),
                preferred_element_type=jnp.float32,
            )
            return 0

        lax.fori_loop(0, D // 128, block, 0)
        chunk = sums.whole.shape[4]

        def store(k, _):
            values = product[pl.ds(pl.multiple_of(k * chunk, 8), chunk), :].astype(BF)
            at = (k // 4, (k // 2) % 2, k % 2)
            if which == 0:
                sums.part[(sums.slot("part", number), *at)] = values
            else:
                sums.whole[(sums.slot("whole", number), *at)] = values
            return 0

        lax.fori_loop(0, D // chunk, store, 0)

    def compute(number):
        for flag in sorted(set(is_tall)):
            wanted = jnp.logical_and(number >= first_tall, flag) if flag else number < first_tall
            k = first_tall if flag else 0

            @pl.when(wanted)
            def _():
                for copy in loads(k, lax.rem(number, 2)):
                    copy.wait()
                multiply(number, 0, rows_of(k))
                sums.core_copy(number).start()
                multiply(number, 1, rows_of(k))

    def out_copies(k):
        slot = k % SLOTS["final"]
        found = []
        for half in range(2):
            _, _, _, out, layer, column = pieces[k][half]
            target = outs[out] if layer is None else outs[out].at[layer]
            source = sums.final.at[slot, jnp.where(core == half, 0, 1)]
            found.append(pltpu.make_async_copy(source, target.at[:, pl.ds(column, D)], out_sem.at[slot, half]))
        return found

    greet(place, sizes)
    small_loads = []
    for k, target in enumerate((once.part.at[0], once.whole.at[0])):
        copy = pltpu.make_async_copy(gains, target, out_sem.at[SLOTS["final"], k])
        copy.start()
        small_loads.append(copy)
    start_loads(0)

    def tick(time, _):
        for step in reversed(range(8)):

            @pl.when(time == START[step])
            def _():
                if step == 0:
                    for copy in small_loads:
                        copy.wait()
                    once.core_copy(0).start()
                elif step == 7:
                    once.final_copy(0).wait()
                    copy = pltpu.make_async_copy(once.final.at[0, 0], outs[9], out_sem.at[SLOTS["final"], 0])
                    copy.start()
                    copy.wait()
                else:
                    if step == 1:
                        once.add_core(0)
                    once.step(step, 0, *ORDERS[-1])

        for step in reversed(range(9)):
            number = time - START[step]

            @pl.when(jnp.logical_and(number >= 0, number < count))
            def _():
                if step == 0:
                    start_loads(number + 1)
                    compute(number)
                elif step == 8:
                    for copy in out_copies_at(number):
                        copy.wait()
                elif step == 7:
                    sums.final_copy(number).wait()
                    for k in range(count):

                        @pl.when(number == k)
                        def _():
                            for copy in out_copies(k):
                                copy.start()

                else:
                    if step == 1:
                        sums.add_core(number)
                    for order in sorted(set(ORDERS)):
                        here = functools.reduce(jnp.logical_or, [number == k for k, one in enumerate(ORDERS) if one == order])

                        @pl.when(here)
                        def _():
                            sums.step(step, number, *order)

        return 0

    def out_copies_at(number):
        slot = lax.rem(number, SLOTS["final"])
        return [
            pltpu.make_async_copy(sums.final.at[slot, 0], outs[3].at[0, :, pl.ds(0, D)], out_sem.at[slot, half])
            for half in range(2)
        ]

    lax.fori_loop(0, count + START[8], tick, 0)


def reduce_gradients(operands, gains, layers_rows):
    sizes = grid_sizes()
    rows = layers_rows
    chunk = 2 * rows
    lead = sizes[:3] + (chunk,)
    longest = max(x.shape[0] for x in operands)
    shortest = min(x.shape[0] for x in operands)
    tall = tuple(x.shape[0] == longest for x in operands)
    f32 = jnp.float32
    shapes = [(2, rows, FF), (2, rows, FF), (2, rows, 3 * D), (2, rows, D), (2, rows, FF), (2, rows, FF)]
    shapes += [(rows, D), (rows, 2 * D), (rows, D), (rows, 128)]

    def rooms(slots, width):
        z = sizes[0]
        return [
            pltpu.VMEM((slots["part"],) + lead + (width,), BF),
            pltpu.VMEM((slots["whole"],) + lead + (width,), BF),
            pltpu.VMEM((slots["half"], z, 2, chunk, width), BF),
            pltpu.VMEM((slots["sibling"],) + lead + (width,), BF),
            pltpu.VMEM((slots["heavy"], z, 2, chunk, width), BF),
            pltpu.VMEM((slots["middle"], z, chunk, width), BF),
            pltpu.VMEM((slots["last"], chunk, width), BF),
            pltpu.VMEM((slots["zed"], z - 1, 2, 2, chunk, width), BF),
            pltpu.VMEM((slots["final"], 3, rows, width), f32),
        ]

    count = len(gradient_pieces())
    return pl.pallas_call(
        functools.partial(reduce_kernel, sizes, tall),
        out_shape=[jax.ShapeDtypeStruct(shape, f32) for shape in shapes],
        in_specs=[ANY] * (N_OPERANDS + 1),
        out_specs=[ANY] * 10,
        scratch_shapes=[
            pltpu.VMEM((2, 2, longest, D), BF),
            pltpu.VMEM((2, 2, longest, D), BF),
            pltpu.VMEM((D, D), f32),
            *rooms(SLOTS, D),
            *rooms({name: 1 for name in SLOTS}, 128),
            pltpu.SemaphoreType.DMA((PER_PIECE * count,)),
            pltpu.SemaphoreType.DMA((PER_PIECE * count,)),
            pltpu.SemaphoreType.DMA((PER_PIECE,)),
            pltpu.SemaphoreType.DMA((PER_PIECE,)),
            pltpu.SemaphoreType.DMA((2, 4)),
            pltpu.SemaphoreType.DMA((SLOTS["final"] + 1, 2)),
        ],
        compiler_params=pltpu.CompilerParams(collective_id=1, has_side_effects=True, vmem_limit_bytes=62 << 20),
        name="reduce_gradients",
    )(*operands, gains.reshape(lead + (128,)))


NN = (((1,), (0,)), ((), ()))
NT = (((1,), (1,)), ((), ()))
TN = (((0,), (0,)), ((), ()))


def dot(left, right, dims):
    return lax.dot_general(left, right, dims, preferred_element_type=jnp.float32)


def head_sides(values):
    lane = lax.broadcasted_iota(jnp.int32, values.shape, 1)
    zero = jnp.zeros_like(values)
    return [jnp.where(lane < HEAD, values, zero), jnp.where(lane >= HEAD, values, zero)]


def attend_kernel(q_ref, k_ref, v_ref, bias_ref, out_ref, total_ref):
    keys, vals = k_ref[...], v_ref[...]
    outs = []
    for side, queries in enumerate(head_sides(q_ref[...])):
        scores = dot(keys, queries, NT) * SCORE_SCALE + bias_ref[...]
        peak = jnp.max(scores, 0, keepdims=True)
        powers = jnp.exp(scores - peak)
        total = jnp.sum(powers, 0, keepdims=True)
        total_ref[0, side : side + 1, :] = peak + jnp.log(total)
        probs = (powers * (1.0 / total)).astype(BF)
        outs.append(dot(probs, vals, TN))
    lane = lax.broadcasted_iota(jnp.int32, outs[0].shape, 1)
    out_ref[...] = jnp.where(lane < HEAD, outs[0], outs[1]).astype(BF)


def attend(joined, keys_vals, bias):
    queries, keys = joined.shape[0], keys_vals.shape[0]
    pairs = D // 128
    return pl.pallas_call(
        attend_kernel,
        grid=(pairs,),
        out_shape=[jax.ShapeDtypeStruct((queries, D), BF), jax.ShapeDtypeStruct((pairs, 2, queries), jnp.float32)],
        in_specs=[
            pl.BlockSpec((queries, 128), lambda p: (0, p)),
            pl.BlockSpec((keys, 128), lambda p: (0, p)),
            pl.BlockSpec((keys, 128), lambda p: (0, pairs + p)),
            pl.BlockSpec((keys, queries), lambda p: (0, 0)),
        ],
        out_specs=[pl.BlockSpec((queries, 128), lambda p: (0, p)), pl.BlockSpec((1, 2, queries), lambda p: (p, 0, 0))],
        cost_estimate=pl.CostEstimate(
            flops=4 * queries * keys * D * 2, bytes_accessed=2 * keys * 2 * D, transcendentals=14 * queries * keys
        ),
        name="attend",
    )(joined, keys_vals, keys_vals, bias)


def attend_back_kernel(q_ref, k_ref, v_ref, bias_ref, total_ref, grad_ref, gq_ref, gkv_ref):
    pair = pl.program_id(0)
    keys, vals = k_ref[...], v_ref[...]
    q_sides, g_sides = head_sides(q_ref[...]), head_sides(grad_ref[...])
    grad_q, grad_k, grad_v = [], 0.0, 0.0
    for side in range(2):
        scores = dot(keys, q_sides[side], NT) * SCORE_SCALE + bias_ref[...]
        probs = jnp.exp(scores - total_ref[0, side : side + 1, :])
        grad_probs = dot(vals, g_sides[side], NT)
        delta = jnp.sum(probs * grad_probs, 0, keepdims=True)
        grad_scores = (probs * (grad_probs - delta)).astype(BF)
        grad_v = grad_v + dot(probs.astype(BF), g_sides[side], NN)
        grad_k = grad_k + dot(grad_scores, q_sides[side], NN)
        grad_q.append(dot(grad_scores, keys, TN))
    lane = lax.broadcasted_iota(jnp.int32, grad_q[0].shape, 1)
    gq_ref[...] = (jnp.where(lane < HEAD, grad_q[0], grad_q[1]) * SCORE_SCALE).astype(BF)
    gkv_ref[:, pl.ds(pl.multiple_of(pair * 128, 128), 128)] = (grad_k * SCORE_SCALE).astype(BF)
    gkv_ref[:, pl.ds(pl.multiple_of(D + pair * 128, 128), 128)] = grad_v.astype(BF)


def attend_back(joined, keys_vals, bias, log_total, grad_mixed):
    queries, keys = joined.shape[0], keys_vals.shape[0]
    pairs = D // 128
    return pl.pallas_call(
        attend_back_kernel,
        grid=(pairs,),
        out_shape=[jax.ShapeDtypeStruct((queries, D), BF), jax.ShapeDtypeStruct((keys, 2 * D), BF)],
        in_specs=[
            pl.BlockSpec((queries, 128), lambda p: (0, p)),
            pl.BlockSpec((keys, 128), lambda p: (0, p)),
            pl.BlockSpec((keys, 128), lambda p: (0, pairs + p)),
            pl.BlockSpec((keys, queries), lambda p: (0, 0)),
            pl.BlockSpec((1, 2, queries), lambda p: (p, 0, 0)),
            pl.BlockSpec((queries, 128), lambda p: (0, p)),
        ],
        out_specs=[pl.BlockSpec((queries, 128), lambda p: (0, p)), pl.BlockSpec((keys, 2 * D), lambda p: (0, 0))],
        cost_estimate=pl.CostEstimate(
            flops=10 * queries * keys * D * 2, bytes_accessed=4 * keys * 2 * D, transcendentals=14 * queries * keys
        ),
        name="attend_back",
    )(joined, keys_vals, keys_vals, bias, log_total, grad_mixed)


PAIR_GROUPS = (((0, 1), (2, 1)), ((2, 3), (1, 2)), ((4, 5), (2, 1)), ((6,), (1, 2)))
BACK_GROUPS = tuple(((pair,), ((2, 1), (1, 2))[pair % 2]) for pair in range(7))
BACK_LAGS = (2, 5, 7)


def greet_plane(place):
    barrier = pltpu.get_barrier_semaphore()
    for axis in (1, 2, 3):
        other = place[:axis] + (1 - place[axis],) + place[axis + 1 :]
        pl.semaphore_signal(barrier, inc=1, device_id=device_at(other), device_id_type=MESH_ID)
    pl.semaphore_wait(barrier, 3)


def group_columns(pairs):
    return [pl.ds(side * D + 128 * pairs[0], 128 * len(pairs)) for side in range(2)]


def plane_copies(place, axis, sources, targets, send_sem, recv_sem, index):
    device = place[:axis] + (1 - place[axis],) + place[axis + 1 :]
    return [
        pltpu.make_async_remote_copy(
            src_ref=source,
            dst_ref=target,
            send_sem=send_sem.at[index, k],
            recv_sem=recv_sem.at[index, k],
            device_id=device_at(device),
            device_id_type=MESH_ID,
        )
        for k, (source, target) in enumerate(zip(sources, targets))
    ]


def start_all(copies):
    for copy in copies:
        copy.start()


def wait_all(copies):
    for copy in copies:
        copy.wait()


def attend_gather_kernel(joined_ref, bias_ref, out_ref, total_ref, kept_ref, held, queries, send_sem, recv_sem, load_sem):
    place = grid_place()
    _, y, x, core = place
    loads = [
        pltpu.make_async_copy(joined_ref.at[:, pl.ds(D, 2 * D)], held.at[y, x, core], load_sem.at[0]),
        pltpu.make_async_copy(joined_ref.at[:, pl.ds(0, D)], queries, load_sem.at[1]),
    ]
    start_all(loads)
    greet_plane(place)
    wait_all(loads)

    def step(number, k):
        pairs, route = PAIR_GROUPS[number]
        if k == 0:
            views = [held.at[y, x, core, :, columns] for columns in group_columns(pairs)]
            axis = route[0]
        elif k == 1:
            axis = route[1]
            views = [(held.at[y, :, core, :, c] if axis == 1 else held.at[:, x, core, :, c]) for c in group_columns(pairs)]
        else:
            axis = 3
            views = [held.at[:, :, core, :, c] for c in group_columns(pairs)]
        return plane_copies(place, axis, views, views, send_sem, recv_sem, 3 * number + k)

    lane = lax.broadcasted_iota(jnp.int32, (queries.shape[0], 128), 1)
    rows = bias_ref.shape[0]

    def compute(number):
        for pair in PAIR_GROUPS[number][0]:
            keys = held[:, :, :, :, pl.ds(128 * pair, 128)].reshape(rows, 128)
            vals = held[:, :, :, :, pl.ds(D + 128 * pair, 128)].reshape(rows, 128)
            outs = []
            for side, sided in enumerate(head_sides(queries[:, pl.ds(128 * pair, 128)])):
                scores = dot(keys, sided, NT) * SCORE_SCALE + bias_ref[...]
                peak = jnp.max(scores, 0, keepdims=True)
                powers = jnp.exp(scores - peak)
                total = jnp.sum(powers, 0, keepdims=True)
                total_ref[pair, side : side + 1, :] = peak + jnp.log(total)
                outs.append(dot((powers * (1.0 / total)).astype(BF), vals, TN))
            out_ref[:, pl.ds(128 * pair, 128)] = jnp.where(lane < HEAD, outs[0], outs[1]).astype(BF)

    count = len(PAIR_GROUPS)
    for number in range(count):
        start_all(step(number, 0))
    for number in range(count):
        wait_all(step(number, 0))
        start_all(step(number, 1))
    for number in range(count):
        wait_all(step(number, 1))
        start_all(step(number, 2))
        if number > 0:
            wait_all(step(number - 1, 2))
            if number < count - 1:
                compute(number - 1)
    wait_all(step(count - 1, 2))
    keep = pltpu.make_async_copy(held, kept_ref, load_sem.at[0])
    keep.start()
    compute(count - 2)
    compute(count - 1)
    keep.wait()


def whole_block(shape):
    return pl.BlockSpec(shape, lambda: (0,) * len(shape))


def attend_gather(joined, bias):
    rows = joined.shape[0]
    _, n_y, n_x, n_core = grid_sizes()
    lead = (n_y, n_x, n_core)
    pairs, count = D // 128, len(PAIR_GROUPS)
    mixed, log_total, kept = pl.pallas_call(
        attend_gather_kernel,
        out_shape=[
            jax.ShapeDtypeStruct((rows, D), BF),
            jax.ShapeDtypeStruct((pairs, 2, rows), jnp.float32),
            jax.ShapeDtypeStruct(lead + (rows, 2 * D), BF),
        ],
        in_specs=[ANY, whole_block(bias.shape)],
        out_specs=[whole_block((rows, D)), whole_block((pairs, 2, rows)), ANY],
        scratch_shapes=[
            pltpu.VMEM(lead + (rows, 2 * D), BF),
            pltpu.VMEM((rows, D), BF),
            pltpu.SemaphoreType.DMA((3 * count, 2)),
            pltpu.SemaphoreType.DMA((3 * count, 2)),
            pltpu.SemaphoreType.DMA((2,)),
        ],
        compiler_params=pltpu.CompilerParams(collective_id=2, has_side_effects=True, vmem_limit_bytes=32 << 20),
        name="attend_gather",
    )(joined, bias)
    return mixed, log_total, kept.reshape(-1, 2 * D)


def attend_scatter_kernel(joined_ref, held_ref, bias_ref, total_ref, grad_ref, gq_ref, own_ref, *scratch):
    queries, part, from_core, from_first, from_second, send_sem, recv_sem, load_sem = scratch
    place = grid_place()
    _, y, x, core = place
    load = pltpu.make_async_copy(joined_ref.at[:, pl.ds(0, D)], queries, load_sem.at[0])
    load.start()
    greet_plane(place)
    load.wait()
    rows = bias_ref.shape[0]
    lane = lax.broadcasted_iota(jnp.int32, (queries.shape[0], 128), 1)

    def compute(number):
        for pair in BACK_GROUPS[number][0]:
            columns, beside = pl.ds(128 * pair, 128), pl.ds(D + 128 * pair, 128)
            keys = held_ref[:, :, :, :, columns].reshape(rows, 128)
            vals = held_ref[:, :, :, :, beside].reshape(rows, 128)
            q_sides, g_sides = head_sides(queries[:, columns]), head_sides(grad_ref[:, columns])
            grad_q, grad_k, grad_v = [], 0.0, 0.0
            for side in range(2):
                scores = dot(keys, q_sides[side], NT) * SCORE_SCALE + bias_ref[...]
                probs = jnp.exp(scores - total_ref[pair, side : side + 1, :])
                grad_probs = dot(vals, g_sides[side], NT)
                delta = jnp.sum(probs * grad_probs, 0, keepdims=True)
                grad_scores = (probs * (grad_probs - delta)).astype(BF)
                grad_v = grad_v + dot(probs.astype(BF), g_sides[side], NN)
                grad_k = grad_k + dot(grad_scores, q_sides[side], NN)
                grad_q.append(dot(grad_scores, keys, TN))
            gq_ref[:, columns] = (jnp.where(lane < HEAD, grad_q[0], grad_q[1]) * SCORE_SCALE).astype(BF)
            shape = part.shape[:4] + (128,)
            part[:, :, :, :, columns] = (grad_k * SCORE_SCALE).astype(BF).reshape(shape)
            part[:, :, :, :, beside] = grad_v.astype(BF).reshape(shape)

    def step(number, k):
        pairs, route = BACK_GROUPS[number]
        columns = group_columns(pairs)
        if k == 0:
            axis = 3
            sources = [part.at[:, :, 1 - core, :, c] for c in columns]
            targets = [from_core.at[:, :, :, c] for c in columns]
        elif k == 1:
            axis = route[1]
            sources = [(part.at[1 - y, :, core, :, c] if axis == 1 else part.at[:, 1 - x, core, :, c]) for c in columns]
            targets = [from_first.at[:, :, c] for c in columns]
        else:
            axis = route[0]
            sources = [(part.at[1 - y, x, core, :, c] if axis == 1 else part.at[y, 1 - x, core, :, c]) for c in columns]
            targets = [from_second.at[:, c] for c in columns]
        return plane_copies(place, axis, sources, targets, send_sem, recv_sem, 3 * number + k)

    def add(number, k):
        pairs, route = BACK_GROUPS[number]
        wait_all(step(number, k))
        for c in group_columns(pairs):
            if k == 0:
                part[:, :, core, :, c] = part[:, :, core, :, c] + from_core[:, :, :, c]
            elif k == 1 and route[1] == 1:
                part[y, :, core, :, c] = part[y, :, core, :, c] + from_first[:, :, c]
            elif k == 1:
                part[:, x, core, :, c] = part[:, x, core, :, c] + from_first[:, :, c]
            else:
                own_ref[:, c] = part[y, x, core, :, c] + from_second[:, c]

    count = len(BACK_GROUPS)
    for time in range(count + BACK_LAGS[-1]):
        if time < count:
            compute(time)
            start_all(step(time, 0))
        for k, lag in enumerate(BACK_LAGS):
            number = time - lag
            if 0 <= number < count:
                add(number, k)
                if k < 2:
                    start_all(step(number, k + 1))


def attend_scatter(joined, keys_vals, bias, log_total, grad_mixed):
    rows = joined.shape[0]
    _, n_y, n_x, n_core = grid_sizes()
    lead = (n_y, n_x, n_core)
    count = len(BACK_GROUPS)
    held = keys_vals.reshape(lead + (rows, 2 * D))
    return pl.pallas_call(
        attend_scatter_kernel,
        out_shape=[jax.ShapeDtypeStruct((rows, D), BF), jax.ShapeDtypeStruct((rows, 2 * D), BF)],
        in_specs=[ANY] + [whole_block(v.shape) for v in (held, bias, log_total, grad_mixed)],
        out_specs=[whole_block((rows, D)), whole_block((rows, 2 * D))],
        scratch_shapes=[
            pltpu.VMEM((rows, D), BF),
            pltpu.VMEM(lead + (rows, 2 * D), BF),
            pltpu.VMEM((n_y, n_x, rows, 2 * D), BF),
            pltpu.VMEM((2, rows, 2 * D), BF),
            pltpu.VMEM((rows, 2 * D), BF),
            pltpu.SemaphoreType.DMA((3 * count, 2)),
            pltpu.SemaphoreType.DMA((3 * count, 2)),
            pltpu.SemaphoreType.DMA((1,)),
        ],
        compiler_params=pltpu.CompilerParams(collective_id=3, has_side_effects=True, vmem_limit_bytes=40 << 20),
        name="attend_scatter",
    )(joined, held, bias, log_total, grad_mixed)


def gelu_parts(values):
    size = jnp.abs(values)
    bell = jnp.exp(-0.5 * size * size)
    t = 1.0 / (1.0 + (0.3275911 * 0.7071067811865476) * size)
    tail = t * (0.127414796 + t * (-0.142248368 + t * (0.7107068705 + t * (-0.7265760135 + t * 0.5307027145)))) * bell
    share = jnp.where(values >= 0, 1.0 - tail, tail)
    return values * share, share + values * (0.3989422804014327 * bell)


def norm_parts(values):
    scale = lax.rsqrt(jnp.mean(values * values, -1, keepdims=True) + EPSILON)
    return values * scale, scale


def norm_gradient(values, norm_gain, upstream):
    unit, scale = norm_parts(values)
    inner = upstream * norm_gain
    back = scale * (inner - unit * jnp.mean(inner * unit, -1, keepdims=True))
    return back, jnp.sum(upstream * unit, 0, keepdims=True)


def hidden_block(rows):
    return 2 * D if rows <= 128 else D


def ffn_kernel(stream_ref, gain_ref, in_ref, down_ref, out_ref, inputs_ref, hidden_ref, slope_ref):
    step = pl.program_id(0)

    @pl.when(step == 0)
    def _():
        stream = stream_ref[...].astype(jnp.float32)
        out_ref[...] = stream
        inputs_ref[...] = (norm_parts(stream)[0] * gain_ref[...].astype(jnp.float32)).astype(BF)

    value, slope = gelu_parts(dot(inputs_ref[...], in_ref[...], NN))
    hidden = value.astype(BF)
    hidden_ref[...] = hidden
    slope_ref[...] = slope.astype(BF)
    out_ref[...] += dot(hidden, down_ref[...], NN)


def ffn(stream, norm_gain, weight_in, weight_down):
    rows = stream.shape[0]
    block = hidden_block(rows)
    still = lambda j: (0, 0)
    return pl.pallas_call(
        ffn_kernel,
        grid=(FF // block,),
        out_shape=[
            jax.ShapeDtypeStruct((rows, D), jnp.float32),
            jax.ShapeDtypeStruct((rows, D), BF),
            jax.ShapeDtypeStruct((rows, FF), BF),
            jax.ShapeDtypeStruct((rows, FF), BF),
        ],
        in_specs=[
            pl.BlockSpec((rows, D), still),
            pl.BlockSpec((1, D), still),
            pl.BlockSpec((D, block), lambda j: (0, j)),
            pl.BlockSpec((block, D), lambda j: (j, 0)),
        ],
        out_specs=[
            pl.BlockSpec((rows, D), still),
            pl.BlockSpec((rows, D), still),
            pl.BlockSpec((rows, block), lambda j: (0, j)),
            pl.BlockSpec((rows, block), lambda j: (0, j)),
        ],
        cost_estimate=pl.CostEstimate(
            flops=4 * rows * D * FF, bytes_accessed=4 * D * FF + 4 * rows * FF + 8 * rows * D, transcendentals=rows * FF
        ),
        name="ffn",
    )(stream, norm_gain, weight_in, weight_down)


def ffn_back_kernel(grad_ref, stream_ref, gain_ref, slope_ref, in_ref, down_ref, out_ref, low_ref, pre_ref, gain_out, total):
    step = pl.program_id(0)

    @pl.when(step == 0)
    def _():
        low_ref[...] = grad_ref[...].astype(BF)
        total[...] = jnp.zeros_like(total)

    pre = (dot(low_ref[...], down_ref[...], NT) * slope_ref[...].astype(jnp.float32)).astype(BF)
    pre_ref[...] = pre
    total[...] += dot(pre, in_ref[...], NT)

    @pl.when(step == pl.num_programs(0) - 1)
    def _():
        back, gain = norm_gradient(stream_ref[...].astype(jnp.float32), gain_ref[...].astype(jnp.float32), total[...])
        out_ref[...] = grad_ref[...].astype(jnp.float32) + back
        gain_out[...] = gain


def ffn_back(upstream, stream, norm_gain, slope, weight_in, weight_down):
    rows = stream.shape[0]
    block = hidden_block(rows)
    still = lambda j: (0, 0)
    return pl.pallas_call(
        ffn_back_kernel,
        grid=(FF // block,),
        out_shape=[
            jax.ShapeDtypeStruct((rows, D), jnp.float32),
            jax.ShapeDtypeStruct((rows, D), BF),
            jax.ShapeDtypeStruct((rows, FF), BF),
            jax.ShapeDtypeStruct((1, D), jnp.float32),
        ],
        in_specs=[
            pl.BlockSpec((rows, D), still),
            pl.BlockSpec((rows, D), still),
            pl.BlockSpec((1, D), still),
            pl.BlockSpec((rows, block), lambda j: (0, j)),
            pl.BlockSpec((D, block), lambda j: (0, j)),
            pl.BlockSpec((block, D), lambda j: (j, 0)),
        ],
        out_specs=[
            pl.BlockSpec((rows, D), still),
            pl.BlockSpec((rows, D), still),
            pl.BlockSpec((rows, block), lambda j: (0, j)),
            pl.BlockSpec((1, D), still),
        ],
        scratch_shapes=[pltpu.VMEM((rows, D), jnp.float32)],
        cost_estimate=pl.CostEstimate(
            flops=4 * rows * D * FF, bytes_accessed=4 * D * FF + 4 * rows * FF + 16 * rows * D, transcendentals=0
        ),
        name="ffn_back",
    )(upstream, stream, norm_gain, slope, weight_in, weight_down)


def spread_matrix(devices):
    rows = D // devices
    source = lax.broadcasted_iota(jnp.int32, (D, devices * ROOM), 0)
    target = lax.broadcasted_iota(jnp.int32, (D, devices * ROOM), 1)
    return jnp.where((target // ROOM * rows + target % ROOM == source) & (target % ROOM < rows), 1.0, 0.0).astype(BF)


def late_blocks(late, tall):
    devices = late.shape[0]
    per_block = D // tall
    return [
        pl.BlockSpec((devices, ROOM, D), lambda j: (0, 4 + j, 0)),
        pl.BlockSpec((per_block, 4 * ROOM, D), lambda j: (j, 0, 0)),
    ]


def late_in_block(ref):
    return ref[...].reshape(-1, D)


def late_down_block(ref):
    values = ref[...]
    return values[:, : D // values.shape[0]].reshape(D, D)


def late_ffn_kernel(stream_ref, gain_ref, spread_ref, in_ref, down_ref, out_ref, inputs_ref, hidden_ref, slope_ref, spread):
    step = pl.program_id(0)

    @pl.when(step == 0)
    def _():
        stream = stream_ref[...].astype(jnp.float32)
        out_ref[...] = stream
        inputs = (norm_parts(stream)[0] * gain_ref[...].astype(jnp.float32)).astype(BF)
        inputs_ref[...] = inputs
        spread[...] = dot(inputs, spread_ref[...], NN).astype(BF)

    value, slope = gelu_parts(dot(spread[...], late_in_block(in_ref), NN))
    hidden = value.astype(BF)
    hidden_ref[...] = hidden
    slope_ref[...] = slope.astype(BF)
    out_ref[...] += dot(hidden, late_down_block(down_ref), NN)


def late_ffn(stream, norm_gain, spread, late, tall):
    rows = stream.shape[0]
    still = lambda j: (0, 0)
    return pl.pallas_call(
        late_ffn_kernel,
        grid=(FF // D,),
        out_shape=[
            jax.ShapeDtypeStruct((rows, D), jnp.float32),
            jax.ShapeDtypeStruct((rows, D), BF),
            jax.ShapeDtypeStruct((rows, FF), BF),
            jax.ShapeDtypeStruct((rows, FF), BF),
        ],
        in_specs=[pl.BlockSpec((rows, D), still), pl.BlockSpec((1, D), still), pl.BlockSpec(spread.shape, still)]
        + late_blocks(late, tall),
        out_specs=[
            pl.BlockSpec((rows, D), still),
            pl.BlockSpec((rows, D), still),
            pl.BlockSpec((rows, D), lambda j: (0, j)),
            pl.BlockSpec((rows, D), lambda j: (0, j)),
        ],
        scratch_shapes=[pltpu.VMEM((rows, spread.shape[1]), BF)],
        cost_estimate=pl.CostEstimate(flops=4 * rows * D * FF, bytes_accessed=5 * D * FF, transcendentals=rows * FF),
        name="late_ffn",
    )(stream, norm_gain, spread, late, late)


def late_back_kernel(grad_ref, stream_ref, gain_ref, spread_ref, slope_ref, in_ref, down_ref, out_ref, low_ref, pre_ref, gain_out, total):
    step = pl.program_id(0)

    @pl.when(step == 0)
    def _():
        low_ref[...] = grad_ref[...].astype(BF)
        total[...] = jnp.zeros_like(total)

    pre = (dot(low_ref[...], late_down_block(down_ref), NT) * slope_ref[...].astype(jnp.float32)).astype(BF)
    pre_ref[...] = pre
    total[...] += dot(pre, late_in_block(in_ref), NT)

    @pl.when(step == pl.num_programs(0) - 1)
    def _():
        whole = total[...]
        high = whole.astype(BF)
        rest = (whole - high.astype(jnp.float32)).astype(BF)
        inner = dot(high, spread_ref[...], NT) + dot(rest, spread_ref[...], NT)
        back, gain = norm_gradient(stream_ref[...].astype(jnp.float32), gain_ref[...].astype(jnp.float32), inner)
        out_ref[...] = grad_ref[...].astype(jnp.float32) + back
        gain_out[...] = gain


def late_ffn_back(upstream, stream, norm_gain, slope, spread, late, tall):
    rows = stream.shape[0]
    still = lambda j: (0, 0)
    return pl.pallas_call(
        late_back_kernel,
        grid=(FF // D,),
        out_shape=[
            jax.ShapeDtypeStruct((rows, D), jnp.float32),
            jax.ShapeDtypeStruct((rows, D), BF),
            jax.ShapeDtypeStruct((rows, FF), BF),
            jax.ShapeDtypeStruct((1, D), jnp.float32),
        ],
        in_specs=[
            pl.BlockSpec((rows, D), still),
            pl.BlockSpec((rows, D), still),
            pl.BlockSpec((1, D), still),
            pl.BlockSpec(spread.shape, still),
            pl.BlockSpec((rows, D), lambda j: (0, j)),
        ]
        + late_blocks(late, tall),
        out_specs=[
            pl.BlockSpec((rows, D), still),
            pl.BlockSpec((rows, D), still),
            pl.BlockSpec((rows, D), lambda j: (0, j)),
            pl.BlockSpec((1, D), still),
        ],
        scratch_shapes=[pltpu.VMEM((rows, spread.shape[1]), jnp.float32)],
        cost_estimate=pl.CostEstimate(flops=4 * rows * D * FF, bytes_accessed=5 * D * FF, transcendentals=0),
        name="late_ffn_back",
    )(upstream, stream, norm_gain, spread, slope, late, late)


def shifted(x, axis, by):
    count = lax.axis_size(axis)
    pairs = [(i, i + by) for i in range(count) if 0 <= i + by < count]
    return lax.ppermute(x, axis, pairs)


def slab_term(left, right):
    return dot(left, right, TN)


def normed(values, norm_gain):
    return (norm_parts(values)[0] * norm_gain.astype(jnp.float32)).astype(BF)


def norm_back(values, norm_gain, upstream):
    return norm_gradient(values, norm_gain.astype(jnp.float32), upstream)


def self_forward(stream, norm_gain, weight_qkv, weight_out, bias):
    inputs = normed(stream, norm_gain)
    joined = dot(inputs, weight_qkv, NN).astype(BF)
    if grid_sizes() == (4, 2, 2, 2):
        mixed, log_total, keys_vals = attend_gather(joined, bias)
    else:
        keys_vals = lax.all_gather(joined[:, D:], "seq", axis=0, tiled=True)
        mixed, log_total = attend(joined, keys_vals, bias)
    return stream + dot(mixed, weight_out, NN), (stream, inputs, joined, keys_vals, log_total, mixed)


def self_back(stored, norm_gain, weight_qkv, weight_out, bias, upstream, covered):
    stream, inputs, joined, keys_vals, log_total, mixed = stored
    grad_low = upstream.astype(BF)
    grad_mixed = dot(grad_low, weight_out, NT).astype(BF)
    if grid_sizes() == (4, 2, 2, 2) and not covered:
        grad_queries, own_pairs = attend_scatter(joined, keys_vals, bias, log_total, grad_mixed)
    else:
        grad_queries, grad_pairs = attend_back(joined, keys_vals, bias, log_total, grad_mixed)
        own_pairs = lax.psum_scatter(grad_pairs, "seq", scatter_dimension=0, tiled=True)
    grad_joined = jnp.concatenate([grad_queries, own_pairs], -1)
    back, gain_grad = norm_back(stream, norm_gain, dot(grad_joined, weight_qkv, NT))
    return upstream + back, gain_grad, ((inputs, grad_joined), (mixed, grad_low))


def causal_bias(queries, keys):
    offset = lax.axis_index("seq") * queries
    key_place = lax.broadcasted_iota(jnp.int32, (keys, queries), 0)
    query_place = offset + lax.broadcasted_iota(jnp.int32, (keys, queries), 1)
    return jnp.where(key_place <= query_place, 0.0, MASKED_SCORE).astype(jnp.float32)


def span_bias(prior_flag, queries):
    spans = prior_flag.shape[0]
    keys = spans * NEIGH * RET
    key_span = lax.broadcasted_iota(jnp.int32, (keys, queries), 0) // (NEIGH * RET)
    query_span = lax.broadcasted_iota(jnp.int32, (keys, queries), 1) // SPAN
    allowed = jnp.repeat(prior_flag.reshape(-1), RET)[:, None] > 0.5
    return jnp.where(key_span == query_span, jnp.where(allowed, 0.0, MASKED_SCORE), 2 * MASKED_SCORE).astype(jnp.float32)


def row_gate(prior_flag):
    return jnp.repeat(jnp.max(prior_flag, -1).astype(jnp.float32), SPAN)[:, None]


def prior_spans(encoded, keep_flag):
    last_enc, last_flag = shifted((encoded[-1:], keep_flag[-1:]), "seq", 1)
    return jnp.concatenate([last_enc, encoded[:-1]], 0), jnp.concatenate([last_flag, keep_flag[:-1]], 0)


def cross_forward(stream, encoded, keep_flag, norm_gain, weight_q, weight_kv, weight_out):
    prior_enc, prior_flag = prior_spans(encoded, keep_flag)
    prior_enc = prior_enc.reshape(-1, D)
    inputs = normed(stream, norm_gain)
    queries = dot(inputs, weight_q, NN).astype(BF)
    keys_vals = jnp.concatenate([dot(prior_enc, side, NN).astype(BF) for side in weight_kv], 1)
    bias = span_bias(prior_flag, stream.shape[0])
    mixed, log_total = attend(queries, keys_vals, bias)
    branch = row_gate(prior_flag) * dot(mixed, weight_out, NN)
    return stream + branch, (stream, inputs, prior_enc, prior_flag, queries, keys_vals, bias, log_total, mixed)


def cross_back(stored, norm_gain, weight_q, weight_kv, weight_out, upstream):
    stream, inputs, prior_enc, prior_flag, queries, keys_vals, bias, log_total, mixed = stored
    grad_low = (upstream * row_gate(prior_flag)).astype(BF)
    grad_mixed = dot(grad_low, weight_out, NT).astype(BF)
    grad_queries, grad_pairs = attend_back(queries, keys_vals, bias, log_total, grad_mixed)
    grad_prior = dot(grad_pairs[:, :D], weight_kv[0], NT) + dot(grad_pairs[:, D:], weight_kv[1], NT)
    grad_prior = grad_prior.reshape(prior_flag.shape[0], NEIGH * RET, D)
    from_next = shifted(grad_prior[:1].astype(BF), "seq", -1).astype(jnp.float32)
    encoded_grad = jnp.concatenate([grad_prior[1:], from_next], 0).reshape(-1, D)
    back, gain_grad = norm_back(stream, norm_gain, dot(grad_queries, weight_q, NT))
    pairs = ((inputs, grad_queries), (prior_enc, grad_pairs), (mixed, grad_low))
    return upstream + back, gain_grad, pairs, encoded_grad


def on_device(
    tokens,
    retrieved,
    span_doc,
    neigh_doc,
    cotangent,
    dec_gain,
    dec_qkv,
    dec_out,
    dec_in,
    dec_down,
    cca_gain,
    cca_q,
    cca_kv,
    cca_out,
    enc_gain,
    enc_in,
    enc_down,
    enc_final,
):
    assert tokens.shape[0] == 1
    rows = cca_q.shape[0]
    own_gains = jnp.concatenate([dec_gain.reshape(4, rows), cca_gain[None], enc_gain, enc_final[None]], 0).T
    own_gains = jnp.pad(own_gains, ((0, 0), (0, 120)))
    neighbours = retrieved.reshape(-1, D)
    full = gather_weights(
        neighbours, enc_in, enc_down, dec_qkv, dec_out, dec_in, dec_down, cca_q, cca_kv, cca_out, own_gains
    )
    gains = full["gains"].T
    attn_gain, ffn_gain = (gains[0:1], gains[2:3]), (gains[1:2], gains[3:4])
    cross_gain, encode_gain, final_gain = gains[4:5], (gains[5:6], gains[6:7]), gains[7:8]
    cross_weights = (cross_gain, full["cca_q"], full["cca_kv"], full["cca_out"])
    queries = tokens.shape[1]
    bias = causal_bias(queries, queries * lax.axis_size("seq"))

    encoder, encoder_kept, encoded = full["encoder"]
    encoded = encoded.reshape(span_doc.shape[1], NEIGH * RET, D)
    keep_flag = (neigh_doc[0] != span_doc[0][:, None]).astype(BF)

    stream = tokens[0].astype(jnp.float32)
    attn_kept, ffn_kept = [], []
    for layer in range(DEC_LAYERS):
        stream, kept = self_forward(stream, attn_gain[layer], full["dec_qkv"][layer], full["dec_out"][layer], bias)
        attn_kept.append(kept)
        if layer == 0:
            stream, cross_kept = cross_forward(stream, encoded, keep_flag, *cross_weights)
        before = stream
        if full["dec_in"][layer] is None:
            late, tall = full["dec_down"][layer], dec_down.shape[1]
            spread = spread_matrix(late.shape[0])
            stream, inputs, hidden, slope = late_ffn(before, ffn_gain[layer], spread, late, tall)
        else:
            stream, inputs, hidden, slope = ffn(before, ffn_gain[layer], full["dec_in"][layer], full["dec_down"][layer])
        ffn_kept.append((before, inputs, hidden, slope))
    result = stream.astype(BF)

    upstream = cotangent[0].astype(jnp.float32)
    attn_gain_g, ffn_gain_g = [None] * DEC_LAYERS, [None] * DEC_LAYERS
    attn_pairs, ffn_pairs = [None] * DEC_LAYERS, [None] * DEC_LAYERS
    for layer in reversed(range(DEC_LAYERS)):
        before, inputs, hidden, slope = ffn_kept[layer]
        if full["dec_in"][layer] is None:
            back = late_ffn_back(upstream, before, ffn_gain[layer], slope, spread, late, tall)
        else:
            back = ffn_back(upstream, before, ffn_gain[layer], slope, full["dec_in"][layer], full["dec_down"][layer])
        upstream, grad_low, grad_pre, ffn_gain_g[layer] = back
        ffn_pairs[layer] = ((inputs, grad_pre), (grad_low, hidden))
        if layer == 0:
            upstream, cross_gain_g, cross_pairs, encoded_grad = cross_back(cross_kept, *cross_weights, upstream)
        upstream, attn_gain_g[layer], attn_pairs[layer] = self_back(
            attn_kept[layer], attn_gain[layer], full["dec_qkv"][layer], full["dec_out"][layer], bias, upstream, layer == 0
        )

    enc_upstream, final_gain_g = norm_back(encoder, final_gain, encoded_grad)
    enc_gain_g, enc_pairs = [None] * ENC_LAYERS, [None] * ENC_LAYERS
    for layer in reversed(range(ENC_LAYERS)):
        before, inputs, hidden, slope = encoder_kept[layer]
        enc_upstream, grad_low, grad_pre, enc_gain_g[layer] = ffn_back(
            enc_upstream, before, encode_gain[layer], slope, full["enc_in"][layer], full["enc_down"][layer]
        )
        enc_pairs[layer] = ((inputs, grad_pre), (grad_low, hidden))

    pair_list = []
    for layer in range(DEC_LAYERS):
        pair_list += list(attn_pairs[layer]) + list(ffn_pairs[layer])
    pair_list += list(cross_pairs)
    for layer in range(ENC_LAYERS):
        pair_list += list(enc_pairs[layer])
    gain_list = []
    for layer in range(DEC_LAYERS):
        gain_list += [attn_gain_g[layer], ffn_gain_g[layer]]
    gain_list = [gain.reshape(D) for gain in gain_list + [cross_gain_g] + enc_gain_g + [final_gain_g]]

    grads = sum_gradients(pair_list, gain_list, rows)
    (enc_in_g, enc_down_g, dec_qkv_g, dec_out_g, dec_in_g, dec_down_g, cross_q_g, cross_kv_g, cross_out_g, gain_cols) = grads
    gain_rows = gain_cols[:, :8].T
    return (
        result[None],
        upstream[None],
        gain_rows[:4].reshape(2, 2, rows),
        dec_qkv_g,
        dec_out_g,
        dec_in_g,
        jnp.swapaxes(dec_down_g, 1, 2),
        gain_rows[4],
        cross_q_g,
        cross_kv_g,
        cross_out_g,
        gain_rows[5:7],
        enc_in_g,
        jnp.swapaxes(enc_down_g, 1, 2),
        gain_rows[7],
    )


def sum_plainly(pair_list, gain_list):
    blocks = [slab_term(left, right) for left, right in pair_list] + [vector[:, None] for vector in gain_list]
    owned = lax.psum_scatter(
        jnp.concatenate(blocks, 1).astype(BF), ("dp", "seq"), scatter_dimension=0, tiled=True
    ).astype(jnp.float32)
    pieces, cursor = [], 0
    for _, right in pair_list:
        pieces.append(owned[:, cursor : cursor + right.shape[-1]])
        cursor += right.shape[-1]
    two = lambda first, second: jnp.stack([pieces[first], pieces[second]])
    return [
        two(11, 13), two(12, 14), two(0, 4), two(1, 5), two(2, 6), two(3, 7), pieces[8], pieces[9], pieces[10], owned[:, cursor:]
    ]


def sum_gradients(pair_list, gain_list, rows):
    sizes = grid_sizes()
    if rows % 4 or sizes != (4, 2, 2, 2):
        return sum_plainly(pair_list, gain_list)
    operands = [x.reshape(-1, x.shape[-1]) for pair in pair_list for x in pair]
    gains = jnp.pad(jnp.stack(gain_list).astype(BF).T, ((0, 0), (0, 128 - len(gain_list))))
    return reduce_gradients(operands, gains, rows)


def solution(mesh):
    return jax.shard_map(
        on_device,
        mesh=mesh,
        in_specs=(
            P("dp", "seq", None),
            P("dp", "seq", None, None, None),
            P("dp", "seq"),
            P("dp", "seq", None),
            P("dp", "seq", None),
            P(None, None, ("dp", "seq")),
            P(None, ("dp", "seq"), None),
            P(None, ("dp", "seq"), None),
            P(None, ("dp", "seq"), None),
            P(None, ("dp", "seq"), None),
            P(("dp", "seq")),
            P(("dp", "seq"), None),
            P(("dp", "seq"), None),
            P(("dp", "seq"), None),
            P(None, ("dp", "seq")),
            P(None, ("dp", "seq"), None),
            P(None, ("dp", "seq"), None),
            P(("dp", "seq")),
        ),
        out_specs=(
            P("dp", "seq", None),
            P("dp", "seq", None),
            P(None, None, ("dp", "seq")),
            P(None, ("dp", "seq"), None),
            P(None, ("dp", "seq"), None),
            P(None, ("dp", "seq"), None),
            P(None, None, ("dp", "seq")),
            P(("dp", "seq")),
            P(("dp", "seq"), None),
            P(("dp", "seq"), None),
            P(("dp", "seq"), None),
            P(None, ("dp", "seq")),
            P(None, ("dp", "seq"), None),
            P(None, None, ("dp", "seq")),
            P(("dp", "seq")),
        ),
        check_vma=False,
    )
```

```python
import functools
import heapq
import jax
import jax.numpy as jnp
from jax import lax
from jax.experimental import pallas as pl
from jax.experimental.pallas import tpu as pltpu
from jax.sharding import PartitionSpec as P

D = 896
FF = 3584
HEADS = 14
HEAD = 64
SPAN = 64
NEIGH = 2
RET = 128
ENC_LAYERS = 2
DEC_LAYERS = 2
EPSILON = 1e-06
SCORE_SCALE = 0.125
MASKED_SCORE = -1000000000.0
BF = jnp.bfloat16
MESH_ID = pl.DeviceIdType.MESH
ANY = pl.BlockSpec(memory_space=pl.ANY)


def grid_sizes():
    return (lax.axis_size("dp"), lax.axis_size("seq") // 4, 2, 2)


def grid_place():
    seq = lax.axis_index("seq")
    return (lax.axis_index("dp"), seq // 4, (seq // 2) % 2, seq % 2)


def device_at(place):
    z, y, x, core = place
    return (z, (y * 2 + x) * 2 + core)


def moved(place, sizes, axis, by):
    size = sizes[axis]
    there = lax.rem(place[axis] + (by % size), size)
    return place[:axis] + (there,) + place[axis + 1 :]


def greet(place, sizes):
    barrier = pltpu.get_barrier_semaphore()
    for axis in range(4):
        size, here = sizes[axis], place[axis]
        for by in (1, -1):
            there = here + by

            @pl.when(inside(there, size))
            def _():
                other = place[:axis] + (jnp.clip(there, 0, size - 1),) + place[axis + 1 :]
                pl.semaphore_signal(barrier, inc=1, device_id=device_at(other), device_id_type=MESH_ID)

    count = 0
    for axis in range(4):
        for by in (1, -1):
            count = count + inside(place[axis] + by, sizes[axis]).astype(jnp.int32)
    pl.semaphore_wait(barrier, count)


class Hop:
    def __init__(self, copy, sends, receives):
        self.copy, self.sends, self.receives = copy, sends, receives

    def start(self):
        pl.when(self.sends)(self.copy[0].start)

    def wait(self):
        pl.when(self.sends)(self.copy[0].wait_send)
        pl.when(self.receives)(self.copy[1].wait_recv)


def inside(place, size):
    return jnp.logical_and(place >= 0, place < size)


ZYX, ZXY, YZX, XZY, YXZ, XYZ = (0, 1, 2), (0, 2, 1), (1, 0, 2), (2, 0, 1), (1, 2, 0), (2, 1, 0)
ROUTES = (YXZ, ZYX, ZXY, ZYX, ZXY, ZXY, YZX, ZXY, ZYX, ZYX)
ROUTES += (ZXY, XZY, ZYX, YZX, XZY, XZY, YZX, YXZ, XYZ)
UNIT_US, HOP_US, CORE_US = 2.2, 2.5, 0.17


def schedule(pieces, routes, sizes):
    chains = []
    for number, piece in enumerate(pieces):
        scale, held, chain = piece[3] / PIECE, 1, []
        for axis in routes[number]:
            chain += [(axis, held * UNIT_US * scale)] * (sizes[axis] - 1)
            held *= sizes[axis]
        chains.append(chain + [(3, held * CORE_US * scale)])
    free, flying, ready = [0.0] * 4, [0] * 4, [[] for _ in range(4)]
    for number, chain in enumerate(chains):
        heapq.heappush(ready[chain[0][0]], (number, number, 0))
    now, events, order = 0.0, [], []
    while True:
        for link in range(4):
            while ready[link] and flying[link] < 2:
                _, number, step = heapq.heappop(ready[link])
                free[link] = max(free[link], now) + chains[number][step][1]
                flying[link] += 1
                order.append(("start", number, step, now))
                heapq.heappush(events, (free[link] + HOP_US, number, step, link))
        if not events:
            return order
        now, number, step, link = heapq.heappop(events)
        flying[link] -= 1
        order.append(("wait", number, step, now))
        if step + 1 < len(chains[number]):
            heapq.heappush(ready[chains[number][step + 1][0]], (number, number, step + 1))


PIECE = 896


def narrow_groups():
    qkv = 3 * D
    wide = FF // 2
    whole = lambda arg, layer: [[(arg, layer, 0, wide)], [(arg, layer, wide, wide)]]
    return [
        whole(0, 0),
        whole(0, 1),
        [
            [(7, None, 0, D), (6, None, 0, D), (2, 0, 0, qkv), (3, 0, 0, D)],
            [(7, None, D, D), (8, None, 0, D), (2, 1, 0, qkv), (3, 1, 0, D)],
        ],
        whole(4, 0),
        [[(9, None, 0, 128)], [(9, None, 0, 128)]],
    ]


def half_width(group):
    return sum(part[3] for part in group[0])


def gather_plan():
    groups = narrow_groups()
    starts, cursor = [], 0
    for group in groups:
        starts.append(cursor)
        cursor += half_width(group)
    pieces = []
    for kind, number in (("n", 4), ("n", 0), ("r", 0), ("n", 1), ("r", 1), ("n", 2), ("n", 3), ("r", 2)):
        if kind == "n":
            width = half_width(groups[number])
            for first in range(0, width, PIECE):
                pieces.append((kind, number, first, min(PIECE, width - first)))
        else:
            pieces.append((kind, number, 0, D))
            pieces.append((kind, number, 1, D))
    return groups, starts, cursor, pieces


N_GROUPS = 5
N_TALL = 3


def gather_kernel(sizes, *refs):
    groups, starts, _, pieces = gather_plan()
    ins, neighbours = refs[:10], refs[10]
    n_outs = N_GROUPS + N_TALL
    outs, encoder_outs, late_out = refs[11 : 11 + n_outs], refs[11 + n_outs : 20 + n_outs], refs[20 + n_outs]
    halves, other, joined, own_rows, send_sem, recv_sem, load_sem, swap_sem = refs[21 + n_outs : 29 + n_outs]
    late_in, late_down, late, late_sem = refs[29 + n_outs : 33 + n_outs]
    encoder_rooms = refs[33 + n_outs :]
    place = grid_place()
    z, y, x, core = place
    sibling = device_at(moved(place, sizes, 3, 1))
    loads = []
    for number, group in enumerate(groups):
        for half in range(2):
            cursor = starts[number]
            for arg, layer, first, size in group[half]:
                source = ins[arg] if layer is None else ins[arg].at[layer]
                loads.append((source.at[:, pl.ds(first, size)], halves.at[half, :, pl.ds(cursor, size)]))
                cursor += size
    for number, (arg, layer) in enumerate(((1, 0), (1, 1), (5, 0))):
        for part in range(2):
            loads.append((ins[arg].at[layer, part], own_rows.at[2 * number + part]))
    late_loads = [
        pltpu.make_async_copy(ins[4].at[1], late_in, late_sem.at[0]),
        pltpu.make_async_copy(ins[5].at[1], late_down, late_sem.at[1]),
    ]
    late_store = pltpu.make_async_copy(late, late_out, late_sem.at[2])

    def late_unit():
        for copy in late_loads:
            copy.wait()
        down = late_down[...].astype(jnp.float32).reshape(-1, D)
        fill = jnp.zeros((4 * ROOM - down.shape[0], D), jnp.float32)
        late[pl.ds(0, 4 * ROOM), :] = jnp.concatenate([down, fill], 0).astype(BF)
        fill = jnp.zeros((ROOM - late_in.shape[0], D), jnp.float32)
        for k in range(FF // D):
            rows = late_in[:, pl.ds(k * D, D)].astype(jnp.float32)
            late[pl.ds((4 + k) * ROOM, ROOM), :] = jnp.concatenate([rows, fill], 0).astype(BF)
        late_store.start()

    started = []
    for copy in late_loads:
        copy.start()
    for k, (source, target) in enumerate(loads):
        copy = pltpu.make_async_copy(source, target, load_sem.at[k])
        copy.start()
        started.append(copy)
    greet(place, sizes)
    for copy in started:
        copy.wait()
    placed = []
    for number in range(N_TALL):
        for part in range(2):
            k = 2 * number + part
            target = outs[N_GROUPS + number].at[z, y, x, core, part]
            placed.append(pltpu.make_async_copy(own_rows.at[k], target, load_sem.at[len(loads) + len(groups) + k]))
            placed[-1].start()
    swaps = []
    for number, group in enumerate(groups):
        columns = pl.ds(starts[number], half_width(group))
        copy = pltpu.make_async_remote_copy(
            src_ref=halves.at[1 - core, :, columns],
            dst_ref=other.at[:, columns],
            send_sem=swap_sem.at[0, number],
            recv_sem=swap_sem.at[1, number],
            device_id=sibling,
            device_id_type=MESH_ID,
        )
        copy.start()
        swaps.append(copy)

    def view(piece, where):
        kind, number, first, size = piece
        iz, iy, ix = where[:3]
        if kind == "n":
            start = pl.multiple_of(core * half_width(groups[number]) + first, 128)
            return outs[number].at[iz, iy, ix, :, pl.ds(start, size)]
        return outs[N_GROUPS + number].at[iz, iy, ix, core, first]

    prepared = {}

    def prepare(piece):
        kind, number, first, size = piece
        if kind == "n" and number not in prepared:
            swaps[number].wait()
            group = groups[number]
            for begin in range(starts[number], starts[number] + half_width(group), 128):
                columns = pl.ds(begin, 128)
                mine = halves[core, :, columns].astype(jnp.float32)
                theirs = other[:, columns].astype(jnp.float32)
                both = [jnp.where(core == 0, mine, theirs), jnp.where(core == 0, theirs, mine)]
                joined[:, columns] = jnp.concatenate(both, 0).astype(BF)
            width = half_width(group)
            copy = pltpu.make_async_copy(
                joined.at[:, pl.ds(starts[number], width)],
                outs[number].at[z, y, x, :, pl.ds(pl.multiple_of(core * width, 128), width)],
                load_sem.at[len(loads) + number],
            )
            copy.start()
            copy.wait()
            prepared[number] = True
        elif kind == "r" and "r" not in prepared:
            for copy in placed:
                copy.wait()
            prepared["r"] = True

    semaphores = [0]

    def transfers(number):
        piece = pieces[number]
        steps, done = [], []
        for axis in routes[number] + (3,):
            size, here = sizes[axis], place[axis]

            def block(at):
                where = list(place)
                for old in done:
                    where[old] = slice(None)
                where[axis] = jnp.clip(at, 0, size - 1)
                return view(piece, where)

            for hop in range(1, size):
                hops = []
                for way in (1, -1):
                    ahead, behind = here + way, here - way
                    sent, got = here - way * (hop - 1), here - way * hop
                    if size == 2 and way == -1:
                        continue
                    if size == 2:
                        ahead, behind, got = 1 - here, 1 - here, 1 - here
                    pair = []
                    for at, other_end in ((sent, ahead), (got, behind)):
                        ref = block(at)
                        target = place[:axis] + (jnp.clip(other_end, 0, size - 1),) + place[axis + 1 :]
                        pair.append(
                            pltpu.make_async_remote_copy(
                                src_ref=ref,
                                dst_ref=ref,
                                send_sem=send_sem.at[semaphores[0]],
                                recv_sem=recv_sem.at[semaphores[0]],
                                device_id=device_at(target),
                                device_id_type=MESH_ID,
                            )
                        )
                    semaphores[0] += 1
                    sends = jnp.logical_and(inside(sent, size), inside(ahead, size))
                    hops.append(Hop(pair, sends, inside(got, size)))
                steps.append(hops)
            done.append(axis)
        return steps

    routes = [ROUTES[number % len(ROUTES)] for number in range(len(pieces))]
    running = [transfers(number) for number in range(len(pieces))]
    units = encoder_units(
        neighbours, outs[N_GROUPS - 1], (outs[0], outs[1]), (outs[N_GROUPS], outs[N_GROUPS + 1]), encoder_outs, encoder_rooms
    )
    units.insert(0, late_unit)
    needs = [{k for k, piece in enumerate(pieces) if piece[:2] in wanted} for wanted in [set()] + UNIT_NEEDS]
    due, arrived = 0.0, set()
    for what, number, step, time in schedule(pieces, routes, sizes):
        if what == "wait":
            for copy in running[number][step]:
                copy.wait()
            if step + 1 == len(running[number]):
                arrived.add(number)
        else:
            prepare(pieces[number])
            for copy in running[number][step]:
                copy.start()
        if units and time >= due and needs[len(needs) - len(units)] <= arrived:
            units.pop(0)()
            due = time + UNIT_TIME
    for unit in units:
        unit()
    late_store.wait()


ROOM = 32


HIDDEN_UNITS = 4
UNIT_TIME = 7.0
GAINS, FIRST, SECOND = {("n", 4)}, {("n", 0), ("r", 0)}, {("n", 1), ("r", 1)}
UNIT_NEEDS = [GAINS | FIRST] * (1 + HIDDEN_UNITS) + [SECOND] * (1 + HIDDEN_UNITS) + [set()]


def encoder_units(neighbours, gain_columns, weights_in, weights_down, outs, rooms):
    after, inputs_out, hidden_out, slope_out, encoded_out = outs[0:2], outs[2:4], outs[4:6], outs[6:8], outs[8]
    stream, inputs, columns, gain_rows, block_in, block_down, hidden, slope, sems = rooms
    block = FF // HIDDEN_UNITS

    def flat(values, rows):
        return values.astype(jnp.float32).reshape(rows, values.shape[-1])

    def weights(layer, k):
        slot = k % 2
        return [
            pltpu.make_async_copy(weights_in[layer].at[:, :, :, :, pl.ds(k * block, block)], block_in.at[slot], sems.at[0, slot]),
            pltpu.make_async_copy(weights_down[layer].at[k], block_down.at[slot], sems.at[1, slot]),
        ]

    def results(layer, k):
        slot = k % 2
        place = pl.ds(k * block, block)
        return [
            pltpu.make_async_copy(hidden.at[slot], hidden_out[layer].at[:, place], sems.at[2, slot]),
            pltpu.make_async_copy(slope.at[slot], slope_out[layer].at[:, place], sems.at[3, slot]),
        ]

    def stream_copy(layer):
        return pltpu.make_async_copy(stream, after[layer], sems.at[4, layer])

    def inputs_copy(layer):
        return pltpu.make_async_copy(inputs, (*inputs_out, encoded_out)[layer], sems.at[5, layer % 2])

    def norm_unit(layer):
        if layer == 0:
            first = pltpu.make_async_copy(neighbours, inputs, sems.at[6, 0])
            second = pltpu.make_async_copy(gain_columns.at[:, :, :, :, pl.ds(0, 128)], columns, sems.at[6, 1])
            first.start()
            second.start()
            first.wait()
            second.wait()
            gain_rows[...] = flat(columns[...], D).T
            stream[...] = inputs[...].astype(jnp.float32)
        else:
            for k in (HIDDEN_UNITS - 2, HIDDEN_UNITS - 1):
                for copy in results(layer - 1, k):
                    copy.wait()
            inputs_copy(layer - 1).wait()
            stream_copy(layer - 1).start()
        if layer < ENC_LAYERS:
            for copy in weights(layer, 0):
                copy.start()
        gain = gain_rows[5 + layer : 6 + layer, :]
        inputs[...] = (norm_parts(stream[...])[0] * gain).astype(BF)
        inputs_copy(layer).start()
        if layer == ENC_LAYERS:
            stream_copy(layer - 1).wait()
            inputs_copy(layer).wait()

    def hidden_unit(layer, k):
        slot = k % 2
        if k + 1 < HIDDEN_UNITS:
            for copy in weights(layer, k + 1):
                copy.start()
        for copy in weights(layer, k):
            copy.wait()
        if k >= 2:
            for copy in results(layer, k - 2):
                copy.wait()
        value, rate = gelu_parts(dot(inputs[...], flat(block_in[slot], D).astype(BF), NN))
        hidden[slot] = value.astype(BF)
        slope[slot] = rate.astype(BF)
        for copy in results(layer, k):
            copy.start()
        if k == 0 and layer > 0:
            stream_copy(layer - 1).wait()
        stream[...] += dot(hidden[slot], flat(block_down[slot], block).astype(BF), NN)

    units = []
    for layer in range(ENC_LAYERS):
        units.append(functools.partial(norm_unit, layer))
        for k in range(HIDDEN_UNITS):
            units.append(functools.partial(hidden_unit, layer, k))
    units.append(functools.partial(norm_unit, ENC_LAYERS))
    return units


def gather_plainly(neighbours, enc_in, enc_down, dec_qkv, dec_out, dec_in, dec_down, cca_q, cca_kv, cca_out, gains):
    get = lambda w: lax.all_gather(w, ("dp", "seq"), axis=w.ndim - 2, tiled=True)
    kv = get(cca_kv)
    enc_in, enc_down, columns = get(enc_in), get(enc_down), get(gains)[:, :8]
    stream, kept = neighbours, []
    for layer in range(ENC_LAYERS):
        gain = columns[:, 5 + layer][None]
        after, inputs, hidden, slope = ffn(stream, gain, enc_in[layer], enc_down[layer])
        kept.append((stream, inputs, hidden, slope))
        stream = after
    return dict(
        encoder=(stream, kept, normed(stream, columns[:, 7][None])),
        enc_in=enc_in, enc_down=enc_down, dec_in=get(dec_in), dec_down=get(dec_down), dec_qkv=get(dec_qkv),
        dec_out=get(dec_out), cca_kv=[kv[:, :D], kv[:, D:]], cca_q=get(cca_q), cca_out=get(cca_out), gains=columns,
    )


def gather_weights(neighbours, enc_in, enc_down, dec_qkv, dec_out, dec_in, dec_down, cca_q, cca_kv, cca_out, gains):
    sizes = grid_sizes()
    rows = cca_q.shape[0]
    groups, starts, total, pieces = gather_plan()
    part = enc_down.shape[1] // 2
    if rows % 4 or part % 8 or sizes != (HIDDEN_UNITS, 2, 2, 2):
        return gather_plainly(neighbours, enc_in, enc_down, dec_qkv, dec_out, dec_in, dec_down, cca_q, cca_kv, cca_out, gains)
    lead = sizes[:3]
    shapes = [lead + (2 * rows, 2 * half_width(group)) for group in groups] + [lead + (2, 2, part, D)] * N_TALL
    out_shape = [jax.ShapeDtypeStruct(shape, BF) for shape in shapes]
    count = neighbours.shape[0]
    block = FF // HIDDEN_UNITS
    out_shape += [jax.ShapeDtypeStruct((count, D), jnp.float32)] * 2 + [jax.ShapeDtypeStruct((count, D), BF)] * 2
    out_shape += [jax.ShapeDtypeStruct((count, FF), BF)] * 4 + [jax.ShapeDtypeStruct((count, D), BF)]
    out_shape += [jax.ShapeDtypeStruct((8 * ROOM, D), BF)]
    per_piece = sum((size - 1) * (1 if size == 2 else 2) for size in sizes)
    n_loads = sum(len(half) for group in groups for half in group) + 4 * N_TALL + len(groups)
    split = lambda w: w.reshape(w.shape[0], 2, part, D)
    outs = pl.pallas_call(
        functools.partial(gather_kernel, sizes),
        out_shape=out_shape,
        in_specs=[ANY] * 11,
        out_specs=[ANY] * len(out_shape),
        scratch_shapes=[
            pltpu.VMEM((2, rows, total), BF),
            pltpu.VMEM((rows, total), BF),
            pltpu.VMEM((2 * rows, total), BF),
            pltpu.VMEM((2 * N_TALL, part, D), BF),
            pltpu.SemaphoreType.DMA((per_piece * len(pieces),)),
            pltpu.SemaphoreType.DMA((per_piece * len(pieces),)),
            pltpu.SemaphoreType.DMA((n_loads,)),
            pltpu.SemaphoreType.DMA((2, len(groups))),
            pltpu.VMEM((rows, FF), BF),
            pltpu.VMEM((2, part, D), BF),
            pltpu.VMEM((8 * ROOM, D), BF),
            pltpu.SemaphoreType.DMA((3,)),
            pltpu.VMEM((count, D), jnp.float32),
            pltpu.VMEM((count, D), BF),
            pltpu.VMEM(lead + (2 * rows, 128), BF),
            pltpu.VMEM((128, D), jnp.float32),
            pltpu.VMEM((2,) + lead + (2 * rows, block), BF),
            pltpu.VMEM((2,) + sizes[1:3] + (2, 2, part, D), BF),
            pltpu.VMEM((2, count, block), BF),
            pltpu.VMEM((2, count, block), BF),
            pltpu.SemaphoreType.DMA((7, 2)),
        ],
        compiler_params=pltpu.CompilerParams(collective_id=0, has_side_effects=True, vmem_limit_bytes=56 << 20),
        name="gather_weights",
    )(enc_in, split(enc_down), dec_qkv, dec_out, dec_in, split(dec_down), cca_q, cca_kv, cca_out, gains, neighbours)
    narrow = [out.reshape(D, out.shape[-1]) for out in outs[:N_GROUPS]]
    tall = [out.reshape(FF, D) for out in outs[N_GROUPS : N_GROUPS + N_TALL]]
    first, second, inputs_0, inputs_1, hidden_0, hidden_1, slope_0, slope_1, encoded, late = outs[N_GROUPS + N_TALL :]
    late = lax.all_gather(late, ("dp", "seq"), axis=0, tiled=False)
    kept = [(neighbours, inputs_0, hidden_0, slope_0), (first, inputs_1, hidden_1, slope_1)]
    mixed = narrow[2]
    half = mixed.shape[1] // 2
    sides = [mixed[:, :half], mixed[:, half:]]
    qkv = [side[:, 2 * D : 5 * D] for side in sides]
    out = [side[:, 5 * D : 6 * D] for side in sides]
    return dict(
        encoder=(second, kept, encoded),
        enc_in=narrow[:2], enc_down=tall[:2], dec_in=[narrow[3], None], dec_down=[tall[2], late], dec_qkv=qkv, dec_out=out,
        cca_kv=[side[:, :D] for side in sides], cca_q=sides[0][:, D : 2 * D], cca_out=sides[1][:, D : 2 * D],
        gains=narrow[4][:, :8],
    )


YZX_SUM, XZY_SUM, YXZ_SUM, XYZ_SUM = (1, False), (2, False), (1, True), (2, True)
ORDERS = (YZX_SUM, XZY_SUM, YZX_SUM, XZY_SUM, YXZ_SUM, XZY_SUM, YZX_SUM, XYZ_SUM, YZX_SUM, XZY_SUM, YXZ_SUM)
ORDERS += (XZY_SUM, YZX_SUM, XYZ_SUM, YZX_SUM, XZY_SUM, YXZ_SUM, XYZ_SUM, YZX_SUM, XYZ_SUM, YXZ_SUM, XYZ_SUM)
CORE, HEAVY, ZED, PAIR, CORE_AGAIN, PER_PIECE = 0, 1, 2, 8, 9, 10
START = (0, 1, 4, 6, 7, 8, 10, 11, 12)
SLOTS = dict(part=2, whole=5, half=8, sibling=3, heavy=8, middle=8, last=8, zed=7, final=4)


def gradient_pieces():
    pieces = []
    both = lambda left, right, out, layer, k: tuple(
        (left, right, 2 * D * half + D * k, out, layer, 2 * D * half + D * k) for half in range(2)
    )
    for layer in reversed(range(2)):
        base = 8 * layer
        for k in range(2):
            pieces.append(both(base + 6, base + 7, 5, layer, k))
        for k in range(2):
            pieces.append(both(base + 4, base + 5, 4, layer, k))
    pieces.append(tuple((8 * layer + 2, 8 * layer + 3, 0, 3, layer, 0) for layer in range(2)))
    for k in range(3):
        pieces.append(tuple((8 * layer, 8 * layer + 1, D * k, 2, layer, D * k) for layer in range(2)))
    pieces.append(((16, 17, 0, 6, None, 0), (20, 21, 0, 8, None, 0)))
    pieces.append(tuple((18, 19, D * half, 7, None, D * half) for half in range(2)))
    for layer in reversed(range(2)):
        base = 22 + 4 * layer
        for k in range(2):
            pieces.append(both(base + 2, base + 3, 1, layer, k))
        for k in range(2):
            pieces.append(both(base, base + 1, 0, layer, k))
    return pieces


N_OPERANDS = 30


class Sums:
    def __init__(self, place, sizes, sems, buffers, slots, width):
        self.place, self.sizes, self.width = place, sizes, width
        self.send_sem, self.recv_sem = sems
        self.part, self.whole, self.half, self.sibling, self.heavy, self.middle, self.last, self.zed, self.final = buffers
        self.slots = slots

    def slot(self, name, number):
        return lax.rem(number, self.slots[name])

    def copy(self, number, which, source, target, device):
        index = number * PER_PIECE + which
        return pltpu.make_async_remote_copy(
            src_ref=source,
            dst_ref=target,
            send_sem=self.send_sem.at[index],
            recv_sem=self.recv_sem.at[index],
            device_id=device_at(device),
            device_id_type=MESH_ID,
        )

    def core_copy(self, number):
        return self.copy(
            number,
            CORE,
            self.part.at[self.slot("part", number)],
            self.sibling.at[self.slot("sibling", number)],
            self.swapped(3),
        )

    def swapped(self, axis):
        return self.place[:axis] + (1 - self.place[axis],) + self.place[axis + 1 :]

    def heavy_copy(self, number, axis):
        whole = self.whole.at[self.slot("whole", number)]
        there = 1 - self.place[axis]
        source = whole.at[:, there] if axis == 1 else whole.at[:, :, there]
        return self.copy(number, HEAVY, source, self.heavy.at[self.slot("heavy", number)], self.swapped(axis))

    def pair_copy(self, number, axis, early):
        half = self.half.at[self.slot("half", number)]
        there = 1 - self.place[axis]
        if early:
            source, target = half.at[:, there], self.middle.at[self.slot("middle", number)]
        else:
            source, target = half.at[self.place[0], there], self.last.at[self.slot("last", number)]
        return self.copy(number, PAIR, source, target, self.swapped(axis))

    def zed_block(self, number, axis, early, at):
        half = self.half.at[self.slot("half", number)]
        at = jnp.clip(at, 0, self.sizes[0] - 1)
        return half.at[at, pl.ds(self.place[axis], 1)] if early else half.at[at]

    def zed_room(self, number, early, hop, way):
        room = self.zed.at[self.slot("zed", number), hop - 1, way]
        return room.at[pl.ds(0, 1)] if early else room

    def zed_hops(self, number, axis, early, hop):
        z, size = self.place[0], self.sizes[0]
        found = []
        for way, by in enumerate((-1, 1)):
            sent, ahead = z + by * hop, z + by
            behind, got = z - by, z - by + by * hop
            room = self.zed_room(number, early, hop, way)
            device = (jnp.clip(ahead, 0, size - 1),) + self.place[1:]
            copy = self.copy(number, ZED + 2 * (hop - 1) + way, self.zed_block(number, axis, early, sent), room, device)
            sends = jnp.logical_and(inside(sent, size), inside(ahead, size))
            receives = jnp.logical_and(inside(got, size), inside(behind, size))
            found.append((copy, sends, receives, self.zed_block(number, axis, early, got), room))
        return found

    def start_zed(self, number, axis, early, hop):
        for copy, sends, _, _, _ in self.zed_hops(number, axis, early, hop):
            pl.when(sends)(copy.start)

    def finish_zed(self, number, axis, early, hop):
        for copy, sends, receives, block, room in self.zed_hops(number, axis, early, hop):
            pl.when(sends)(copy.wait_send)

            @pl.when(receives)
            def _():
                copy.wait_recv()
                for k in range(1 if early else 2):
                    block[k] = block[k] + room[k]

    def add_core(self, number):
        self.core_copy(number).wait()
        whole, sibling = self.slot("whole", number), self.slot("sibling", number)

        def one(k, _):
            at = (k // 4, (k // 2) % 2, k % 2)
            self.whole[(whole, *at)] = self.whole[(whole, *at)] + self.sibling[(sibling, *at)]
            return 0

        lax.fori_loop(0, 4 * self.sizes[0], one, 0)

    def add_heavy(self, number, axis):
        self.heavy_copy(number, axis).wait()
        whole, half, heavy = (self.slot(name, number) for name in ("whole", "half", "heavy"))

        def one(k, _):
            z, o = k // 2, k % 2
            at = (z, self.place[1], o) if axis == 1 else (z, o, self.place[2])
            self.half[half, z, o] = self.whole[(whole, *at)] + self.heavy[heavy, z, o]
            return 0

        lax.fori_loop(0, 2 * self.sizes[0], one, 0)

    def add_pair(self, number, axis, early):
        self.pair_copy(number, axis, early).wait()
        half, here = self.slot("half", number), self.place[axis]
        if early:
            for z in range(self.sizes[0]):
                self.half[half, z, here] = self.half[half, z, here] + self.middle[self.slot("middle", number), z]
        else:
            z = self.place[0]
            self.half[half, z, here] = self.half[half, z, here] + self.last[self.slot("last", number)]

    def split_rows(self, number, axis):
        half, final = self.slot("half", number), self.slot("final", number)
        rows = self.half[half, self.place[0], self.place[axis]].astype(jnp.float32)
        count = rows.shape[0] // 2
        first, second = rows[:count], rows[count:]
        self.final[final, 0] = jnp.where(self.place[3] == 0, first, second)
        self.final[final, 2] = jnp.where(self.place[3] == 0, second, first)

    def final_copy(self, number):
        final = self.slot("final", number)
        return self.copy(number, CORE_AGAIN, self.final.at[final, 2], self.final.at[final, 1], self.swapped(3))

    def step(self, step, number, first, early):
        other = 3 - first
        sequence = [("pair", 0), ("zed", 3), ("zed", 2), ("zed", 1)] if early else [("zed", 3), ("zed", 2), ("zed", 1), ("pair", 0)]
        if step == 1:
            self.heavy_copy(number, first).start()
            return
        if step == 2:
            self.add_heavy(number, first)
        else:
            kind, hop = sequence[step - 3]
            if kind == "pair":
                self.add_pair(number, other, early)
            else:
                self.finish_zed(number, other, early, hop)
        if step < 6:
            kind, hop = sequence[step - 2]
            if kind == "pair":
                self.pair_copy(number, other, early).start()
            else:
                self.start_zed(number, other, early, hop)
        else:
            self.split_rows(number, other)
            self.final_copy(number).start()


def reduce_kernel(sizes, tall, *refs):
    pieces = gradient_pieces()
    operands, gains = refs[:N_OPERANDS], refs[N_OPERANDS]
    outs = refs[N_OPERANDS + 1 : N_OPERANDS + 11]
    scratch = refs[N_OPERANDS + 11 :]
    left, right, product = scratch[:3]
    buffers, small = scratch[3:12], scratch[12:21]
    send_sem, recv_sem, small_send, small_recv, load_sem, out_sem = scratch[21:]
    place = grid_place()
    core = place[3]
    count = len(pieces)
    sums = Sums(place, sizes, (send_sem, recv_sem), buffers, SLOTS, D)
    once = Sums(place, sizes, (small_send, small_recv), small, {name: 1 for name in SLOTS}, 128)
    is_tall = [tall[piece[0][0]] for piece in pieces]
    first_tall = is_tall.index(True)
    long_rows, short_rows = left.shape[2], None

    def rows_of(k):
        return operands[pieces[k][0][0]].shape[0]

    def loads(k, slot):
        rows = rows_of(k)
        found = []
        for half in range(2):
            l, r, column, _, _, _ = pieces[k][half]
            mine = jnp.where(core == half, 1, 0)
            found.append((operands[l], left.at[slot, mine, pl.ds(0, rows)], load_sem.at[slot, half]))
            found.append((operands[r].at[:, pl.ds(column, D)], right.at[slot, mine, pl.ds(0, rows)], load_sem.at[slot, 2 + half]))
        return [pltpu.make_async_copy(*args) for args in found]

    def start_loads(number):
        for k in range(count):

            @pl.when(number == k)
            def _():
                for copy in loads(k, k % 2):
                    copy.start()

    def multiply(number, which, rows):
        slot = lax.rem(number, 2)

        def block(k, _):
            columns = pl.ds(pl.multiple_of(k * 128, 128), 128)
            product[pl.ds(pl.multiple_of(k * 128, 128), 128), :] = lax.dot_general(
                left[slot, which, pl.ds(0, rows), columns],
                right[slot, which, pl.ds(0, rows), :],
                (((0,), (0,)), ((), ())),
                preferred_element_type=jnp.float32,
            )
            return 0

        lax.fori_loop(0, D // 128, block, 0)
        chunk = sums.whole.shape[4]

        def store(k, _):
            values = product[pl.ds(pl.multiple_of(k * chunk, 8), chunk), :].astype(BF)
            at = (k // 4, (k // 2) % 2, k % 2)
            if which == 0:
                sums.part[(sums.slot("part", number), *at)] = values
            else:
                sums.whole[(sums.slot("whole", number), *at)] = values
            return 0

        lax.fori_loop(0, D // chunk, store, 0)

    def compute(number):
        for flag in sorted(set(is_tall)):
            wanted = jnp.logical_and(number >= first_tall, flag) if flag else number < first_tall
            k = first_tall if flag else 0

            @pl.when(wanted)
            def _():
                for copy in loads(k, lax.rem(number, 2)):
                    copy.wait()
                multiply(number, 0, rows_of(k))
                sums.core_copy(number).start()
                multiply(number, 1, rows_of(k))

    def out_copies(k):
        slot = k % SLOTS["final"]
        found = []
        for half in range(2):
            _, _, _, out, layer, column = pieces[k][half]
            target = outs[out] if layer is None else outs[out].at[layer]
            source = sums.final.at[slot, jnp.where(core == half, 0, 1)]
            found.append(pltpu.make_async_copy(source, target.at[:, pl.ds(column, D)], out_sem.at[slot, half]))
        return found

    greet(place, sizes)
    small_loads = []
    for k, target in enumerate((once.part.at[0], once.whole.at[0])):
        copy = pltpu.make_async_copy(gains, target, out_sem.at[SLOTS["final"], k])
        copy.start()
        small_loads.append(copy)
    start_loads(0)

    def tick(time, _):
        for step in reversed(range(8)):

            @pl.when(time == START[step])
            def _():
                if step == 0:
                    for copy in small_loads:
                        copy.wait()
                    once.core_copy(0).start()
                elif step == 7:
                    once.final_copy(0).wait()
                    copy = pltpu.make_async_copy(once.final.at[0, 0], outs[9], out_sem.at[SLOTS["final"], 0])
                    copy.start()
                    copy.wait()
                else:
                    if step == 1:
                        once.add_core(0)
                    once.step(step, 0, *ORDERS[-1])

        for step in reversed(range(9)):
            number = time - START[step]

            @pl.when(jnp.logical_and(number >= 0, number < count))
            def _():
                if step == 0:
                    start_loads(number + 1)
                    compute(number)
                elif step == 8:
                    for copy in out_copies_at(number):
                        copy.wait()
                elif step == 7:
                    sums.final_copy(number).wait()
                    for k in range(count):

                        @pl.when(number == k)
                        def _():
                            for copy in out_copies(k):
                                copy.start()

                else:
                    if step == 1:
                        sums.add_core(number)
                    for order in sorted(set(ORDERS)):
                        here = functools.reduce(jnp.logical_or, [number == k for k, one in enumerate(ORDERS) if one == order])

                        @pl.when(here)
                        def _():
                            sums.step(step, number, *order)

        return 0

    def out_copies_at(number):
        slot = lax.rem(number, SLOTS["final"])
        return [
            pltpu.make_async_copy(sums.final.at[slot, 0], outs[3].at[0, :, pl.ds(0, D)], out_sem.at[slot, half])
            for half in range(2)
        ]

    lax.fori_loop(0, count + START[8], tick, 0)


def reduce_gradients(operands, gains, layers_rows):
    sizes = grid_sizes()
    rows = layers_rows
    chunk = 2 * rows
    lead = sizes[:3] + (chunk,)
    longest = max(x.shape[0] for x in operands)
    shortest = min(x.shape[0] for x in operands)
    tall = tuple(x.shape[0] == longest for x in operands)
    f32 = jnp.float32
    shapes = [(2, rows, FF), (2, rows, FF), (2, rows, 3 * D), (2, rows, D), (2, rows, FF), (2, rows, FF)]
    shapes += [(rows, D), (rows, 2 * D), (rows, D), (rows, 128)]

    def rooms(slots, width):
        z = sizes[0]
        return [
            pltpu.VMEM((slots["part"],) + lead + (width,), BF),
            pltpu.VMEM((slots["whole"],) + lead + (width,), BF),
            pltpu.VMEM((slots["half"], z, 2, chunk, width), BF),
            pltpu.VMEM((slots["sibling"],) + lead + (width,), BF),
            pltpu.VMEM((slots["heavy"], z, 2, chunk, width), BF),
            pltpu.VMEM((slots["middle"], z, chunk, width), BF),
            pltpu.VMEM((slots["last"], chunk, width), BF),
            pltpu.VMEM((slots["zed"], z - 1, 2, 2, chunk, width), BF),
            pltpu.VMEM((slots["final"], 3, rows, width), f32),
        ]

    count = len(gradient_pieces())
    return pl.pallas_call(
        functools.partial(reduce_kernel, sizes, tall),
        out_shape=[jax.ShapeDtypeStruct(shape, f32) for shape in shapes],
        in_specs=[ANY] * (N_OPERANDS + 1),
        out_specs=[ANY] * 10,
        scratch_shapes=[
            pltpu.VMEM((2, 2, longest, D), BF),
            pltpu.VMEM((2, 2, longest, D), BF),
            pltpu.VMEM((D, D), f32),
            *rooms(SLOTS, D),
            *rooms({name: 1 for name in SLOTS}, 128),
            pltpu.SemaphoreType.DMA((PER_PIECE * count,)),
            pltpu.SemaphoreType.DMA((PER_PIECE * count,)),
            pltpu.SemaphoreType.DMA((PER_PIECE,)),
            pltpu.SemaphoreType.DMA((PER_PIECE,)),
            pltpu.SemaphoreType.DMA((2, 4)),
            pltpu.SemaphoreType.DMA((SLOTS["final"] + 1, 2)),
        ],
        compiler_params=pltpu.CompilerParams(collective_id=1, has_side_effects=True, vmem_limit_bytes=62 << 20),
        name="reduce_gradients",
    )(*operands, gains.reshape(lead + (128,)))


def whole_block(shape):
    return pl.BlockSpec(shape, lambda *_: (0,) * len(shape))


NN = (((1,), (0,)), ((), ()))
NT = (((1,), (1,)), ((), ()))
TN = (((0,), (0,)), ((), ()))


def dot(left, right, dims):
    return lax.dot_general(left, right, dims, preferred_element_type=jnp.float32)


def head_sides(values):
    lane = lax.broadcasted_iota(jnp.int32, values.shape, 1)
    zero = jnp.zeros_like(values)
    return [jnp.where(lane < HEAD, values, zero), jnp.where(lane >= HEAD, values, zero)]


def attend_kernel(q_ref, kv_ref, bias_ref, out_ref, total_ref):
    bias = bias_ref[...]
    for pair in range(D // 128):
        columns = pl.ds(128 * pair, 128)
        keys, vals = kv_ref[:, columns], kv_ref[:, pl.ds(D + 128 * pair, 128)]
        outs = []
        for side, queries in enumerate(head_sides(q_ref[:, columns])):
            scores = dot(keys, queries, NT) * SCORE_SCALE + bias
            peak = jnp.max(scores, 0, keepdims=True)
            powers = jnp.exp(scores - peak)
            total = jnp.sum(powers, 0, keepdims=True)
            total_ref[pair, side : side + 1, :] = peak + jnp.log(total)
            outs.append(dot((powers * (1.0 / total)).astype(BF), vals, TN))
        lane = lax.broadcasted_iota(jnp.int32, outs[0].shape, 1)
        out_ref[:, columns] = jnp.where(lane < HEAD, outs[0], outs[1]).astype(BF)


def attend(joined, keys_vals, bias):
    queries, keys = joined.shape[0], keys_vals.shape[0]
    pairs = D // 128
    return pl.pallas_call(
        attend_kernel,
        out_shape=[jax.ShapeDtypeStruct((queries, D), BF), jax.ShapeDtypeStruct((pairs, 2, queries), jnp.float32)],
        grid=(1,),
        in_specs=[whole_block((queries, D))] + [whole_block(v.shape) for v in (keys_vals, bias)],
        out_specs=[whole_block((queries, D)), whole_block((pairs, 2, queries))],
        cost_estimate=pl.CostEstimate(
            flops=4 * queries * keys * D * 2, bytes_accessed=2 * keys * 2 * D, transcendentals=14 * queries * keys
        ),
        name="attend",
    )(joined, keys_vals, bias)


def attend_back_kernel(q_ref, kv_ref, bias_ref, total_ref, grad_ref, gq_ref, gkv_ref):
    bias = bias_ref[...]
    for pair in range(D // 128):
        columns, beside = pl.ds(128 * pair, 128), pl.ds(D + 128 * pair, 128)
        keys, vals = kv_ref[:, columns], kv_ref[:, beside]
        q_sides, g_sides = head_sides(q_ref[:, columns]), head_sides(grad_ref[:, columns])
        grad_q, grad_k, grad_v = [], 0.0, 0.0
        for side in range(2):
            scores = dot(keys, q_sides[side], NT) * SCORE_SCALE + bias
            probs = jnp.exp(scores - total_ref[pair, side : side + 1, :])
            grad_probs = dot(vals, g_sides[side], NT)
            delta = jnp.sum(probs * grad_probs, 0, keepdims=True)
            grad_scores = (probs * (grad_probs - delta)).astype(BF)
            grad_v = grad_v + dot(probs.astype(BF), g_sides[side], NN)
            grad_k = grad_k + dot(grad_scores, q_sides[side], NN)
            grad_q.append(dot(grad_scores, keys, TN))
        lane = lax.broadcasted_iota(jnp.int32, grad_q[0].shape, 1)
        gq_ref[:, columns] = (jnp.where(lane < HEAD, grad_q[0], grad_q[1]) * SCORE_SCALE).astype(BF)
        gkv_ref[:, columns] = (grad_k * SCORE_SCALE).astype(BF)
        gkv_ref[:, beside] = grad_v.astype(BF)


def attend_back(joined, keys_vals, bias, log_total, grad_mixed):
    queries, keys = joined.shape[0], keys_vals.shape[0]
    return pl.pallas_call(
        attend_back_kernel,
        out_shape=[jax.ShapeDtypeStruct((queries, D), BF), jax.ShapeDtypeStruct((keys, 2 * D), BF)],
        grid=(1,),
        in_specs=[whole_block((queries, D))] + [whole_block(v.shape) for v in (keys_vals, bias, log_total, grad_mixed)],
        out_specs=[whole_block((queries, D)), whole_block((keys, 2 * D))],
        cost_estimate=pl.CostEstimate(
            flops=10 * queries * keys * D * 2, bytes_accessed=4 * keys * 2 * D, transcendentals=14 * queries * keys
        ),
        name="attend_back",
    )(joined, keys_vals, bias, log_total, grad_mixed)


PAIR_GROUPS = (((0, 1), (2, 1)), ((2, 3), (1, 2)), ((4, 5), (2, 1)), ((6,), (1, 2)))
BACK_GROUPS = tuple(((pair,), ((2, 1), (1, 2))[pair % 2]) for pair in range(7))
BACK_LAGS = (2, 5, 7)


def greet_plane(place):
    barrier = pltpu.get_barrier_semaphore()
    for axis in (1, 2, 3):
        other = place[:axis] + (1 - place[axis],) + place[axis + 1 :]
        pl.semaphore_signal(barrier, inc=1, device_id=device_at(other), device_id_type=MESH_ID)
    pl.semaphore_wait(barrier, 3)


def group_columns(pairs):
    return [pl.ds(side * D + 128 * pairs[0], 128 * len(pairs)) for side in range(2)]


def plane_copies(place, axis, sources, targets, send_sem, recv_sem, index):
    device = place[:axis] + (1 - place[axis],) + place[axis + 1 :]
    return [
        pltpu.make_async_remote_copy(
            src_ref=source,
            dst_ref=target,
            send_sem=send_sem.at[index, k],
            recv_sem=recv_sem.at[index, k],
            device_id=device_at(device),
            device_id_type=MESH_ID,
        )
        for k, (source, target) in enumerate(zip(sources, targets))
    ]


def start_all(copies):
    for copy in copies:
        copy.start()


def wait_all(copies):
    for copy in copies:
        copy.wait()


def attend_gather_kernel(joined_ref, bias_ref, out_ref, total_ref, kept_ref, held, queries, send_sem, recv_sem, load_sem):
    place = grid_place()
    _, y, x, core = place
    loads = [
        pltpu.make_async_copy(joined_ref.at[:, pl.ds(D, 2 * D)], held.at[y, x, core], load_sem.at[0]),
        pltpu.make_async_copy(joined_ref.at[:, pl.ds(0, D)], queries, load_sem.at[1]),
    ]
    start_all(loads)
    greet_plane(place)
    wait_all(loads)

    def step(number, k):
        pairs, route = PAIR_GROUPS[number]
        if k == 0:
            views = [held.at[y, x, core, :, columns] for columns in group_columns(pairs)]
            axis = route[0]
        elif k == 1:
            axis = route[1]
            views = [(held.at[y, :, core, :, c] if axis == 1 else held.at[:, x, core, :, c]) for c in group_columns(pairs)]
        else:
            axis = 3
            views = [held.at[:, :, core, :, c] for c in group_columns(pairs)]
        return plane_copies(place, axis, views, views, send_sem, recv_sem, 3 * number + k)

    lane = lax.broadcasted_iota(jnp.int32, (queries.shape[0], 128), 1)
    rows = bias_ref.shape[0]

    def compute(number):
        for pair in PAIR_GROUPS[number][0]:
            keys = held[:, :, :, :, pl.ds(128 * pair, 128)].reshape(rows, 128)
            vals = held[:, :, :, :, pl.ds(D + 128 * pair, 128)].reshape(rows, 128)
            outs = []
            for side, sided in enumerate(head_sides(queries[:, pl.ds(128 * pair, 128)])):
                scores = dot(keys, sided, NT) * SCORE_SCALE + bias_ref[...]
                peak = jnp.max(scores, 0, keepdims=True)
                powers = jnp.exp(scores - peak)
                total = jnp.sum(powers, 0, keepdims=True)
                total_ref[pair, side : side + 1, :] = peak + jnp.log(total)
                outs.append(dot((powers * (1.0 / total)).astype(BF), vals, TN))
            out_ref[:, pl.ds(128 * pair, 128)] = jnp.where(lane < HEAD, outs[0], outs[1]).astype(BF)

    count = len(PAIR_GROUPS)
    for number in range(count):
        start_all(step(number, 0))
    for number in range(count):
        wait_all(step(number, 0))
        start_all(step(number, 1))
    for number in range(count):
        wait_all(step(number, 1))
        start_all(step(number, 2))
        if number > 0:
            wait_all(step(number - 1, 2))
            if number < count - 1:
                compute(number - 1)
    wait_all(step(count - 1, 2))
    keep = pltpu.make_async_copy(held, kept_ref, load_sem.at[0])
    keep.start()
    compute(count - 2)
    compute(count - 1)
    keep.wait()


def attend_gather(joined, bias):
    rows = joined.shape[0]
    _, n_y, n_x, n_core = grid_sizes()
    lead = (n_y, n_x, n_core)
    pairs, count = D // 128, len(PAIR_GROUPS)
    mixed, log_total, kept = pl.pallas_call(
        attend_gather_kernel,
        out_shape=[
            jax.ShapeDtypeStruct((rows, D), BF),
            jax.ShapeDtypeStruct((pairs, 2, rows), jnp.float32),
            jax.ShapeDtypeStruct(lead + (rows, 2 * D), BF),
        ],
        in_specs=[ANY, whole_block(bias.shape)],
        out_specs=[whole_block((rows, D)), whole_block((pairs, 2, rows)), ANY],
        scratch_shapes=[
            pltpu.VMEM(lead + (rows, 2 * D), BF),
            pltpu.VMEM((rows, D), BF),
            pltpu.SemaphoreType.DMA((3 * count, 2)),
            pltpu.SemaphoreType.DMA((3 * count, 2)),
            pltpu.SemaphoreType.DMA((2,)),
        ],
        compiler_params=pltpu.CompilerParams(collective_id=2, has_side_effects=True, vmem_limit_bytes=32 << 20),
        name="attend_gather",
    )(joined, bias)
    return mixed, log_total, kept.reshape(-1, 2 * D)


def attend_scatter_kernel(joined_ref, held_ref, bias_ref, total_ref, grad_ref, gq_ref, own_ref, *scratch):
    queries, part, from_core, from_first, from_second, send_sem, recv_sem, load_sem = scratch
    place = grid_place()
    _, y, x, core = place
    load = pltpu.make_async_copy(joined_ref.at[:, pl.ds(0, D)], queries, load_sem.at[0])
    load.start()
    greet_plane(place)
    load.wait()
    rows = bias_ref.shape[0]
    lane = lax.broadcasted_iota(jnp.int32, (queries.shape[0], 128), 1)

    def compute(number):
        for pair in BACK_GROUPS[number][0]:
            columns, beside = pl.ds(128 * pair, 128), pl.ds(D + 128 * pair, 128)
            keys = held_ref[:, :, :, :, columns].reshape(rows, 128)
            vals = held_ref[:, :, :, :, beside].reshape(rows, 128)
            q_sides, g_sides = head_sides(queries[:, columns]), head_sides(grad_ref[:, columns])
            grad_q, grad_k, grad_v = [], 0.0, 0.0
            for side in range(2):
                scores = dot(keys, q_sides[side], NT) * SCORE_SCALE + bias_ref[...]
                probs = jnp.exp(scores - total_ref[pair, side : side + 1, :])
                grad_probs = dot(vals, g_sides[side], NT)
                delta = jnp.sum(probs * grad_probs, 0, keepdims=True)
                grad_scores = (probs * (grad_probs - delta)).astype(BF)
                grad_v = grad_v + dot(probs.astype(BF), g_sides[side], NN)
                grad_k = grad_k + dot(grad_scores, q_sides[side], NN)
                grad_q.append(dot(grad_scores, keys, TN))
            gq_ref[:, columns] = (jnp.where(lane < HEAD, grad_q[0], grad_q[1]) * SCORE_SCALE).astype(BF)
            shape = part.shape[:4] + (128,)
            part[:, :, :, :, columns] = (grad_k * SCORE_SCALE).astype(BF).reshape(shape)
            part[:, :, :, :, beside] = grad_v.astype(BF).reshape(shape)

    def step(number, k):
        pairs, route = BACK_GROUPS[number]
        columns = group_columns(pairs)
        if k == 0:
            axis = 3
            sources = [part.at[:, :, 1 - core, :, c] for c in columns]
            targets = [from_core.at[:, :, :, c] for c in columns]
        elif k == 1:
            axis = route[1]
            sources = [(part.at[1 - y, :, core, :, c] if axis == 1 else part.at[:, 1 - x, core, :, c]) for c in columns]
            targets = [from_first.at[:, :, c] for c in columns]
        else:
            axis = route[0]
            sources = [(part.at[1 - y, x, core, :, c] if axis == 1 else part.at[y, 1 - x, core, :, c]) for c in columns]
            targets = [from_second.at[:, c] for c in columns]
        return plane_copies(place, axis, sources, targets, send_sem, recv_sem, 3 * number + k)

    def add(number, k):
        pairs, route = BACK_GROUPS[number]
        wait_all(step(number, k))
        for c in group_columns(pairs):
            if k == 0:
                part[:, :, core, :, c] = part[:, :, core, :, c] + from_core[:, :, :, c]
            elif k == 1 and route[1] == 1:
                part[y, :, core, :, c] = part[y, :, core, :, c] + from_first[:, :, c]
            elif k == 1:
                part[:, x, core, :, c] = part[:, x, core, :, c] + from_first[:, :, c]
            else:
                own_ref[:, c] = part[y, x, core, :, c] + from_second[:, c]

    count = len(BACK_GROUPS)
    for time in range(count + BACK_LAGS[-1]):
        if time < count:
            compute(time)
            start_all(step(time, 0))
        for k, lag in enumerate(BACK_LAGS):
            number = time - lag
            if 0 <= number < count:
                add(number, k)
                if k < 2:
                    start_all(step(number, k + 1))


def attend_scatter(joined, keys_vals, bias, log_total, grad_mixed):
    rows = joined.shape[0]
    _, n_y, n_x, n_core = grid_sizes()
    lead = (n_y, n_x, n_core)
    count = len(BACK_GROUPS)
    held = keys_vals.reshape(lead + (rows, 2 * D))
    return pl.pallas_call(
        attend_scatter_kernel,
        out_shape=[jax.ShapeDtypeStruct((rows, D), BF), jax.ShapeDtypeStruct((rows, 2 * D), BF)],
        in_specs=[ANY] + [whole_block(v.shape) for v in (held, bias, log_total, grad_mixed)],
        out_specs=[whole_block((rows, D)), whole_block((rows, 2 * D))],
        scratch_shapes=[
            pltpu.VMEM((rows, D), BF),
            pltpu.VMEM(lead + (rows, 2 * D), BF),
            pltpu.VMEM((n_y, n_x, rows, 2 * D), BF),
            pltpu.VMEM((2, rows, 2 * D), BF),
            pltpu.VMEM((rows, 2 * D), BF),
            pltpu.SemaphoreType.DMA((3 * count, 2)),
            pltpu.SemaphoreType.DMA((3 * count, 2)),
            pltpu.SemaphoreType.DMA((1,)),
        ],
        compiler_params=pltpu.CompilerParams(collective_id=3, has_side_effects=True, vmem_limit_bytes=40 << 20),
        name="attend_scatter",
    )(joined, held, bias, log_total, grad_mixed)


def gelu_parts(values):
    size = jnp.abs(values)
    bell = jnp.exp(-0.5 * size * size)
    t = 1.0 / (1.0 + (0.3275911 * 0.7071067811865476) * size)
    tail = t * (0.127414796 + t * (-0.142248368 + t * (0.7107068705 + t * (-0.7265760135 + t * 0.5307027145)))) * bell
    share = jnp.where(values >= 0, 1.0 - tail, tail)
    return values * share, share + values * (0.3989422804014327 * bell)


def norm_parts(values):
    scale = lax.rsqrt(jnp.mean(values * values, -1, keepdims=True) + EPSILON)
    return values * scale, scale


def norm_gradient(values, norm_gain, upstream):
    unit, scale = norm_parts(values)
    inner = upstream * norm_gain
    back = scale * (inner - unit * jnp.mean(inner * unit, -1, keepdims=True))
    return back, jnp.sum(upstream * unit, 0, keepdims=True)


def hidden_block(rows):
    return 2 * D if rows <= 128 else D


def ffn_kernel(stream_ref, gain_ref, in_ref, down_ref, out_ref, inputs_ref, hidden_ref, slope_ref):
    step = pl.program_id(0)

    @pl.when(step == 0)
    def _():
        stream = stream_ref[...].astype(jnp.float32)
        out_ref[...] = stream
        inputs_ref[...] = (norm_parts(stream)[0] * gain_ref[...].astype(jnp.float32)).astype(BF)

    value, slope = gelu_parts(dot(inputs_ref[...], in_ref[...], NN))
    hidden = value.astype(BF)
    hidden_ref[...] = hidden
    slope_ref[...] = slope.astype(BF)
    out_ref[...] += dot(hidden, down_ref[...], NN)


def ffn(stream, norm_gain, weight_in, weight_down):
    rows = stream.shape[0]
    block = hidden_block(rows)
    still = lambda j: (0, 0)
    return pl.pallas_call(
        ffn_kernel,
        grid=(FF // block,),
        out_shape=[
            jax.ShapeDtypeStruct((rows, D), jnp.float32),
            jax.ShapeDtypeStruct((rows, D), BF),
            jax.ShapeDtypeStruct((rows, FF), BF),
            jax.ShapeDtypeStruct((rows, FF), BF),
        ],
        in_specs=[
            pl.BlockSpec((rows, D), still),
            pl.BlockSpec((1, D), still),
            pl.BlockSpec((D, block), lambda j: (0, j)),
            pl.BlockSpec((block, D), lambda j: (j, 0)),
        ],
        out_specs=[
            pl.BlockSpec((rows, D), still),
            pl.BlockSpec((rows, D), still),
            pl.BlockSpec((rows, block), lambda j: (0, j)),
            pl.BlockSpec((rows, block), lambda j: (0, j)),
        ],
        cost_estimate=pl.CostEstimate(
            flops=4 * rows * D * FF, bytes_accessed=4 * D * FF + 4 * rows * FF + 8 * rows * D, transcendentals=rows * FF
        ),
        name="ffn",
    )(stream, norm_gain, weight_in, weight_down)


def ffn_back_kernel(grad_ref, stream_ref, gain_ref, slope_ref, in_ref, down_ref, out_ref, low_ref, pre_ref, gain_out, total):
    step = pl.program_id(0)

    @pl.when(step == 0)
    def _():
        low_ref[...] = grad_ref[...].astype(BF)
        total[...] = jnp.zeros_like(total)

    pre = (dot(low_ref[...], down_ref[...], NT) * slope_ref[...].astype(jnp.float32)).astype(BF)
    pre_ref[...] = pre
    total[...] += dot(pre, in_ref[...], NT)

    @pl.when(step == pl.num_programs(0) - 1)
    def _():
        back, gain = norm_gradient(stream_ref[...].astype(jnp.float32), gain_ref[...].astype(jnp.float32), total[...])
        out_ref[...] = grad_ref[...].astype(jnp.float32) + back
        gain_out[...] = gain


def ffn_back(upstream, stream, norm_gain, slope, weight_in, weight_down):
    rows = stream.shape[0]
    block = hidden_block(rows)
    still = lambda j: (0, 0)
    return pl.pallas_call(
        ffn_back_kernel,
        grid=(FF // block,),
        out_shape=[
            jax.ShapeDtypeStruct((rows, D), jnp.float32),
            jax.ShapeDtypeStruct((rows, D), BF),
            jax.ShapeDtypeStruct((rows, FF), BF),
            jax.ShapeDtypeStruct((1, D), jnp.float32),
        ],
        in_specs=[
            pl.BlockSpec((rows, D), still),
            pl.BlockSpec((rows, D), still),
            pl.BlockSpec((1, D), still),
            pl.BlockSpec((rows, block), lambda j: (0, j)),
            pl.BlockSpec((D, block), lambda j: (0, j)),
            pl.BlockSpec((block, D), lambda j: (j, 0)),
        ],
        out_specs=[
            pl.BlockSpec((rows, D), still),
            pl.BlockSpec((rows, D), still),
            pl.BlockSpec((rows, block), lambda j: (0, j)),
            pl.BlockSpec((1, D), still),
        ],
        scratch_shapes=[pltpu.VMEM((rows, D), jnp.float32)],
        cost_estimate=pl.CostEstimate(
            flops=4 * rows * D * FF, bytes_accessed=4 * D * FF + 4 * rows * FF + 16 * rows * D, transcendentals=0
        ),
        name="ffn_back",
    )(upstream, stream, norm_gain, slope, weight_in, weight_down)


def spread_matrix(devices):
    rows = D // devices
    source = lax.broadcasted_iota(jnp.int32, (D, devices * ROOM), 0)
    target = lax.broadcasted_iota(jnp.int32, (D, devices * ROOM), 1)
    return jnp.where((target // ROOM * rows + target % ROOM == source) & (target % ROOM < rows), 1.0, 0.0).astype(BF)


def late_blocks(late, tall):
    devices = late.shape[0]
    per_block = D // tall
    return [
        pl.BlockSpec((devices, ROOM, D), lambda j: (0, 4 + j, 0)),
        pl.BlockSpec((per_block, 4 * ROOM, D), lambda j: (j, 0, 0)),
    ]


def late_in_block(ref):
    return ref[...].reshape(-1, D)


def late_down_block(ref):
    values = ref[...]
    return values[:, : D // values.shape[0]].reshape(D, D)


def late_ffn_kernel(stream_ref, gain_ref, spread_ref, in_ref, down_ref, out_ref, inputs_ref, hidden_ref, slope_ref, spread):
    step = pl.program_id(0)

    @pl.when(step == 0)
    def _():
        stream = stream_ref[...].astype(jnp.float32)
        out_ref[...] = stream
        inputs = (norm_parts(stream)[0] * gain_ref[...].astype(jnp.float32)).astype(BF)
        inputs_ref[...] = inputs
        spread[...] = dot(inputs, spread_ref[...], NN).astype(BF)

    value, slope = gelu_parts(dot(spread[...], late_in_block(in_ref), NN))
    hidden = value.astype(BF)
    hidden_ref[...] = hidden
    slope_ref[...] = slope.astype(BF)
    out_ref[...] += dot(hidden, late_down_block(down_ref), NN)


def late_ffn(stream, norm_gain, spread, late, tall):
    rows = stream.shape[0]
    still = lambda j: (0, 0)
    return pl.pallas_call(
        late_ffn_kernel,
        grid=(FF // D,),
        out_shape=[
            jax.ShapeDtypeStruct((rows, D), jnp.float32),
            jax.ShapeDtypeStruct((rows, D), BF),
            jax.ShapeDtypeStruct((rows, FF), BF),
            jax.ShapeDtypeStruct((rows, FF), BF),
        ],
        in_specs=[pl.BlockSpec((rows, D), still), pl.BlockSpec((1, D), still), pl.BlockSpec(spread.shape, still)]
        + late_blocks(late, tall),
        out_specs=[
            pl.BlockSpec((rows, D), still),
            pl.BlockSpec((rows, D), still),
            pl.BlockSpec((rows, D), lambda j: (0, j)),
            pl.BlockSpec((rows, D), lambda j: (0, j)),
        ],
        scratch_shapes=[pltpu.VMEM((rows, spread.shape[1]), BF)],
        cost_estimate=pl.CostEstimate(flops=4 * rows * D * FF, bytes_accessed=5 * D * FF, transcendentals=rows * FF),
        name="late_ffn",
    )(stream, norm_gain, spread, late, late)


def late_back_kernel(grad_ref, stream_ref, gain_ref, spread_ref, slope_ref, in_ref, down_ref, out_ref, low_ref, pre_ref, gain_out, total):
    step = pl.program_id(0)

    @pl.when(step == 0)
    def _():
        low_ref[...] = grad_ref[...].astype(BF)
        total[...] = jnp.zeros_like(total)

    pre = (dot(low_ref[...], late_down_block(down_ref), NT) * slope_ref[...].astype(jnp.float32)).astype(BF)
    pre_ref[...] = pre
    total[...] += dot(pre, late_in_block(in_ref), NT)

    @pl.when(step == pl.num_programs(0) - 1)
    def _():
        whole = total[...]
        high = whole.astype(BF)
        rest = (whole - high.astype(jnp.float32)).astype(BF)
        inner = dot(high, spread_ref[...], NT) + dot(rest, spread_ref[...], NT)
        back, gain = norm_gradient(stream_ref[...].astype(jnp.float32), gain_ref[...].astype(jnp.float32), inner)
        out_ref[...] = grad_ref[...].astype(jnp.float32) + back
        gain_out[...] = gain


def late_ffn_back(upstream, stream, norm_gain, slope, spread, late, tall):
    rows = stream.shape[0]
    still = lambda j: (0, 0)
    return pl.pallas_call(
        late_back_kernel,
        grid=(FF // D,),
        out_shape=[
            jax.ShapeDtypeStruct((rows, D), jnp.float32),
            jax.ShapeDtypeStruct((rows, D), BF),
            jax.ShapeDtypeStruct((rows, FF), BF),
            jax.ShapeDtypeStruct((1, D), jnp.float32),
        ],
        in_specs=[
            pl.BlockSpec((rows, D), still),
            pl.BlockSpec((rows, D), still),
            pl.BlockSpec((1, D), still),
            pl.BlockSpec(spread.shape, still),
            pl.BlockSpec((rows, D), lambda j: (0, j)),
        ]
        + late_blocks(late, tall),
        out_specs=[
            pl.BlockSpec((rows, D), still),
            pl.BlockSpec((rows, D), still),
            pl.BlockSpec((rows, D), lambda j: (0, j)),
            pl.BlockSpec((1, D), still),
        ],
        scratch_shapes=[pltpu.VMEM((rows, spread.shape[1]), jnp.float32)],
        cost_estimate=pl.CostEstimate(flops=4 * rows * D * FF, bytes_accessed=5 * D * FF, transcendentals=0),
        name="late_ffn_back",
    )(upstream, stream, norm_gain, spread, slope, late, late)


def shifted(x, axis, by):
    count = lax.axis_size(axis)
    pairs = [(i, i + by) for i in range(count) if 0 <= i + by < count]
    return lax.ppermute(x, axis, pairs)


def slab_term(left, right):
    return dot(left, right, TN)


def normed(values, norm_gain):
    return (norm_parts(values)[0] * norm_gain.astype(jnp.float32)).astype(BF)


def norm_back(values, norm_gain, upstream):
    return norm_gradient(values, norm_gain.astype(jnp.float32), upstream)


def self_forward(stream, norm_gain, weight_qkv, weight_out, bias):
    inputs = normed(stream, norm_gain)
    joined = dot(inputs, weight_qkv, NN).astype(BF)
    if grid_sizes() == (4, 2, 2, 2):
        mixed, log_total, keys_vals = attend_gather(joined, bias)
    else:
        keys_vals = lax.all_gather(joined[:, D:], "seq", axis=0, tiled=True)
        mixed, log_total = attend(joined, keys_vals, bias)
    return stream + dot(mixed, weight_out, NN), (stream, inputs, joined, keys_vals, log_total, mixed)


def self_back(stored, norm_gain, weight_qkv, weight_out, bias, upstream, covered):
    stream, inputs, joined, keys_vals, log_total, mixed = stored
    grad_low = upstream.astype(BF)
    grad_mixed = dot(grad_low, weight_out, NT).astype(BF)
    if grid_sizes() == (4, 2, 2, 2) and not covered:
        grad_queries, own_pairs = attend_scatter(joined, keys_vals, bias, log_total, grad_mixed)
    else:
        grad_queries, grad_pairs = attend_back(joined, keys_vals, bias, log_total, grad_mixed)
        own_pairs = lax.psum_scatter(grad_pairs, "seq", scatter_dimension=0, tiled=True)
    grad_joined = jnp.concatenate([grad_queries, own_pairs], -1)
    back, gain_grad = norm_back(stream, norm_gain, dot(grad_joined, weight_qkv, NT))
    return upstream + back, gain_grad, ((inputs, grad_joined), (mixed, grad_low))


def causal_bias(queries, keys):
    offset = lax.axis_index("seq") * queries
    key_place = lax.broadcasted_iota(jnp.int32, (keys, queries), 0)
    query_place = offset + lax.broadcasted_iota(jnp.int32, (keys, queries), 1)
    return jnp.where(key_place <= query_place, 0.0, MASKED_SCORE).astype(jnp.float32)


def span_bias(prior_flag, queries):
    spans = prior_flag.shape[0]
    keys = spans * NEIGH * RET
    key_span = lax.broadcasted_iota(jnp.int32, (keys, queries), 0) // (NEIGH * RET)
    query_span = lax.broadcasted_iota(jnp.int32, (keys, queries), 1) // SPAN
    allowed = jnp.repeat(prior_flag.reshape(-1), RET)[:, None] > 0.5
    return jnp.where(key_span == query_span, jnp.where(allowed, 0.0, MASKED_SCORE), 2 * MASKED_SCORE).astype(jnp.float32)


def row_gate(prior_flag):
    return jnp.repeat(jnp.max(prior_flag, -1).astype(jnp.float32), SPAN)[:, None]


def prior_spans(encoded, keep_flag):
    last_enc, last_flag = shifted((encoded[-1:], keep_flag[-1:]), "seq", 1)
    return jnp.concatenate([last_enc, encoded[:-1]], 0), jnp.concatenate([last_flag, keep_flag[:-1]], 0)


def cross_forward(stream, encoded, keep_flag, norm_gain, weight_q, weight_kv, weight_out):
    prior_enc, prior_flag = prior_spans(encoded, keep_flag)
    prior_enc = prior_enc.reshape(-1, D)
    inputs = normed(stream, norm_gain)
    queries = dot(inputs, weight_q, NN).astype(BF)
    keys_vals = jnp.concatenate([dot(prior_enc, side, NN).astype(BF) for side in weight_kv], 1)
    bias = span_bias(prior_flag, stream.shape[0])
    mixed, log_total = attend(queries, keys_vals, bias)
    branch = row_gate(prior_flag) * dot(mixed, weight_out, NN)
    return stream + branch, (stream, inputs, prior_enc, prior_flag, queries, keys_vals, bias, log_total, mixed)


def cross_back(stored, norm_gain, weight_q, weight_kv, weight_out, upstream):
    stream, inputs, prior_enc, prior_flag, queries, keys_vals, bias, log_total, mixed = stored
    grad_low = (upstream * row_gate(prior_flag)).astype(BF)
    grad_mixed = dot(grad_low, weight_out, NT).astype(BF)
    grad_queries, grad_pairs = attend_back(queries, keys_vals, bias, log_total, grad_mixed)
    grad_prior = dot(grad_pairs[:, :D], weight_kv[0], NT) + dot(grad_pairs[:, D:], weight_kv[1], NT)
    grad_prior = grad_prior.reshape(prior_flag.shape[0], NEIGH * RET, D)
    from_next = shifted(grad_prior[:1].astype(BF), "seq", -1).astype(jnp.float32)
    encoded_grad = jnp.concatenate([grad_prior[1:], from_next], 0).reshape(-1, D)
    back, gain_grad = norm_back(stream, norm_gain, dot(grad_queries, weight_q, NT))
    pairs = ((inputs, grad_queries), (prior_enc, grad_pairs), (mixed, grad_low))
    return upstream + back, gain_grad, pairs, encoded_grad


def on_device(
    tokens,
    retrieved,
    span_doc,
    neigh_doc,
    cotangent,
    dec_gain,
    dec_qkv,
    dec_out,
    dec_in,
    dec_down,
    cca_gain,
    cca_q,
    cca_kv,
    cca_out,
    enc_gain,
    enc_in,
    enc_down,
    enc_final,
):
    assert tokens.shape[0] == 1
    rows = cca_q.shape[0]
    own_gains = jnp.concatenate([dec_gain.reshape(4, rows), cca_gain[None], enc_gain, enc_final[None]], 0).T
    own_gains = jnp.pad(own_gains, ((0, 0), (0, 120)))
    neighbours = retrieved.reshape(-1, D)
    full = gather_weights(
        neighbours, enc_in, enc_down, dec_qkv, dec_out, dec_in, dec_down, cca_q, cca_kv, cca_out, own_gains
    )
    gains = full["gains"].T
    attn_gain, ffn_gain = (gains[0:1], gains[2:3]), (gains[1:2], gains[3:4])
    cross_gain, encode_gain, final_gain = gains[4:5], (gains[5:6], gains[6:7]), gains[7:8]
    cross_weights = (cross_gain, full["cca_q"], full["cca_kv"], full["cca_out"])
    queries = tokens.shape[1]
    bias = causal_bias(queries, queries * lax.axis_size("seq"))

    encoder, encoder_kept, encoded = full["encoder"]
    encoded = encoded.reshape(span_doc.shape[1], NEIGH * RET, D)
    keep_flag = (neigh_doc[0] != span_doc[0][:, None]).astype(BF)

    stream = tokens[0].astype(jnp.float32)
    attn_kept, ffn_kept = [], []
    for layer in range(DEC_LAYERS):
        stream, kept = self_forward(stream, attn_gain[layer], full["dec_qkv"][layer], full["dec_out"][layer], bias)
        attn_kept.append(kept)
        if layer == 0:
            stream, cross_kept = cross_forward(stream, encoded, keep_flag, *cross_weights)
        before = stream
        if full["dec_in"][layer] is None:
            late, tall = full["dec_down"][layer], dec_down.shape[1]
            spread = spread_matrix(late.shape[0])
            stream, inputs, hidden, slope = late_ffn(before, ffn_gain[layer], spread, late, tall)
        else:
            stream, inputs, hidden, slope = ffn(before, ffn_gain[layer], full["dec_in"][layer], full["dec_down"][layer])
        ffn_kept.append((before, inputs, hidden, slope))
    result = stream.astype(BF)

    upstream = cotangent[0].astype(jnp.float32)
    attn_gain_g, ffn_gain_g = [None] * DEC_LAYERS, [None] * DEC_LAYERS
    attn_pairs, ffn_pairs = [None] * DEC_LAYERS, [None] * DEC_LAYERS
    for layer in reversed(range(DEC_LAYERS)):
        before, inputs, hidden, slope = ffn_kept[layer]
        if full["dec_in"][layer] is None:
            back = late_ffn_back(upstream, before, ffn_gain[layer], slope, spread, late, tall)
        else:
            back = ffn_back(upstream, before, ffn_gain[layer], slope, full["dec_in"][layer], full["dec_down"][layer])
        upstream, grad_low, grad_pre, ffn_gain_g[layer] = back
        ffn_pairs[layer] = ((inputs, grad_pre), (grad_low, hidden))
        if layer == 0:
            upstream, cross_gain_g, cross_pairs, encoded_grad = cross_back(cross_kept, *cross_weights, upstream)
        upstream, attn_gain_g[layer], attn_pairs[layer] = self_back(
            attn_kept[layer], attn_gain[layer], full["dec_qkv"][layer], full["dec_out"][layer], bias, upstream, layer == 0
        )

    enc_upstream, final_gain_g = norm_back(encoder, final_gain, encoded_grad)
    enc_gain_g, enc_pairs = [None] * ENC_LAYERS, [None] * ENC_LAYERS
    for layer in reversed(range(ENC_LAYERS)):
        before, inputs, hidden, slope = encoder_kept[layer]
        enc_upstream, grad_low, grad_pre, enc_gain_g[layer] = ffn_back(
            enc_upstream, before, encode_gain[layer], slope, full["enc_in"][layer], full["enc_down"][layer]
        )
        enc_pairs[layer] = ((inputs, grad_pre), (grad_low, hidden))

    pair_list = []
    for layer in range(DEC_LAYERS):
        pair_list += list(attn_pairs[layer]) + list(ffn_pairs[layer])
    pair_list += list(cross_pairs)
    for layer in range(ENC_LAYERS):
        pair_list += list(enc_pairs[layer])
    gain_list = []
    for layer in range(DEC_LAYERS):
        gain_list += [attn_gain_g[layer], ffn_gain_g[layer]]
    gain_list = [gain.reshape(D) for gain in gain_list + [cross_gain_g] + enc_gain_g + [final_gain_g]]

    grads = sum_gradients(pair_list, gain_list, rows)
    (enc_in_g, enc_down_g, dec_qkv_g, dec_out_g, dec_in_g, dec_down_g, cross_q_g, cross_kv_g, cross_out_g, gain_cols) = grads
    gain_rows = gain_cols[:, :8].T
    return (
        result[None],
        upstream[None],
        gain_rows[:4].reshape(2, 2, rows),
        dec_qkv_g,
        dec_out_g,
        dec_in_g,
        jnp.swapaxes(dec_down_g, 1, 2),
        gain_rows[4],
        cross_q_g,
        cross_kv_g,
        cross_out_g,
        gain_rows[5:7],
        enc_in_g,
        jnp.swapaxes(enc_down_g, 1, 2),
        gain_rows[7],
    )


def sum_plainly(pair_list, gain_list):
    blocks = [slab_term(left, right) for left, right in pair_list] + [vector[:, None] for vector in gain_list]
    owned = lax.psum_scatter(
        jnp.concatenate(blocks, 1).astype(BF), ("dp", "seq"), scatter_dimension=0, tiled=True
    ).astype(jnp.float32)
    pieces, cursor = [], 0
    for _, right in pair_list:
        pieces.append(owned[:, cursor : cursor + right.shape[-1]])
        cursor += right.shape[-1]
    two = lambda first, second: jnp.stack([pieces[first], pieces[second]])
    return [
        two(11, 13), two(12, 14), two(0, 4), two(1, 5), two(2, 6), two(3, 7), pieces[8], pieces[9], pieces[10], owned[:, cursor:]
    ]


def sum_gradients(pair_list, gain_list, rows):
    sizes = grid_sizes()
    if rows % 4 or sizes != (4, 2, 2, 2):
        return sum_plainly(pair_list, gain_list)
    operands = [x.reshape(-1, x.shape[-1]) for pair in pair_list for x in pair]
    gains = jnp.pad(jnp.stack(gain_list).astype(BF).T, ((0, 0), (0, 128 - len(gain_list))))
    return reduce_gradients(operands, gains, rows)


def solution(mesh):
    return jax.shard_map(
        on_device,
        mesh=mesh,
        in_specs=(
            P("dp", "seq", None),
            P("dp", "seq", None, None, None),
            P("dp", "seq"),
            P("dp", "seq", None),
            P("dp", "seq", None),
            P(None, None, ("dp", "seq")),
            P(None, ("dp", "seq"), None),
            P(None, ("dp", "seq"), None),
            P(None, ("dp", "seq"), None),
            P(None, ("dp", "seq"), None),
            P(("dp", "seq")),
            P(("dp", "seq"), None),
            P(("dp", "seq"), None),
            P(("dp", "seq"), None),
            P(None, ("dp", "seq")),
            P(None, ("dp", "seq"), None),
            P(None, ("dp", "seq"), None),
            P(("dp", "seq")),
        ),
        out_specs=(
            P("dp", "seq", None),
            P("dp", "seq", None),
            P(None, None, ("dp", "seq")),
            P(None, ("dp", "seq"), None),
            P(None, ("dp", "seq"), None),
            P(None, ("dp", "seq"), None),
            P(None, None, ("dp", "seq")),
            P(("dp", "seq")),
            P(("dp", "seq"), None),
            P(("dp", "seq"), None),
            P(("dp", "seq"), None),
            P(None, ("dp", "seq")),
            P(None, ("dp", "seq"), None),
            P(None, None, ("dp", "seq")),
            P(("dp", "seq")),
        ),
        check_vma=False,
    )
```

```python
import functools
import heapq
import jax
import jax.numpy as jnp
from jax import lax
from jax.experimental import pallas as pl
from jax.experimental.pallas import tpu as pltpu
from jax.sharding import PartitionSpec as P

D = 896
FF = 3584
HEADS = 14
HEAD = 64
SPAN = 64
NEIGH = 2
RET = 128
ENC_LAYERS = 2
DEC_LAYERS = 2
EPSILON = 1e-06
SCORE_SCALE = 0.125
MASKED_SCORE = -1000000000.0
BF = jnp.bfloat16
MESH_ID = pl.DeviceIdType.MESH
ANY = pl.BlockSpec(memory_space=pl.ANY)


def grid_sizes():
    return (lax.axis_size("dp"), lax.axis_size("seq") // 4, 2, 2)


def grid_place():
    seq = lax.axis_index("seq")
    return (lax.axis_index("dp"), seq // 4, (seq // 2) % 2, seq % 2)


def device_at(place):
    z, y, x, core = place
    return (z, (y * 2 + x) * 2 + core)


def moved(place, sizes, axis, by):
    size = sizes[axis]
    there = lax.rem(place[axis] + (by % size), size)
    return place[:axis] + (there,) + place[axis + 1 :]


def greet(place, sizes):
    barrier = pltpu.get_barrier_semaphore()
    for axis in range(4):
        size, here = sizes[axis], place[axis]
        for by in (1, -1):
            there = here + by

            @pl.when(inside(there, size))
            def _():
                other = place[:axis] + (jnp.clip(there, 0, size - 1),) + place[axis + 1 :]
                pl.semaphore_signal(barrier, inc=1, device_id=device_at(other), device_id_type=MESH_ID)

    count = 0
    for axis in range(4):
        for by in (1, -1):
            count = count + inside(place[axis] + by, sizes[axis]).astype(jnp.int32)
    pl.semaphore_wait(barrier, count)


class Hop:
    def __init__(self, copy, sends, receives):
        self.copy, self.sends, self.receives = copy, sends, receives

    def start(self):
        pl.when(self.sends)(self.copy[0].start)

    def wait(self):
        pl.when(self.sends)(self.copy[0].wait_send)
        pl.when(self.receives)(self.copy[1].wait_recv)


def inside(place, size):
    return jnp.logical_and(place >= 0, place < size)


ZYX, ZXY, YZX, XZY, YXZ, XYZ = (0, 1, 2), (0, 2, 1), (1, 0, 2), (2, 0, 1), (1, 2, 0), (2, 1, 0)
ROUTES = (YXZ, ZYX, ZXY, ZYX, ZXY, ZXY, YZX, ZXY, ZYX, ZYX)
ROUTES += (ZXY, XZY, ZYX, YZX, XZY, XZY, YZX, YXZ, XYZ)
UNIT_US, HOP_US, CORE_US = 2.2, 2.5, 0.17


def schedule(pieces, routes, sizes):
    chains = []
    for number, piece in enumerate(pieces):
        scale, held, chain = piece[3] / PIECE, 1, []
        for axis in routes[number]:
            chain += [(axis, held * UNIT_US * scale)] * (sizes[axis] - 1)
            held *= sizes[axis]
        chains.append(chain + [(3, held * CORE_US * scale)])
    free, flying, ready = [0.0] * 4, [0] * 4, [[] for _ in range(4)]
    for number, chain in enumerate(chains):
        heapq.heappush(ready[chain[0][0]], (number, number, 0))
    now, events, order = 0.0, [], []
    while True:
        for link in range(4):
            while ready[link] and flying[link] < 2:
                _, number, step = heapq.heappop(ready[link])
                free[link] = max(free[link], now) + chains[number][step][1]
                flying[link] += 1
                order.append(("start", number, step, now))
                heapq.heappush(events, (free[link] + HOP_US, number, step, link))
        if not events:
            return order
        now, number, step, link = heapq.heappop(events)
        flying[link] -= 1
        order.append(("wait", number, step, now))
        if step + 1 < len(chains[number]):
            heapq.heappush(ready[chains[number][step + 1][0]], (number, number, step + 1))


PIECE = 896


def narrow_groups():
    qkv = 3 * D
    wide = FF // 2
    whole = lambda arg, layer: [[(arg, layer, 0, wide)], [(arg, layer, wide, wide)]]
    return [
        whole(0, 0),
        whole(0, 1),
        [
            [(7, None, 0, D), (6, None, 0, D), (2, 0, 0, qkv), (3, 0, 0, D)],
            [(7, None, D, D), (8, None, 0, D), (2, 1, 0, qkv), (3, 1, 0, D)],
        ],
        whole(4, 0),
        [[(9, None, 0, 128)], [(9, None, 0, 128)]],
    ]


def half_width(group):
    return sum(part[3] for part in group[0])


def gather_plan():
    groups = narrow_groups()
    starts, cursor = [], 0
    for group in groups:
        starts.append(cursor)
        cursor += half_width(group)
    pieces = []
    for kind, number in (("n", 4), ("n", 0), ("r", 0), ("n", 1), ("r", 1), ("n", 2), ("n", 3), ("r", 2)):
        if kind == "n":
            width = half_width(groups[number])
            for first in range(0, width, PIECE):
                pieces.append((kind, number, first, min(PIECE, width - first)))
        else:
            pieces.append((kind, number, 0, D))
            pieces.append((kind, number, 1, D))
    return groups, starts, cursor, pieces


N_GROUPS = 5
N_TALL = 3


def gather_kernel(sizes, *refs):
    groups, starts, _, pieces = gather_plan()
    ins, neighbours = refs[:10], refs[10]
    n_outs = N_GROUPS + N_TALL
    outs, encoder_outs, late_out = refs[11 : 11 + n_outs], refs[11 + n_outs : 20 + n_outs], refs[20 + n_outs]
    halves, other, joined, own_rows, send_sem, recv_sem, load_sem, swap_sem = refs[21 + n_outs : 29 + n_outs]
    late_in, late_down, late, late_sem = refs[29 + n_outs : 33 + n_outs]
    encoder_rooms = refs[33 + n_outs :]
    place = grid_place()
    z, y, x, core = place
    sibling = device_at(moved(place, sizes, 3, 1))
    loads = []
    for number, group in enumerate(groups):
        for half in range(2):
            cursor = starts[number]
            for arg, layer, first, size in group[half]:
                source = ins[arg] if layer is None else ins[arg].at[layer]
                loads.append((source.at[:, pl.ds(first, size)], halves.at[half, :, pl.ds(cursor, size)]))
                cursor += size
    for number, (arg, layer) in enumerate(((1, 0), (1, 1), (5, 0))):
        for part in range(2):
            loads.append((ins[arg].at[layer, part], own_rows.at[2 * number + part]))
    late_loads = [
        pltpu.make_async_copy(ins[4].at[1], late_in, late_sem.at[0]),
        pltpu.make_async_copy(ins[5].at[1], late_down, late_sem.at[1]),
    ]
    late_store = pltpu.make_async_copy(late, late_out, late_sem.at[2])

    def late_unit():
        for copy in late_loads:
            copy.wait()
        down = late_down[...].astype(jnp.float32).reshape(-1, D)
        fill = jnp.zeros((4 * ROOM - down.shape[0], D), jnp.float32)
        late[pl.ds(0, 4 * ROOM), :] = jnp.concatenate([down, fill], 0).astype(BF)
        fill = jnp.zeros((ROOM - late_in.shape[0], D), jnp.float32)
        for k in range(FF // D):
            rows = late_in[:, pl.ds(k * D, D)].astype(jnp.float32)
            late[pl.ds((4 + k) * ROOM, ROOM), :] = jnp.concatenate([rows, fill], 0).astype(BF)
        late_store.start()

    started = []
    for copy in late_loads:
        copy.start()
    for k, (source, target) in enumerate(loads):
        copy = pltpu.make_async_copy(source, target, load_sem.at[k])
        copy.start()
        started.append(copy)
    greet(place, sizes)
    for copy in started:
        copy.wait()
    placed = []
    for number in range(N_TALL):
        for part in range(2):
            k = 2 * number + part
            target = outs[N_GROUPS + number].at[z, y, x, core, part]
            placed.append(pltpu.make_async_copy(own_rows.at[k], target, load_sem.at[len(loads) + len(groups) + k]))
            placed[-1].start()
    swaps = []
    for number, group in enumerate(groups):
        columns = pl.ds(starts[number], half_width(group))
        copy = pltpu.make_async_remote_copy(
            src_ref=halves.at[1 - core, :, columns],
            dst_ref=other.at[:, columns],
            send_sem=swap_sem.at[0, number],
            recv_sem=swap_sem.at[1, number],
            device_id=sibling,
            device_id_type=MESH_ID,
        )
        copy.start()
        swaps.append(copy)

    def view(piece, where):
        kind, number, first, size = piece
        iz, iy, ix = where[:3]
        if kind == "n":
            start = pl.multiple_of(core * half_width(groups[number]) + first, 128)
            return outs[number].at[iz, iy, ix, :, pl.ds(start, size)]
        return outs[N_GROUPS + number].at[iz, iy, ix, core, first]

    prepared = {}

    def prepare(piece):
        kind, number, first, size = piece
        if kind == "n" and number not in prepared:
            swaps[number].wait()
            group = groups[number]
            for begin in range(starts[number], starts[number] + half_width(group), 128):
                columns = pl.ds(begin, 128)
                mine = halves[core, :, columns].astype(jnp.float32)
                theirs = other[:, columns].astype(jnp.float32)
                both = [jnp.where(core == 0, mine, theirs), jnp.where(core == 0, theirs, mine)]
                joined[:, columns] = jnp.concatenate(both, 0).astype(BF)
            width = half_width(group)
            copy = pltpu.make_async_copy(
                joined.at[:, pl.ds(starts[number], width)],
                outs[number].at[z, y, x, :, pl.ds(pl.multiple_of(core * width, 128), width)],
                load_sem.at[len(loads) + number],
            )
            copy.start()
            copy.wait()
            prepared[number] = True
        elif kind == "r" and "r" not in prepared:
            for copy in placed:
                copy.wait()
            prepared["r"] = True

    semaphores = [0]

    def transfers(number):
        piece = pieces[number]
        steps, done = [], []
        for axis in routes[number] + (3,):
            size, here = sizes[axis], place[axis]

            def block(at):
                where = list(place)
                for old in done:
                    where[old] = slice(None)
                where[axis] = jnp.clip(at, 0, size - 1)
                return view(piece, where)

            for hop in range(1, size):
                hops = []
                for way in (1, -1):
                    ahead, behind = here + way, here - way
                    sent, got = here - way * (hop - 1), here - way * hop
                    if size == 2 and way == -1:
                        continue
                    if size == 2:
                        ahead, behind, got = 1 - here, 1 - here, 1 - here
                    pair = []
                    for at, other_end in ((sent, ahead), (got, behind)):
                        ref = block(at)
                        target = place[:axis] + (jnp.clip(other_end, 0, size - 1),) + place[axis + 1 :]
                        pair.append(
                            pltpu.make_async_remote_copy(
                                src_ref=ref,
                                dst_ref=ref,
                                send_sem=send_sem.at[semaphores[0]],
                                recv_sem=recv_sem.at[semaphores[0]],
                                device_id=device_at(target),
                                device_id_type=MESH_ID,
                            )
                        )
                    semaphores[0] += 1
                    sends = jnp.logical_and(inside(sent, size), inside(ahead, size))
                    hops.append(Hop(pair, sends, inside(got, size)))
                steps.append(hops)
            done.append(axis)
        return steps

    routes = [ROUTES[number % len(ROUTES)] for number in range(len(pieces))]
    running = [transfers(number) for number in range(len(pieces))]
    units = encoder_units(
        neighbours, outs[N_GROUPS - 1], (outs[0], outs[1]), (outs[N_GROUPS], outs[N_GROUPS + 1]), encoder_outs, encoder_rooms
    )
    units.insert(0, late_unit)
    needs = [{k for k, piece in enumerate(pieces) if piece[:2] in wanted} for wanted in [set()] + UNIT_NEEDS]
    due, arrived = 0.0, set()
    for what, number, step, time in schedule(pieces, routes, sizes):
        if what == "wait":
            for copy in running[number][step]:
                copy.wait()
            if step + 1 == len(running[number]):
                arrived.add(number)
        else:
            prepare(pieces[number])
            for copy in running[number][step]:
                copy.start()
        if units and time >= due and needs[len(needs) - len(units)] <= arrived:
            units.pop(0)()
            due = time + UNIT_TIME
    for unit in units:
        unit()
    late_store.wait()


ROOM = 32


HIDDEN_UNITS = 4
UNIT_TIME = 7.0
GAINS, FIRST, SECOND = {("n", 4)}, {("n", 0), ("r", 0)}, {("n", 1), ("r", 1)}
UNIT_NEEDS = [GAINS | FIRST] * (1 + HIDDEN_UNITS) + [SECOND] * (1 + HIDDEN_UNITS) + [set()]


def encoder_units(neighbours, gain_columns, weights_in, weights_down, outs, rooms):
    after, inputs_out, hidden_out, slope_out, encoded_out = outs[0:2], outs[2:4], outs[4:6], outs[6:8], outs[8]
    stream, inputs, columns, gain_rows, block_in, block_down, hidden, slope, sems = rooms
    block = FF // HIDDEN_UNITS

    def flat(values, rows):
        return values.astype(jnp.float32).reshape(rows, values.shape[-1])

    def weights(layer, k):
        slot = k % 2
        return [
            pltpu.make_async_copy(weights_in[layer].at[:, :, :, :, pl.ds(k * block, block)], block_in.at[slot], sems.at[0, slot]),
            pltpu.make_async_copy(weights_down[layer].at[k], block_down.at[slot], sems.at[1, slot]),
        ]

    def results(layer, k):
        slot = k % 2
        place = pl.ds(k * block, block)
        return [
            pltpu.make_async_copy(hidden.at[slot], hidden_out[layer].at[:, place], sems.at[2, slot]),
            pltpu.make_async_copy(slope.at[slot], slope_out[layer].at[:, place], sems.at[3, slot]),
        ]

    def stream_copy(layer):
        return pltpu.make_async_copy(stream, after[layer], sems.at[4, layer])

    def inputs_copy(layer):
        return pltpu.make_async_copy(inputs, (*inputs_out, encoded_out)[layer], sems.at[5, layer % 2])

    def norm_unit(layer):
        if layer == 0:
            first = pltpu.make_async_copy(neighbours, inputs, sems.at[6, 0])
            second = pltpu.make_async_copy(gain_columns.at[:, :, :, :, pl.ds(0, 128)], columns, sems.at[6, 1])
            first.start()
            second.start()
            first.wait()
            second.wait()
            gain_rows[...] = flat(columns[...], D).T
            stream[...] = inputs[...].astype(jnp.float32)
        else:
            for k in (HIDDEN_UNITS - 2, HIDDEN_UNITS - 1):
                for copy in results(layer - 1, k):
                    copy.wait()
            inputs_copy(layer - 1).wait()
            stream_copy(layer - 1).start()
        if layer < ENC_LAYERS:
            for copy in weights(layer, 0):
                copy.start()
        gain = gain_rows[5 + layer : 6 + layer, :]
        inputs[...] = (norm_parts(stream[...])[0] * gain).astype(BF)
        inputs_copy(layer).start()
        if layer == ENC_LAYERS:
            stream_copy(layer - 1).wait()
            inputs_copy(layer).wait()

    def hidden_unit(layer, k):
        slot = k % 2
        if k + 1 < HIDDEN_UNITS:
            for copy in weights(layer, k + 1):
                copy.start()
        for copy in weights(layer, k):
            copy.wait()
        if k >= 2:
            for copy in results(layer, k - 2):
                copy.wait()
        value, rate = gelu_parts(dot(inputs[...], flat(block_in[slot], D).astype(BF), NN))
        hidden[slot] = value.astype(BF)
        slope[slot] = rate.astype(BF)
        for copy in results(layer, k):
            copy.start()
        if k == 0 and layer > 0:
            stream_copy(layer - 1).wait()
        stream[...] += dot(hidden[slot], flat(block_down[slot], block).astype(BF), NN)

    units = []
    for layer in range(ENC_LAYERS):
        units.append(functools.partial(norm_unit, layer))
        for k in range(HIDDEN_UNITS):
            units.append(functools.partial(hidden_unit, layer, k))
    units.append(functools.partial(norm_unit, ENC_LAYERS))
    return units


def gather_plainly(neighbours, enc_in, enc_down, dec_qkv, dec_out, dec_in, dec_down, cca_q, cca_kv, cca_out, gains):
    get = lambda w: lax.all_gather(w, ("dp", "seq"), axis=w.ndim - 2, tiled=True)
    kv = get(cca_kv)
    enc_in, enc_down, columns = get(enc_in), get(enc_down), get(gains)[:, :8]
    stream, kept = neighbours, []
    for layer in range(ENC_LAYERS):
        gain = columns[:, 5 + layer][None]
        after, inputs, hidden, slope = ffn(stream, gain, enc_in[layer], enc_down[layer])
        kept.append((stream, inputs, hidden, slope))
        stream = after
    return dict(
        encoder=(stream, kept, normed(stream, columns[:, 7][None])),
        enc_in=enc_in, enc_down=enc_down, dec_in=get(dec_in), dec_down=get(dec_down), dec_qkv=get(dec_qkv),
        dec_out=get(dec_out), cca_kv=[kv[:, :D], kv[:, D:]], cca_q=get(cca_q), cca_out=get(cca_out), gains=columns,
    )


def gather_weights(neighbours, enc_in, enc_down, dec_qkv, dec_out, dec_in, dec_down, cca_q, cca_kv, cca_out, gains):
    sizes = grid_sizes()
    rows = cca_q.shape[0]
    groups, starts, total, pieces = gather_plan()
    part = enc_down.shape[1] // 2
    if rows % 4 or part % 8 or sizes != (HIDDEN_UNITS, 2, 2, 2):
        return gather_plainly(neighbours, enc_in, enc_down, dec_qkv, dec_out, dec_in, dec_down, cca_q, cca_kv, cca_out, gains)
    lead = sizes[:3]
    shapes = [lead + (2 * rows, 2 * half_width(group)) for group in groups] + [lead + (2, 2, part, D)] * N_TALL
    out_shape = [jax.ShapeDtypeStruct(shape, BF) for shape in shapes]
    count = neighbours.shape[0]
    block = FF // HIDDEN_UNITS
    out_shape += [jax.ShapeDtypeStruct((count, D), jnp.float32)] * 2 + [jax.ShapeDtypeStruct((count, D), BF)] * 2
    out_shape += [jax.ShapeDtypeStruct((count, FF), BF)] * 4 + [jax.ShapeDtypeStruct((count, D), BF)]
    out_shape += [jax.ShapeDtypeStruct((8 * ROOM, D), BF)]
    per_piece = sum((size - 1) * (1 if size == 2 else 2) for size in sizes)
    n_loads = sum(len(half) for group in groups for half in group) + 4 * N_TALL + len(groups)
    split = lambda w: w.reshape(w.shape[0], 2, part, D)
    outs = pl.pallas_call(
        functools.partial(gather_kernel, sizes),
        out_shape=out_shape,
        in_specs=[ANY] * 11,
        out_specs=[ANY] * len(out_shape),
        scratch_shapes=[
            pltpu.VMEM((2, rows, total), BF),
            pltpu.VMEM((rows, total), BF),
            pltpu.VMEM((2 * rows, total), BF),
            pltpu.VMEM((2 * N_TALL, part, D), BF),
            pltpu.SemaphoreType.DMA((per_piece * len(pieces),)),
            pltpu.SemaphoreType.DMA((per_piece * len(pieces),)),
            pltpu.SemaphoreType.DMA((n_loads,)),
            pltpu.SemaphoreType.DMA((2, len(groups))),
            pltpu.VMEM((rows, FF), BF),
            pltpu.VMEM((2, part, D), BF),
            pltpu.VMEM((8 * ROOM, D), BF),
            pltpu.SemaphoreType.DMA((3,)),
            pltpu.VMEM((count, D), jnp.float32),
            pltpu.VMEM((count, D), BF),
            pltpu.VMEM(lead + (2 * rows, 128), BF),
            pltpu.VMEM((128, D), jnp.float32),
            pltpu.VMEM((2,) + lead + (2 * rows, block), BF),
            pltpu.VMEM((2,) + sizes[1:3] + (2, 2, part, D), BF),
            pltpu.VMEM((2, count, block), BF),
            pltpu.VMEM((2, count, block), BF),
            pltpu.SemaphoreType.DMA((7, 2)),
        ],
        compiler_params=pltpu.CompilerParams(collective_id=0, has_side_effects=True, vmem_limit_bytes=56 << 20),
        name="gather_weights",
    )(enc_in, split(enc_down), dec_qkv, dec_out, dec_in, split(dec_down), cca_q, cca_kv, cca_out, gains, neighbours)
    narrow = [out.reshape(D, out.shape[-1]) for out in outs[:N_GROUPS]]
    tall = [out.reshape(FF, D) for out in outs[N_GROUPS : N_GROUPS + N_TALL]]
    first, second, inputs_0, inputs_1, hidden_0, hidden_1, slope_0, slope_1, encoded, late = outs[N_GROUPS + N_TALL :]
    late = lax.all_gather(late, ("dp", "seq"), axis=0, tiled=False)
    kept = [(neighbours, inputs_0, hidden_0, slope_0), (first, inputs_1, hidden_1, slope_1)]
    mixed = narrow[2]
    half = mixed.shape[1] // 2
    sides = [mixed[:, :half], mixed[:, half:]]
    qkv = [side[:, 2 * D : 5 * D] for side in sides]
    out = [side[:, 5 * D : 6 * D] for side in sides]
    return dict(
        encoder=(second, kept, encoded),
        enc_in=narrow[:2], enc_down=tall[:2], dec_in=[narrow[3], None], dec_down=[tall[2], late], dec_qkv=qkv, dec_out=out,
        cca_kv=[side[:, :D] for side in sides], cca_q=sides[0][:, D : 2 * D], cca_out=sides[1][:, D : 2 * D],
        gains=narrow[4][:, :8],
    )


YZX_SUM, XZY_SUM, YXZ_SUM, XYZ_SUM = (1, False), (2, False), (1, True), (2, True)
ORDERS = (YZX_SUM, XZY_SUM, YZX_SUM, XZY_SUM, YXZ_SUM, XZY_SUM, YZX_SUM, XYZ_SUM, YZX_SUM, XZY_SUM, YXZ_SUM)
ORDERS += (XZY_SUM, YZX_SUM, XYZ_SUM, YZX_SUM, XZY_SUM, YXZ_SUM, XYZ_SUM, YZX_SUM, XYZ_SUM, YXZ_SUM, XYZ_SUM)
CORE, HEAVY, ZED, PAIR, CORE_AGAIN, PER_PIECE = 0, 1, 2, 8, 9, 10
START = (0, 1, 4, 6, 7, 8, 10, 11, 12)
SLOTS = dict(part=2, whole=5, half=8, sibling=3, heavy=8, middle=8, last=8, zed=7, final=4)


def gradient_pieces():
    pieces = []
    both = lambda left, right, out, layer, k: tuple(
        (left, right, 2 * D * half + D * k, out, layer, 2 * D * half + D * k) for half in range(2)
    )
    for layer in reversed(range(2)):
        base = 8 * layer
        for k in range(2):
            pieces.append(both(base + 6, base + 7, 5, layer, k))
        for k in range(2):
            pieces.append(both(base + 4, base + 5, 4, layer, k))
    pieces.append(tuple((8 * layer + 2, 8 * layer + 3, 0, 3, layer, 0) for layer in range(2)))
    for k in range(3):
        pieces.append(tuple((8 * layer, 8 * layer + 1, D * k, 2, layer, D * k) for layer in range(2)))
    pieces.append(((16, 17, 0, 6, None, 0), (20, 21, 0, 8, None, 0)))
    pieces.append(tuple((18, 19, D * half, 7, None, D * half) for half in range(2)))
    for layer in reversed(range(2)):
        base = 22 + 4 * layer
        for k in range(2):
            pieces.append(both(base + 2, base + 3, 1, layer, k))
        for k in range(2):
            pieces.append(both(base, base + 1, 0, layer, k))
    return pieces


N_OPERANDS = 30


class Sums:
    def __init__(self, place, sizes, sems, buffers, slots, width):
        self.place, self.sizes, self.width = place, sizes, width
        self.send_sem, self.recv_sem = sems
        self.part, self.whole, self.half, self.sibling, self.heavy, self.middle, self.last, self.zed, self.final = buffers
        self.slots = slots

    def slot(self, name, number):
        return lax.rem(number, self.slots[name])

    def copy(self, number, which, source, target, device):
        index = number * PER_PIECE + which
        return pltpu.make_async_remote_copy(
            src_ref=source,
            dst_ref=target,
            send_sem=self.send_sem.at[index],
            recv_sem=self.recv_sem.at[index],
            device_id=device_at(device),
            device_id_type=MESH_ID,
        )

    def core_copy(self, number):
        return self.copy(
            number,
            CORE,
            self.part.at[self.slot("part", number)],
            self.sibling.at[self.slot("sibling", number)],
            self.swapped(3),
        )

    def swapped(self, axis):
        return self.place[:axis] + (1 - self.place[axis],) + self.place[axis + 1 :]

    def heavy_copy(self, number, axis):
        whole = self.whole.at[self.slot("whole", number)]
        there = 1 - self.place[axis]
        source = whole.at[:, there] if axis == 1 else whole.at[:, :, there]
        return self.copy(number, HEAVY, source, self.heavy.at[self.slot("heavy", number)], self.swapped(axis))

    def pair_copy(self, number, axis, early):
        half = self.half.at[self.slot("half", number)]
        there = 1 - self.place[axis]
        if early:
            source, target = half.at[:, there], self.middle.at[self.slot("middle", number)]
        else:
            source, target = half.at[self.place[0], there], self.last.at[self.slot("last", number)]
        return self.copy(number, PAIR, source, target, self.swapped(axis))

    def zed_block(self, number, axis, early, at):
        half = self.half.at[self.slot("half", number)]
        at = jnp.clip(at, 0, self.sizes[0] - 1)
        return half.at[at, pl.ds(self.place[axis], 1)] if early else half.at[at]

    def zed_room(self, number, early, hop, way):
        room = self.zed.at[self.slot("zed", number), hop - 1, way]
        return room.at[pl.ds(0, 1)] if early else room

    def zed_hops(self, number, axis, early, hop):
        z, size = self.place[0], self.sizes[0]
        found = []
        for way, by in enumerate((-1, 1)):
            sent, ahead = z + by * hop, z + by
            behind, got = z - by, z - by + by * hop
            room = self.zed_room(number, early, hop, way)
            device = (jnp.clip(ahead, 0, size - 1),) + self.place[1:]
            copy = self.copy(number, ZED + 2 * (hop - 1) + way, self.zed_block(number, axis, early, sent), room, device)
            sends = jnp.logical_and(inside(sent, size), inside(ahead, size))
            receives = jnp.logical_and(inside(got, size), inside(behind, size))
            found.append((copy, sends, receives, self.zed_block(number, axis, early, got), room))
        return found

    def start_zed(self, number, axis, early, hop):
        for copy, sends, _, _, _ in self.zed_hops(number, axis, early, hop):
            pl.when(sends)(copy.start)

    def finish_zed(self, number, axis, early, hop):
        for copy, sends, receives, block, room in self.zed_hops(number, axis, early, hop):
            pl.when(sends)(copy.wait_send)

            @pl.when(receives)
            def _():
                copy.wait_recv()
                for k in range(1 if early else 2):
                    block[k] = block[k] + room[k]

    def add_core(self, number):
        self.core_copy(number).wait()
        whole, sibling = self.slot("whole", number), self.slot("sibling", number)

        def one(k, _):
            at = (k // 4, (k // 2) % 2, k % 2)
            self.whole[(whole, *at)] = self.whole[(whole, *at)] + self.sibling[(sibling, *at)]
            return 0

        lax.fori_loop(0, 4 * self.sizes[0], one, 0)

    def add_heavy(self, number, axis):
        self.heavy_copy(number, axis).wait()
        whole, half, heavy = (self.slot(name, number) for name in ("whole", "half", "heavy"))

        def one(k, _):
            z, o = k // 2, k % 2
            at = (z, self.place[1], o) if axis == 1 else (z, o, self.place[2])
            self.half[half, z, o] = self.whole[(whole, *at)] + self.heavy[heavy, z, o]
            return 0

        lax.fori_loop(0, 2 * self.sizes[0], one, 0)

    def add_pair(self, number, axis, early):
        self.pair_copy(number, axis, early).wait()
        half, here = self.slot("half", number), self.place[axis]
        if early:
            for z in range(self.sizes[0]):
                self.half[half, z, here] = self.half[half, z, here] + self.middle[self.slot("middle", number), z]
        else:
            z = self.place[0]
            self.half[half, z, here] = self.half[half, z, here] + self.last[self.slot("last", number)]

    def split_rows(self, number, axis):
        half, final = self.slot("half", number), self.slot("final", number)
        rows = self.half[half, self.place[0], self.place[axis]].astype(jnp.float32)
        count = rows.shape[0] // 2
        first, second = rows[:count], rows[count:]
        self.final[final, 0] = jnp.where(self.place[3] == 0, first, second)
        self.final[final, 2] = jnp.where(self.place[3] == 0, second, first)

    def final_copy(self, number):
        final = self.slot("final", number)
        return self.copy(number, CORE_AGAIN, self.final.at[final, 2], self.final.at[final, 1], self.swapped(3))

    def step(self, step, number, first, early):
        other = 3 - first
        sequence = [("pair", 0), ("zed", 3), ("zed", 2), ("zed", 1)] if early else [("zed", 3), ("zed", 2), ("zed", 1), ("pair", 0)]
        if step == 1:
            self.heavy_copy(number, first).start()
            return
        if step == 2:
            self.add_heavy(number, first)
        else:
            kind, hop = sequence[step - 3]
            if kind == "pair":
                self.add_pair(number, other, early)
            else:
                self.finish_zed(number, other, early, hop)
        if step < 6:
            kind, hop = sequence[step - 2]
            if kind == "pair":
                self.pair_copy(number, other, early).start()
            else:
                self.start_zed(number, other, early, hop)
        else:
            self.split_rows(number, other)
            self.final_copy(number).start()


def reduce_kernel(sizes, tall, *refs):
    pieces = gradient_pieces()
    operands, gains = refs[:N_OPERANDS], refs[N_OPERANDS]
    outs = refs[N_OPERANDS + 1 : N_OPERANDS + 11]
    scratch = refs[N_OPERANDS + 11 :]
    left, right, product = scratch[:3]
    buffers, small = scratch[3:12], scratch[12:21]
    send_sem, recv_sem, small_send, small_recv, load_sem, out_sem = scratch[21:]
    place = grid_place()
    core = place[3]
    count = len(pieces)
    sums = Sums(place, sizes, (send_sem, recv_sem), buffers, SLOTS, D)
    once = Sums(place, sizes, (small_send, small_recv), small, {name: 1 for name in SLOTS}, 128)
    is_tall = [tall[piece[0][0]] for piece in pieces]
    first_tall = is_tall.index(True)
    long_rows, short_rows = left.shape[2], None

    def rows_of(k):
        return operands[pieces[k][0][0]].shape[0]

    def loads(k, slot):
        rows = rows_of(k)
        found = []
        for half in range(2):
            l, r, column, _, _, _ = pieces[k][half]
            mine = jnp.where(core == half, 1, 0)
            found.append((operands[l], left.at[slot, mine, pl.ds(0, rows)], load_sem.at[slot, half]))
            found.append((operands[r].at[:, pl.ds(column, D)], right.at[slot, mine, pl.ds(0, rows)], load_sem.at[slot, 2 + half]))
        return [pltpu.make_async_copy(*args) for args in found]

    def start_loads(number):
        for k in range(count):

            @pl.when(number == k)
            def _():
                for copy in loads(k, k % 2):
                    copy.start()

    def multiply(number, which, rows):
        slot = lax.rem(number, 2)

        def block(k, _):
            columns = pl.ds(pl.multiple_of(k * 128, 128), 128)
            product[pl.ds(pl.multiple_of(k * 128, 128), 128), :] = lax.dot_general(
                left[slot, which, pl.ds(0, rows), columns],
                right[slot, which, pl.ds(0, rows), :],
                (((0,), (0,)), ((), ())),
                preferred_element_type=jnp.float32,
            )
            return 0

        lax.fori_loop(0, D // 128, block, 0)
        chunk = sums.whole.shape[4]

        def store(k, _):
            values = product[pl.ds(pl.multiple_of(k * chunk, 8), chunk), :].astype(BF)
            at = (k // 4, (k // 2) % 2, k % 2)
            if which == 0:
                sums.part[(sums.slot("part", number), *at)] = values
            else:
                sums.whole[(sums.slot("whole", number), *at)] = values
            return 0

        lax.fori_loop(0, D // chunk, store, 0)

    def compute(number):
        for flag in sorted(set(is_tall)):
            wanted = jnp.logical_and(number >= first_tall, flag) if flag else number < first_tall
            k = first_tall if flag else 0

            @pl.when(wanted)
            def _():
                for copy in loads(k, lax.rem(number, 2)):
                    copy.wait()
                multiply(number, 0, rows_of(k))
                sums.core_copy(number).start()
                multiply(number, 1, rows_of(k))

    def out_copies(k):
        slot = k % SLOTS["final"]
        found = []
        for half in range(2):
            _, _, _, out, layer, column = pieces[k][half]
            target = outs[out] if layer is None else outs[out].at[layer]
            source = sums.final.at[slot, jnp.where(core == half, 0, 1)]
            found.append(pltpu.make_async_copy(source, target.at[:, pl.ds(column, D)], out_sem.at[slot, half]))
        return found

    greet(place, sizes)
    small_loads = []
    for k, target in enumerate((once.part.at[0], once.whole.at[0])):
        copy = pltpu.make_async_copy(gains, target, out_sem.at[SLOTS["final"], k])
        copy.start()
        small_loads.append(copy)
    start_loads(0)

    def tick(time, _):
        for step in reversed(range(8)):

            @pl.when(time == START[step])
            def _():
                if step == 0:
                    for copy in small_loads:
                        copy.wait()
                    once.core_copy(0).start()
                elif step == 7:
                    once.final_copy(0).wait()
                    copy = pltpu.make_async_copy(once.final.at[0, 0], outs[9], out_sem.at[SLOTS["final"], 0])
                    copy.start()
                    copy.wait()
                else:
                    if step == 1:
                        once.add_core(0)
                    once.step(step, 0, *ORDERS[-1])

        for step in reversed(range(9)):
            number = time - START[step]

            @pl.when(jnp.logical_and(number >= 0, number < count))
            def _():
                if step == 0:
                    start_loads(number + 1)
                    compute(number)
                elif step == 8:
                    for copy in out_copies_at(number):
                        copy.wait()
                elif step == 7:
                    sums.final_copy(number).wait()
                    for k in range(count):

                        @pl.when(number == k)
                        def _():
                            for copy in out_copies(k):
                                copy.start()

                else:
                    if step == 1:
                        sums.add_core(number)
                    for order in sorted(set(ORDERS)):
                        here = functools.reduce(jnp.logical_or, [number == k for k, one in enumerate(ORDERS) if one == order])

                        @pl.when(here)
                        def _():
                            sums.step(step, number, *order)

        return 0

    def out_copies_at(number):
        slot = lax.rem(number, SLOTS["final"])
        return [
            pltpu.make_async_copy(sums.final.at[slot, 0], outs[3].at[0, :, pl.ds(0, D)], out_sem.at[slot, half])
            for half in range(2)
        ]

    lax.fori_loop(0, count + START[8], tick, 0)


def reduce_gradients(operands, gains, layers_rows):
    sizes = grid_sizes()
    rows = layers_rows
    chunk = 2 * rows
    lead = sizes[:3] + (chunk,)
    longest = max(x.shape[0] for x in operands)
    shortest = min(x.shape[0] for x in operands)
    tall = tuple(x.shape[0] == longest for x in operands)
    f32 = jnp.float32
    shapes = [(2, rows, FF), (2, rows, FF), (2, rows, 3 * D), (2, rows, D), (2, rows, FF), (2, rows, FF)]
    shapes += [(rows, D), (rows, 2 * D), (rows, D), (rows, 128)]

    def rooms(slots, width):
        z = sizes[0]
        return [
            pltpu.VMEM((slots["part"],) + lead + (width,), BF),
            pltpu.VMEM((slots["whole"],) + lead + (width,), BF),
            pltpu.VMEM((slots["half"], z, 2, chunk, width), BF),
            pltpu.VMEM((slots["sibling"],) + lead + (width,), BF),
            pltpu.VMEM((slots["heavy"], z, 2, chunk, width), BF),
            pltpu.VMEM((slots["middle"], z, chunk, width), BF),
            pltpu.VMEM((slots["last"], chunk, width), BF),
            pltpu.VMEM((slots["zed"], z - 1, 2, 2, chunk, width), BF),
            pltpu.VMEM((slots["final"], 3, rows, width), f32),
        ]

    count = len(gradient_pieces())
    return pl.pallas_call(
        functools.partial(reduce_kernel, sizes, tall),
        out_shape=[jax.ShapeDtypeStruct(shape, f32) for shape in shapes],
        in_specs=[ANY] * (N_OPERANDS + 1),
        out_specs=[ANY] * 10,
        scratch_shapes=[
            pltpu.VMEM((2, 2, longest, D), BF),
            pltpu.VMEM((2, 2, longest, D), BF),
            pltpu.VMEM((D, D), f32),
            *rooms(SLOTS, D),
            *rooms({name: 1 for name in SLOTS}, 128),
            pltpu.SemaphoreType.DMA((PER_PIECE * count,)),
            pltpu.SemaphoreType.DMA((PER_PIECE * count,)),
            pltpu.SemaphoreType.DMA((PER_PIECE,)),
            pltpu.SemaphoreType.DMA((PER_PIECE,)),
            pltpu.SemaphoreType.DMA((2, 4)),
            pltpu.SemaphoreType.DMA((SLOTS["final"] + 1, 2)),
        ],
        compiler_params=pltpu.CompilerParams(collective_id=1, has_side_effects=True, vmem_limit_bytes=62 << 20),
        name="reduce_gradients",
    )(*operands, gains.reshape(lead + (128,)))


def whole_block(shape):
    return pl.BlockSpec(shape, lambda *_: (0,) * len(shape))


NN = (((1,), (0,)), ((), ()))
NT = (((1,), (1,)), ((), ()))
TN = (((0,), (0,)), ((), ()))


def dot(left, right, dims):
    return lax.dot_general(left, right, dims, preferred_element_type=jnp.float32)


def head_sides(values):
    lane = lax.broadcasted_iota(jnp.int32, values.shape, 1)
    zero = jnp.zeros_like(values)
    return [jnp.where(lane < HEAD, values, zero), jnp.where(lane >= HEAD, values, zero)]


def attend_kernel(q_ref, kv_ref, bias_ref, out_ref, total_ref):
    bias = bias_ref[...]
    for pair in range(D // 128):
        columns = pl.ds(128 * pair, 128)
        keys, vals = kv_ref[:, columns], kv_ref[:, pl.ds(D + 128 * pair, 128)]
        outs = []
        for side, queries in enumerate(head_sides(q_ref[:, columns])):
            scores = dot(keys, queries, NT) * SCORE_SCALE + bias
            peak = jnp.max(scores, 0, keepdims=True)
            powers = jnp.exp(scores - peak)
            total = jnp.sum(powers, 0, keepdims=True)
            total_ref[pair, side : side + 1, :] = peak + jnp.log(total)
            outs.append(dot((powers * (1.0 / total)).astype(BF), vals, TN))
        lane = lax.broadcasted_iota(jnp.int32, outs[0].shape, 1)
        out_ref[:, columns] = jnp.where(lane < HEAD, outs[0], outs[1]).astype(BF)


def attend(joined, keys_vals, bias):
    queries, keys = joined.shape[0], keys_vals.shape[0]
    pairs = D // 128
    return pl.pallas_call(
        attend_kernel,
        out_shape=[jax.ShapeDtypeStruct((queries, D), BF), jax.ShapeDtypeStruct((pairs, 2, queries), jnp.float32)],
        grid=(1,),
        in_specs=[whole_block((queries, D))] + [whole_block(v.shape) for v in (keys_vals, bias)],
        out_specs=[whole_block((queries, D)), whole_block((pairs, 2, queries))],
        cost_estimate=pl.CostEstimate(
            flops=4 * queries * keys * D * 2, bytes_accessed=2 * keys * 2 * D, transcendentals=14 * queries * keys
        ),
        name="attend",
    )(joined, keys_vals, bias)


def attend_back_kernel(q_ref, kv_ref, bias_ref, total_ref, grad_ref, gq_ref, gkv_ref):
    bias = bias_ref[...]
    for pair in range(D // 128):
        columns, beside = pl.ds(128 * pair, 128), pl.ds(D + 128 * pair, 128)
        keys, vals = kv_ref[:, columns], kv_ref[:, beside]
        q_sides, g_sides = head_sides(q_ref[:, columns]), head_sides(grad_ref[:, columns])
        grad_q, grad_k, grad_v = [], 0.0, 0.0
        for side in range(2):
            scores = dot(keys, q_sides[side], NT) * SCORE_SCALE + bias
            probs = jnp.exp(scores - total_ref[pair, side : side + 1, :])
            grad_probs = dot(vals, g_sides[side], NT)
            delta = jnp.sum(probs * grad_probs, 0, keepdims=True)
            grad_scores = (probs * (grad_probs - delta)).astype(BF)
            grad_v = grad_v + dot(probs.astype(BF), g_sides[side], NN)
            grad_k = grad_k + dot(grad_scores, q_sides[side], NN)
            grad_q.append(dot(grad_scores, keys, TN))
        lane = lax.broadcasted_iota(jnp.int32, grad_q[0].shape, 1)
        gq_ref[:, columns] = (jnp.where(lane < HEAD, grad_q[0], grad_q[1]) * SCORE_SCALE).astype(BF)
        gkv_ref[:, columns] = (grad_k * SCORE_SCALE).astype(BF)
        gkv_ref[:, beside] = grad_v.astype(BF)


def attend_back(joined, keys_vals, bias, log_total, grad_mixed):
    queries, keys = joined.shape[0], keys_vals.shape[0]
    return pl.pallas_call(
        attend_back_kernel,
        out_shape=[jax.ShapeDtypeStruct((queries, D), BF), jax.ShapeDtypeStruct((keys, 2 * D), BF)],
        grid=(1,),
        in_specs=[whole_block((queries, D))] + [whole_block(v.shape) for v in (keys_vals, bias, log_total, grad_mixed)],
        out_specs=[whole_block((queries, D)), whole_block((keys, 2 * D))],
        cost_estimate=pl.CostEstimate(
            flops=10 * queries * keys * D * 2, bytes_accessed=4 * keys * 2 * D, transcendentals=14 * queries * keys
        ),
        name="attend_back",
    )(joined, keys_vals, bias, log_total, grad_mixed)


PAIR_GROUPS = tuple(((pair,), ((2, 1), (1, 2))[pair % 2]) for pair in range(7))
BACK_GROUPS = PAIR_GROUPS
BACK_LAGS = (2, 5, 7)


def greet_plane(place):
    barrier = pltpu.get_barrier_semaphore()
    for axis in (1, 2, 3):
        other = place[:axis] + (1 - place[axis],) + place[axis + 1 :]
        pl.semaphore_signal(barrier, inc=1, device_id=device_at(other), device_id_type=MESH_ID)
    pl.semaphore_wait(barrier, 3)


def group_columns(pairs):
    return [pl.ds(side * D + 128 * pairs[0], 128 * len(pairs)) for side in range(2)]


def plane_copies(place, axis, sources, targets, send_sem, recv_sem, index):
    device = place[:axis] + (1 - place[axis],) + place[axis + 1 :]
    return [
        pltpu.make_async_remote_copy(
            src_ref=source,
            dst_ref=target,
            send_sem=send_sem.at[index, k],
            recv_sem=recv_sem.at[index, k],
            device_id=device_at(device),
            device_id_type=MESH_ID,
        )
        for k, (source, target) in enumerate(zip(sources, targets))
    ]


def start_all(copies):
    for copy in copies:
        copy.start()


def wait_all(copies):
    for copy in copies:
        copy.wait()


def attend_gather_kernel(joined_ref, bias_ref, out_ref, total_ref, kept_ref, held, queries, send_sem, recv_sem, load_sem):
    place = grid_place()
    _, y, x, core = place
    loads = [
        pltpu.make_async_copy(joined_ref.at[:, pl.ds(D, 2 * D)], held.at[y, x, core], load_sem.at[0]),
        pltpu.make_async_copy(joined_ref.at[:, pl.ds(0, D)], queries, load_sem.at[1]),
    ]
    start_all(loads)
    greet_plane(place)
    wait_all(loads)

    def step(number, k):
        pairs, route = PAIR_GROUPS[number]
        if k == 0:
            views = [held.at[y, x, core, :, columns] for columns in group_columns(pairs)]
            axis = route[0]
        elif k == 1:
            axis = route[1]
            views = [(held.at[y, :, core, :, c] if axis == 1 else held.at[:, x, core, :, c]) for c in group_columns(pairs)]
        else:
            axis = 3
            views = [held.at[:, :, core, :, c] for c in group_columns(pairs)]
        return plane_copies(place, axis, views, views, send_sem, recv_sem, 3 * number + k)

    lane = lax.broadcasted_iota(jnp.int32, (queries.shape[0], 128), 1)
    rows = bias_ref.shape[0]

    def compute(number):
        for pair in PAIR_GROUPS[number][0]:
            keys = held[:, :, :, :, pl.ds(128 * pair, 128)].reshape(rows, 128)
            vals = held[:, :, :, :, pl.ds(D + 128 * pair, 128)].reshape(rows, 128)
            outs = []
            for side, sided in enumerate(head_sides(queries[:, pl.ds(128 * pair, 128)])):
                scores = dot(keys, sided, NT) * SCORE_SCALE + bias_ref[...]
                peak = jnp.max(scores, 0, keepdims=True)
                powers = jnp.exp(scores - peak)
                total = jnp.sum(powers, 0, keepdims=True)
                total_ref[pair, side : side + 1, :] = peak + jnp.log(total)
                outs.append(dot((powers * (1.0 / total)).astype(BF), vals, TN))
            out_ref[:, pl.ds(128 * pair, 128)] = jnp.where(lane < HEAD, outs[0], outs[1]).astype(BF)

    count = len(PAIR_GROUPS)
    for number in range(count):
        start_all(step(number, 0))
    for number in range(count):
        wait_all(step(number, 0))
        start_all(step(number, 1))
    for time in range(count + 2):
        if time < count:
            wait_all(step(time, 1))
            start_all(step(time, 2))
        if time >= 2:
            wait_all(step(time - 2, 2))
            compute(time - 2)
    keep = pltpu.make_async_copy(held, kept_ref, load_sem.at[0])
    keep.start()
    keep.wait()


def attend_gather(joined, bias):
    rows = joined.shape[0]
    _, n_y, n_x, n_core = grid_sizes()
    lead = (n_y, n_x, n_core)
    pairs, count = D // 128, len(PAIR_GROUPS)
    mixed, log_total, kept = pl.pallas_call(
        attend_gather_kernel,
        out_shape=[
            jax.ShapeDtypeStruct((rows, D), BF),
            jax.ShapeDtypeStruct((pairs, 2, rows), jnp.float32),
            jax.ShapeDtypeStruct(lead + (rows, 2 * D), BF),
        ],
        in_specs=[ANY, whole_block(bias.shape)],
        out_specs=[whole_block((rows, D)), whole_block((pairs, 2, rows)), ANY],
        scratch_shapes=[
            pltpu.VMEM(lead + (rows, 2 * D), BF),
            pltpu.VMEM((rows, D), BF),
            pltpu.SemaphoreType.DMA((3 * count, 2)),
            pltpu.SemaphoreType.DMA((3 * count, 2)),
            pltpu.SemaphoreType.DMA((2,)),
        ],
        compiler_params=pltpu.CompilerParams(collective_id=2, has_side_effects=True, vmem_limit_bytes=32 << 20),
        name="attend_gather",
    )(joined, bias)
    return mixed, log_total, kept.reshape(-1, 2 * D)


def attend_scatter_kernel(joined_ref, held_ref, bias_ref, total_ref, grad_ref, gq_ref, own_ref, *scratch):
    queries, part, from_core, from_first, from_second, send_sem, recv_sem, load_sem = scratch
    place = grid_place()
    _, y, x, core = place
    load = pltpu.make_async_copy(joined_ref.at[:, pl.ds(0, D)], queries, load_sem.at[0])
    load.start()
    greet_plane(place)
    load.wait()
    rows = bias_ref.shape[0]
    lane = lax.broadcasted_iota(jnp.int32, (queries.shape[0], 128), 1)

    def compute(number):
        for pair in BACK_GROUPS[number][0]:
            columns, beside = pl.ds(128 * pair, 128), pl.ds(D + 128 * pair, 128)
            keys = held_ref[:, :, :, :, columns].reshape(rows, 128)
            vals = held_ref[:, :, :, :, beside].reshape(rows, 128)
            q_sides, g_sides = head_sides(queries[:, columns]), head_sides(grad_ref[:, columns])
            grad_q, grad_k, grad_v = [], 0.0, 0.0
            for side in range(2):
                scores = dot(keys, q_sides[side], NT) * SCORE_SCALE + bias_ref[...]
                probs = jnp.exp(scores - total_ref[pair, side : side + 1, :])
                grad_probs = dot(vals, g_sides[side], NT)
                delta = jnp.sum(probs * grad_probs, 0, keepdims=True)
                grad_scores = (probs * (grad_probs - delta)).astype(BF)
                grad_v = grad_v + dot(probs.astype(BF), g_sides[side], NN)
                grad_k = grad_k + dot(grad_scores, q_sides[side], NN)
                grad_q.append(dot(grad_scores, keys, TN))
            gq_ref[:, columns] = (jnp.where(lane < HEAD, grad_q[0], grad_q[1]) * SCORE_SCALE).astype(BF)
            shape = part.shape[:4] + (128,)
            part[:, :, :, :, columns] = (grad_k * SCORE_SCALE).astype(BF).reshape(shape)
            part[:, :, :, :, beside] = grad_v.astype(BF).reshape(shape)

    def step(number, k):
        pairs, route = BACK_GROUPS[number]
        columns = group_columns(pairs)
        if k == 0:
            axis = 3
            sources = [part.at[:, :, 1 - core, :, c] for c in columns]
            targets = [from_core.at[:, :, :, c] for c in columns]
        elif k == 1:
            axis = route[1]
            sources = [(part.at[1 - y, :, core, :, c] if axis == 1 else part.at[:, 1 - x, core, :, c]) for c in columns]
            targets = [from_first.at[:, :, c] for c in columns]
        else:
            axis = route[0]
            sources = [(part.at[1 - y, x, core, :, c] if axis == 1 else part.at[y, 1 - x, core, :, c]) for c in columns]
            targets = [from_second.at[:, c] for c in columns]
        return plane_copies(place, axis, sources, targets, send_sem, recv_sem, 3 * number + k)

    def add(number, k):
        pairs, route = BACK_GROUPS[number]
        wait_all(step(number, k))
        for c in group_columns(pairs):
            if k == 0:
                part[:, :, core, :, c] = part[:, :, core, :, c] + from_core[:, :, :, c]
            elif k == 1 and route[1] == 1:
                part[y, :, core, :, c] = part[y, :, core, :, c] + from_first[:, :, c]
            elif k == 1:
                part[:, x, core, :, c] = part[:, x, core, :, c] + from_first[:, :, c]
            else:
                own_ref[:, c] = part[y, x, core, :, c] + from_second[:, c]

    count = len(BACK_GROUPS)
    for time in range(count + BACK_LAGS[-1]):
        if time < count:
            compute(time)
            start_all(step(time, 0))
        for k, lag in enumerate(BACK_LAGS):
            number = time - lag
            if 0 <= number < count:
                add(number, k)
                if k < 2:
                    start_all(step(number, k + 1))


def attend_scatter(joined, keys_vals, bias, log_total, grad_mixed):
    rows = joined.shape[0]
    _, n_y, n_x, n_core = grid_sizes()
    lead = (n_y, n_x, n_core)
    count = len(BACK_GROUPS)
    held = keys_vals.reshape(lead + (rows, 2 * D))
    return pl.pallas_call(
        attend_scatter_kernel,
        out_shape=[jax.ShapeDtypeStruct((rows, D), BF), jax.ShapeDtypeStruct((rows, 2 * D), BF)],
        in_specs=[ANY] + [whole_block(v.shape) for v in (held, bias, log_total, grad_mixed)],
        out_specs=[whole_block((rows, D)), whole_block((rows, 2 * D))],
        scratch_shapes=[
            pltpu.VMEM((rows, D), BF),
            pltpu.VMEM(lead + (rows, 2 * D), BF),
            pltpu.VMEM((n_y, n_x, rows, 2 * D), BF),
            pltpu.VMEM((2, rows, 2 * D), BF),
            pltpu.VMEM((rows, 2 * D), BF),
            pltpu.SemaphoreType.DMA((3 * count, 2)),
            pltpu.SemaphoreType.DMA((3 * count, 2)),
            pltpu.SemaphoreType.DMA((1,)),
        ],
        compiler_params=pltpu.CompilerParams(collective_id=3, has_side_effects=True, vmem_limit_bytes=40 << 20),
        name="attend_scatter",
    )(joined, held, bias, log_total, grad_mixed)


def gelu_parts(values):
    size = jnp.abs(values)
    bell = jnp.exp(-0.5 * size * size)
    t = 1.0 / (1.0 + (0.3275911 * 0.7071067811865476) * size)
    tail = t * (0.127414796 + t * (-0.142248368 + t * (0.7107068705 + t * (-0.7265760135 + t * 0.5307027145)))) * bell
    share = jnp.where(values >= 0, 1.0 - tail, tail)
    return values * share, share + values * (0.3989422804014327 * bell)


def norm_parts(values):
    scale = lax.rsqrt(jnp.mean(values * values, -1, keepdims=True) + EPSILON)
    return values * scale, scale


def norm_gradient(values, norm_gain, upstream):
    unit, scale = norm_parts(values)
    inner = upstream * norm_gain
    back = scale * (inner - unit * jnp.mean(inner * unit, -1, keepdims=True))
    return back, jnp.sum(upstream * unit, 0, keepdims=True)


def hidden_block(rows):
    return 2 * D if rows <= 128 else D


def ffn_kernel(stream_ref, gain_ref, in_ref, down_ref, out_ref, inputs_ref, hidden_ref, slope_ref):
    step = pl.program_id(0)

    @pl.when(step == 0)
    def _():
        stream = stream_ref[...].astype(jnp.float32)
        out_ref[...] = stream
        inputs_ref[...] = (norm_parts(stream)[0] * gain_ref[...].astype(jnp.float32)).astype(BF)

    value, slope = gelu_parts(dot(inputs_ref[...], in_ref[...], NN))
    hidden = value.astype(BF)
    hidden_ref[...] = hidden
    slope_ref[...] = slope.astype(BF)
    out_ref[...] += dot(hidden, down_ref[...], NN)


def ffn(stream, norm_gain, weight_in, weight_down):
    rows = stream.shape[0]
    block = hidden_block(rows)
    still = lambda j: (0, 0)
    return pl.pallas_call(
        ffn_kernel,
        grid=(FF // block,),
        out_shape=[
            jax.ShapeDtypeStruct((rows, D), jnp.float32),
            jax.ShapeDtypeStruct((rows, D), BF),
            jax.ShapeDtypeStruct((rows, FF), BF),
            jax.ShapeDtypeStruct((rows, FF), BF),
        ],
        in_specs=[
            pl.BlockSpec((rows, D), still),
            pl.BlockSpec((1, D), still),
            pl.BlockSpec((D, block), lambda j: (0, j)),
            pl.BlockSpec((block, D), lambda j: (j, 0)),
        ],
        out_specs=[
            pl.BlockSpec((rows, D), still),
            pl.BlockSpec((rows, D), still),
            pl.BlockSpec((rows, block), lambda j: (0, j)),
            pl.BlockSpec((rows, block), lambda j: (0, j)),
        ],
        cost_estimate=pl.CostEstimate(
            flops=4 * rows * D * FF, bytes_accessed=4 * D * FF + 4 * rows * FF + 8 * rows * D, transcendentals=rows * FF
        ),
        name="ffn",
    )(stream, norm_gain, weight_in, weight_down)


def ffn_back_kernel(grad_ref, stream_ref, gain_ref, slope_ref, in_ref, down_ref, out_ref, low_ref, pre_ref, gain_out, total):
    step = pl.program_id(0)

    @pl.when(step == 0)
    def _():
        low_ref[...] = grad_ref[...].astype(BF)
        total[...] = jnp.zeros_like(total)

    pre = (dot(low_ref[...], down_ref[...], NT) * slope_ref[...].astype(jnp.float32)).astype(BF)
    pre_ref[...] = pre
    total[...] += dot(pre, in_ref[...], NT)

    @pl.when(step == pl.num_programs(0) - 1)
    def _():
        back, gain = norm_gradient(stream_ref[...].astype(jnp.float32), gain_ref[...].astype(jnp.float32), total[...])
        out_ref[...] = grad_ref[...].astype(jnp.float32) + back
        gain_out[...] = gain


def ffn_back(upstream, stream, norm_gain, slope, weight_in, weight_down):
    rows = stream.shape[0]
    block = hidden_block(rows)
    still = lambda j: (0, 0)
    return pl.pallas_call(
        ffn_back_kernel,
        grid=(FF // block,),
        out_shape=[
            jax.ShapeDtypeStruct((rows, D), jnp.float32),
            jax.ShapeDtypeStruct((rows, D), BF),
            jax.ShapeDtypeStruct((rows, FF), BF),
            jax.ShapeDtypeStruct((1, D), jnp.float32),
        ],
        in_specs=[
            pl.BlockSpec((rows, D), still),
            pl.BlockSpec((rows, D), still),
            pl.BlockSpec((1, D), still),
            pl.BlockSpec((rows, block), lambda j: (0, j)),
            pl.BlockSpec((D, block), lambda j: (0, j)),
            pl.BlockSpec((block, D), lambda j: (j, 0)),
        ],
        out_specs=[
            pl.BlockSpec((rows, D), still),
            pl.BlockSpec((rows, D), still),
            pl.BlockSpec((rows, block), lambda j: (0, j)),
            pl.BlockSpec((1, D), still),
        ],
        scratch_shapes=[pltpu.VMEM((rows, D), jnp.float32)],
        cost_estimate=pl.CostEstimate(
            flops=4 * rows * D * FF, bytes_accessed=4 * D * FF + 4 * rows * FF + 16 * rows * D, transcendentals=0
        ),
        name="ffn_back",
    )(upstream, stream, norm_gain, slope, weight_in, weight_down)


def spread_matrix(devices):
    rows = D // devices
    source = lax.broadcasted_iota(jnp.int32, (D, devices * ROOM), 0)
    target = lax.broadcasted_iota(jnp.int32, (D, devices * ROOM), 1)
    return jnp.where((target // ROOM * rows + target % ROOM == source) & (target % ROOM < rows), 1.0, 0.0).astype(BF)


def late_blocks(late, tall):
    devices = late.shape[0]
    per_block = D // tall
    return [
        pl.BlockSpec((devices, ROOM, D), lambda j: (0, 4 + j, 0)),
        pl.BlockSpec((per_block, 4 * ROOM, D), lambda j: (j, 0, 0)),
    ]


def late_in_block(ref):
    return ref[...].reshape(-1, D)


def late_down_block(ref):
    values = ref[...]
    return values[:, : D // values.shape[0]].reshape(D, D)


def late_ffn_kernel(stream_ref, gain_ref, spread_ref, in_ref, down_ref, out_ref, inputs_ref, hidden_ref, slope_ref, spread):
    step = pl.program_id(0)

    @pl.when(step == 0)
    def _():
        stream = stream_ref[...].astype(jnp.float32)
        out_ref[...] = stream
        inputs = (norm_parts(stream)[0] * gain_ref[...].astype(jnp.float32)).astype(BF)
        inputs_ref[...] = inputs
        spread[...] = dot(inputs, spread_ref[...], NN).astype(BF)

    value, slope = gelu_parts(dot(spread[...], late_in_block(in_ref), NN))
    hidden = value.astype(BF)
    hidden_ref[...] = hidden
    slope_ref[...] = slope.astype(BF)
    out_ref[...] += dot(hidden, late_down_block(down_ref), NN)


def late_ffn(stream, norm_gain, spread, late, tall):
    rows = stream.shape[0]
    still = lambda j: (0, 0)
    return pl.pallas_call(
        late_ffn_kernel,
        grid=(FF // D,),
        out_shape=[
            jax.ShapeDtypeStruct((rows, D), jnp.float32),
            jax.ShapeDtypeStruct((rows, D), BF),
            jax.ShapeDtypeStruct((rows, FF), BF),
            jax.ShapeDtypeStruct((rows, FF), BF),
        ],
        in_specs=[pl.BlockSpec((rows, D), still), pl.BlockSpec((1, D), still), pl.BlockSpec(spread.shape, still)]
        + late_blocks(late, tall),
        out_specs=[
            pl.BlockSpec((rows, D), still),
            pl.BlockSpec((rows, D), still),
            pl.BlockSpec((rows, D), lambda j: (0, j)),
            pl.BlockSpec((rows, D), lambda j: (0, j)),
        ],
        scratch_shapes=[pltpu.VMEM((rows, spread.shape[1]), BF)],
        cost_estimate=pl.CostEstimate(flops=4 * rows * D * FF, bytes_accessed=5 * D * FF, transcendentals=rows * FF),
        name="late_ffn",
    )(stream, norm_gain, spread, late, late)


def late_back_kernel(grad_ref, stream_ref, gain_ref, spread_ref, slope_ref, in_ref, down_ref, out_ref, low_ref, pre_ref, gain_out, total):
    step = pl.program_id(0)

    @pl.when(step == 0)
    def _():
        low_ref[...] = grad_ref[...].astype(BF)
        total[...] = jnp.zeros_like(total)

    pre = (dot(low_ref[...], late_down_block(down_ref), NT) * slope_ref[...].astype(jnp.float32)).astype(BF)
    pre_ref[...] = pre
    total[...] += dot(pre, late_in_block(in_ref), NT)

    @pl.when(step == pl.num_programs(0) - 1)
    def _():
        whole = total[...]
        high = whole.astype(BF)
        rest = (whole - high.astype(jnp.float32)).astype(BF)
        inner = dot(high, spread_ref[...], NT) + dot(rest, spread_ref[...], NT)
        back, gain = norm_gradient(stream_ref[...].astype(jnp.float32), gain_ref[...].astype(jnp.float32), inner)
        out_ref[...] = grad_ref[...].astype(jnp.float32) + back
        gain_out[...] = gain


def late_ffn_back(upstream, stream, norm_gain, slope, spread, late, tall):
    rows = stream.shape[0]
    still = lambda j: (0, 0)
    return pl.pallas_call(
        late_back_kernel,
        grid=(FF // D,),
        out_shape=[
            jax.ShapeDtypeStruct((rows, D), jnp.float32),
            jax.ShapeDtypeStruct((rows, D), BF),
            jax.ShapeDtypeStruct((rows, FF), BF),
            jax.ShapeDtypeStruct((1, D), jnp.float32),
        ],
        in_specs=[
            pl.BlockSpec((rows, D), still),
            pl.BlockSpec((rows, D), still),
            pl.BlockSpec((1, D), still),
            pl.BlockSpec(spread.shape, still),
            pl.BlockSpec((rows, D), lambda j: (0, j)),
        ]
        + late_blocks(late, tall),
        out_specs=[
            pl.BlockSpec((rows, D), still),
            pl.BlockSpec((rows, D), still),
            pl.BlockSpec((rows, D), lambda j: (0, j)),
            pl.BlockSpec((1, D), still),
        ],
        scratch_shapes=[pltpu.VMEM((rows, spread.shape[1]), jnp.float32)],
        cost_estimate=pl.CostEstimate(flops=4 * rows * D * FF, bytes_accessed=5 * D * FF, transcendentals=0),
        name="late_ffn_back",
    )(upstream, stream, norm_gain, spread, slope, late, late)


def shifted(x, axis, by):
    count = lax.axis_size(axis)
    pairs = [(i, i + by) for i in range(count) if 0 <= i + by < count]
    return lax.ppermute(x, axis, pairs)


def slab_term(left, right):
    return dot(left, right, TN)


def normed(values, norm_gain):
    return (norm_parts(values)[0] * norm_gain.astype(jnp.float32)).astype(BF)


def norm_back(values, norm_gain, upstream):
    return norm_gradient(values, norm_gain.astype(jnp.float32), upstream)


def self_forward(stream, norm_gain, weight_qkv, weight_out, bias):
    inputs = normed(stream, norm_gain)
    joined = dot(inputs, weight_qkv, NN).astype(BF)
    if grid_sizes() == (4, 2, 2, 2):
        mixed, log_total, keys_vals = attend_gather(joined, bias)
    else:
        keys_vals = lax.all_gather(joined[:, D:], "seq", axis=0, tiled=True)
        mixed, log_total = attend(joined, keys_vals, bias)
    return stream + dot(mixed, weight_out, NN), (stream, inputs, joined, keys_vals, log_total, mixed)


def self_back(stored, norm_gain, weight_qkv, weight_out, bias, upstream, covered):
    stream, inputs, joined, keys_vals, log_total, mixed = stored
    grad_low = upstream.astype(BF)
    grad_mixed = dot(grad_low, weight_out, NT).astype(BF)
    if grid_sizes() == (4, 2, 2, 2) and not covered:
        grad_queries, own_pairs = attend_scatter(joined, keys_vals, bias, log_total, grad_mixed)
    else:
        grad_queries, grad_pairs = attend_back(joined, keys_vals, bias, log_total, grad_mixed)
        own_pairs = lax.psum_scatter(grad_pairs, "seq", scatter_dimension=0, tiled=True)
    grad_joined = jnp.concatenate([grad_queries, own_pairs], -1)
    back, gain_grad = norm_back(stream, norm_gain, dot(grad_joined, weight_qkv, NT))
    return upstream + back, gain_grad, ((inputs, grad_joined), (mixed, grad_low))


def causal_bias(queries, keys):
    offset = lax.axis_index("seq") * queries
    key_place = lax.broadcasted_iota(jnp.int32, (keys, queries), 0)
    query_place = offset + lax.broadcasted_iota(jnp.int32, (keys, queries), 1)
    return jnp.where(key_place <= query_place, 0.0, MASKED_SCORE).astype(jnp.float32)


def span_bias(prior_flag, queries):
    spans = prior_flag.shape[0]
    keys = spans * NEIGH * RET
    key_span = lax.broadcasted_iota(jnp.int32, (keys, queries), 0) // (NEIGH * RET)
    query_span = lax.broadcasted_iota(jnp.int32, (keys, queries), 1) // SPAN
    allowed = jnp.repeat(prior_flag.reshape(-1), RET)[:, None] > 0.5
    return jnp.where(key_span == query_span, jnp.where(allowed, 0.0, MASKED_SCORE), 2 * MASKED_SCORE).astype(jnp.float32)


def row_gate(prior_flag):
    return jnp.repeat(jnp.max(prior_flag, -1).astype(jnp.float32), SPAN)[:, None]


def prior_spans(encoded, keep_flag):
    last_enc, last_flag = shifted((encoded[-1:], keep_flag[-1:]), "seq", 1)
    return jnp.concatenate([last_enc, encoded[:-1]], 0), jnp.concatenate([last_flag, keep_flag[:-1]], 0)


def cross_forward(stream, encoded, keep_flag, norm_gain, weight_q, weight_kv, weight_out):
    prior_enc, prior_flag = prior_spans(encoded, keep_flag)
    prior_enc = prior_enc.reshape(-1, D)
    inputs = normed(stream, norm_gain)
    queries = dot(inputs, weight_q, NN).astype(BF)
    keys_vals = jnp.concatenate([dot(prior_enc, side, NN).astype(BF) for side in weight_kv], 1)
    bias = span_bias(prior_flag, stream.shape[0])
    mixed, log_total = attend(queries, keys_vals, bias)
    branch = row_gate(prior_flag) * dot(mixed, weight_out, NN)
    return stream + branch, (stream, inputs, prior_enc, prior_flag, queries, keys_vals, bias, log_total, mixed)


def cross_back(stored, norm_gain, weight_q, weight_kv, weight_out, upstream):
    stream, inputs, prior_enc, prior_flag, queries, keys_vals, bias, log_total, mixed = stored
    grad_low = (upstream * row_gate(prior_flag)).astype(BF)
    grad_mixed = dot(grad_low, weight_out, NT).astype(BF)
    grad_queries, grad_pairs = attend_back(queries, keys_vals, bias, log_total, grad_mixed)
    grad_prior = dot(grad_pairs[:, :D], weight_kv[0], NT) + dot(grad_pairs[:, D:], weight_kv[1], NT)
    grad_prior = grad_prior.reshape(prior_flag.shape[0], NEIGH * RET, D)
    from_next = shifted(grad_prior[:1].astype(BF), "seq", -1).astype(jnp.float32)
    encoded_grad = jnp.concatenate([grad_prior[1:], from_next], 0).reshape(-1, D)
    back, gain_grad = norm_back(stream, norm_gain, dot(grad_queries, weight_q, NT))
    pairs = ((inputs, grad_queries), (prior_enc, grad_pairs), (mixed, grad_low))
    return upstream + back, gain_grad, pairs, encoded_grad


def on_device(
    tokens,
    retrieved,
    span_doc,
    neigh_doc,
    cotangent,
    dec_gain,
    dec_qkv,
    dec_out,
    dec_in,
    dec_down,
    cca_gain,
    cca_q,
    cca_kv,
    cca_out,
    enc_gain,
    enc_in,
    enc_down,
    enc_final,
):
    assert tokens.shape[0] == 1
    rows = cca_q.shape[0]
    own_gains = jnp.concatenate([dec_gain.reshape(4, rows), cca_gain[None], enc_gain, enc_final[None]], 0).T
    own_gains = jnp.pad(own_gains, ((0, 0), (0, 120)))
    neighbours = retrieved.reshape(-1, D)
    full = gather_weights(
        neighbours, enc_in, enc_down, dec_qkv, dec_out, dec_in, dec_down, cca_q, cca_kv, cca_out, own_gains
    )
    gains = full["gains"].T
    attn_gain, ffn_gain = (gains[0:1], gains[2:3]), (gains[1:2], gains[3:4])
    cross_gain, encode_gain, final_gain = gains[4:5], (gains[5:6], gains[6:7]), gains[7:8]
    cross_weights = (cross_gain, full["cca_q"], full["cca_kv"], full["cca_out"])
    queries = tokens.shape[1]
    bias = causal_bias(queries, queries * lax.axis_size("seq"))

    encoder, encoder_kept, encoded = full["encoder"]
    encoded = encoded.reshape(span_doc.shape[1], NEIGH * RET, D)
    keep_flag = (neigh_doc[0] != span_doc[0][:, None]).astype(BF)

    stream = tokens[0].astype(jnp.float32)
    attn_kept, ffn_kept = [], []
    for layer in range(DEC_LAYERS):
        stream, kept = self_forward(stream, attn_gain[layer], full["dec_qkv"][layer], full["dec_out"][layer], bias)
        attn_kept.append(kept)
        if layer == 0:
            stream, cross_kept = cross_forward(stream, encoded, keep_flag, *cross_weights)
        before = stream
        if full["dec_in"][layer] is None:
            late, tall = full["dec_down"][layer], dec_down.shape[1]
            spread = spread_matrix(late.shape[0])
            stream, inputs, hidden, slope = late_ffn(before, ffn_gain[layer], spread, late, tall)
        else:
            stream, inputs, hidden, slope = ffn(before, ffn_gain[layer], full["dec_in"][layer], full["dec_down"][layer])
        ffn_kept.append((before, inputs, hidden, slope))
    result = stream.astype(BF)

    upstream = cotangent[0].astype(jnp.float32)
    attn_gain_g, ffn_gain_g = [None] * DEC_LAYERS, [None] * DEC_LAYERS
    attn_pairs, ffn_pairs = [None] * DEC_LAYERS, [None] * DEC_LAYERS
    for layer in reversed(range(DEC_LAYERS)):
        before, inputs, hidden, slope = ffn_kept[layer]
        if full["dec_in"][layer] is None:
            back = late_ffn_back(upstream, before, ffn_gain[layer], slope, spread, late, tall)
        else:
            back = ffn_back(upstream, before, ffn_gain[layer], slope, full["dec_in"][layer], full["dec_down"][layer])
        upstream, grad_low, grad_pre, ffn_gain_g[layer] = back
        ffn_pairs[layer] = ((inputs, grad_pre), (grad_low, hidden))
        if layer == 0:
            upstream, cross_gain_g, cross_pairs, encoded_grad = cross_back(cross_kept, *cross_weights, upstream)
        upstream, attn_gain_g[layer], attn_pairs[layer] = self_back(
            attn_kept[layer], attn_gain[layer], full["dec_qkv"][layer], full["dec_out"][layer], bias, upstream, layer == 0
        )

    enc_upstream, final_gain_g = norm_back(encoder, final_gain, encoded_grad)
    enc_gain_g, enc_pairs = [None] * ENC_LAYERS, [None] * ENC_LAYERS
    for layer in reversed(range(ENC_LAYERS)):
        before, inputs, hidden, slope = encoder_kept[layer]
        enc_upstream, grad_low, grad_pre, enc_gain_g[layer] = ffn_back(
            enc_upstream, before, encode_gain[layer], slope, full["enc_in"][layer], full["enc_down"][layer]
        )
        enc_pairs[layer] = ((inputs, grad_pre), (grad_low, hidden))

    pair_list = []
    for layer in range(DEC_LAYERS):
        pair_list += list(attn_pairs[layer]) + list(ffn_pairs[layer])
    pair_list += list(cross_pairs)
    for layer in range(ENC_LAYERS):
        pair_list += list(enc_pairs[layer])
    gain_list = []
    for layer in range(DEC_LAYERS):
        gain_list += [attn_gain_g[layer], ffn_gain_g[layer]]
    gain_list = [gain.reshape(D) for gain in gain_list + [cross_gain_g] + enc_gain_g + [final_gain_g]]

    grads = sum_gradients(pair_list, gain_list, rows)
    (enc_in_g, enc_down_g, dec_qkv_g, dec_out_g, dec_in_g, dec_down_g, cross_q_g, cross_kv_g, cross_out_g, gain_cols) = grads
    gain_rows = gain_cols[:, :8].T
    return (
        result[None],
        upstream[None],
        gain_rows[:4].reshape(2, 2, rows),
        dec_qkv_g,
        dec_out_g,
        dec_in_g,
        jnp.swapaxes(dec_down_g, 1, 2),
        gain_rows[4],
        cross_q_g,
        cross_kv_g,
        cross_out_g,
        gain_rows[5:7],
        enc_in_g,
        jnp.swapaxes(enc_down_g, 1, 2),
        gain_rows[7],
    )


def sum_plainly(pair_list, gain_list):
    blocks = [slab_term(left, right) for left, right in pair_list] + [vector[:, None] for vector in gain_list]
    owned = lax.psum_scatter(
        jnp.concatenate(blocks, 1).astype(BF), ("dp", "seq"), scatter_dimension=0, tiled=True
    ).astype(jnp.float32)
    pieces, cursor = [], 0
    for _, right in pair_list:
        pieces.append(owned[:, cursor : cursor + right.shape[-1]])
        cursor += right.shape[-1]
    two = lambda first, second: jnp.stack([pieces[first], pieces[second]])
    return [
        two(11, 13), two(12, 14), two(0, 4), two(1, 5), two(2, 6), two(3, 7), pieces[8], pieces[9], pieces[10], owned[:, cursor:]
    ]


def sum_gradients(pair_list, gain_list, rows):
    sizes = grid_sizes()
    if rows % 4 or sizes != (4, 2, 2, 2):
        return sum_plainly(pair_list, gain_list)
    operands = [x.reshape(-1, x.shape[-1]) for pair in pair_list for x in pair]
    gains = jnp.pad(jnp.stack(gain_list).astype(BF).T, ((0, 0), (0, 128 - len(gain_list))))
    return reduce_gradients(operands, gains, rows)


def solution(mesh):
    return jax.shard_map(
        on_device,
        mesh=mesh,
        in_specs=(
            P("dp", "seq", None),
            P("dp", "seq", None, None, None),
            P("dp", "seq"),
            P("dp", "seq", None),
            P("dp", "seq", None),
            P(None, None, ("dp", "seq")),
            P(None, ("dp", "seq"), None),
            P(None, ("dp", "seq"), None),
            P(None, ("dp", "seq"), None),
            P(None, ("dp", "seq"), None),
            P(("dp", "seq")),
            P(("dp", "seq"), None),
            P(("dp", "seq"), None),
            P(("dp", "seq"), None),
            P(None, ("dp", "seq")),
            P(None, ("dp", "seq"), None),
            P(None, ("dp", "seq"), None),
            P(("dp", "seq")),
        ),
        out_specs=(
            P("dp", "seq", None),
            P("dp", "seq", None),
            P(None, None, ("dp", "seq")),
            P(None, ("dp", "seq"), None),
            P(None, ("dp", "seq"), None),
            P(None, ("dp", "seq"), None),
            P(None, None, ("dp", "seq")),
            P(("dp", "seq")),
            P(("dp", "seq"), None),
            P(("dp", "seq"), None),
            P(("dp", "seq"), None),
            P(None, ("dp", "seq")),
            P(None, ("dp", "seq"), None),
            P(None, None, ("dp", "seq")),
            P(("dp", "seq")),
        ),
        check_vma=False,
    )
```
